32 devices in a mesh: fsdp: 16 (over z, y, core), seq: 2 (over x).
Axes of the slice: x: 2, y: 2, z: 4, core: 2. Of those that a mesh axis runs over, the one named last changes fastest.
Arguments:
- tokens: bfloat16 [16, 1024, 1024], P('fsdp', 'seq'), may hold values from -6 to 6
- condition: bfloat16 [16, 1024], P('fsdp'), may hold values from -6 to 6
- w_ada: bfloat16 [1024, 6144], P('fsdp'), may hold values from -0.1875 to 0.1875
- b_ada: bfloat16 [6144], P('fsdp'), may hold values from -3 to 3
- w_qkv: bfloat16 [1024, 3072], P('fsdp'), may hold values from -0.1875 to 0.1875
- b_qv: bfloat16 [2048], P('fsdp'), may hold values from -1.1953125 to 1.1953125
- w_proj: bfloat16 [1024, 1024], P('fsdp'), may hold values from -0.1875 to 0.1875
- b_proj: bfloat16 [1024], P('fsdp'), may hold values from -1.1953125 to 1.1953125
- w_fc1: bfloat16 [1024, 4096], P('fsdp'), may hold values from -0.1875 to 0.1875
- b_fc1: bfloat16 [4096], P('fsdp'), may hold values from -1.1953125 to 1.1953125
- w_fc2: bfloat16 [4096, 1024], P('fsdp'), may hold values from -0.09375 to 0.09375
- b_fc2: bfloat16 [1024], P('fsdp'), may hold values from -1.1953125 to 1.1953125
- cotangent: bfloat16 [16, 1024, 1024], P('fsdp', 'seq'), may hold values from -6 to 6
Outputs:
- out_tokens: bfloat16 [16, 1024, 1024], P('fsdp', 'seq')
- grad_tokens: float32 [16, 1024, 1024], P('fsdp', 'seq')
- grad_condition: float32 [16, 1024], P('fsdp')
- grad_w_ada: float32 [1024, 6144], P('fsdp')
- grad_b_ada: float32 [6144], P('fsdp')
- grad_w_qkv: float32 [1024, 3072], P('fsdp')
- grad_b_qv: float32 [2048], P('fsdp')
- grad_w_proj: float32 [1024, 1024], P('fsdp')
- grad_b_proj: float32 [1024], P('fsdp')
- grad_w_fc1: float32 [1024, 4096], P('fsdp')
- grad_b_fc1: float32 [4096], P('fsdp')
- grad_w_fc2: float32 [4096, 1024], P('fsdp')
- grad_b_fc2: float32 [1024], P('fsdp')
The draws below stay inside these ranges and needn't reach their ends.
All inputs are finite; a program needn't handle non-finite values.
Results may differ from the reference program's by a relative error of at most 0.018.
The reference program's roundings to bfloat16 on the way count: a program that leaves them out, or rounds other values in their place, can miss the bound.
Values may be sent and summed in bfloat16 or wider, within the bound.
A program may use at most 256 MiB of HBM per device.

```python
import jax
import jax.numpy as jnp
from jax import lax

D = 1024
H = 16
HD = 64
FF = 4096
L = 1024
LATENTS = 16


def spiked(entries, key, source, target, parts, factor):
    owner, partner = [(jnp.arange(entries.shape[position]) // (entries.shape[position] // parts)).reshape([-1 if axis == position else 1 for axis in range(entries.ndim)]) for position in (source, target)]
    chosen = jax.random.permutation(key, parts)[partner]
    strong = (owner == chosen) | (owner == (partner + parts // 2) % parts)
    return jnp.where(strong, factor * entries, entries)


def level_of(stream_key, dims, shards, smallest, largest):
    gain, own = 1.0, jax.random.fold_in(stream_key, 6)
    for axis_at, blocks in shards:
        heights = jnp.exp(jax.random.uniform(jax.random.fold_in(own, axis_at), (blocks,), jnp.float32, smallest / len(shards), largest / len(shards)))
        gain = gain * jnp.repeat(heights, dims[axis_at] // blocks).reshape([-1 if axis == axis_at else 1 for axis in range(len(dims))])
    return gain


def gaussian(stream_key, shape, spread, most, cuts=(), dtype=jnp.bfloat16):
    array = jax.random.normal(stream_key, shape, jnp.float32) * spread
    if len(cuts) > 0:
        array = level_of(stream_key, shape, cuts, -0.22, 0.18) * array
    return jnp.clip(array, min=-most, max=most).astype(dtype)


def bell_draw_with(own_key, dims, spread, bound, cuts, heavy, kind=jnp.bfloat16):
    values = spread * jax.random.normal(own_key, dims, jnp.float32)
    if cuts:
        values = values * level_of(own_key, dims, cuts, -0.22, 0.18)
    return jnp.clip(spiked(values, jax.random.fold_in(own_key, 3), *heavy), -bound, bound).astype(kind)


def setup_inputs(seed: int = 0) -> dict:
    keys = jax.random.split(jax.random.key(seed), 14)
    return {
        "tokens": gaussian(keys[0], (LATENTS, L, D), 1.0, 6.0, ((0, 16), (1, 2))),
        "condition": gaussian(keys[1], (LATENTS, D), 1.0, 6.0, ((0, 16),)),
        "w_ada": gaussian(keys[2], (D, 6 * D), D ** -0.5, 0.1875, ((0, 16),)),
        "b_ada": gaussian(keys[3], (6 * D,), 0.5, 3.0, ((0, 16),)),
        "w_qkv": gaussian(keys[4], (D, 3 * D), D ** -0.5, 0.1875, ((0, 16),)),
        "b_qv": gaussian(keys[5], (2 * D,), 0.2, 1.1953125, ((0, 16),)),
        "w_proj": gaussian(keys[6], (D, D), D ** -0.5, 0.1875, ((0, 16),)),
        "b_proj": gaussian(keys[7], (D,), 0.2, 1.1953125, ((0, 16),)),
        "w_fc1": gaussian(keys[8], (D, FF), D ** -0.5, 0.1875, ((0, 16),)),
        "b_fc1": gaussian(keys[9], (FF,), 0.2, 1.1953125, ((0, 16),)),
        "w_fc2": gaussian(keys[10], (FF, D), FF ** -0.5, 0.09375, ((0, 16),)),
        "b_fc2": gaussian(keys[11], (D,), 0.2, 1.1953125, ((0, 16),)),
        "cotangent": bell_draw_with(keys[12], (LATENTS, L, D), 1.0, 6.0, ((0, 16), (1, 2)), (0, 2, 16, 2.0)),
    }


@jax.custom_vjp
def low(v):
    return lax.optimization_barrier(v.astype(jnp.bfloat16)).astype(jnp.float32)

@jax.custom_vjp
def low_back(v):
    return v

def low_keep(v):
    return (low(v), None)

def low_pass(kept, grad):
    return (grad,)

def back_keep(v):
    return (v, None)

def back_low(kept, grad):
    return (low(grad),)
low.defvjp(low_keep, low_pass)
low_back.defvjp(back_keep, back_low)
highest = lax.Precision.HIGHEST
norm_eps = 1e-06

def layer_norm(values):
    center = values - lax.optimization_barrier(jnp.mean(values, axis=-1, keepdims=True))
    return center * lax.rsqrt(lax.optimization_barrier(jnp.mean(center * center, axis=-1, keepdims=True)) + norm_eps)

def head_attention(inputs):
    queries, keys_head, values_head = inputs
    raw_scores = low_back(jnp.dot(queries, keys_head.T, precision=highest))
    scores = raw_scores * HD ** (-0.5)
    shifted = jnp.exp(scores - lax.optimization_barrier(jnp.max(scores, axis=-1, keepdims=True)))
    attn_prob = low(shifted / lax.optimization_barrier(jnp.sum(shifted, axis=-1, keepdims=True)))
    return jnp.dot(attn_prob, values_head, precision=highest)

def layer_step(params, lat_tokens, lat_cond):
    w_ada_f, b_ada_f, w_qkv_f, b_qv_f, w_proj_f, b_proj_f, w_fc1_f, b_fc1_f, w_fc2_f, b_fc2_f = params
    lifted = low(jax.nn.silu(lat_cond))
    modulation = low_back(jnp.dot(lifted, w_ada_f, precision=highest) + b_ada_f)
    shift_one, scale_one, gate_one, shift_two, scale_two, gate_two = jnp.split(modulation, 6)
    hidden_one = low(layer_norm(lat_tokens) * (1.0 + scale_one) + shift_one)
    qkv_bias = jnp.concatenate([b_qv_f[:D], jnp.zeros_like(b_qv_f[:D]), b_qv_f[D:]])
    qkv = low_back(low(jnp.dot(hidden_one, w_qkv_f, precision=highest) + qkv_bias)).reshape(L, 3, H, HD)
    head_inputs = (jnp.transpose(qkv[:, 0], (1, 0, 2)), jnp.transpose(qkv[:, 1], (1, 0, 2)), jnp.transpose(qkv[:, 2], (1, 0, 2)))
    attended = lax.map(jax.checkpoint(head_attention), head_inputs)
    attended = low_back(low(jnp.transpose(attended, (1, 0, 2)).reshape(L, D)))
    branch = low_back(jnp.dot(attended, w_proj_f, precision=highest) + b_proj_f)
    middle = lat_tokens + gate_one * branch
    hidden_two = low(layer_norm(middle) * (1.0 + scale_two) + shift_two)
    pre_act = low_back(jnp.dot(hidden_two, w_fc1_f, precision=highest) + b_fc1_f)
    act_val = low(jax.nn.gelu(pre_act, approximate=True))
    mlp_out = low_back(jnp.dot(act_val, w_fc2_f, precision=highest) + b_fc2_f)
    return middle + gate_two * mlp_out

def reference(tokens, condition, w_ada, b_ada, w_qkv, b_qv, w_proj, b_proj, w_fc1, b_fc1, w_fc2, b_fc2, cotangent):
    params = (w_ada.astype(jnp.float32), b_ada.astype(jnp.float32), w_qkv.astype(jnp.float32), b_qv.astype(jnp.float32), w_proj.astype(jnp.float32), b_proj.astype(jnp.float32), w_fc1.astype(jnp.float32), b_fc1.astype(jnp.float32), w_fc2.astype(jnp.float32), b_fc2.astype(jnp.float32))

    def forward(weights, tokens_f, cond_f):

        def scan_step(carry, items):
            return (carry, jax.checkpoint(layer_step)(weights, items[0], items[1]))
        unused, outputs = lax.scan(scan_step, jnp.zeros((), jnp.float32), (tokens_f, cond_f))
        return outputs
    result, pull_back = jax.vjp(forward, params, tokens.astype(jnp.float32), condition.astype(jnp.float32))
    grads, grad_tokens, grad_condition = pull_back(cotangent.astype(jnp.float32))
    return (result.astype(jnp.bfloat16), grad_tokens, grad_condition, grads[0], grads[1], grads[2], grads[3], grads[4], grads[5], grads[6], grads[7], grads[8], grads[9])
```

```python
from functools import partial

import jax
import jax.numpy as jnp
from jax import lax
from jax.experimental import pallas as pl
from jax.experimental.pallas import tpu as pltpu
from jax.sharding import PartitionSpec as P

HD = 64
norm_eps = 1e-06
f32 = jnp.float32
bf16 = jnp.bfloat16
MESH = pl.DeviceIdType.MESH


def grid_of(n):
    b = 2 if n == 16 else 4
    return n // (2 * b), b


def nt(a, b):
    return lax.dot_general(a, b, (((1,), (1,)), ((), ())), preferred_element_type=f32)


def nn(a, b):
    return lax.dot_general(a, b, (((1,), (0,)), ((), ())), preferred_element_type=f32)


def tn(a, b):
    return lax.dot_general(a, b, (((0,), (0,)), ((), ())), preferred_element_type=f32)


def gather_weights(shards, chunks, n, s):
    A, B = grid_of(n)
    nc, ns = len(chunks), len(shards)
    NB = (A - 1) + (B - 1)
    steps = 2 * NB + 1

    def kern(*refs):
        ins, outs = refs[:ns], refs[ns : 2 * ns]
        own_sem, send, recv = refs[2 * ns :]
        me, x = lax.axis_index("fsdp"), lax.axis_index("seq")
        a, b, c = me // (2 * B), (me // 2) % B, me % 2

        def dev(a, b, c):
            return {"fsdp": (a * B + b) * 2 + c}

        apeers = [lax.rem(a + k, A) for k in range(1, A)]
        bpeers = [lax.rem(b + k, B) for k in range(1, B)]
        peers = [dev(p, b, c) for p in apeers] + [dev(a, p, c) for p in bpeers]
        peers.append(dev(a, b, 1 - c))
        if s == 2:
            peers.append({"seq": 1 - x})
        bar = pltpu.get_barrier_semaphore()
        for p in peers:
            pl.semaphore_signal(bar, inc=1, device_id=p, device_id_type=MESH)
        pl.semaphore_wait(bar, len(peers))
        owns = [pltpu.make_async_copy(ins[i], outs[i].at[a, b, c], own_sem.at[i]) for i in range(ns)]
        for o in owns:
            o.start()

        def cp(i, k, src, dst, d):
            r = pltpu.make_async_remote_copy(
                src_ref=src,
                dst_ref=dst,
                send_sem=send.at[i, k],
                recv_sem=recv.at[i, k],
                device_id=d,
                device_id_type=MESH,
            )
            r.start()
            return r

        za, zb, zx, zc = {}, {}, {}, {}

        def part(i):
            w, lo, sz, sh = chunks[i]
            if sh and s == 2:
                return w, pl.ds(pl.multiple_of(lo + x * (sz // 2), 128), sz // 2)
            return w, pl.ds(lo, sz)

        for i in range(nc):
            w, cols = part(i)
            za[i] = [
                cp(i, k, ins[w].at[:, cols], outs[w].at[a, b, c, :, cols], dev(p, b, c))
                for k, p in enumerate(apeers)
            ]
        for o in owns:
            o.wait()

        def phase_b(i):
            w, cols = part(i)
            for r in za[i]:
                r.wait_recv()
            sl = outs[w].at[:, b, c, :, cols]
            zb[i] = [cp(i, A - 1 + k, sl, sl, dev(a, p, c)) for k, p in enumerate(bpeers)]

        def phase_x(i):
            w, cols = part(i)
            for r in zb[i]:
                r.wait_recv()
            zx[i] = []
            if chunks[i][3] and s == 2:
                for k, p in enumerate(apeers):
                    sl = outs[w].at[p, :, c, :, cols]
                    zx[i].append(cp(i, NB + k, sl, sl, {"seq": 1 - x}))
                for k, p in enumerate(bpeers):
                    sl = outs[w].at[a, p, c, :, cols]
                    zx[i].append(cp(i, NB + A - 1 + k, sl, sl, {"seq": 1 - x}))

        def phase_c(i):
            w, lo, sz, sh = chunks[i]
            for r in zx[i]:
                r.wait_recv()
            sl = outs[w].at[:, :, c, :, pl.ds(lo, sz)]
            zc[i] = cp(i, 2 * NB, sl, sl, dev(a, b, 1 - c))

        for i in range(nc + 2):
            if i < nc:
                phase_b(i)
            if 0 <= i - 1 < nc:
                phase_x(i - 1)
            if 0 <= i - 2 < nc:
                phase_c(i - 2)
        for i in range(nc):
            zc[i].wait_recv()
            for r in za[i] + zb[i] + zx[i] + [zc[i]]:
                r.wait_send()

    res = pl.pallas_call(
        kern,
        out_shape=[jax.ShapeDtypeStruct((A, B, 2) + w.shape, w.dtype) for w in shards],
        in_specs=[pl.BlockSpec(memory_space=pltpu.VMEM)] * ns,
        out_specs=[pl.BlockSpec(memory_space=pl.ANY)] * ns,
        scratch_shapes=[
            pltpu.SemaphoreType.DMA((ns,)),
            pltpu.SemaphoreType.DMA((nc, steps)),
            pltpu.SemaphoreType.DMA((nc, steps)),
        ],
        compiler_params=pltpu.CompilerParams(collective_id=0, has_side_effects=True),
        name="gather_weights",
    )(*shards)
    return [r.reshape((n * w.shape[0], w.shape[1])) for r, w in zip(res, shards)]


def fsdp_peers(n, me):
    return [lax.rem(me + k, n) for k in range(1, n)]


def modulation_forward(lifted, w_ada, bias, n):
    rows, E = w_ada.shape
    m = bias.shape[-1]

    def kern(l_ref, w_ref, bias_ref, mod_ref, lf_ref, bout_ref, part, acc, send, recv):
        me = lax.axis_index("fsdp")
        peers = fsdp_peers(n, me)
        bar = pltpu.get_barrier_semaphore()
        for p in peers:
            pl.semaphore_signal(bar, inc=1, device_id={"fsdp": p}, device_id_type=MESH)
        pl.semaphore_wait(bar, n - 1)

        def cp(i, k, src, dst):
            r = pltpu.make_async_remote_copy(
                src_ref=src,
                dst_ref=dst,
                send_sem=send.at[i, k],
                recv_sem=recv.at[i, k],
                device_id={"fsdp": peers[k]},
                device_id_type=MESH,
            )
            r.start()
            return r

        lf_ref[me] = l_ref[me]
        bout_ref[me] = bias_ref[...]
        first = [cp(0, k, l_ref.at[p], lf_ref.at[me]) for k, p in enumerate(peers)]
        other = [cp(1, k, bias_ref, bout_ref.at[me]) for k, p in enumerate(peers)]
        for r in first:
            r.wait_recv()
        lf = lf_ref[...].reshape(n, rows).astype(bf16)
        part[...] = nn(lf, w_ref[...]).reshape(n, 1, E)
        acc[0] = part[me]
        last = [cp(2, k, part.at[p], acc.at[k + 1]) for k, p in enumerate(peers)]
        for r in last:
            r.wait_recv()
        mod_ref[...] = jnp.sum(acc[...], axis=0)
        for r in other:
            r.wait_recv()
        for r in first + other + last:
            r.wait_send()

    vm = pl.BlockSpec(memory_space=pltpu.VMEM)
    return pl.pallas_call(
        kern,
        out_shape=[
            jax.ShapeDtypeStruct((1, E), f32),
            jax.ShapeDtypeStruct((n, 1, rows), f32),
            jax.ShapeDtypeStruct((n, 1, m), f32),
        ],
        in_specs=[vm] * 3,
        out_specs=[vm] * 3,
        scratch_shapes=[
            pltpu.VMEM((n, 1, E), f32),
            pltpu.VMEM((n, 1, E), f32),
            pltpu.SemaphoreType.DMA((3, n - 1)),
            pltpu.SemaphoreType.DMA((3, n - 1)),
        ],
        compiler_params=pltpu.CompilerParams(collective_id=1, has_side_effects=True),
        name="modulation_forward",
    )(lifted, w_ada, bias)


def modulation_backward(d_part, bias_part, lf, w_ada, n, s):
    rows, E = w_ada.shape
    m = bias_part.shape[-1]

    def kern(d_ref, bp_ref, lf_ref, w_ref, gw_ref, gb_ref, dl_ref, bo_ref, dx, dm, lp, bx, bs, bsx, send, recv, xsend, xrecv):
        me, x = lax.axis_index("fsdp"), lax.axis_index("seq")
        peers = fsdp_peers(n, me)
        xpeers = [lax.rem(x + k, s) for k in range(1, s)]
        bar = pltpu.get_barrier_semaphore()
        for p in peers:
            pl.semaphore_signal(bar, inc=1, device_id={"fsdp": p}, device_id_type=MESH)
        for p in xpeers:
            pl.semaphore_signal(bar, inc=1, device_id={"seq": p}, device_id_type=MESH)
        pl.semaphore_wait(bar, n - 1 + s - 1)

        def cp(i, k, src, dst):
            r = pltpu.make_async_remote_copy(
                src_ref=src,
                dst_ref=dst,
                send_sem=send.at[i, k],
                recv_sem=recv.at[i, k],
                device_id={"fsdp": peers[k]},
                device_id_type=MESH,
            )
            r.start()
            return r

        def cpx(i, k, src, dst):
            r = pltpu.make_async_remote_copy(
                src_ref=src,
                dst_ref=dst,
                send_sem=xsend.at[i, k],
                recv_sem=xrecv.at[i, k],
                device_id={"seq": xpeers[k]},
                device_id_type=MESH,
            )
            r.start()
            return r

        q0 = [cpx(0, k, d_ref, dx.at[x]) for k in range(s - 1)]
        q1 = [cp(0, k, bp_ref.at[p], bx.at[me]) for k, p in enumerate(peers)]
        dx[x] = d_ref[...]
        bx[me] = bp_ref[me]
        for r in q0:
            r.wait_recv()
        dm[me] = jnp.sum(dx[...], axis=0).astype(bf16).astype(f32)
        q2 = [cp(1, k, dm.at[me], dm.at[me]) for k, p in enumerate(peers)]
        for r in q1:
            r.wait_recv()
        bs[...] = jnp.sum(bx[...], axis=0)
        bsx[x] = bs[...]
        q3 = [cpx(1, k, bs, bsx.at[x]) for k in range(s - 1)]
        for r in q2:
            r.wait_recv()
        dmod = dm[...].reshape(n, E).astype(bf16)
        lp[...] = nt(dmod, w_ref[...]).reshape(n, 1, rows)
        dl_ref[me] = lp[me]
        q4 = [cp(2, k, lp.at[p], dl_ref.at[me]) for k, p in enumerate(peers)]
        gw_ref[...] = tn(lf_ref[...].reshape(n, rows).astype(bf16), dmod)
        gb_ref[...] = jnp.sum(dm[...], axis=0)
        for r in q3:
            r.wait_recv()
        bo_ref[...] = jnp.sum(bsx[...], axis=0)
        for r in q4:
            r.wait_recv()
        for r in q0 + q1 + q2 + q3 + q4:
            r.wait_send()

    vm = pl.BlockSpec(memory_space=pltpu.VMEM)
    return pl.pallas_call(
        kern,
        out_shape=[
            jax.ShapeDtypeStruct((rows, E), f32),
            jax.ShapeDtypeStruct((1, E), f32),
            jax.ShapeDtypeStruct((n, 1, rows), f32),
            jax.ShapeDtypeStruct((1, m), f32),
        ],
        in_specs=[vm] * 4,
        out_specs=[vm] * 4,
        scratch_shapes=[
            pltpu.VMEM((s, 1, E), f32),
            pltpu.VMEM((n, 1, E), f32),
            pltpu.VMEM((n, 1, rows), f32),
            pltpu.VMEM((n, 1, m), f32),
            pltpu.VMEM((1, m), f32),
            pltpu.VMEM((s, 1, m), f32),
            pltpu.SemaphoreType.DMA((3, n - 1)),
            pltpu.SemaphoreType.DMA((3, n - 1)),
            pltpu.SemaphoreType.DMA((2, s - 1)),
            pltpu.SemaphoreType.DMA((2, s - 1)),
        ],
        compiler_params=pltpu.CompilerParams(collective_id=2, has_side_effects=True),
        name="modulation_backward",
    )(d_part, bias_part, lf, w_ada)


def head_mask(ref_shape, h):
    low = lax.broadcasted_iota(jnp.int32, ref_shape, 1) < HD
    return low if h == 0 else ~low


def pick(values, h):
    return jnp.where(head_mask(values.shape, h), values, jnp.zeros_like(values))


def attend_forward_kernel(n, q_ref, *refs):
    k_refs, v_refs, (o_ref, lse_ref) = refs[:n], refs[n : 2 * n], refs[2 * n :]
    q = q_ref[...] * bf16(HD**-0.5)
    total = None
    for h in range(2):
        qh = pick(q, h)
        scores = [nt(k[...], qh) for k in k_refs]
        top = scores[0].max(axis=0, keepdims=True)
        for sc in scores[1:]:
            top = jnp.maximum(top, sc.max(axis=0, keepdims=True))
        mass, out = None, None
        for sc, v in zip(scores, v_refs):
            p = jnp.exp(sc - top)
            part = p.sum(axis=0, keepdims=True)
            mass = part if mass is None else mass + part
            o = tn(pick(v[...], h), p.astype(bf16))
            out = o if out is None else out + o
        out = out * (1.0 / mass)
        total = out if total is None else total + out
        lse_ref[0, h : h + 1, :] = top + jnp.log(mass)
    o_ref[...] = total.T.astype(bf16)


def attend_forward(q, ks, vs):
    T, D = q.shape
    n = len(ks)

    def col(rows):
        return pl.BlockSpec((rows, 128), lambda i: (0, i))

    keys = sum(k.shape[0] for k in ks)
    return pl.pallas_call(
        partial(attend_forward_kernel, n),
        grid=(D // 128,),
        in_specs=[col(T)] + [col(k.shape[0]) for k in ks] * 2,
        out_specs=[col(T), pl.BlockSpec((1, 2, T), lambda i: (i, 0, 0))],
        out_shape=[jax.ShapeDtypeStruct((T, D), bf16), jax.ShapeDtypeStruct((D // 128, 2, T), f32)],
        cost_estimate=pl.CostEstimate(flops=16 * T * keys * D, bytes_accessed=4 * (T + keys) * D, transcendentals=0),
        name="attend_forward",
    )(q, *ks, *vs)


def attend_backward_kernel(n, q_ref, e_ref, lse_ref, *refs):
    k_refs, v_refs = refs[:n], refs[n : 2 * n]
    dq_ref, dk_refs, dv_refs = refs[2 * n], refs[2 * n + 1 : 3 * n + 1], refs[3 * n + 1 :]
    q, e = q_ref[...] * bf16(HD**-0.5), e_ref[...]
    dqt = None
    dks, dvs = [None] * n, [None] * n
    for h in range(2):
        qh, eh = pick(q, h), pick(e, h)
        lse = lse_ref[0, h : h + 1, :]
        probs, dprobs, cross = [], [], None
        for j in range(n):
            p = jnp.exp(nt(k_refs[j][...], qh) - lse)
            dp = nt(v_refs[j][...], eh)
            part = (p * dp).sum(axis=0, keepdims=True)
            cross = part if cross is None else cross + part
            dv = nn(p.astype(bf16), eh)
            dvs[j] = dv if dvs[j] is None else dvs[j] + dv
            probs.append(p)
            dprobs.append(dp)
        for j in range(n):
            ds = (probs[j] * (dprobs[j] - cross)).astype(bf16)
            dk = nn(ds, qh)
            dks[j] = dk if dks[j] is None else dks[j] + dk
            t = tn(pick(k_refs[j][...], h), ds)
            dqt = t if dqt is None else dqt + t
    dq_ref[...] = (dqt * (HD**-0.5)).T.astype(bf16)
    for j in range(n):
        dk_refs[j][...] = dks[j].astype(dk_refs[j].dtype)
        dv_refs[j][...] = dvs[j].astype(dv_refs[j].dtype)


def attend_backward(q, e, lse, ks, vs):
    T, D = q.shape
    n = len(ks)

    def col(rows):
        return pl.BlockSpec((rows, 128), lambda i: (0, i))

    keys = sum(k.shape[0] for k in ks)
    cols = [col(k.shape[0]) for k in ks]
    kv = [jax.ShapeDtypeStruct(k.shape, f32 if j == 0 else bf16) for j, k in enumerate(ks)]
    res = pl.pallas_call(
        partial(attend_backward_kernel, n),
        grid=(D // 128,),
        in_specs=[col(T), col(T), pl.BlockSpec((1, 2, T), lambda i: (i, 0, 0))] + cols * 2,
        out_specs=[col(T)] + cols * 2,
        out_shape=[jax.ShapeDtypeStruct((T, D), bf16)] + kv * 2,
        cost_estimate=pl.CostEstimate(flops=30 * T * keys * D, bytes_accessed=8 * (T + keys) * D, transcendentals=0),
        name="attend_backward",
    )(q, e, lse, *ks, *vs)
    return res[0], res[1 : n + 1], res[n + 1 :]


def seq_shift(value, k, s):
    return lax.ppermute(value, "seq", [(i, (i + k) % s) for i in range(s)])


def reduce_rows(make, mine_c, n, s):
    A, B = grid_of(n)

    def at(a, b, c):
        return (a * B + b) * 2 + c

    every = [(a, b, c) for a in range(A) for b in range(B) for c in range(2)]
    me = lax.axis_index("fsdp")
    a, b, c = me // (2 * B), (me // 2) % B, me % 2
    away = make(1 - c).astype(bf16)
    away = lax.ppermute(away, "fsdp", [(at(*p), at(p[0], p[1], 1 - p[2])) for p in every])
    total = make(c) + away.astype(f32)
    parts = []
    for k in range(1, B):
        send = lax.dynamic_index_in_dim(total, (b + k) % B, 1, keepdims=False).astype(bf16)
        parts.append(lax.ppermute(send, "fsdp", [(at(*p), at(p[0], (p[1] + k) % B, p[2])) for p in every]))
    total = lax.dynamic_index_in_dim(total, b, 1, keepdims=False)
    for p in parts:
        total = total + p.astype(f32)
    parts = []
    for k in range(1, A):
        send = lax.dynamic_index_in_dim(total, (a + k) % A, 0, keepdims=False).astype(bf16)
        parts.append(lax.ppermute(send, "fsdp", [(at(*p), at((p[0] + k) % A, p[1], p[2])) for p in every]))
    total = lax.dynamic_index_in_dim(total, a, 0, keepdims=False)
    for p in parts:
        total = total + p.astype(f32)
    if s != 2:
        return lax.psum(total, "seq")
    total = total.astype(bf16)
    return total.astype(f32) + seq_shift(total, 1, 2).astype(f32)


def weight_grad(lhs, rhs, n, s):
    A, B = grid_of(n)
    T, R = lhs.shape
    r = R // n
    split = lhs.reshape(T, A * B, 2, r)

    def make(c):
        rows = lax.dynamic_index_in_dim(split, c, 2, keepdims=False).reshape(T, A * B * r)
        return tn(rows, rhs).reshape(A, B, r, rhs.shape[1])

    return reduce_rows(make, None, n, s)


def layer_norm(values):
    center = values - jnp.mean(values, axis=-1, keepdims=True)
    rscale = lax.rsqrt(jnp.mean(center * center, axis=-1, keepdims=True) + norm_eps)
    return (center * rscale, rscale)


def norm_back(upstream, normed, rscale):
    mean_up = jnp.mean(upstream, axis=-1, keepdims=True)
    mean_cross = jnp.mean(upstream * normed, axis=-1, keepdims=True)
    return rscale * (upstream - mean_up - normed * mean_cross)


def on_device(
    tokens,
    condition,
    w_ada,
    b_ada,
    w_qkv,
    b_qv,
    w_proj,
    b_proj,
    w_fc1,
    b_fc1,
    w_fc2,
    b_fc2,
    cotangent,
):
    n, s = lax.axis_size("fsdp"), lax.axis_size("seq")
    width = tokens.shape[-1]
    T = tokens.shape[1]
    tokens_f = tokens[0].astype(f32)
    grad_out = cotangent[0].astype(f32)

    lifted, silu_back = jax.vjp(jax.nn.silu, condition.astype(f32))
    lifted_q = lifted.astype(bf16).astype(f32).reshape(n, 1, width // n)
    packed = [b_qv, b_proj, b_fc1, b_fc2, b_ada]
    edges = [sum(v.shape[0] for v in packed[:i]) for i in range(6)]
    modulation, lf, biases = modulation_forward(lifted_q, w_ada, jnp.concatenate(packed).astype(f32)[None], n)
    qv_b, proj_b, fc1_b, fc2_b, ada_b = [biases[:, 0, edges[i] : edges[i + 1]].reshape(1, -1) for i in range(5)]
    modulation = modulation + ada_b
    shift_one, scale_one, gate_one, shift_two, scale_two, gate_two = jnp.split(modulation, 6, axis=-1)

    h, q4 = w_fc1.shape[1], w_fc2.shape[1]
    chunks = [(0, width, width, True), (0, 2 * width, width, True), (0, 0, width, True), (1, 0, width, True)]
    chunks += [(3, i * (q4 // 4), q4 // 4, i != 2) for i in range(4)]
    chunks += [(2, i * (h // 8), h // 8, i % 2 == 0) for i in range(8)]
    qkv_w, proj_w, fc1_w, fc2_w = gather_weights([w_qkv, w_proj, w_fc1, w_fc2], chunks, n, s)

    normed_one, rscale_one = layer_norm(tokens_f)
    hidden_one = (normed_one * (1.0 + scale_one) + shift_one).astype(bf16)
    keys = nn(hidden_one, qkv_w[:, width : 2 * width]).astype(bf16)
    values = (nn(hidden_one, qkv_w[:, 2 * width :]) + qv_b[:, width:]).astype(bf16)
    ks = [keys] + [seq_shift(keys, k, s) for k in range(1, s)]
    vs = [values] + [seq_shift(values, k, s) for k in range(1, s)]
    queries = (nn(hidden_one, qkv_w[:, :width]) + qv_b[:, :width]).astype(bf16)
    attn, lse = attend_forward(queries, ks, vs)
    branch = nn(attn, proj_w) + proj_b
    middle = tokens_f + gate_one * branch

    normed_two, rscale_two = layer_norm(middle)
    hidden_two = (normed_two * (1.0 + scale_two) + shift_two).astype(bf16)
    pre_act = nn(hidden_two, fc1_w) + fc1_b
    act_f, gelu_back = jax.vjp(partial(jax.nn.gelu, approximate=True), pre_act)
    act_b = act_f.astype(bf16)
    mlp_out = nn(act_b, fc2_w) + fc2_b
    result = (middle + gate_two * mlp_out).astype(bf16)

    d_gate_two = jnp.sum(grad_out * mlp_out, axis=0, keepdims=True)
    d_mlp = (grad_out * gate_two).astype(bf16)
    total_fc2 = weight_grad(act_b, d_mlp, n, s)
    bias_fc2 = jnp.sum(d_mlp, axis=0, dtype=f32)
    d_act = nt(d_mlp, fc2_w)
    d_pre = gelu_back(d_act)[0].astype(bf16)
    total_fc1 = weight_grad(hidden_two, d_pre, n, s)
    bias_fc1 = jnp.sum(d_pre, axis=0, dtype=f32)
    d_hidden_two = nt(d_pre, fc1_w)
    d_shift_two = jnp.sum(d_hidden_two, axis=0, keepdims=True)
    d_scale_two = jnp.sum(d_hidden_two * normed_two, axis=0, keepdims=True)
    d_middle = grad_out + norm_back(d_hidden_two * (1.0 + scale_two), normed_two, rscale_two)

    d_gate_one = jnp.sum(d_middle * branch, axis=0, keepdims=True)
    d_branch = (d_middle * gate_one).astype(bf16)
    total_proj = weight_grad(attn, d_branch, n, s)
    bias_proj = jnp.sum(d_branch, axis=0, dtype=f32)
    d_attn = nt(d_branch, proj_w).astype(bf16)
    grad_q, dks, dvs = attend_backward(queries, d_attn, lse, ks, vs)
    grad_k, grad_v = dks[0], dvs[0]
    for k in range(1, s):
        grad_k = grad_k + seq_shift(dks[k], s - k, s).astype(f32)
        grad_v = grad_v + seq_shift(dvs[k], s - k, s).astype(f32)
    d_qkv = jnp.concatenate([grad_q, grad_k.astype(bf16), grad_v.astype(bf16)], axis=1)
    total_qkv = weight_grad(hidden_one, d_qkv, n, s)
    column_sums = jnp.sum(d_qkv, axis=0, dtype=f32)
    bias_qv = jnp.concatenate([column_sums[:width], column_sums[2 * width :]])
    d_hidden_one = nt(d_qkv, qkv_w)
    d_shift_one = jnp.sum(d_hidden_one, axis=0, keepdims=True)
    d_scale_one = jnp.sum(d_hidden_one * normed_one, axis=0, keepdims=True)
    grad_input = d_middle + norm_back(d_hidden_one * (1.0 + scale_one), normed_one, rscale_one)

    d_part = jnp.concatenate(
        [d_shift_one, d_scale_one, d_gate_one, d_shift_two, d_scale_two, d_gate_two], axis=-1
    )
    bias_part = jnp.concatenate(
        [bias_qv.reshape(n, -1), bias_proj.reshape(n, -1), bias_fc1.reshape(n, -1), bias_fc2.reshape(n, -1)], axis=1
    )[:, None, :]
    total_ada, sums_ada, d_lifted, total_bias = modulation_backward(d_part, bias_part, lf, w_ada, n, s)
    share = b_ada.shape[0]
    total_bada = lax.dynamic_slice_in_dim(sums_ada[0], lax.axis_index("fsdp") * share, share)
    grad_condition = silu_back(d_lifted.reshape(1, width))[0]
    total_bqv, total_bproj, total_bfc1, total_bfc2 = [total_bias[0, edges[i] : edges[i + 1]] for i in range(4)]
    return (
        result[None],
        grad_input[None],
        grad_condition,
        total_ada,
        total_bada,
        total_qkv,
        total_bqv,
        total_proj,
        total_bproj,
        total_fc1,
        total_bfc1,
        total_fc2,
        total_bfc2,
    )


def solution(mesh):
    weights = (P("fsdp", None), P("fsdp")) * 5
    return jax.shard_map(
        on_device,
        mesh=mesh,
        in_specs=(P("fsdp", "seq", None), P("fsdp", None)) + weights + (P("fsdp", "seq", None),),
        out_specs=(P("fsdp", "seq", None), P("fsdp", "seq", None), P("fsdp", None)) + weights,
        check_vma=False,
    )
```

```python
from functools import partial

import jax
import jax.numpy as jnp
from jax import lax
from jax.experimental import pallas as pl
from jax.experimental.pallas import tpu as pltpu
from jax.sharding import PartitionSpec as P

HD = 64
norm_eps = 1e-06
f32 = jnp.float32
bf16 = jnp.bfloat16
MESH = pl.DeviceIdType.MESH


def grid_of(n):
    b = 2 if n == 16 else 4
    return n // (2 * b), b


def nt(a, b):
    return lax.dot_general(a, b, (((1,), (1,)), ((), ())), preferred_element_type=f32)


def nn(a, b):
    return lax.dot_general(a, b, (((1,), (0,)), ((), ())), preferred_element_type=f32)


def tn(a, b):
    return lax.dot_general(a, b, (((0,), (0,)), ((), ())), preferred_element_type=f32)


def gather_weights(shards, chunks, n, s):
    A, B = grid_of(n)
    nc, ns = len(chunks), len(shards)
    NB = (A - 1) + (B - 1)
    steps = 2 * NB + 1

    def kern(*refs):
        ins, outs = refs[:ns], refs[ns : 2 * ns]
        own_sem, send, recv = refs[2 * ns :]
        me, x = lax.axis_index("fsdp"), lax.axis_index("seq")
        a, b, c = me // (2 * B), (me // 2) % B, me % 2

        def dev(a, b, c):
            return {"fsdp": (a * B + b) * 2 + c}

        apeers = [lax.rem(a + k, A) for k in range(1, A)]
        bpeers = [lax.rem(b + k, B) for k in range(1, B)]
        peers = [dev(p, b, c) for p in apeers] + [dev(a, p, c) for p in bpeers]
        peers.append(dev(a, b, 1 - c))
        if s == 2:
            peers.append({"seq": 1 - x})
        bar = pltpu.get_barrier_semaphore()
        for p in peers:
            pl.semaphore_signal(bar, inc=1, device_id=p, device_id_type=MESH)
        pl.semaphore_wait(bar, len(peers))
        owns = [pltpu.make_async_copy(ins[i], outs[i].at[a, b, c], own_sem.at[i]) for i in range(ns)]
        for o in owns:
            o.start()

        def cp(i, k, src, dst, d):
            r = pltpu.make_async_remote_copy(
                src_ref=src,
                dst_ref=dst,
                send_sem=send.at[i, k],
                recv_sem=recv.at[i, k],
                device_id=d,
                device_id_type=MESH,
            )
            r.start()
            return r

        za, zb, zx, zc = {}, {}, {}, {}

        def part(i):
            w, lo, sz, sh = chunks[i]
            if sh and s == 2:
                return w, pl.ds(pl.multiple_of(lo + x * (sz // 2), 128), sz // 2)
            return w, pl.ds(lo, sz)

        for i in range(nc):
            w, cols = part(i)
            za[i] = [
                cp(i, k, ins[w].at[:, cols], outs[w].at[a, b, c, :, cols], dev(p, b, c))
                for k, p in enumerate(apeers)
            ]
        for o in owns:
            o.wait()

        def phase_b(i):
            w, cols = part(i)
            for r in za[i]:
                r.wait_recv()
            sl = outs[w].at[:, b, c, :, cols]
            zb[i] = [cp(i, A - 1 + k, sl, sl, dev(a, p, c)) for k, p in enumerate(bpeers)]

        def phase_x(i):
            w, cols = part(i)
            for r in zb[i]:
                r.wait_recv()
            zx[i] = []
            if chunks[i][3] and s == 2:
                for k, p in enumerate(apeers):
                    sl = outs[w].at[p, :, c, :, cols]
                    zx[i].append(cp(i, NB + k, sl, sl, {"seq": 1 - x}))
                for k, p in enumerate(bpeers):
                    sl = outs[w].at[a, p, c, :, cols]
                    zx[i].append(cp(i, NB + A - 1 + k, sl, sl, {"seq": 1 - x}))

        def phase_c(i):
            w, lo, sz, sh = chunks[i]
            for r in zx[i]:
                r.wait_recv()
            sl = outs[w].at[:, :, c, :, pl.ds(lo, sz)]
            zc[i] = cp(i, 2 * NB, sl, sl, dev(a, b, 1 - c))

        for i in range(nc + 2):
            if i < nc:
                phase_b(i)
            if 0 <= i - 1 < nc:
                phase_x(i - 1)
            if 0 <= i - 2 < nc:
                phase_c(i - 2)
        for i in range(nc):
            zc[i].wait_recv()
            for r in za[i] + zb[i] + zx[i] + [zc[i]]:
                r.wait_send()

    res = pl.pallas_call(
        kern,
        out_shape=[jax.ShapeDtypeStruct((A, B, 2) + w.shape, w.dtype) for w in shards],
        in_specs=[pl.BlockSpec(memory_space=pltpu.VMEM)] * ns,
        out_specs=[pl.BlockSpec(memory_space=pl.ANY)] * ns,
        scratch_shapes=[
            pltpu.SemaphoreType.DMA((ns,)),
            pltpu.SemaphoreType.DMA((nc, steps)),
            pltpu.SemaphoreType.DMA((nc, steps)),
        ],
        compiler_params=pltpu.CompilerParams(collective_id=0, has_side_effects=True),
        name="gather_weights",
    )(*shards)
    return [r.reshape((n * w.shape[0], w.shape[1])) for r, w in zip(res, shards)]


def fsdp_peers(n, me):
    return [lax.rem(me + k, n) for k in range(1, n)]


def modulation_forward(lifted, w_ada, bias, n):
    rows, E = w_ada.shape
    m = bias.shape[-1]

    def kern(l_ref, w_ref, bias_ref, mod_ref, lf_ref, bout_ref, part, acc, send, recv):
        me = lax.axis_index("fsdp")
        peers = fsdp_peers(n, me)
        bar = pltpu.get_barrier_semaphore()
        for p in peers:
            pl.semaphore_signal(bar, inc=1, device_id={"fsdp": p}, device_id_type=MESH)
        pl.semaphore_wait(bar, n - 1)

        def cp(i, k, src, dst):
            r = pltpu.make_async_remote_copy(
                src_ref=src,
                dst_ref=dst,
                send_sem=send.at[i, k],
                recv_sem=recv.at[i, k],
                device_id={"fsdp": peers[k]},
                device_id_type=MESH,
            )
            r.start()
            return r

        lf_ref[me] = l_ref[me]
        bout_ref[me] = bias_ref[...]
        first = [cp(0, k, l_ref.at[p], lf_ref.at[me]) for k, p in enumerate(peers)]
        other = [cp(1, k, bias_ref, bout_ref.at[me]) for k, p in enumerate(peers)]
        for r in first:
            r.wait_recv()
        lf = lf_ref[...].reshape(n, rows).astype(bf16)
        part[...] = nn(lf, w_ref[...]).reshape(n, 1, E)
        acc[0] = part[me]
        last = [cp(2, k, part.at[p], acc.at[k + 1]) for k, p in enumerate(peers)]
        for r in last:
            r.wait_recv()
        mod_ref[...] = jnp.sum(acc[...], axis=0)
        for r in other:
            r.wait_recv()
        for r in first + other + last:
            r.wait_send()

    vm = pl.BlockSpec(memory_space=pltpu.VMEM)
    return pl.pallas_call(
        kern,
        out_shape=[
            jax.ShapeDtypeStruct((1, E), f32),
            jax.ShapeDtypeStruct((n, 1, rows), f32),
            jax.ShapeDtypeStruct((n, 1, m), f32),
        ],
        in_specs=[vm] * 3,
        out_specs=[vm] * 3,
        scratch_shapes=[
            pltpu.VMEM((n, 1, E), f32),
            pltpu.VMEM((n, 1, E), f32),
            pltpu.SemaphoreType.DMA((3, n - 1)),
            pltpu.SemaphoreType.DMA((3, n - 1)),
        ],
        compiler_params=pltpu.CompilerParams(collective_id=1, has_side_effects=True),
        name="modulation_forward",
    )(lifted, w_ada, bias)


def modulation_backward(d_part, bias_part, lf, w_ada, n, s):
    rows, E = w_ada.shape
    m = bias_part.shape[-1]

    def kern(d_ref, bp_ref, lf_ref, w_ref, gw_ref, gb_ref, dl_ref, bo_ref, dx, dm, lp, bx, bs, bsx, send, recv, xsend, xrecv):
        me, x = lax.axis_index("fsdp"), lax.axis_index("seq")
        peers = fsdp_peers(n, me)
        xpeers = [lax.rem(x + k, s) for k in range(1, s)]
        bar = pltpu.get_barrier_semaphore()
        for p in peers:
            pl.semaphore_signal(bar, inc=1, device_id={"fsdp": p}, device_id_type=MESH)
        for p in xpeers:
            pl.semaphore_signal(bar, inc=1, device_id={"seq": p}, device_id_type=MESH)
        pl.semaphore_wait(bar, n - 1 + s - 1)

        def cp(i, k, src, dst):
            r = pltpu.make_async_remote_copy(
                src_ref=src,
                dst_ref=dst,
                send_sem=send.at[i, k],
                recv_sem=recv.at[i, k],
                device_id={"fsdp": peers[k]},
                device_id_type=MESH,
            )
            r.start()
            return r

        def cpx(i, k, src, dst):
            r = pltpu.make_async_remote_copy(
                src_ref=src,
                dst_ref=dst,
                send_sem=xsend.at[i, k],
                recv_sem=xrecv.at[i, k],
                device_id={"seq": xpeers[k]},
                device_id_type=MESH,
            )
            r.start()
            return r

        q0 = [cpx(0, k, d_ref, dx.at[x]) for k in range(s - 1)]
        q1 = [cp(0, k, bp_ref.at[p], bx.at[me]) for k, p in enumerate(peers)]
        dx[x] = d_ref[...]
        bx[me] = bp_ref[me]
        for r in q0:
            r.wait_recv()
        dm[me] = jnp.sum(dx[...], axis=0).astype(bf16).astype(f32)
        q2 = [cp(1, k, dm.at[me], dm.at[me]) for k, p in enumerate(peers)]
        for r in q1:
            r.wait_recv()
        bs[...] = jnp.sum(bx[...], axis=0)
        bsx[x] = bs[...]
        q3 = [cpx(1, k, bs, bsx.at[x]) for k in range(s - 1)]
        for r in q2:
            r.wait_recv()
        dmod = dm[...].reshape(n, E).astype(bf16)
        lp[...] = nt(dmod, w_ref[...]).reshape(n, 1, rows)
        dl_ref[me] = lp[me]
        q4 = [cp(2, k, lp.at[p], dl_ref.at[me]) for k, p in enumerate(peers)]
        gw_ref[...] = tn(lf_ref[...].reshape(n, rows).astype(bf16), dmod)
        gb_ref[...] = jnp.sum(dm[...], axis=0)
        for r in q3:
            r.wait_recv()
        bo_ref[...] = jnp.sum(bsx[...], axis=0)
        for r in q4:
            r.wait_recv()
        for r in q0 + q1 + q2 + q3 + q4:
            r.wait_send()

    vm = pl.BlockSpec(memory_space=pltpu.VMEM)
    return pl.pallas_call(
        kern,
        out_shape=[
            jax.ShapeDtypeStruct((rows, E), f32),
            jax.ShapeDtypeStruct((1, E), f32),
            jax.ShapeDtypeStruct((n, 1, rows), f32),
            jax.ShapeDtypeStruct((1, m), f32),
        ],
        in_specs=[vm] * 4,
        out_specs=[vm] * 4,
        scratch_shapes=[
            pltpu.VMEM((s, 1, E), f32),
            pltpu.VMEM((n, 1, E), f32),
            pltpu.VMEM((n, 1, rows), f32),
            pltpu.VMEM((n, 1, m), f32),
            pltpu.VMEM((1, m), f32),
            pltpu.VMEM((s, 1, m), f32),
            pltpu.SemaphoreType.DMA((3, n - 1)),
            pltpu.SemaphoreType.DMA((3, n - 1)),
            pltpu.SemaphoreType.DMA((2, s - 1)),
            pltpu.SemaphoreType.DMA((2, s - 1)),
        ],
        compiler_params=pltpu.CompilerParams(collective_id=2, has_side_effects=True),
        name="modulation_backward",
    )(d_part, bias_part, lf, w_ada)


def head_mask(ref_shape, h):
    low = lax.broadcasted_iota(jnp.int32, ref_shape, 1) < HD
    return low if h == 0 else ~low


def pick(values, h):
    return jnp.where(head_mask(values.shape, h), values, jnp.zeros_like(values))


def attend_forward_kernel(n, q_ref, *refs):
    k_refs, v_refs, (o_ref, lse_ref) = refs[:n], refs[n : 2 * n], refs[2 * n :]
    q = q_ref[...] * bf16(HD**-0.5)
    total = None
    for h in range(2):
        qh = pick(q, h)
        scores = [nt(k[...], qh) for k in k_refs]
        top = scores[0].max(axis=0, keepdims=True)
        for sc in scores[1:]:
            top = jnp.maximum(top, sc.max(axis=0, keepdims=True))
        mass, out = None, None
        for sc, v in zip(scores, v_refs):
            p = jnp.exp(sc - top)
            part = p.sum(axis=0, keepdims=True)
            mass = part if mass is None else mass + part
            o = tn(pick(v[...], h), p.astype(bf16))
            out = o if out is None else out + o
        out = out * (1.0 / mass)
        total = out if total is None else total + out
        lse_ref[0, h : h + 1, :] = top + jnp.log(mass)
    o_ref[...] = total.T.astype(bf16)


def attend_forward(q, ks, vs):
    T, D = q.shape
    n = len(ks)

    def col(rows):
        return pl.BlockSpec((rows, 128), lambda i: (0, i))

    keys = sum(k.shape[0] for k in ks)
    return pl.pallas_call(
        partial(attend_forward_kernel, n),
        grid=(D // 128,),
        in_specs=[col(T)] + [col(k.shape[0]) for k in ks] * 2,
        out_specs=[col(T), pl.BlockSpec((1, 2, T), lambda i: (i, 0, 0))],
        out_shape=[jax.ShapeDtypeStruct((T, D), bf16), jax.ShapeDtypeStruct((D // 128, 2, T), f32)],
        cost_estimate=pl.CostEstimate(flops=16 * T * keys * D, bytes_accessed=4 * (T + keys) * D, transcendentals=0),
        name="attend_forward",
    )(q, *ks, *vs)


def attend_backward_kernel(n, q_ref, e_ref, lse_ref, *refs):
    k_refs, v_refs = refs[:n], refs[n : 2 * n]
    dq_ref, dk_refs, dv_refs = refs[2 * n], refs[2 * n + 1 : 3 * n + 1], refs[3 * n + 1 :]
    q, e = q_ref[...] * bf16(HD**-0.5), e_ref[...]
    dqt = None
    dks, dvs = [None] * n, [None] * n
    for h in range(2):
        qh, eh = pick(q, h), pick(e, h)
        lse = lse_ref[0, h : h + 1, :]
        probs, dprobs, cross = [], [], None
        for j in range(n):
            p = jnp.exp(nt(k_refs[j][...], qh) - lse)
            dp = nt(v_refs[j][...], eh)
            part = (p * dp).sum(axis=0, keepdims=True)
            cross = part if cross is None else cross + part
            dv = nn(p.astype(bf16), eh)
            dvs[j] = dv if dvs[j] is None else dvs[j] + dv
            probs.append(p)
            dprobs.append(dp)
        for j in range(n):
            ds = (probs[j] * (dprobs[j] - cross)).astype(bf16)
            dk = nn(ds, qh)
            dks[j] = dk if dks[j] is None else dks[j] + dk
            t = tn(pick(k_refs[j][...], h), ds)
            dqt = t if dqt is None else dqt + t
    dq_ref[...] = (dqt * (HD**-0.5)).T.astype(bf16)
    for j in range(n):
        dk_refs[j][...] = dks[j].astype(dk_refs[j].dtype)
        dv_refs[j][...] = dvs[j].astype(dv_refs[j].dtype)


def attend_backward(q, e, lse, ks, vs):
    T, D = q.shape
    n = len(ks)

    def col(rows):
        return pl.BlockSpec((rows, 128), lambda i: (0, i))

    keys = sum(k.shape[0] for k in ks)
    cols = [col(k.shape[0]) for k in ks]
    kv = [jax.ShapeDtypeStruct(k.shape, f32 if j == 0 else bf16) for j, k in enumerate(ks)]
    res = pl.pallas_call(
        partial(attend_backward_kernel, n),
        grid=(D // 128,),
        in_specs=[col(T), col(T), pl.BlockSpec((1, 2, T), lambda i: (i, 0, 0))] + cols * 2,
        out_specs=[col(T)] + cols * 2,
        out_shape=[jax.ShapeDtypeStruct((T, D), bf16)] + kv * 2,
        cost_estimate=pl.CostEstimate(flops=30 * T * keys * D, bytes_accessed=8 * (T + keys) * D, transcendentals=0),
        name="attend_backward",
    )(q, e, lse, *ks, *vs)
    return res[0], res[1 : n + 1], res[n + 1 :]


def seq_shift(value, k, s):
    return lax.ppermute(value, "seq", [(i, (i + k) % s) for i in range(s)])


def tie(*values):
    return lax.optimization_barrier(values)


class Exchange:
    def __init__(self, grad, n, s):
        A, B = grid_of(n)
        self.A, self.B, self.s = A, B, s
        self.grad = grad.reshape(A, B, 2, grad.shape[0] // n, grad.shape[1])
        me = lax.axis_index("fsdp")
        self.a, self.b, self.c = me // (2 * B), (me // 2) % B, me % 2

    def shift(self, value, da, db, dc):
        A, B = self.A, self.B

        def at(a, b, c):
            return (a * B + b) * 2 + c

        pairs = [
            (at(a, b, c), at((a + da) % A, (b + db) % B, (c + dc) % 2))
            for a in range(A)
            for b in range(B)
            for c in range(2)
        ]
        return lax.ppermute(value, "fsdp", pairs)

    def take(self, value, index, axis):
        return lax.dynamic_index_in_dim(value, index, axis, keepdims=False)

    def c_send(self):
        self.out = [self.take(self.grad, 1 - self.c, 2)]
        return self.out

    def c_start(self, out):
        self.into = self.shift(out[0], 0, 0, 1)

    def b_sum(self, index):
        mine = self.take(self.take(self.grad, self.c, 2), index, 1)
        return mine.astype(f32) + self.take(self.into, index, 1).astype(f32)

    def b_send(self):
        return [self.b_sum((self.b + k) % self.B).astype(bf16) for k in range(1, self.B)]

    def b_start(self, out):
        self.from_b = [self.shift(v, 0, k + 1, 0) for k, v in enumerate(out)]

    def a_send(self):
        total = self.b_sum(self.b)
        for v in self.from_b:
            total = total + v.astype(f32)
        self.total = total
        return [self.take(total, (self.a + k) % self.A, 0).astype(bf16) for k in range(1, self.A)]

    def a_start(self, out):
        self.from_a = [self.shift(v, k + 1, 0, 0) for k, v in enumerate(out)]

    def x_send(self):
        total = self.take(self.total, self.a, 0)
        for v in self.from_a:
            total = total + v.astype(f32)
        if self.s != 2:
            self.total = lax.psum(total, "seq")
            return []
        self.total = total.astype(bf16)
        return [self.total]

    def x_start(self, out):
        if self.s == 2:
            self.from_x = seq_shift(out[0], 1, 2)
            self.total = out[0]

    def result(self):
        if self.s != 2:
            return self.total
        return self.total.astype(f32) + self.from_x.astype(f32)


def layer_norm(values):
    center = values - jnp.mean(values, axis=-1, keepdims=True)
    rscale = lax.rsqrt(jnp.mean(center * center, axis=-1, keepdims=True) + norm_eps)
    return (center * rscale, rscale)


def norm_back(upstream, normed, rscale):
    mean_up = jnp.mean(upstream, axis=-1, keepdims=True)
    mean_cross = jnp.mean(upstream * normed, axis=-1, keepdims=True)
    return rscale * (upstream - mean_up - normed * mean_cross)


def on_device(
    tokens,
    condition,
    w_ada,
    b_ada,
    w_qkv,
    b_qv,
    w_proj,
    b_proj,
    w_fc1,
    b_fc1,
    w_fc2,
    b_fc2,
    cotangent,
):
    n, s = lax.axis_size("fsdp"), lax.axis_size("seq")
    width = tokens.shape[-1]
    T = tokens.shape[1]
    tokens_f = tokens[0].astype(f32)
    grad_out = cotangent[0].astype(f32)

    lifted, silu_back = jax.vjp(jax.nn.silu, condition.astype(f32))
    lifted_q = lifted.astype(bf16).astype(f32).reshape(n, 1, width // n)
    packed = [b_qv, b_proj, b_fc1, b_fc2, b_ada]
    edges = [sum(v.shape[0] for v in packed[:i]) for i in range(6)]
    modulation, lf, biases = modulation_forward(lifted_q, w_ada, jnp.concatenate(packed).astype(f32)[None], n)
    qv_b, proj_b, fc1_b, fc2_b, ada_b = [biases[:, 0, edges[i] : edges[i + 1]].reshape(1, -1) for i in range(5)]
    modulation = modulation + ada_b
    shift_one, scale_one, gate_one, shift_two, scale_two, gate_two = jnp.split(modulation, 6, axis=-1)

    h, q4 = w_fc1.shape[1], w_fc2.shape[1]
    chunks = [(0, width, width, True), (0, 2 * width, width, True), (0, 0, width, True), (1, 0, width, True)]
    chunks += [(3, i * (q4 // 4), q4 // 4, i != 2) for i in range(4)]
    chunks += [(2, i * (h // 8), h // 8, i % 2 == 0) for i in range(8)]
    qkv_w, proj_w, fc1_w, fc2_w = gather_weights([w_qkv, w_proj, w_fc1, w_fc2], chunks, n, s)

    normed_one, rscale_one = layer_norm(tokens_f)
    hidden_one = (normed_one * (1.0 + scale_one) + shift_one).astype(bf16)
    keys = nn(hidden_one, qkv_w[:, width : 2 * width]).astype(bf16)
    values = (nn(hidden_one, qkv_w[:, 2 * width :]) + qv_b[:, width:]).astype(bf16)
    ks = [keys] + [seq_shift(keys, k, s) for k in range(1, s)]
    vs = [values] + [seq_shift(values, k, s) for k in range(1, s)]
    queries = (nn(hidden_one, qkv_w[:, :width]) + qv_b[:, :width]).astype(bf16)
    attn, lse = attend_forward(queries, ks, vs)
    branch = nn(attn, proj_w) + proj_b
    middle = tokens_f + gate_one * branch

    normed_two, rscale_two = layer_norm(middle)
    hidden_two = (normed_two * (1.0 + scale_two) + shift_two).astype(bf16)
    pre_act = nn(hidden_two, fc1_w) + fc1_b
    act_f, gelu_back = jax.vjp(partial(jax.nn.gelu, approximate=True), pre_act)
    act_b = act_f.astype(bf16)
    d_mlp = (grad_out * gate_two).astype(bf16)
    half_d, half_f = width // 2, fc1_w.shape[1] // 2

    def exchange(lhs, rhs):
        return Exchange(tn(lhs, rhs).astype(bf16), n, s)

    fc2a, fc2b = exchange(act_b, d_mlp[:, :half_d]), exchange(act_b, d_mlp[:, half_d:])
    d_mlp, sa, sb = tie(d_mlp, fc2a.c_send(), fc2b.c_send())
    fc2a.c_start(sa)
    fc2b.c_start(sb)
    bias_fc2 = jnp.sum(d_mlp, axis=0, dtype=f32)
    d_pre = gelu_back(nt(d_mlp, fc2_w))[0].astype(bf16)
    d_pre, sa, sb = tie(d_pre, fc2a.b_send(), fc2b.b_send())
    fc2a.b_start(sa)
    fc2b.b_start(sb)
    fc1a, fc1b = exchange(hidden_two, d_pre[:, :half_f]), exchange(hidden_two, d_pre[:, half_f:])
    bias_fc1 = jnp.sum(d_pre, axis=0, dtype=f32)
    d_pre, sa, sb = tie(d_pre, fc1a.c_send(), fc1b.c_send())
    fc1a.c_start(sa)
    fc1b.c_start(sb)
    d_hidden_two = nt(d_pre, fc1_w)
    d_shift_two = jnp.sum(d_hidden_two, axis=0, keepdims=True)
    d_scale_two = jnp.sum(d_hidden_two * normed_two, axis=0, keepdims=True)
    d_middle = grad_out + norm_back(d_hidden_two * (1.0 + scale_two), normed_two, rscale_two)
    d_gate_one = jnp.sum(d_middle * branch, axis=0, keepdims=True)
    d_branch = (d_middle * gate_one).astype(bf16)
    d_branch, sa, sb, sc = tie(d_branch, fc1a.b_send(), fc1b.b_send(), fc2a.a_send())
    fc1a.b_start(sa)
    fc1b.b_start(sb)
    fc2a.a_start(sc)
    proj = exchange(attn, d_branch)
    bias_proj = jnp.sum(d_branch, axis=0, dtype=f32)
    d_attn = nt(d_branch, proj_w).astype(bf16)
    d_attn, sa = tie(d_attn, proj.c_send())
    proj.c_start(sa)
    halves = []
    lo = slice(0, half_d)
    hi = slice(half_d, width)

    def attention(part):
        heads = slice(part.start // 128, part.stop // 128)
        grads = attend_backward(
            queries[:, part], d_attn[:, part], lse[heads], [k[:, part] for k in ks], [v[:, part] for v in vs]
        )
        return grads

    def back(dk):
        return [seq_shift(dk[k], s - k, s) for k in range(1, s)]

    q1, dk1, dv1 = attention(lo)
    q1, dk1, dv1, sa, sb = tie(q1, dk1, dv1, proj.b_send(), fc2b.a_send())
    rk1, rv1 = back(dk1), back(dv1)
    proj.b_start(sa)
    fc2b.a_start(sb)
    d_attn, q1 = tie(d_attn, q1)
    q2, dk2, dv2 = attention(hi)
    q2, dk2, dv2, sa, sb = tie(q2, dk2, dv2, fc1a.a_send(), fc2a.x_send())
    rk2, rv2 = back(dk2), back(dv2)
    fc1a.a_start(sa)
    fc2a.x_start(sb)

    def joined(q, dk, rk, dv, rv):
        gk, gv = dk[0], dv[0]
        for v in rk:
            gk = gk + v.astype(f32)
        for v in rv:
            gv = gv + v.astype(f32)
        return jnp.concatenate([q, gk.astype(bf16), gv.astype(bf16)], axis=1)

    d1 = joined(q1, dk1, rk1, dv1, rv1)
    qkv1 = exchange(hidden_one, d1)
    act_b, sa = tie(act_b, qkv1.c_send())
    qkv1.c_start(sa)
    mlp_out = nn(act_b, fc2_w) + fc2_b
    result = (middle + gate_two * mlp_out).astype(bf16)
    d_gate_two = jnp.sum(grad_out * mlp_out, axis=0, keepdims=True)
    d_gate_two, sa, sb, sc = tie(d_gate_two, qkv1.b_send(), fc1b.a_send(), fc2b.x_send())
    qkv1.b_start(sa)
    fc1b.a_start(sb)
    fc2b.x_start(sc)
    d2 = joined(q2, dk2, rk2, dv2, rv2)
    hidden_one_, d_gate_two = tie(hidden_one, d_gate_two)
    qkv2 = exchange(hidden_one_, d2)
    d2, sa = tie(d2, qkv2.c_send())
    qkv2.c_start(sa)
    sums1, sums2 = jnp.sum(d1, axis=0, dtype=f32), jnp.sum(d2, axis=0, dtype=f32)
    bias_qv = jnp.concatenate([sums1[:half_d], sums2[:half_d], sums1[width:], sums2[width:]])
    d_qkv = jnp.concatenate([v[:, i * half_d : (i + 1) * half_d] for i in range(3) for v in (d1, d2)], axis=1)
    d_hidden_one = nt(d_qkv, qkv_w)
    d_shift_one = jnp.sum(d_hidden_one, axis=0, keepdims=True)
    d_scale_one = jnp.sum(d_hidden_one * normed_one, axis=0, keepdims=True)
    grad_input = d_middle + norm_back(d_hidden_one * (1.0 + scale_one), normed_one, rscale_one)
    d_scale_one, sa, sb, sc = tie(d_scale_one, qkv2.b_send(), proj.a_send(), fc1a.x_send())
    qkv2.b_start(sa)
    proj.a_start(sb)
    fc1a.x_start(sc)

    d_part = jnp.concatenate(
        [d_shift_one, d_scale_one, d_gate_one, d_shift_two, d_scale_two, d_gate_two], axis=-1
    )
    bias_part = jnp.concatenate(
        [bias_qv.reshape(n, -1), bias_proj.reshape(n, -1), bias_fc1.reshape(n, -1), bias_fc2.reshape(n, -1)], axis=1
    )[:, None, :]
    total_ada, sums_ada, d_lifted, total_bias = modulation_backward(d_part, bias_part, lf, w_ada, n, s)
    share = b_ada.shape[0]
    total_bada = lax.dynamic_slice_in_dim(sums_ada[0], lax.axis_index("fsdp") * share, share)
    grad_condition = silu_back(d_lifted.reshape(1, width))[0]
    total_bias, sa, sb, sc = tie(total_bias, qkv1.a_send(), fc1b.x_send(), proj.x_send())
    qkv1.a_start(sa)
    fc1b.x_start(sb)
    proj.x_start(sc)
    qkv2.a_start(qkv2.a_send())
    qkv1.x_start(qkv1.x_send())
    qkv2.x_start(qkv2.x_send())
    total_fc2 = jnp.concatenate([fc2a.result(), fc2b.result()], axis=1)
    total_fc1 = jnp.concatenate([fc1a.result(), fc1b.result()], axis=1)
    total_proj = proj.result()
    r1, r2 = qkv1.result(), qkv2.result()
    total_qkv = jnp.concatenate([v[:, i * half_d : (i + 1) * half_d] for i in range(3) for v in (r1, r2)], axis=1)
    total_bqv, total_bproj, total_bfc1, total_bfc2 = [total_bias[0, edges[i] : edges[i + 1]] for i in range(4)]
    return (
        result[None],
        grad_input[None],
        grad_condition,
        total_ada,
        total_bada,
        total_qkv,
        total_bqv,
        total_proj,
        total_bproj,
        total_fc1,
        total_bfc1,
        total_fc2,
        total_bfc2,
    )


def solution(mesh):
    weights = (P("fsdp", None), P("fsdp")) * 5
    return jax.shard_map(
        on_device,
        mesh=mesh,
        in_specs=(P("fsdp", "seq", None), P("fsdp", None)) + weights + (P("fsdp", "seq", None),),
        out_specs=(P("fsdp", "seq", None), P("fsdp", "seq", None), P("fsdp", None)) + weights,
        check_vma=False,
    )
```

```python
from functools import partial

import jax
import jax.numpy as jnp
from jax import lax
from jax.experimental import pallas as pl
from jax.experimental.pallas import tpu as pltpu
from jax.sharding import PartitionSpec as P

HD = 64
norm_eps = 1e-06
f32 = jnp.float32
bf16 = jnp.bfloat16
MESH = pl.DeviceIdType.MESH


def grid_of(n):
    b = 2 if n == 16 else 4
    return n // (2 * b), b


def nt(a, b):
    return lax.dot_general(a, b, (((1,), (1,)), ((), ())), preferred_element_type=f32)


def nn(a, b):
    return lax.dot_general(a, b, (((1,), (0,)), ((), ())), preferred_element_type=f32)


def tn(a, b):
    return lax.dot_general(a, b, (((0,), (0,)), ((), ())), preferred_element_type=f32)


def gather_weights(shards, chunks, n, s):
    A, B = grid_of(n)
    nc, ns = len(chunks), len(shards)
    NB = (A - 1) + (B - 1)
    steps = 2 * NB + 1

    def kern(*refs):
        ins, outs = refs[:ns], refs[ns : 2 * ns]
        own_sem, send, recv = refs[2 * ns :]
        me, x = lax.axis_index("fsdp"), lax.axis_index("seq")
        a, b, c = me // (2 * B), (me // 2) % B, me % 2

        def dev(a, b, c):
            return {"fsdp": (a * B + b) * 2 + c}

        apeers = [lax.rem(a + k, A) for k in range(1, A)]
        bpeers = [lax.rem(b + k, B) for k in range(1, B)]
        peers = [dev(p, b, c) for p in apeers] + [dev(a, p, c) for p in bpeers]
        peers.append(dev(a, b, 1 - c))
        if s == 2:
            peers.append({"seq": 1 - x})
        bar = pltpu.get_barrier_semaphore()
        for p in peers:
            pl.semaphore_signal(bar, inc=1, device_id=p, device_id_type=MESH)
        pl.semaphore_wait(bar, len(peers))
        owns = [pltpu.make_async_copy(ins[i], outs[i].at[a, b, c], own_sem.at[i]) for i in range(ns)]
        for o in owns:
            o.start()

        def cp(i, k, src, dst, d):
            r = pltpu.make_async_remote_copy(
                src_ref=src,
                dst_ref=dst,
                send_sem=send.at[i, k],
                recv_sem=recv.at[i, k],
                device_id=d,
                device_id_type=MESH,
            )
            r.start()
            return r

        za, zb, zx, zc = {}, {}, {}, {}

        def part(i):
            w, lo, sz, sh = chunks[i]
            if sh and s == 2:
                return w, pl.ds(pl.multiple_of(lo + x * (sz // 2), 128), sz // 2)
            return w, pl.ds(lo, sz)

        for i in range(nc):
            w, cols = part(i)
            za[i] = [
                cp(i, k, ins[w].at[:, cols], outs[w].at[a, b, c, :, cols], dev(p, b, c))
                for k, p in enumerate(apeers)
            ]
        for o in owns:
            o.wait()

        def phase_b(i):
            w, cols = part(i)
            for r in za[i]:
                r.wait_recv()
            sl = outs[w].at[:, b, c, :, cols]
            zb[i] = [cp(i, A - 1 + k, sl, sl, dev(a, p, c)) for k, p in enumerate(bpeers)]

        def phase_x(i):
            w, cols = part(i)
            for r in zb[i]:
                r.wait_recv()
            zx[i] = []
            if chunks[i][3] and s == 2:
                for k, p in enumerate(apeers):
                    sl = outs[w].at[p, :, c, :, cols]
                    zx[i].append(cp(i, NB + k, sl, sl, {"seq": 1 - x}))
                for k, p in enumerate(bpeers):
                    sl = outs[w].at[a, p, c, :, cols]
                    zx[i].append(cp(i, NB + A - 1 + k, sl, sl, {"seq": 1 - x}))

        def phase_c(i):
            w, lo, sz, sh = chunks[i]
            for r in zx[i]:
                r.wait_recv()
            sl = outs[w].at[:, :, c, :, pl.ds(lo, sz)]
            zc[i] = cp(i, 2 * NB, sl, sl, dev(a, b, 1 - c))

        for i in range(nc + 2):
            if i < nc:
                phase_b(i)
            if 0 <= i - 1 < nc:
                phase_x(i - 1)
            if 0 <= i - 2 < nc:
                phase_c(i - 2)
        for i in range(nc):
            zc[i].wait_recv()
            for r in za[i] + zb[i] + zx[i] + [zc[i]]:
                r.wait_send()

    res = pl.pallas_call(
        kern,
        out_shape=[jax.ShapeDtypeStruct((A, B, 2) + w.shape, w.dtype) for w in shards],
        in_specs=[pl.BlockSpec(memory_space=pltpu.VMEM)] * ns,
        out_specs=[pl.BlockSpec(memory_space=pl.ANY)] * ns,
        scratch_shapes=[
            pltpu.SemaphoreType.DMA((ns,)),
            pltpu.SemaphoreType.DMA((nc, steps)),
            pltpu.SemaphoreType.DMA((nc, steps)),
        ],
        compiler_params=pltpu.CompilerParams(collective_id=0, has_side_effects=True),
        name="gather_weights",
    )(*shards)
    return [r.reshape((n * w.shape[0], w.shape[1])) for r, w in zip(res, shards)]


def fsdp_peers(n, me):
    return [lax.rem(me + k, n) for k in range(1, n)]


def modulation_forward(lifted, w_ada, bias, n):
    rows, E = w_ada.shape
    m = bias.shape[-1]

    def kern(l_ref, w_ref, bias_ref, mod_ref, lf_ref, bout_ref, part, acc, send, recv):
        me = lax.axis_index("fsdp")
        peers = fsdp_peers(n, me)
        bar = pltpu.get_barrier_semaphore()
        for p in peers:
            pl.semaphore_signal(bar, inc=1, device_id={"fsdp": p}, device_id_type=MESH)
        pl.semaphore_wait(bar, n - 1)

        def cp(i, k, src, dst):
            r = pltpu.make_async_remote_copy(
                src_ref=src,
                dst_ref=dst,
                send_sem=send.at[i, k],
                recv_sem=recv.at[i, k],
                device_id={"fsdp": peers[k]},
                device_id_type=MESH,
            )
            r.start()
            return r

        lf_ref[me] = l_ref[me]
        bout_ref[me] = bias_ref[...]
        first = [cp(0, k, l_ref.at[p], lf_ref.at[me]) for k, p in enumerate(peers)]
        other = [cp(1, k, bias_ref, bout_ref.at[me]) for k, p in enumerate(peers)]
        for r in first:
            r.wait_recv()
        lf = lf_ref[...].reshape(n, rows).astype(bf16)
        part[...] = nn(lf, w_ref[...]).reshape(n, 1, E)
        acc[0] = part[me]
        last = [cp(2, k, part.at[p], acc.at[k + 1]) for k, p in enumerate(peers)]
        for r in last:
            r.wait_recv()
        mod_ref[...] = jnp.sum(acc[...], axis=0)
        for r in other:
            r.wait_recv()
        for r in first + other + last:
            r.wait_send()

    vm = pl.BlockSpec(memory_space=pltpu.VMEM)
    return pl.pallas_call(
        kern,
        out_shape=[
            jax.ShapeDtypeStruct((1, E), f32),
            jax.ShapeDtypeStruct((n, 1, rows), f32),
            jax.ShapeDtypeStruct((n, 1, m), f32),
        ],
        in_specs=[vm] * 3,
        out_specs=[vm] * 3,
        scratch_shapes=[
            pltpu.VMEM((n, 1, E), f32),
            pltpu.VMEM((n, 1, E), f32),
            pltpu.SemaphoreType.DMA((3, n - 1)),
            pltpu.SemaphoreType.DMA((3, n - 1)),
        ],
        compiler_params=pltpu.CompilerParams(collective_id=1, has_side_effects=True),
        name="modulation_forward",
    )(lifted, w_ada, bias)


def modulation_backward(d_part, bias_part, lf, w_ada, n, s):
    rows, E = w_ada.shape
    m = bias_part.shape[-1]

    def kern(d_ref, bp_ref, lf_ref, w_ref, gw_ref, gb_ref, dl_ref, bo_ref, dx, dm, lp, bx, bs, bsx, send, recv, xsend, xrecv):
        me, x = lax.axis_index("fsdp"), lax.axis_index("seq")
        peers = fsdp_peers(n, me)
        xpeers = [lax.rem(x + k, s) for k in range(1, s)]
        bar = pltpu.get_barrier_semaphore()
        for p in peers:
            pl.semaphore_signal(bar, inc=1, device_id={"fsdp": p}, device_id_type=MESH)
        for p in xpeers:
            pl.semaphore_signal(bar, inc=1, device_id={"seq": p}, device_id_type=MESH)
        pl.semaphore_wait(bar, n - 1 + s - 1)

        def cp(i, k, src, dst):
            r = pltpu.make_async_remote_copy(
                src_ref=src,
                dst_ref=dst,
                send_sem=send.at[i, k],
                recv_sem=recv.at[i, k],
                device_id={"fsdp": peers[k]},
                device_id_type=MESH,
            )
            r.start()
            return r

        def cpx(i, k, src, dst):
            r = pltpu.make_async_remote_copy(
                src_ref=src,
                dst_ref=dst,
                send_sem=xsend.at[i, k],
                recv_sem=xrecv.at[i, k],
                device_id={"seq": xpeers[k]},
                device_id_type=MESH,
            )
            r.start()
            return r

        q0 = [cpx(0, k, d_ref, dx.at[x]) for k in range(s - 1)]
        q1 = [cp(0, k, bp_ref.at[p], bx.at[me]) for k, p in enumerate(peers)]
        dx[x] = d_ref[...]
        bx[me] = bp_ref[me]
        for r in q0:
            r.wait_recv()
        dm[me] = jnp.sum(dx[...], axis=0).astype(bf16).astype(f32)
        q2 = [cp(1, k, dm.at[me], dm.at[me]) for k, p in enumerate(peers)]
        for r in q1:
            r.wait_recv()
        bs[...] = jnp.sum(bx[...], axis=0)
        bsx[x] = bs[...]
        q3 = [cpx(1, k, bs, bsx.at[x]) for k in range(s - 1)]
        for r in q2:
            r.wait_recv()
        dmod = dm[...].reshape(n, E).astype(bf16)
        lp[...] = nt(dmod, w_ref[...]).reshape(n, 1, rows)
        dl_ref[me] = lp[me]
        q4 = [cp(2, k, lp.at[p], dl_ref.at[me]) for k, p in enumerate(peers)]
        gw_ref[...] = tn(lf_ref[...].reshape(n, rows).astype(bf16), dmod)
        gb_ref[...] = jnp.sum(dm[...], axis=0)
        for r in q3:
            r.wait_recv()
        bo_ref[...] = jnp.sum(bsx[...], axis=0)
        for r in q4:
            r.wait_recv()
        for r in q0 + q1 + q2 + q3 + q4:
            r.wait_send()

    vm = pl.BlockSpec(memory_space=pltpu.VMEM)
    return pl.pallas_call(
        kern,
        out_shape=[
            jax.ShapeDtypeStruct((rows, E), f32),
            jax.ShapeDtypeStruct((1, E), f32),
            jax.ShapeDtypeStruct((n, 1, rows), f32),
            jax.ShapeDtypeStruct((1, m), f32),
        ],
        in_specs=[vm] * 4,
        out_specs=[vm] * 4,
        scratch_shapes=[
            pltpu.VMEM((s, 1, E), f32),
            pltpu.VMEM((n, 1, E), f32),
            pltpu.VMEM((n, 1, rows), f32),
            pltpu.VMEM((n, 1, m), f32),
            pltpu.VMEM((1, m), f32),
            pltpu.VMEM((s, 1, m), f32),
            pltpu.SemaphoreType.DMA((3, n - 1)),
            pltpu.SemaphoreType.DMA((3, n - 1)),
            pltpu.SemaphoreType.DMA((2, s - 1)),
            pltpu.SemaphoreType.DMA((2, s - 1)),
        ],
        compiler_params=pltpu.CompilerParams(collective_id=2, has_side_effects=True),
        name="modulation_backward",
    )(d_part, bias_part, lf, w_ada)


def head_mask(ref_shape, h):
    low = lax.broadcasted_iota(jnp.int32, ref_shape, 1) < HD
    return low if h == 0 else ~low


def pick(values, h):
    return jnp.where(head_mask(values.shape, h), values, jnp.zeros_like(values))


def attend_forward_kernel(n, q_ref, *refs):
    k_refs, v_refs, (o_ref, lse_ref) = refs[:n], refs[n : 2 * n], refs[2 * n :]
    q = q_ref[...] * bf16(HD**-0.5)
    total = None
    for h in range(2):
        qh = pick(q, h)
        scores = [nt(k[...], qh) for k in k_refs]
        top = scores[0].max(axis=0, keepdims=True)
        for sc in scores[1:]:
            top = jnp.maximum(top, sc.max(axis=0, keepdims=True))
        mass, out = None, None
        for sc, v in zip(scores, v_refs):
            p = jnp.exp(sc - top)
            part = p.sum(axis=0, keepdims=True)
            mass = part if mass is None else mass + part
            o = tn(pick(v[...], h), p.astype(bf16))
            out = o if out is None else out + o
        out = out * (1.0 / mass)
        total = out if total is None else total + out
        lse_ref[0, h : h + 1, :] = top + jnp.log(mass)
    o_ref[...] = total.T.astype(bf16)


def attend_forward(q, ks, vs):
    T, D = q.shape
    n = len(ks)

    def col(rows):
        return pl.BlockSpec((rows, 128), lambda i: (0, i))

    keys = sum(k.shape[0] for k in ks)
    return pl.pallas_call(
        partial(attend_forward_kernel, n),
        grid=(D // 128,),
        in_specs=[col(T)] + [col(k.shape[0]) for k in ks] * 2,
        out_specs=[col(T), pl.BlockSpec((1, 2, T), lambda i: (i, 0, 0))],
        out_shape=[jax.ShapeDtypeStruct((T, D), bf16), jax.ShapeDtypeStruct((D // 128, 2, T), f32)],
        cost_estimate=pl.CostEstimate(flops=16 * T * keys * D, bytes_accessed=4 * (T + keys) * D, transcendentals=0),
        name="attend_forward",
    )(q, *ks, *vs)


def attend_backward_kernel(n, q_ref, e_ref, lse_ref, *refs):
    k_refs, v_refs = refs[:n], refs[n : 2 * n]
    dq_ref, dk_refs, dv_refs = refs[2 * n], refs[2 * n + 1 : 3 * n + 1], refs[3 * n + 1 :]
    q, e = q_ref[...] * bf16(HD**-0.5), e_ref[...]
    dqt = None
    dks, dvs = [None] * n, [None] * n
    for h in range(2):
        qh, eh = pick(q, h), pick(e, h)
        lse = lse_ref[0, h : h + 1, :]
        probs, dprobs, cross = [], [], None
        for j in range(n):
            p = jnp.exp(nt(k_refs[j][...], qh) - lse)
            dp = nt(v_refs[j][...], eh)
            part = (p * dp).sum(axis=0, keepdims=True)
            cross = part if cross is None else cross + part
            dv = nn(p.astype(bf16), eh)
            dvs[j] = dv if dvs[j] is None else dvs[j] + dv
            probs.append(p)
            dprobs.append(dp)
        for j in range(n):
            ds = (probs[j] * (dprobs[j] - cross)).astype(bf16)
            dk = nn(ds, qh)
            dks[j] = dk if dks[j] is None else dks[j] + dk
            t = tn(pick(k_refs[j][...], h), ds)
            dqt = t if dqt is None else dqt + t
    dq_ref[...] = (dqt * (HD**-0.5)).T.astype(bf16)
    for j in range(n):
        dk_refs[j][...] = dks[j].astype(dk_refs[j].dtype)
        dv_refs[j][...] = dvs[j].astype(dv_refs[j].dtype)


def attend_backward(q, e, lse, ks, vs):
    T, D = q.shape
    n = len(ks)

    def col(rows):
        return pl.BlockSpec((rows, 128), lambda i: (0, i))

    keys = sum(k.shape[0] for k in ks)
    cols = [col(k.shape[0]) for k in ks]
    kv = [jax.ShapeDtypeStruct(k.shape, f32 if j == 0 else bf16) for j, k in enumerate(ks)]
    res = pl.pallas_call(
        partial(attend_backward_kernel, n),
        grid=(D // 128,),
        in_specs=[col(T), col(T), pl.BlockSpec((1, 2, T), lambda i: (i, 0, 0))] + cols * 2,
        out_specs=[col(T)] + cols * 2,
        out_shape=[jax.ShapeDtypeStruct((T, D), bf16)] + kv * 2,
        cost_estimate=pl.CostEstimate(flops=30 * T * keys * D, bytes_accessed=8 * (T + keys) * D, transcendentals=0),
        name="attend_backward",
    )(q, e, lse, *ks, *vs)
    return res[0], res[1 : n + 1], res[n + 1 :]


def seq_shift(value, k, s):
    return lax.ppermute(value, "seq", [(i, (i + k) % s) for i in range(s)])


def tie(*values):
    return lax.optimization_barrier(values)


class Exchange:
    def __init__(self, grad, n, s):
        A, B = grid_of(n)
        self.A, self.B, self.s = A, B, s
        self.into = None
        if grad.ndim == 2:
            self.grad = grad.reshape(A, B, 2, -1, grad.shape[1])
        me = lax.axis_index("fsdp")
        self.a, self.b, self.c = me // (2 * B), (me // 2) % B, me % 2

    @staticmethod
    def halved(grad, n, s):
        ex = Exchange(grad, n, s)
        ex.half = grad.reshape((ex.A, ex.B) + grad.shape[1:])
        return ex

    @staticmethod
    def summed(grad, n, s):
        ex = Exchange(grad[None], n, s)
        ex.total, ex.a, ex.from_a = grad[None], 0, []
        return ex

    def shift(self, value, da, db, dc):
        A, B = self.A, self.B

        def at(a, b, c):
            return (a * B + b) * 2 + c

        pairs = [
            (at(a, b, c), at((a + da) % A, (b + db) % B, (c + dc) % 2))
            for a in range(A)
            for b in range(B)
            for c in range(2)
        ]
        return lax.ppermute(value, "fsdp", pairs)

    def take(self, value, index, axis):
        return lax.dynamic_index_in_dim(value, index, axis, keepdims=False)

    def c_send(self):
        self.out = [self.take(self.grad, 1 - self.c, 2)]
        return self.out

    def c_start(self, out):
        self.into = self.shift(out[0], 0, 0, 1)

    def b_sum(self, index):
        if self.into is None:
            return self.take(self.half, index, 1).astype(f32)
        mine = self.take(self.take(self.grad, self.c, 2), index, 1)
        return mine.astype(f32) + self.take(self.into, index, 1).astype(f32)

    def b_send(self):
        return [self.b_sum((self.b + k) % self.B).astype(bf16) for k in range(1, self.B)]

    def b_start(self, out):
        self.from_b = [self.shift(v, 0, k + 1, 0) for k, v in enumerate(out)]

    def a_send(self):
        total = self.b_sum(self.b)
        for v in self.from_b:
            total = total + v.astype(f32)
        self.total = total
        return [self.take(total, (self.a + k) % self.A, 0).astype(bf16) for k in range(1, self.A)]

    def a_start(self, out):
        self.from_a = [self.shift(v, k + 1, 0, 0) for k, v in enumerate(out)]

    def x_send(self):
        total = self.take(self.total, self.a, 0).astype(f32)
        for v in self.from_a:
            total = total + v.astype(f32)
        if self.s != 2:
            self.total = lax.psum(total, "seq")
            return []
        self.total = total.astype(bf16)
        return [self.total]

    def x_start(self, out):
        if self.s == 2:
            self.from_x = seq_shift(out[0], 1, 2)
            self.total = out[0]

    def result(self):
        if self.s != 2:
            return self.total
        return self.total.astype(f32) + self.from_x.astype(f32)


def remote(src, dst, send, recv, device):
    return pltpu.make_async_remote_copy(
        src_ref=src, dst_ref=dst, send_sem=send, recv_sem=recv, device_id=device, device_id_type=MESH
    )


def greet(devices):
    bar = pltpu.get_barrier_semaphore()
    for d in devices:
        pl.semaphore_signal(bar, inc=1, device_id=d, device_id_type=MESH)
    pl.semaphore_wait(bar, len(devices))


class Place:
    def __init__(self, n):
        self.A, self.B = grid_of(n)
        me = lax.axis_index("fsdp")
        self.me = me
        self.a, self.b, self.c = me // (2 * self.B), lax.rem(me // 2, self.B), lax.rem(me, 2)

    def dev(self, a, b, c):
        return {"fsdp": (a * self.B + b) * 2 + c}

    def at_a(self, k):
        return self.dev(lax.rem(self.a + k, self.A), self.b, self.c)

    def at_b(self, k):
        return self.dev(self.a, lax.rem(self.b + k, self.B), self.c)

    def sibling(self):
        return self.dev(self.a, self.b, 1 - self.c)

    def all(self):
        return [self.at_a(k) for k in range(1, self.A)] + [self.at_b(k) for k in range(1, self.B)] + [self.sibling()]


def add32(*values):
    total = values[0].astype(f32)
    for v in values[1:]:
        total = total + v.astype(f32)
    return total


def gelu_both(x):
    k = 0.7978845608028654
    sq = x * x
    th = jnp.tanh(k * (x + 0.044715 * (sq * x)))
    half = 0.5 * (1.0 + th)
    slope = half + (0.5 * k) * x * (1.0 - th * th) * (1.0 + (3 * 0.044715) * sq)
    return x * half, slope


def normalize(v):
    center = v - jnp.mean(v, axis=-1, keepdims=True)
    rscale = lax.rsqrt(jnp.mean(center * center, axis=-1, keepdims=True) + norm_eps)
    return center * rscale, rscale


def feed_forward(middle, branch, attn, g, vectors, b_fc1, proj_w, w1, w2, n):
    T, D = middle.shape
    FF = w1.shape[1]
    A, B = grid_of(n)
    J, r1, r2 = A * B, D // n, FF // n
    W = 2 * r2
    RB = min(T, 64)

    def kern(
        mid_ref, br_ref, attn_ref, g_ref, vec_ref, b1_ref, pw_ref, w1_ref, w2_ref,
        out_ref, dmid_ref, dattn_ref, sums_ref, bfc1_ref, gproj_ref, g1_ref, g2_ref,
        h2, h2t, dm, dh2, mlp, dbr, w1b, w2b, gb, cr, ys, yr, zs, zr, t1, c1, s1,
        wsem, osem, cs, crs, c1s, c1r, yss, yrs, zss, zrs,
    ):
        at = Place(n)
        greet(at.all())
        shift2, scale2, gate2, gate1, bias2 = [vec_ref[i : i + 1, :] for i in range(5)]

        def tile(t):
            k, m = t // B, lax.rem(t, B)
            return lax.rem(at.a + 1 + k, A) * B + lax.rem(at.b + 1 + m, B)

        def weights(t, slot):
            lo = pl.multiple_of(tile(t) * W, W)
            return (
                pltpu.make_async_copy(w1_ref.at[:, pl.ds(lo, W)], w1b.at[slot], wsem.at[0, slot]),
                pltpu.make_async_copy(w2_ref.at[pl.ds(lo, W), :], w2b.at[slot], wsem.at[1, slot]),
            )

        for w in weights(0, 0):
            w.start()

        def head(i, _):
            rows = pl.ds(pl.multiple_of(i * RB, RB), RB)
            normed, _r = normalize(mid_ref[rows, :])
            h2[rows, :] = (normed * (1.0 + scale2) + shift2).astype(bf16)
            dm[rows, :] = (g_ref[rows, :].astype(f32) * gate2).astype(bf16)
            return 0

        lax.fori_loop(0, T // RB, head, 0)
        for i in range(0, D, 256):
            h2t[i : i + 256, :] = h2[:, i : i + 256].T
        dh2[...] = jnp.zeros_like(dh2)
        mlp[...] = jnp.zeros_like(mlp)
        sums_ref[...] = jnp.zeros_like(sums_ref)

        def c2_copy(t):
            return remote(gb.at[t, 1 - at.c], cr.at[t], cs.at[t], crs.at[t], at.sibling())

        def c1_copy(t, slot):
            return remote(t1.at[slot, :, 1 - at.c], c1.at[t], c1s.at[t], c1r.at[t], at.sibling())

        def y_copy(k, m):
            return remote(ys.at[k, m], yr.at[k, m], yss.at[k, m], yrs.at[k, m], at.at_b(m + 1))

        def z_copy(k):
            return remote(zs.at[k], zr.at[k], zss.at[k], zrs.at[k], at.at_a(k + 1))

        def s1_copy(t, slot):
            lo = pl.multiple_of(tile(t) * W, W)
            return pltpu.make_async_copy(s1.at[slot], g1_ref.at[:, :, pl.ds(lo, W)], osem.at[slot])

        def chip_sum1(t, slot, first):
            c1_copy(t, slot).wait()

            @pl.when(jnp.logical_not(first))
            def _():
                s1_copy(t, slot).wait()

            def part(i, _):
                s1[slot, i] = add32(t1[slot, i, at.c], c1[t, i]).astype(bf16)
                return 0

            lax.fori_loop(0, J, part, 0)
            s1_copy(t, slot).start()

        R2 = min(r2, 64)

        def own_sum(t, k):
            c2_copy(t).wait()
            for m in range(B - 1):
                y_copy(k, m).wait()

        def send_y(k, m):
            t = k * B + m
            c2_copy(t).wait()

            def part(i, _):
                rows = pl.ds(pl.multiple_of(i * R2, R2), R2)
                ys[k, m, rows, :] = add32(gb[t, at.c, rows, :], cr[t, rows, :]).astype(bf16)
                return 0

            lax.fori_loop(0, r2 // R2, part, 0)
            y_copy(k, m).start()

        def send_z(k):
            t = k * B + B - 1
            own_sum(t, k)

            def part(i, _):
                rows = pl.ds(pl.multiple_of(i * R2, R2), R2)
                total = add32(gb[t, at.c, rows, :], cr[t, rows, :], *[yr[k, m, rows, :] for m in range(B - 1)])
                zs[k, rows, :] = total.astype(bf16)
                return 0

            lax.fori_loop(0, r2 // R2, part, 0)
            z_copy(k).start()

        def pair(k, _):
            for m in range(B):
                t = k * B + m
                slot = m % 2
                for w in weights(t, slot):
                    w.wait()

                @pl.when(t + 1 < J)
                def _():
                    for w in weights(t + 1, 1 - slot):
                        w.start()

                j = tile(t)
                act, slope = gelu_both(nn(h2[...], w1b[slot]) + b1_ref[j])
                act = act.astype(bf16)
                g2t = tn(act, dm[...]).astype(bf16)
                gb[t, 0] = g2t[:r2]
                gb[t, 1] = g2t[r2:]
                c2_copy(t).start()
                dpre = (nt(dm[...], w2b[slot]) * slope).astype(bf16)
                bfc1_ref[j] = jnp.sum(dpre.astype(f32), axis=0, keepdims=True)
                t1[slot] = nn(h2t[...], dpre).astype(bf16).reshape(J, 2, r1, W)
                c1_copy(t, slot).start()
                mlp[...] += nn(act, w2b[slot])
                dh2[...] += nt(dpre, w1b[slot])
                if m > 0:
                    chip_sum1(t - 1, 1 - slot, jnp.logical_and(k == 0, m < 3))
                    send_y(k, m - 1)
                else:

                    @pl.when(k > 0)
                    def _():
                        chip_sum1(t - 1, 1 - slot, k * B < 3)

                if m == B - 1:

                    @pl.when(k > 0)
                    def _():
                        send_z(k - 1)

            return 0

        lax.fori_loop(0, A, pair, 0)
        chip_sum1(J - 1, (B - 1) % 2, jnp.bool_(J < 3))

        def back(i, _):
            rows = pl.ds(pl.multiple_of(i * RB, RB), RB)
            mid = mid_ref[rows, :]
            gf = g_ref[rows, :].astype(f32)
            normed, rscale = normalize(mid)
            dh = dh2[rows, :]
            up = dh * (1.0 + scale2)
            dmid = gf + rscale * (
                up
                - jnp.mean(up, axis=-1, keepdims=True)
                - normed * jnp.mean(up * normed, axis=-1, keepdims=True)
            )
            dmid_ref[rows, :] = dmid
            db = (dmid * gate1).astype(bf16)
            dbr[rows, :] = db
            ml = mlp[rows, :] + bias2
            out_ref[rows, :] = (mid + gate2 * ml).astype(bf16)
            for row, v in enumerate((dh, dh * normed, gf * ml, dmid * br_ref[rows, :], dm[rows, :], db)):
                sums_ref[row : row + 1, :] += jnp.sum(v.astype(f32), axis=0, keepdims=True)
            return 0

        lax.fori_loop(0, T // RB, back, 0)
        dattn_ref[...] = nt(dbr[...], pw_ref[...]).astype(bf16)

        def proj(i, _):
            cols = pl.ds(pl.multiple_of(i * 256, 256), 256)
            gproj_ref[cols, :] = tn(attn_ref[:, cols], dbr[...]).astype(bf16)
            return 0

        lax.fori_loop(0, D // 256, proj, 0)

        last = J - 1
        own_sum(last, A - 1)
        for k in range(A - 1):
            z_copy(k).wait()

        def part(i, _):
            rows = pl.ds(pl.multiple_of(i * R2, R2), R2)
            total = add32(
                gb[last, at.c, rows, :],
                cr[last, rows, :],
                *[yr[A - 1, m, rows, :] for m in range(B - 1)],
                *[zr[k, rows, :] for k in range(A - 1)],
            )
            g2_ref[rows, :] = total.astype(bf16)
            return 0

        lax.fori_loop(0, r2 // R2, part, 0)
        s1_copy(J - 2, 0).wait()
        s1_copy(J - 1, 1).wait()

    vm, hbm = pl.BlockSpec(memory_space=pltpu.VMEM), pl.BlockSpec(memory_space=pl.ANY)
    sds = jax.ShapeDtypeStruct
    dma = pltpu.SemaphoreType.DMA
    return pl.pallas_call(
        kern,
        out_shape=[
            sds((T, D), bf16), sds((T, D), f32), sds((T, D), bf16), sds((8, D), f32), sds((J, 1, W), f32),
            sds((D, D), bf16), sds((J, r1, FF), bf16), sds((r2, D), bf16),
        ],
        in_specs=[vm] * 7 + [hbm] * 2,
        out_specs=[vm] * 6 + [hbm, vm],
        scratch_shapes=[
            pltpu.VMEM((T, D), bf16), pltpu.VMEM((D, T), bf16), pltpu.VMEM((T, D), bf16),
            pltpu.VMEM((T, D), f32), pltpu.VMEM((T, D), f32), pltpu.VMEM((T, D), bf16),
            pltpu.VMEM((2, D, W), bf16), pltpu.VMEM((2, W, D), bf16),
            pltpu.VMEM((J, 2, r2, D), bf16), pltpu.VMEM((J, r2, D), bf16),
            pltpu.VMEM((A, B - 1, r2, D), bf16), pltpu.VMEM((A, B - 1, r2, D), bf16),
            pltpu.VMEM((A - 1, r2, D), bf16), pltpu.VMEM((A - 1, r2, D), bf16),
            pltpu.VMEM((2, J, 2, r1, W), bf16), pltpu.VMEM((J, J, r1, W), bf16), pltpu.VMEM((2, J, r1, W), bf16),
            dma((2, 2)), dma((2,)), dma((J,)), dma((J,)), dma((J,)), dma((J,)),
            dma((A, B - 1)), dma((A, B - 1)), dma((A - 1,)), dma((A - 1,)),
        ],
        compiler_params=pltpu.CompilerParams(
            collective_id=3, has_side_effects=True, vmem_limit_bytes=64 * 1024 * 1024 - 65536
        ),
        name="feed_forward",
    )(middle, branch, attn, g, vectors, b_fc1.reshape(J, 1, W), proj_w, w1, w2)


def layer_norm(values):
    center = values - jnp.mean(values, axis=-1, keepdims=True)
    rscale = lax.rsqrt(jnp.mean(center * center, axis=-1, keepdims=True) + norm_eps)
    return (center * rscale, rscale)


def norm_back(upstream, normed, rscale):
    mean_up = jnp.mean(upstream, axis=-1, keepdims=True)
    mean_cross = jnp.mean(upstream * normed, axis=-1, keepdims=True)
    return rscale * (upstream - mean_up - normed * mean_cross)


def on_device(
    tokens,
    condition,
    w_ada,
    b_ada,
    w_qkv,
    b_qv,
    w_proj,
    b_proj,
    w_fc1,
    b_fc1,
    w_fc2,
    b_fc2,
    cotangent,
):
    n, s = lax.axis_size("fsdp"), lax.axis_size("seq")
    width = tokens.shape[-1]
    T = tokens.shape[1]
    tokens_f = tokens[0].astype(f32)
    grad_out = cotangent[0].astype(f32)

    lifted, silu_back = jax.vjp(jax.nn.silu, condition.astype(f32))
    lifted_q = lifted.astype(bf16).astype(f32).reshape(n, 1, width // n)
    packed = [b_qv, b_proj, b_fc1, b_fc2, b_ada]
    edges = [sum(v.shape[0] for v in packed[:i]) for i in range(6)]
    modulation, lf, biases = modulation_forward(lifted_q, w_ada, jnp.concatenate(packed).astype(f32)[None], n)
    qv_b, proj_b, fc1_b, fc2_b, ada_b = [biases[:, 0, edges[i] : edges[i + 1]].reshape(1, -1) for i in range(5)]
    modulation = modulation + ada_b
    shift_one, scale_one, gate_one, shift_two, scale_two, gate_two = jnp.split(modulation, 6, axis=-1)

    h, q4 = w_fc1.shape[1], w_fc2.shape[1]
    chunks = [(0, width, width, True), (0, 2 * width, width, True), (0, 0, width, True), (1, 0, width, True)]
    chunks += [(3, i * (q4 // 4), q4 // 4, i != 2) for i in range(4)]
    chunks += [(2, i * (h // 8), h // 8, i % 2 == 0) for i in range(8)]
    qkv_w, proj_w, fc1_w, fc2_w = gather_weights([w_qkv, w_proj, w_fc1, w_fc2], chunks, n, s)

    normed_one, rscale_one = layer_norm(tokens_f)
    hidden_one = (normed_one * (1.0 + scale_one) + shift_one).astype(bf16)
    keys = nn(hidden_one, qkv_w[:, width : 2 * width]).astype(bf16)
    values = (nn(hidden_one, qkv_w[:, 2 * width :]) + qv_b[:, width:]).astype(bf16)
    ks = [keys] + [seq_shift(keys, k, s) for k in range(1, s)]
    vs = [values] + [seq_shift(values, k, s) for k in range(1, s)]
    queries = (nn(hidden_one, qkv_w[:, :width]) + qv_b[:, :width]).astype(bf16)
    attn, lse = attend_forward(queries, ks, vs)
    branch = nn(attn, proj_w) + proj_b
    middle = tokens_f + gate_one * branch

    half_d = width // 2

    def exchange(lhs, rhs):
        return Exchange(tn(lhs, rhs).astype(bf16), n, s)

    vectors = jnp.concatenate([shift_two, scale_two, gate_two, gate_one, fc2_b, jnp.zeros((3, width), f32)], axis=0)
    result, d_middle, d_attn, sums, bias_fc1, grad_proj, half_fc1, sum_fc2 = feed_forward(
        middle, branch, attn, cotangent[0], vectors, fc1_b, proj_w, fc1_w, fc2_w, n
    )
    d_shift_two, d_scale_two, d_gate_two, d_gate_one, bias_fc2, bias_proj = [sums[i : i + 1] for i in range(6)]
    bias_fc1 = bias_fc1.reshape(-1)
    fc2 = Exchange.summed(sum_fc2, n, s)
    sum_fc2 = fc2.x_send()
    fc2.x_start(sum_fc2)
    half_f = fc1_w.shape[1] // 2
    fc1a, fc1b = Exchange.halved(half_fc1[:, :, :half_f], n, s), Exchange.halved(half_fc1[:, :, half_f:], n, s)
    proj = Exchange(grad_proj, n, s)
    fc1a.b_start(fc1a.b_send())
    fc1b.b_start(fc1b.b_send())
    proj.c_start(proj.c_send())
    halves = []
    lo = slice(0, half_d)
    hi = slice(half_d, width)

    def attention(part):
        heads = slice(part.start // 128, part.stop // 128)
        grads = attend_backward(
            queries[:, part], d_attn[:, part], lse[heads], [k[:, part] for k in ks], [v[:, part] for v in vs]
        )
        return grads

    def back(dk):
        return [seq_shift(dk[k], s - k, s) for k in range(1, s)]

    q1, dk1, dv1 = attention(lo)
    q1, dk1, dv1, sa, sb = tie(q1, dk1, dv1, proj.b_send(), fc1a.a_send())
    rk1, rv1 = back(dk1), back(dv1)
    proj.b_start(sa)
    fc1a.a_start(sb)
    d_attn, q1 = tie(d_attn, q1)
    q2, dk2, dv2 = attention(hi)
    q2, dk2, dv2, sa, sb = tie(q2, dk2, dv2, fc1b.a_send(), proj.a_send())
    rk2, rv2 = back(dk2), back(dv2)
    fc1b.a_start(sa)
    proj.a_start(sb)

    def joined(q, dk, rk, dv, rv):
        gk, gv = dk[0], dv[0]
        for v in rk:
            gk = gk + v.astype(f32)
        for v in rv:
            gv = gv + v.astype(f32)
        return jnp.concatenate([q, gk.astype(bf16), gv.astype(bf16)], axis=1)

    d1 = joined(q1, dk1, rk1, dv1, rv1)
    qkv1 = exchange(hidden_one, d1)
    d2, sa = tie(joined(q2, dk2, rk2, dv2, rv2), qkv1.c_send())
    qkv1.c_start(sa)
    qkv2 = exchange(hidden_one, d2)
    d2, sa, sb = tie(d2, qkv1.b_send(), qkv2.c_send())
    qkv1.b_start(sa)
    qkv2.c_start(sb)
    sums1, sums2 = jnp.sum(d1, axis=0, dtype=f32), jnp.sum(d2, axis=0, dtype=f32)
    bias_qv = jnp.concatenate([sums1[:half_d], sums2[:half_d], sums1[width:], sums2[width:]])
    d_qkv = jnp.concatenate([v[:, i * half_d : (i + 1) * half_d] for i in range(3) for v in (d1, d2)], axis=1)
    d_hidden_one = nt(d_qkv, qkv_w)
    d_shift_one = jnp.sum(d_hidden_one, axis=0, keepdims=True)
    d_scale_one = jnp.sum(d_hidden_one * normed_one, axis=0, keepdims=True)
    grad_input = d_middle + norm_back(d_hidden_one * (1.0 + scale_one), normed_one, rscale_one)
    d_scale_one, sa, sb, sc = tie(d_scale_one, qkv2.b_send(), proj.x_send(), fc1a.x_send())
    qkv2.b_start(sa)
    proj.x_start(sb)
    fc1a.x_start(sc)

    d_part = jnp.concatenate(
        [d_shift_one, d_scale_one, d_gate_one, d_shift_two, d_scale_two, d_gate_two], axis=-1
    )
    bias_part = jnp.concatenate(
        [bias_qv.reshape(n, -1), bias_proj.reshape(n, -1), bias_fc1.reshape(n, -1), bias_fc2.reshape(n, -1)], axis=1
    )[:, None, :]
    total_ada, sums_ada, d_lifted, total_bias = modulation_backward(d_part, bias_part, lf, w_ada, n, s)
    share = b_ada.shape[0]
    total_bada = lax.dynamic_slice_in_dim(sums_ada[0], lax.axis_index("fsdp") * share, share)
    grad_condition = silu_back(d_lifted.reshape(1, width))[0]
    total_bias, sa, sb = tie(total_bias, qkv1.a_send(), fc1b.x_send())
    qkv1.a_start(sa)
    fc1b.x_start(sb)
    qkv2.a_start(qkv2.a_send())
    qkv1.x_start(qkv1.x_send())
    qkv2.x_start(qkv2.x_send())
    total_fc2 = fc2.result()
    total_fc1 = jnp.concatenate([fc1a.result(), fc1b.result()], axis=1)
    total_proj = proj.result()
    r1, r2 = qkv1.result(), qkv2.result()
    total_qkv = jnp.concatenate([v[:, i * half_d : (i + 1) * half_d] for i in range(3) for v in (r1, r2)], axis=1)
    total_bqv, total_bproj, total_bfc1, total_bfc2 = [total_bias[0, edges[i] : edges[i + 1]] for i in range(4)]
    return (
        result[None],
        grad_input[None],
        grad_condition,
        total_ada,
        total_bada,
        total_qkv,
        total_bqv,
        total_proj,
        total_bproj,
        total_fc1,
        total_bfc1,
        total_fc2,
        total_bfc2,
    )


def solution(mesh):
    weights = (P("fsdp", None), P("fsdp")) * 5
    return jax.shard_map(
        on_device,
        mesh=mesh,
        in_specs=(P("fsdp", "seq", None), P("fsdp", None)) + weights + (P("fsdp", "seq", None),),
        out_specs=(P("fsdp", "seq", None), P("fsdp", "seq", None), P("fsdp", None)) + weights,
        check_vma=False,
    )
```

```python
from functools import partial

import jax
import jax.numpy as jnp
from jax import lax
from jax.experimental import pallas as pl
from jax.experimental.pallas import tpu as pltpu
from jax.sharding import PartitionSpec as P

HD = 64
norm_eps = 1e-06
f32 = jnp.float32
bf16 = jnp.bfloat16
MESH = pl.DeviceIdType.MESH


def grid_of(n):
    b = 2 if n == 16 else 4
    return n // (2 * b), b


def nt(a, b):
    return lax.dot_general(a, b, (((1,), (1,)), ((), ())), preferred_element_type=f32)


def nn(a, b):
    return lax.dot_general(a, b, (((1,), (0,)), ((), ())), preferred_element_type=f32)


def tn(a, b):
    return lax.dot_general(a, b, (((0,), (0,)), ((), ())), preferred_element_type=f32)


def gather_weights(shards, chunks, n, s):
    A, B = grid_of(n)
    nc, ns = len(chunks), len(shards)
    NB = (A - 1) + (B - 1)
    steps = 2 * NB + 1

    def kern(*refs):
        ins, outs = refs[:ns], refs[ns : 2 * ns]
        own_sem, send, recv = refs[2 * ns :]
        me, x = lax.axis_index("fsdp"), lax.axis_index("seq")
        a, b, c = me // (2 * B), (me // 2) % B, me % 2

        def dev(a, b, c):
            return {"fsdp": (a * B + b) * 2 + c}

        apeers = [lax.rem(a + k, A) for k in range(1, A)]
        bpeers = [lax.rem(b + k, B) for k in range(1, B)]
        peers = [dev(p, b, c) for p in apeers] + [dev(a, p, c) for p in bpeers]
        peers.append(dev(a, b, 1 - c))
        if s == 2:
            peers.append({"seq": 1 - x})
        bar = pltpu.get_barrier_semaphore()
        for p in peers:
            pl.semaphore_signal(bar, inc=1, device_id=p, device_id_type=MESH)
        pl.semaphore_wait(bar, len(peers))
        owns = [pltpu.make_async_copy(ins[i], outs[i].at[a, b, c], own_sem.at[i]) for i in range(ns)]
        for o in owns:
            o.start()

        def cp(i, k, src, dst, d):
            r = pltpu.make_async_remote_copy(
                src_ref=src,
                dst_ref=dst,
                send_sem=send.at[i, k],
                recv_sem=recv.at[i, k],
                device_id=d,
                device_id_type=MESH,
            )
            r.start()
            return r

        za, zb, zx, zc = {}, {}, {}, {}

        def part(i):
            w, lo, sz, sh = chunks[i]
            if sh and s == 2:
                return w, pl.ds(pl.multiple_of(lo + x * (sz // 2), 128), sz // 2)
            return w, pl.ds(lo, sz)

        for i in range(nc):
            w, cols = part(i)
            za[i] = [
                cp(i, k, ins[w].at[:, cols], outs[w].at[a, b, c, :, cols], dev(p, b, c))
                for k, p in enumerate(apeers)
            ]
        for o in owns:
            o.wait()

        def phase_b(i):
            w, cols = part(i)
            for r in za[i]:
                r.wait_recv()
            sl = outs[w].at[:, b, c, :, cols]
            zb[i] = [cp(i, A - 1 + k, sl, sl, dev(a, p, c)) for k, p in enumerate(bpeers)]

        def phase_x(i):
            w, cols = part(i)
            for r in zb[i]:
                r.wait_recv()
            zx[i] = []
            if chunks[i][3] and s == 2:
                for k, p in enumerate(apeers):
                    sl = outs[w].at[p, :, c, :, cols]
                    zx[i].append(cp(i, NB + k, sl, sl, {"seq": 1 - x}))
                for k, p in enumerate(bpeers):
                    sl = outs[w].at[a, p, c, :, cols]
                    zx[i].append(cp(i, NB + A - 1 + k, sl, sl, {"seq": 1 - x}))

        def phase_c(i):
            w, lo, sz, sh = chunks[i]
            for r in zx[i]:
                r.wait_recv()
            sl = outs[w].at[:, :, c, :, pl.ds(lo, sz)]
            zc[i] = cp(i, 2 * NB, sl, sl, dev(a, b, 1 - c))

        for i in range(nc + 2):
            if i < nc:
                phase_b(i)
            if 0 <= i - 1 < nc:
                phase_x(i - 1)
            if 0 <= i - 2 < nc:
                phase_c(i - 2)
        for i in range(nc):
            zc[i].wait_recv()
            for r in za[i] + zb[i] + zx[i] + [zc[i]]:
                r.wait_send()

    res = pl.pallas_call(
        kern,
        out_shape=[jax.ShapeDtypeStruct((A, B, 2) + w.shape, w.dtype) for w in shards],
        in_specs=[pl.BlockSpec(memory_space=pltpu.VMEM)] * ns,
        out_specs=[pl.BlockSpec(memory_space=pl.ANY)] * ns,
        scratch_shapes=[
            pltpu.SemaphoreType.DMA((ns,)),
            pltpu.SemaphoreType.DMA((nc, steps)),
            pltpu.SemaphoreType.DMA((nc, steps)),
        ],
        compiler_params=pltpu.CompilerParams(collective_id=0, has_side_effects=True),
        name="gather_weights",
    )(*shards)
    return [r.reshape((n * w.shape[0], w.shape[1])) for r, w in zip(res, shards)]


def fsdp_peers(n, me):
    return [lax.rem(me + k, n) for k in range(1, n)]


def modulation_forward(lifted, w_ada, bias, n):
    rows, E = w_ada.shape
    m = bias.shape[-1]

    def kern(l_ref, w_ref, bias_ref, mod_ref, lf_ref, bout_ref, part, acc, send, recv):
        me = lax.axis_index("fsdp")
        peers = fsdp_peers(n, me)
        bar = pltpu.get_barrier_semaphore()
        for p in peers:
            pl.semaphore_signal(bar, inc=1, device_id={"fsdp": p}, device_id_type=MESH)
        pl.semaphore_wait(bar, n - 1)

        def cp(i, k, src, dst):
            r = pltpu.make_async_remote_copy(
                src_ref=src,
                dst_ref=dst,
                send_sem=send.at[i, k],
                recv_sem=recv.at[i, k],
                device_id={"fsdp": peers[k]},
                device_id_type=MESH,
            )
            r.start()
            return r

        lf_ref[me] = l_ref[me]
        bout_ref[me] = bias_ref[...]
        first = [cp(0, k, l_ref.at[p], lf_ref.at[me]) for k, p in enumerate(peers)]
        other = [cp(1, k, bias_ref, bout_ref.at[me]) for k, p in enumerate(peers)]
        for r in first:
            r.wait_recv()
        lf = lf_ref[...].reshape(n, rows).astype(bf16)
        part[...] = nn(lf, w_ref[...]).reshape(n, 1, E)
        acc[0] = part[me]
        last = [cp(2, k, part.at[p], acc.at[k + 1]) for k, p in enumerate(peers)]
        for r in last:
            r.wait_recv()
        mod_ref[...] = jnp.sum(acc[...], axis=0)
        for r in other:
            r.wait_recv()
        for r in first + other + last:
            r.wait_send()

    vm = pl.BlockSpec(memory_space=pltpu.VMEM)
    return pl.pallas_call(
        kern,
        out_shape=[
            jax.ShapeDtypeStruct((1, E), f32),
            jax.ShapeDtypeStruct((n, 1, rows), f32),
            jax.ShapeDtypeStruct((n, 1, m), f32),
        ],
        in_specs=[vm] * 3,
        out_specs=[vm] * 3,
        scratch_shapes=[
            pltpu.VMEM((n, 1, E), f32),
            pltpu.VMEM((n, 1, E), f32),
            pltpu.SemaphoreType.DMA((3, n - 1)),
            pltpu.SemaphoreType.DMA((3, n - 1)),
        ],
        compiler_params=pltpu.CompilerParams(collective_id=1, has_side_effects=True),
        name="modulation_forward",
    )(lifted, w_ada, bias)


def head_mask(ref_shape, h):
    low = lax.broadcasted_iota(jnp.int32, ref_shape, 1) < HD
    return low if h == 0 else ~low


def pick(values, h):
    return jnp.where(head_mask(values.shape, h), values, jnp.zeros_like(values))


def attend_forward_kernel(n, q_ref, *refs):
    k_refs, v_refs, (o_ref, lse_ref) = refs[:n], refs[n : 2 * n], refs[2 * n :]
    q = q_ref[...] * bf16(HD**-0.5)
    total = None
    for h in range(2):
        qh = pick(q, h)
        scores = [nt(k[...], qh) for k in k_refs]
        top = scores[0].max(axis=0, keepdims=True)
        for sc in scores[1:]:
            top = jnp.maximum(top, sc.max(axis=0, keepdims=True))
        mass, out = None, None
        for sc, v in zip(scores, v_refs):
            p = jnp.exp(sc - top)
            part = p.sum(axis=0, keepdims=True)
            mass = part if mass is None else mass + part
            o = tn(pick(v[...], h), p.astype(bf16))
            out = o if out is None else out + o
        out = out * (1.0 / mass)
        total = out if total is None else total + out
        lse_ref[0, h : h + 1, :] = top + jnp.log(mass)
    o_ref[...] = total.T.astype(bf16)


def attend_forward(q, ks, vs):
    T, D = q.shape
    n = len(ks)

    def col(rows):
        return pl.BlockSpec((rows, 128), lambda i: (0, i))

    keys = sum(k.shape[0] for k in ks)
    return pl.pallas_call(
        partial(attend_forward_kernel, n),
        grid=(D // 128,),
        in_specs=[col(T)] + [col(k.shape[0]) for k in ks] * 2,
        out_specs=[col(T), pl.BlockSpec((1, 2, T), lambda i: (i, 0, 0))],
        out_shape=[jax.ShapeDtypeStruct((T, D), bf16), jax.ShapeDtypeStruct((D // 128, 2, T), f32)],
        cost_estimate=pl.CostEstimate(flops=16 * T * keys * D, bytes_accessed=4 * (T + keys) * D, transcendentals=0),
        name="attend_forward",
    )(q, *ks, *vs)


def seq_shift(value, k, s):
    return lax.ppermute(value, "seq", [(i, (i + k) % s) for i in range(s)])


def remote(src, dst, send, recv, device):
    return pltpu.make_async_remote_copy(
        src_ref=src, dst_ref=dst, send_sem=send, recv_sem=recv, device_id=device, device_id_type=MESH
    )


def greet(devices):
    bar = pltpu.get_barrier_semaphore()
    for d in devices:
        pl.semaphore_signal(bar, inc=1, device_id=d, device_id_type=MESH)
    pl.semaphore_wait(bar, len(devices))


class Place:
    def __init__(self, n):
        self.A, self.B = grid_of(n)
        me = lax.axis_index("fsdp")
        self.me = me
        self.a, self.b, self.c = me // (2 * self.B), lax.rem(me // 2, self.B), lax.rem(me, 2)

    def dev(self, a, b, c):
        return {"fsdp": (a * self.B + b) * 2 + c}

    def at_a(self, k):
        return self.dev(lax.rem(self.a + k, self.A), self.b, self.c)

    def at_b(self, k):
        return self.dev(self.a, lax.rem(self.b + k, self.B), self.c)

    def sibling(self):
        return self.dev(self.a, self.b, 1 - self.c)

    def all(self):
        return [self.at_a(k) for k in range(1, self.A)] + [self.at_b(k) for k in range(1, self.B)] + [self.sibling()]


def add32(*values):
    total = values[0].astype(f32)
    for v in values[1:]:
        total = total + v.astype(f32)
    return total


def gelu_both(x):
    k = 0.7978845608028654
    sq = x * x
    th = jnp.tanh(k * (x + 0.044715 * (sq * x)))
    half = 0.5 * (1.0 + th)
    slope = half + (0.5 * k) * x * (1.0 - th * th) * (1.0 + (3 * 0.044715) * sq)
    return x * half, slope


def normalize(v):
    center = v - jnp.mean(v, axis=-1, keepdims=True)
    rscale = lax.rsqrt(jnp.mean(center * center, axis=-1, keepdims=True) + norm_eps)
    return center * rscale, rscale


def feed_forward(middle, branch, attn, g, vectors, b_fc1, proj_w, w1, w2, n):
    T, D = middle.shape
    FF = w1.shape[1]
    A, B = grid_of(n)
    J, r1, r2 = A * B, D // n, FF // n
    W = 2 * r2
    RB = min(T, 64)

    def kern(
        mid_ref, br_ref, attn_ref, g_ref, vec_ref, b1_ref, pw_ref, w1_ref, w2_ref,
        out_ref, dmid_ref, dattn_ref, sums_ref, bfc1_ref, gproj_ref, g1_ref, g2_ref,
        h2, h2t, dm, dh2, mlp, dbr, w1b, w2b, gb, cr, ys, yr, zs, zr, t1, c1, s1,
        wsem, osem, cs, crs, c1s, c1r, yss, yrs, zss, zrs,
    ):
        at = Place(n)
        greet(at.all())
        shift2, scale2, gate2, gate1, bias2 = [vec_ref[i : i + 1, :] for i in range(5)]

        def tile(t):
            k, m = t // B, lax.rem(t, B)
            return lax.rem(at.a + 1 + k, A) * B + lax.rem(at.b + 1 + m, B)

        def weights(t, slot):
            lo = pl.multiple_of(tile(t) * W, W)
            return (
                pltpu.make_async_copy(w1_ref.at[:, pl.ds(lo, W)], w1b.at[slot], wsem.at[0, slot]),
                pltpu.make_async_copy(w2_ref.at[pl.ds(lo, W), :], w2b.at[slot], wsem.at[1, slot]),
            )

        for w in weights(0, 0):
            w.start()

        def head(i, _):
            rows = pl.ds(pl.multiple_of(i * RB, RB), RB)
            normed, _r = normalize(mid_ref[rows, :])
            h2[rows, :] = (normed * (1.0 + scale2) + shift2).astype(bf16)
            dm[rows, :] = (g_ref[rows, :].astype(f32) * gate2).astype(bf16)
            return 0

        lax.fori_loop(0, T // RB, head, 0)
        for i in range(0, D, 256):
            h2t[i : i + 256, :] = h2[:, i : i + 256].T
        dh2[...] = jnp.zeros_like(dh2)
        mlp[...] = jnp.zeros_like(mlp)
        sums_ref[...] = jnp.zeros_like(sums_ref)

        def c2_copy(t):
            return remote(gb.at[t, 1 - at.c], cr.at[t], cs.at[t], crs.at[t], at.sibling())

        def c1_copy(t, slot):
            return remote(t1.at[slot, :, 1 - at.c], c1.at[t], c1s.at[t], c1r.at[t], at.sibling())

        def y_copy(k, m):
            return remote(ys.at[k, m], yr.at[k, m], yss.at[k, m], yrs.at[k, m], at.at_b(m + 1))

        def z_copy(k):
            return remote(zs.at[k], zr.at[k], zss.at[k], zrs.at[k], at.at_a(k + 1))

        def s1_copy(t, slot):
            lo = pl.multiple_of(tile(t) * W, W)
            return pltpu.make_async_copy(s1.at[slot], g1_ref.at[:, :, pl.ds(lo, W)], osem.at[slot])

        def chip_sum1(t, slot, first):
            c1_copy(t, slot).wait()

            @pl.when(jnp.logical_not(first))
            def _():
                s1_copy(t, slot).wait()

            def part(i, _):
                s1[slot, i] = add32(t1[slot, i, at.c], c1[t, i]).astype(bf16)
                return 0

            lax.fori_loop(0, J, part, 0)
            s1_copy(t, slot).start()

        R2 = min(r2, 64)

        def own_sum(t, k):
            c2_copy(t).wait()
            for m in range(B - 1):
                y_copy(k, m).wait()

        def send_y(k, m):
            t = k * B + m
            c2_copy(t).wait()

            def part(i, _):
                rows = pl.ds(pl.multiple_of(i * R2, R2), R2)
                ys[k, m, rows, :] = add32(gb[t, at.c, rows, :], cr[t, rows, :]).astype(bf16)
                return 0

            lax.fori_loop(0, r2 // R2, part, 0)
            y_copy(k, m).start()

        def send_z(k):
            t = k * B + B - 1
            own_sum(t, k)

            def part(i, _):
                rows = pl.ds(pl.multiple_of(i * R2, R2), R2)
                total = add32(gb[t, at.c, rows, :], cr[t, rows, :], *[yr[k, m, rows, :] for m in range(B - 1)])
                zs[k, rows, :] = total.astype(bf16)
                return 0

            lax.fori_loop(0, r2 // R2, part, 0)
            z_copy(k).start()

        def pair(k, _):
            for m in range(B):
                t = k * B + m
                slot = m % 2
                for w in weights(t, slot):
                    w.wait()

                @pl.when(t + 1 < J)
                def _():
                    for w in weights(t + 1, 1 - slot):
                        w.start()

                j = tile(t)
                act, slope = gelu_both(nn(h2[...], w1b[slot]) + b1_ref[j])
                act = act.astype(bf16)
                g2t = tn(act, dm[...]).astype(bf16)
                gb[t, 0] = g2t[:r2]
                gb[t, 1] = g2t[r2:]
                c2_copy(t).start()
                dpre = (nt(dm[...], w2b[slot]) * slope).astype(bf16)
                bfc1_ref[j] = jnp.sum(dpre.astype(f32), axis=0, keepdims=True)
                t1[slot] = nn(h2t[...], dpre).astype(bf16).reshape(J, 2, r1, W)
                c1_copy(t, slot).start()
                mlp[...] += nn(act, w2b[slot])
                dh2[...] += nt(dpre, w1b[slot])
                if m > 0:
                    chip_sum1(t - 1, 1 - slot, jnp.logical_and(k == 0, m < 3))
                    send_y(k, m - 1)
                else:

                    @pl.when(k > 0)
                    def _():
                        chip_sum1(t - 1, 1 - slot, k * B < 3)

                if m == B - 1:

                    @pl.when(k > 0)
                    def _():
                        send_z(k - 1)

            return 0

        lax.fori_loop(0, A, pair, 0)
        chip_sum1(J - 1, (B - 1) % 2, jnp.bool_(J < 3))

        def back(i, _):
            rows = pl.ds(pl.multiple_of(i * RB, RB), RB)
            mid = mid_ref[rows, :]
            gf = g_ref[rows, :].astype(f32)
            normed, rscale = normalize(mid)
            dh = dh2[rows, :]
            up = dh * (1.0 + scale2)
            dmid = gf + rscale * (
                up
                - jnp.mean(up, axis=-1, keepdims=True)
                - normed * jnp.mean(up * normed, axis=-1, keepdims=True)
            )
            dmid_ref[rows, :] = dmid
            db = (dmid * gate1).astype(bf16)
            dbr[rows, :] = db
            ml = mlp[rows, :] + bias2
            out_ref[rows, :] = (mid + gate2 * ml).astype(bf16)
            for row, v in enumerate((dh, dh * normed, gf * ml, dmid * br_ref[rows, :], dm[rows, :], db)):
                sums_ref[row : row + 1, :] += jnp.sum(v.astype(f32), axis=0, keepdims=True)
            return 0

        lax.fori_loop(0, T // RB, back, 0)
        dattn_ref[...] = nt(dbr[...], pw_ref[...]).astype(bf16)

        def proj(i, _):
            cols = pl.ds(pl.multiple_of(i * 256, 256), 256)
            gproj_ref[cols, :] = tn(attn_ref[:, cols], dbr[...]).astype(bf16)
            return 0

        lax.fori_loop(0, D // 256, proj, 0)

        last = J - 1
        own_sum(last, A - 1)
        for k in range(A - 1):
            z_copy(k).wait()

        def part(i, _):
            rows = pl.ds(pl.multiple_of(i * R2, R2), R2)
            total = add32(
                gb[last, at.c, rows, :],
                cr[last, rows, :],
                *[yr[A - 1, m, rows, :] for m in range(B - 1)],
                *[zr[k, rows, :] for k in range(A - 1)],
            )
            g2_ref[rows, :] = total.astype(bf16)
            return 0

        lax.fori_loop(0, r2 // R2, part, 0)
        s1_copy(J - 2, 0).wait()
        s1_copy(J - 1, 1).wait()

    vm, hbm = pl.BlockSpec(memory_space=pltpu.VMEM), pl.BlockSpec(memory_space=pl.ANY)
    sds = jax.ShapeDtypeStruct
    dma = pltpu.SemaphoreType.DMA
    return pl.pallas_call(
        kern,
        out_shape=[
            sds((T, D), bf16), sds((T, D), f32), sds((T, D), bf16), sds((8, D), f32), sds((J, 1, W), f32),
            sds((D, D), bf16), sds((J, r1, FF), bf16), sds((r2, D), bf16),
        ],
        in_specs=[vm] * 7 + [hbm] * 2,
        out_specs=[vm] * 6 + [hbm, vm],
        scratch_shapes=[
            pltpu.VMEM((T, D), bf16), pltpu.VMEM((D, T), bf16), pltpu.VMEM((T, D), bf16),
            pltpu.VMEM((T, D), f32), pltpu.VMEM((T, D), f32), pltpu.VMEM((T, D), bf16),
            pltpu.VMEM((2, D, W), bf16), pltpu.VMEM((2, W, D), bf16),
            pltpu.VMEM((J, 2, r2, D), bf16), pltpu.VMEM((J, r2, D), bf16),
            pltpu.VMEM((A, B - 1, r2, D), bf16), pltpu.VMEM((A, B - 1, r2, D), bf16),
            pltpu.VMEM((A - 1, r2, D), bf16), pltpu.VMEM((A - 1, r2, D), bf16),
            pltpu.VMEM((2, J, 2, r1, W), bf16), pltpu.VMEM((J, J, r1, W), bf16), pltpu.VMEM((2, J, r1, W), bf16),
            dma((2, 2)), dma((2,)), dma((J,)), dma((J,)), dma((J,)), dma((J,)),
            dma((A, B - 1)), dma((A, B - 1)), dma((A - 1,)), dma((A - 1,)),
        ],
        compiler_params=pltpu.CompilerParams(
            collective_id=3, has_side_effects=True, vmem_limit_bytes=64 * 1024 * 1024 - 65536
        ),
        name="feed_forward",
    )(middle, branch, attn, g, vectors, b_fc1.reshape(J, 1, W), proj_w, w1, w2)


class RowSum:
    @staticmethod
    def scratch(U, r, W, A, B, cores):
        dma = pltpu.SemaphoreType.DMA
        shapes = [
            pltpu.VMEM((U, B - 1, A, r, W), bf16), pltpu.VMEM((U, A - 1, r, W), bf16),
            pltpu.VMEM((U, A - 1, r, W), bf16), pltpu.VMEM((U, r, W), bf16), pltpu.VMEM((U, r, W), bf16),
            dma((U, B - 1)), dma((U, B - 1)), dma((U, A - 1)), dma((U, A - 1)), dma((U,)), dma((U,)),
        ]
        if cores:
            shapes += [
                pltpu.VMEM((U, A * B, r, W), bf16), pltpu.VMEM((U, B - 1, A, r, W), bf16), dma((U,)), dma((U,)),
            ]
        return shapes

    def __init__(self, at, s, peer, refs, grad=None, half=None):
        self.at, self.s, self.peer = at, s, peer
        self.grad, self.half = grad, half
        self.yr, self.zs, self.zr, self.xs, self.xr = refs[:5]
        self.yss, self.yrs, self.zss, self.zrs, self.xss, self.xrs = refs[5:11]
        if grad is not None:
            self.cr, self.ys, self.css, self.crs = refs[11:]

    def c_copy(self, u):
        return remote(
            self.grad.at[u, :, 1 - self.at.c], self.cr.at[u], self.css.at[u], self.crs.at[u], self.at.sibling()
        )

    def y_source(self, u, m):
        return self.ys.at[u, m]

    def y_copy(self, u, m):
        src = self.y_source(u, m)
        return remote(src, self.yr.at[u, m], self.yss.at[u, m], self.yrs.at[u, m], self.at.at_b(m + 1))

    def z_copy(self, u, k):
        return remote(self.zs.at[u, k], self.zr.at[u, k], self.zss.at[u, k], self.zrs.at[u, k], self.at.at_a(k + 1))

    def x_copy(self, u):
        return remote(self.xs.at[u], self.xr.at[u], self.xss.at[u], self.xrs.at[u], self.peer)

    def chip(self, u, a, b):
        j = a * self.at.B + b
        return add32(self.grad[u, j, self.at.c], self.cr[u, j])

    def own(self, u, a):
        base = self.chip(u, a, self.at.b) if self.half is None else self.half(u, a)
        return add32(base, *[self.yr[u, m, a] for m in range(self.at.B - 1)])

    def send_y(self, u):
        self.c_copy(u).wait()
        for m in range(self.at.B - 1):
            b = lax.rem(self.at.b + m + 1, self.at.B)
            for a in range(self.at.A):
                self.ys[u, m, a] = self.chip(u, a, b).astype(bf16)
            self.y_copy(u, m).start()

    def send_z(self, u):
        for m in range(self.at.B - 1):
            self.y_copy(u, m).wait()
        for k in range(self.at.A - 1):
            self.zs[u, k] = self.own(u, lax.rem(self.at.a + k + 1, self.at.A)).astype(bf16)
            self.z_copy(u, k).start()

    def send_x(self, u):
        for k in range(self.at.A - 1):
            self.z_copy(u, k).wait()
        total = add32(self.own(u, self.at.a), *[self.zr[u, k] for k in range(self.at.A - 1)])
        if self.s != 2:
            return total
        self.xs[u] = total.astype(bf16)
        self.x_copy(u).start()
        return None

    def finish(self, u):
        self.x_copy(u).wait()
        return add32(self.xs[u], self.xr[u])


def attention_and_sums(
    q, ks, vs, d_attn, lse, hidden, tokens, scale, d_middle, w_qkv, half_fc1, grad_proj, sum_fc2, sums, bias_fc1, lf, w_ada, n, s
):
    T, D = q.shape
    FF = half_fc1.shape[-1]
    A, B = grid_of(n)
    J, r1, r2 = A * B, D // n, FF // n
    GW = 256
    U = D // GW
    F = FF // U
    E = 6 * D
    RB = min(T, 64)
    rows_a = D // n
    m_bias = [2 * D // n, D // n, FF // n, D // n]
    starts = [0, 2 * D, 3 * D, 3 * D + FF]
    NBIAS = 4 * D + FF
    blocks = [max(v, 128) for v in m_bias]
    offs = [sum(blocks[:i]) for i in range(4)]
    M = sum(blocks)
    nq = len(RowSum.scratch(U, r1, 3 * GW, A, B, True))
    nf = len(RowSum.scratch(U, r1, F, A, B, False))

    def kern(*refs):
        it = iter(refs)

        def take(count):
            return [next(it) for _ in range(count)]

        (q_ref,) = take(1)
        k_refs, v_refs = take(s), take(s)
        e_ref, lse_ref, h_ref, tok_ref, sc_ref, dmid_ref, w_ref, f1_ref, gp_ref, f2_ref, sum_ref, bf_ref, lf_ref, wa_ref = take(14)
        gt_ref, oq_ref, op_ref, o1_ref, o2_ref, gw_ref, gb_ref, dl_ref, bo_ref = take(9)
        h1t, dqg, kvl, kvs, kvr, dg, gq, wq, f1o, x2 = take(10)
        dh1 = gt_ref
        wsem, fsem, kss, krs, x2s, x2r = take(6)
        scr_q, scr_p, scr_f = take(nq), take(nq), take(nf)
        dx, dm, lp, bsum, bx, bsx = take(6)
        asend, arecv, lsend, lrecv, bsend, brecv, xsend, xrecv = take(8)

        at = Place(n)
        me, x = at.me, lax.axis_index("seq")
        peers = fsdp_peers(n, me)

        def seq_dev(k):
            return {"seq": lax.rem(x + k, s)}

        greet([{"fsdp": p} for p in peers] + [seq_dev(k) for k in range(1, s)])
        other = seq_dev(1)
        sq = RowSum(at, s, other, scr_q, grad=gq)
        sp = RowSum(at, s, other, scr_p, grad=gp_ref)
        sf = RowSum(at, s, other, scr_f, half=lambda u, a: f1o[u, a])

        def f_source(u, m):
            b = lax.rem(at.b + m + 1, B)
            return f1_ref.at[:, b, :, pl.ds(pl.multiple_of(u * F, F), F)]

        sf.y_source = f_source
        own_f = [
            pltpu.make_async_copy(f1_ref.at[:, at.b, :, pl.ds(u * F, F)], f1o.at[u], fsem.at[u]) for u in range(U)
        ]
        sp.c_copy(0).start()
        for u in range(U):
            for m in range(B - 1):
                sf.y_copy(u, m).start()
        if s == 2:
            x2_copy = remote(f2_ref, x2, x2s, x2r, other)
            x2_copy.start()
        for o in own_f:
            o.start()

        def h_copy(i):
            k = i % 3
            return pltpu.make_async_copy(
                h_ref.at[:, pl.ds(i * GW, GW)], dg.at[:, pl.ds(k * GW, GW)], wsem.at[k]
            )

        for i in range(min(U, 3)):
            h_copy(i).start()
        for i in range(U):
            h_copy(i).wait()
            k = i % 3
            h1t[i * GW : (i + 1) * GW, :] = dg[:, k * GW : (k + 1) * GW].T
            if i + 3 < U:
                h_copy(i + 3).start()
        dh1[...] = jnp.zeros_like(dh1)
        for o in own_f:
            o.wait()

        def w_copy(u, i):
            lo = pl.multiple_of(i * D + u * GW, GW)
            return pltpu.make_async_copy(w_ref.at[:, pl.ds(lo, GW)], wq.at[i], wsem.at[i])

        def kv_copy(u, k):
            return remote(kvs.at[u, k - 1], kvr.at[u, k - 1], kss.at[u, k - 1], krs.at[u, k - 1], seq_dev(s - k))

        def attend(u):
            slot = lax.rem(u, 2)
            for o in range(2):
                pair = u * 2 + o
                cols = pl.ds(pl.multiple_of(pair * 128, 128), 128)
                here = slice(o * 128, o * 128 + 128)
                qv, e = q_ref[:, cols] * bf16(HD**-0.5), e_ref[:, cols]
                dqt, dks, dvs = None, [None] * s, [None] * s
                for h in range(2):
                    qh, eh = pick(qv, h), pick(e, h)
                    total = lse_ref[pair, h : h + 1, :]
                    probs, dprobs, cross = [], [], None
                    for j in range(s):
                        p = jnp.exp(nt(k_refs[j][:, cols], qh) - total)
                        dp = nt(v_refs[j][:, cols], eh)
                        part = (p * dp).sum(axis=0, keepdims=True)
                        cross = part if cross is None else cross + part
                        dv = nn(p.astype(bf16), eh)
                        dvs[j] = dv if dvs[j] is None else dvs[j] + dv
                        probs.append(p)
                        dprobs.append(dp)
                    for j in range(s):
                        ds = (probs[j] * (dprobs[j] - cross)).astype(bf16)
                        dk = nn(ds, qh)
                        dks[j] = dk if dks[j] is None else dks[j] + dk
                        t = tn(pick(k_refs[j][:, cols], h), ds)
                        dqt = t if dqt is None else dqt + t
                dqg[slot, :, here] = (dqt * (HD**-0.5)).T.astype(bf16)
                kvl[slot, 0, :, here] = dks[0]
                kvl[slot, 1, :, here] = dvs[0]
                for j in range(1, s):
                    kvs[u, j - 1, 0, :, here] = dks[j].astype(bf16)
                    kvs[u, j - 1, 1, :, here] = dvs[j].astype(bf16)
            for k in range(1, s):
                kv_copy(u, k).start()

        def project(u):
            slot = lax.rem(u, 2)
            for k in range(1, s):
                kv_copy(u, k).wait()
            dg[:, :GW] = dqg[slot]
            for i in range(2):
                lo = (i + 1) * GW
                dg[:, lo : lo + GW] = add32(kvl[slot, i], *[kvr[u, k, i] for k in range(s - 1)]).astype(bf16)
            part = 256 // (2 * r1)
            for i in range(D // 256):
                g = nn(h1t[i * 256 : (i + 1) * 256, :], dg[...]).astype(bf16)
                gq[u, i * part : (i + 1) * part] = g.reshape(part, 2, r1, 3 * GW)
            sq.c_copy(u).start()
            here = pl.ds(pl.multiple_of(u * GW, GW), GW)
            bsum[:, here] = jnp.sum(dg[:, :GW].astype(f32), axis=0, keepdims=True)
            there = pl.ds(pl.multiple_of(D + u * GW, GW), GW)
            bsum[:, there] = jnp.sum(dg[:, 2 * GW :].astype(f32), axis=0, keepdims=True)
            for i in range(3):
                w_copy(u, i).wait()
            total = nt(dg[:, :GW], wq[0])
            for i in range(1, 3):
                total = total + nt(dg[:, i * GW : (i + 1) * GW], wq[i])
            dh1[...] += total

        def step(i, _):
            @pl.when(i < U)
            def _():
                attend(i)

            @pl.when(jnp.logical_and(i >= 1, i <= U))
            def _():
                project(i - 1)

            @pl.when(i < U)
            def _():
                for k in range(3):
                    w_copy(i, k).start()

            @pl.when(i == 0)
            def _():
                sp.send_y(0)

            @pl.when(i < U)
            def _():
                sf.send_z(i)

            @pl.when(i >= 2)
            def _():
                sq.send_y(i - 2)

            return 0

        lax.fori_loop(0, U + 2, step, 0)
        sp.send_z(0)
        for u in range(U - 2):
            sq.send_z(u)

        sums = [jnp.zeros((1, D), f32), jnp.zeros((1, D), f32)]
        scale1 = sc_ref[...]

        def back(i, carry):
            rows = pl.ds(pl.multiple_of(i * RB, RB), RB)
            normed, rscale = normalize(tok_ref[rows, :].astype(f32))
            dh = dh1[rows, :]
            up = dh * (1.0 + scale1)
            gt_ref[rows, :] = dmid_ref[rows, :] + rscale * (
                up
                - jnp.mean(up, axis=-1, keepdims=True)
                - normed * jnp.mean(up * normed, axis=-1, keepdims=True)
            )
            return (
                carry[0] + jnp.sum(dh, axis=0, keepdims=True),
                carry[1] + jnp.sum(dh * normed, axis=0, keepdims=True),
            )

        shift1_sum, scale1_sum = lax.fori_loop(0, T // RB, back, tuple(sums))
        parts = [shift1_sum, scale1_sum, sum_ref[3:4, :], sum_ref[0:1, :], sum_ref[1:2, :], sum_ref[2:3, :]]
        for i, v in enumerate(parts):
            dx[x, :, i * D : (i + 1) * D] = v
        mod_x = [remote(dx.at[x], dx.at[x], xsend.at[0, k - 1], xrecv.at[0, k - 1], seq_dev(k)) for k in range(1, s)]
        for c in mod_x:
            c.start()
        bsum[:, starts[1] : starts[1] + D] = sum_ref[5:6, :]
        bsum[:, starts[2] : starts[2] + FF] = bf_ref[...]
        bsum[:, starts[3] : starts[3] + D] = sum_ref[4:5, :]

        def block(p, i):
            lo = starts[i] + ((p * m_bias[i]) // blocks[i]) * blocks[i]
            return bsum.at[:, pl.ds(pl.multiple_of(lo, 128), blocks[i])]

        def bias_copy(k, p, i):
            dst = bx.at[me, :, pl.ds(offs[i], blocks[i])]
            return remote(block(p, i), dst, bsend.at[i, k], brecv.at[i, k], {"fsdp": p})

        bias_out = [bias_copy(k, p, i) for k, p in enumerate(peers) for i in range(4)]
        for c in bias_out:
            c.start()
        for i in range(4):
            lo = starts[i] + ((me * m_bias[i]) // blocks[i]) * blocks[i]
            bx[me, :, offs[i] : offs[i] + blocks[i]] = bsum[:, pl.ds(pl.multiple_of(lo, 128), blocks[i])]

        for u in range(U):
            if s == 2:
                sf.send_x(u)
            else:
                o1_ref[:, u * F : (u + 1) * F] = sf.send_x(u)
        sq.send_z(U - 2)
        for c in mod_x:
            c.wait()
        dm[me] = jnp.sum(dx[...], axis=0).astype(bf16).astype(f32)
        mod_all = [remote(dm.at[me], dm.at[me], asend.at[k], arecv.at[k], {"fsdp": p}) for k, p in enumerate(peers)]
        for c in mod_all:
            c.start()
        sq.send_z(U - 1)
        for c in bias_out:
            c.wait()
        bsx[x] = jnp.sum(bx[...], axis=0)
        bias_x = [remote(bsx.at[x], bsx.at[x], xsend.at[1, k - 1], xrecv.at[1, k - 1], seq_dev(k)) for k in range(1, s)]
        for c in bias_x:
            c.start()
        if s == 2:
            sp.send_x(0)
        else:
            op_ref[...] = sp.send_x(0)
        for c in mod_all:
            c.wait()
        dmod = dm[...].reshape(n, E).astype(bf16)
        lp[...] = nt(dmod, wa_ref[...]).reshape(n, 1, rows_a)
        dl_ref[me] = lp[me]
        lift = [remote(lp.at[p], dl_ref.at[me], lsend.at[k], lrecv.at[k], {"fsdp": p}) for k, p in enumerate(peers)]
        for c in lift:
            c.start()
        gw_ref[...] = tn(lf_ref[...].reshape(n, rows_a).astype(bf16), dmod)
        gb_ref[...] = jnp.sum(dm[...], axis=0)

        def put_q(u, value):
            for i in range(3):
                oq_ref[:, i * D + u * GW : i * D + (u + 1) * GW] = value[:, i * GW : (i + 1) * GW]

        for u in range(U):
            value = sq.send_x(u)
            if s != 2:
                put_q(u, value)
        if s == 2:
            x2_copy.wait()
            o2_ref[...] = add32(f2_ref[...], x2[...])
            for u in range(U):
                o1_ref[:, u * F : (u + 1) * F] = sf.finish(u)
            op_ref[...] = sp.finish(0)
            for u in range(U):
                put_q(u, sq.finish(u))
        else:
            o2_ref[...] = f2_ref[...].astype(f32)
        for c in bias_x:
            c.wait()
        bo_ref[...] = jnp.sum(bsx[...], axis=0)
        for c in lift:
            c.wait()

    vm, hbm = pl.BlockSpec(memory_space=pltpu.VMEM), pl.BlockSpec(memory_space=pl.ANY)
    sds, dma = jax.ShapeDtypeStruct, pltpu.SemaphoreType.DMA
    res = pl.pallas_call(
        kern,
        out_shape=[
            sds((T, D), f32), sds((r1, 3 * D), f32), sds((r1, D), f32), sds((r1, FF), f32), sds((r2, D), f32),
            sds((rows_a, E), f32), sds((1, E), f32), sds((n, 1, rows_a), f32), sds((1, M), f32),
        ],
        in_specs=[vm] * (3 + 2 * s) + [hbm] + [vm] * 3 + [hbm, hbm] + [vm] * 6,
        out_specs=[vm] * 9,
        scratch_shapes=[
            pltpu.VMEM((D, T), bf16), pltpu.VMEM((2, T, GW), bf16),
            pltpu.VMEM((2, 2, T, GW), f32), pltpu.VMEM((U, s - 1, 2, T, GW), bf16),
            pltpu.VMEM((U, s - 1, 2, T, GW), bf16), pltpu.VMEM((T, 3 * GW), bf16),
            pltpu.VMEM((U, J, 2, r1, 3 * GW), bf16), pltpu.VMEM((3, D, GW), bf16),
            pltpu.VMEM((U, A, r1, F), bf16), pltpu.VMEM((r2, D), bf16),
            dma((3,)), dma((U,)), dma((U, s - 1)), dma((U, s - 1)), dma(()), dma(()),
        ]
        + RowSum.scratch(U, r1, 3 * GW, A, B, True)
        + RowSum.scratch(1, r1, D, A, B, True)
        + RowSum.scratch(U, r1, F, A, B, False)
        + [
            pltpu.VMEM((s, 1, E), f32), pltpu.VMEM((n, 1, E), f32), pltpu.VMEM((n, 1, rows_a), f32),
            pltpu.VMEM((1, NBIAS), f32), pltpu.VMEM((n, 1, M), f32), pltpu.VMEM((s, 1, M), f32),
            dma((n - 1,)), dma((n - 1,)), dma((n - 1,)), dma((n - 1,)),
            dma((4, n - 1)), dma((4, n - 1)), dma((2, s - 1)), dma((2, s - 1)),
        ],
        compiler_params=pltpu.CompilerParams(
            collective_id=4, has_side_effects=True, vmem_limit_bytes=64 * 1024 * 1024 - 65536
        ),
        name="attention_and_sums",
    )(
        q, *ks, *vs, d_attn, lse, hidden, tokens, scale, d_middle, w_qkv, half_fc1.reshape(A, B, r1, FF),
        grad_proj.reshape(1, J, 2, r1, D), sum_fc2, sums, bias_fc1, lf, w_ada,
    )
    grad_tokens, t_qkv, t_proj, t_fc1, t_fc2, t_ada, ada_sums, d_lifted, bias = res
    if s != 2:
        t_qkv, t_proj, t_fc1, t_fc2 = lax.psum((t_qkv, t_proj, t_fc1, t_fc2), "seq")
    me = lax.axis_index("fsdp")
    biases = []
    for width, wide, off in zip(m_bias, blocks, offs):
        biases.append(lax.dynamic_slice_in_dim(bias[0, off : off + wide], (me * width) % wide, width))
    return grad_tokens, t_qkv, t_proj, t_fc1, t_fc2, t_ada, ada_sums, d_lifted, biases


def layer_norm(values):
    center = values - jnp.mean(values, axis=-1, keepdims=True)
    rscale = lax.rsqrt(jnp.mean(center * center, axis=-1, keepdims=True) + norm_eps)
    return (center * rscale, rscale)


def on_device(
    tokens,
    condition,
    w_ada,
    b_ada,
    w_qkv,
    b_qv,
    w_proj,
    b_proj,
    w_fc1,
    b_fc1,
    w_fc2,
    b_fc2,
    cotangent,
):
    n, s = lax.axis_size("fsdp"), lax.axis_size("seq")
    width = tokens.shape[-1]
    T = tokens.shape[1]
    tokens_f = tokens[0].astype(f32)
    grad_out = cotangent[0].astype(f32)

    lifted, silu_back = jax.vjp(jax.nn.silu, condition.astype(f32))
    lifted_q = lifted.astype(bf16).astype(f32).reshape(n, 1, width // n)
    packed = [b_qv, b_proj, b_fc1, b_fc2, b_ada]
    edges = [sum(v.shape[0] for v in packed[:i]) for i in range(6)]
    modulation, lf, biases = modulation_forward(lifted_q, w_ada, jnp.concatenate(packed).astype(f32)[None], n)
    qv_b, proj_b, fc1_b, fc2_b, ada_b = [biases[:, 0, edges[i] : edges[i + 1]].reshape(1, -1) for i in range(5)]
    modulation = modulation + ada_b
    shift_one, scale_one, gate_one, shift_two, scale_two, gate_two = jnp.split(modulation, 6, axis=-1)

    h, q4 = w_fc1.shape[1], w_fc2.shape[1]
    chunks = [(0, width, width, True), (0, 2 * width, width, True), (0, 0, width, True), (1, 0, width, True)]
    chunks += [(3, i * (q4 // 4), q4 // 4, i != 2) for i in range(4)]
    chunks += [(2, i * (h // 8), h // 8, i % 2 == 0) for i in range(8)]
    qkv_w, proj_w, fc1_w, fc2_w = gather_weights([w_qkv, w_proj, w_fc1, w_fc2], chunks, n, s)

    normed_one, rscale_one = layer_norm(tokens_f)
    hidden_one = (normed_one * (1.0 + scale_one) + shift_one).astype(bf16)
    keys = nn(hidden_one, qkv_w[:, width : 2 * width]).astype(bf16)
    values = (nn(hidden_one, qkv_w[:, 2 * width :]) + qv_b[:, width:]).astype(bf16)
    ks = [keys] + [seq_shift(keys, k, s) for k in range(1, s)]
    vs = [values] + [seq_shift(values, k, s) for k in range(1, s)]
    queries = (nn(hidden_one, qkv_w[:, :width]) + qv_b[:, :width]).astype(bf16)
    attn, lse = attend_forward(queries, ks, vs)
    branch = nn(attn, proj_w) + proj_b
    middle = tokens_f + gate_one * branch

    vectors = jnp.concatenate([shift_two, scale_two, gate_two, gate_one, fc2_b, jnp.zeros((3, width), f32)], axis=0)
    result, d_middle, d_attn, sums, bias_fc1, grad_proj, half_fc1, sum_fc2 = feed_forward(
        middle, branch, attn, cotangent[0], vectors, fc1_b, proj_w, fc1_w, fc2_w, n
    )
    grad_input, total_qkv, total_proj, total_fc1, total_fc2, total_ada, sums_ada, d_lifted, total_bias = (
        attention_and_sums(
            queries, ks, vs, d_attn, lse, hidden_one, tokens[0], scale_one, d_middle, qkv_w, half_fc1,
            grad_proj, sum_fc2, sums, bias_fc1.reshape(1, -1), lf, w_ada, n, s,
        )
    )
    share = b_ada.shape[0]
    total_bada = lax.dynamic_slice_in_dim(sums_ada[0], lax.axis_index("fsdp") * share, share)
    grad_condition = silu_back(d_lifted.reshape(1, width))[0]
    total_bqv, total_bproj, total_bfc1, total_bfc2 = total_bias
    return (
        result[None],
        grad_input[None],
        grad_condition,
        total_ada,
        total_bada,
        total_qkv,
        total_bqv,
        total_proj,
        total_bproj,
        total_fc1,
        total_bfc1,
        total_fc2,
        total_bfc2,
    )


def solution(mesh):
    weights = (P("fsdp", None), P("fsdp")) * 5
    return jax.shard_map(
        on_device,
        mesh=mesh,
        in_specs=(P("fsdp", "seq", None), P("fsdp", None)) + weights + (P("fsdp", "seq", None),),
        out_specs=(P("fsdp", "seq", None), P("fsdp", "seq", None), P("fsdp", None)) + weights,
        check_vma=False,
    )
```

```python
from functools import partial

import jax
import jax.numpy as jnp
from jax import lax
from jax.experimental import pallas as pl
from jax.experimental.pallas import tpu as pltpu
from jax.sharding import PartitionSpec as P

HD = 64
norm_eps = 1e-06
f32 = jnp.float32
bf16 = jnp.bfloat16
MESH = pl.DeviceIdType.MESH


def grid_of(n):
    b = 2 if n == 16 else 4
    return n // (2 * b), b


def nt(a, b):
    return lax.dot_general(a, b, (((1,), (1,)), ((), ())), preferred_element_type=f32)


def nn(a, b):
    return lax.dot_general(a, b, (((1,), (0,)), ((), ())), preferred_element_type=f32)


def tn(a, b):
    return lax.dot_general(a, b, (((0,), (0,)), ((), ())), preferred_element_type=f32)


def fsdp_peers(n, me):
    return [lax.rem(me + k, n) for k in range(1, n)]


def head_mask(ref_shape, h):
    low = lax.broadcasted_iota(jnp.int32, ref_shape, 1) < HD
    return low if h == 0 else ~low


def pick(values, h):
    return jnp.where(head_mask(values.shape, h), values, jnp.zeros_like(values))


def remote(src, dst, send, recv, device):
    return pltpu.make_async_remote_copy(
        src_ref=src, dst_ref=dst, send_sem=send, recv_sem=recv, device_id=device, device_id_type=MESH
    )


def greet(devices):
    bar = pltpu.get_barrier_semaphore()
    for d in devices:
        pl.semaphore_signal(bar, inc=1, device_id=d, device_id_type=MESH)
    pl.semaphore_wait(bar, len(devices))


class Place:
    def __init__(self, n):
        self.A, self.B = grid_of(n)
        me = lax.axis_index("fsdp")
        self.me = me
        self.a, self.b, self.c = me // (2 * self.B), lax.rem(me // 2, self.B), lax.rem(me, 2)

    def dev(self, a, b, c):
        return {"fsdp": (a * self.B + b) * 2 + c}

    def at_a(self, k):
        return self.dev(lax.rem(self.a + k, self.A), self.b, self.c)

    def at_b(self, k):
        return self.dev(self.a, lax.rem(self.b + k, self.B), self.c)

    def sibling(self):
        return self.dev(self.a, self.b, 1 - self.c)

    def all(self):
        return [self.at_a(k) for k in range(1, self.A)] + [self.at_b(k) for k in range(1, self.B)] + [self.sibling()]


def add32(*values):
    total = values[0].astype(f32)
    for v in values[1:]:
        total = total + v.astype(f32)
    return total


def gelu_both(x):
    k = 0.7978845608028654
    sq = x * x
    th = jnp.tanh(k * (x + 0.044715 * (sq * x)))
    half = 0.5 * (1.0 + th)
    slope = half + (0.5 * k) * x * (1.0 - th * th) * (1.0 + (3 * 0.044715) * sq)
    return x * half, slope


def normalize(v):
    center = v - jnp.mean(v, axis=-1, keepdims=True)
    rscale = lax.rsqrt(jnp.mean(center * center, axis=-1, keepdims=True) + norm_eps)
    return center * rscale, rscale


def bias_block(width, n):
    return max(-(-((p * width) % 128 + width) // 128) * 128 for p in range(n))


def placed_bias(bias, n):
    width, wide = bias.shape[0], bias_block(bias.shape[0], n)
    bias = bias.astype(f32)[None]
    if wide == width:
        return bias
    at = (lax.axis_index("fsdp") * width) % 128
    return lax.dynamic_update_slice(jnp.zeros((1, wide), f32), bias, (0, at))


def forward_attention(lifted, w_ada, biases, tokens, w_qkv, w_proj, w_fc1, w_fc2, n, s):
    T, D = tokens.shape
    E = w_ada.shape[1]
    FF = w_fc1.shape[1]
    A, B = grid_of(n)
    rows_a = w_ada.shape[0]
    r1, r2 = w_qkv.shape[0], w_fc2.shape[0]
    widths = [v.shape[0] for v in biases]
    blocks = [bias_block(w, n) for w in widths]
    offs = [sum(blocks[:i]) for i in range(5)]
    bases = [n * sum(widths[:i]) for i in range(5)]
    packed = jnp.concatenate([placed_bias(v, n) for v in biases], axis=1)
    M = packed.shape[1]
    share = s == 2
    NT = 8
    CQ, CF, RF = 4 * D // NT, FF // NT, r2 // NT
    RB = min(T, 64)
    AHEAD, ATTEND = 3, NT + 5
    NA, NY = A - 1, B - 1
    NQ = 2 * (NA + NY) + 1
    NF = 4 * (NA + NY) + 2
    pairs = D // 128

    def kern(
        l_ref, wa_ref, bias_ref, tok_ref, wqkv_ref, wproj_ref, wfc1_ref, wfc2_ref,
        qkv_ref, kvr_ref, h_ref, attn_ref, lse_ref, br_ref, mid_ref, vec_ref, bfc1_ref, lf_ref, w4_ref, f1_ref, f2_ref,
        normed, wq, part, acc, bout, bvec, mod, msend, mrecv, qsend, qrecv, fsend, frecv, ksend, krecv, osem,
    ):
        at = Place(n)
        a, b, c, me, x = at.a, at.b, at.c, at.me, lax.axis_index("seq")
        peers = fsdp_peers(n, me)
        other = {"seq": lax.rem(x + 1, s)}
        greet([{"fsdp": p} for p in peers] + [{"seq": lax.rem(x + k, s)} for k in range(1, s)])

        def small(i, src, dst):
            return [
                remote(src(p), dst(k), msend.at[i, k], mrecv.at[i, k], {"fsdp": p}) for k, p in enumerate(peers)
            ]

        m_lift = small(0, lambda p: l_ref.at[p], lambda k: lf_ref.at[me])
        m_bias = small(1, lambda p: bias_ref, lambda k: bout.at[me])
        m_part = small(2, lambda p: part.at[p], lambda k: acc.at[k + 1])
        for r in m_lift + m_bias:
            r.start()
        owns = [
            pltpu.make_async_copy(wqkv_ref, wq.at[a, b, c, :, pl.ds(0, 3 * D)], osem.at[0]),
            pltpu.make_async_copy(wproj_ref, wq.at[a, b, c, :, pl.ds(3 * D, D)], osem.at[1]),
            pltpu.make_async_copy(wfc1_ref, f1_ref.at[a, b, c], osem.at[2]),
            pltpu.make_async_copy(wfc2_ref, f2_ref.at[a, b, c], osem.at[3]),
        ]
        for o in owns:
            o.start()

        def block(i):
            return jnp.where(i < 6, lax.rem(i + 2, 6), i)

        def span(lo, size, step):
            return pl.ds(pl.multiple_of(lo, step), size)

        class Ticks:
            def __init__(self, pieces, whole, send, recv):
                self.pieces, self.whole, self.send, self.recv = pieces, whole, send, recv

            def copy(self, j, i, src, dst, device):
                return remote(src, dst, self.send.at[j, i], self.recv.at[j, i], device)

            def z(self, j):
                return [
                    self.copy(j, i * NA + k, src.at[rows, cols], buf.at[a, b, c, rows, cols], at.at_a(k + 1))
                    for i, (src, buf, rows, cols, _) in enumerate(self.pieces(j))
                    for k in range(NA)
                ]

            def y(self, j):
                out, ps = [], self.pieces(j)
                for i, (_, buf, rows, cols, _) in enumerate(ps):
                    sl = buf.at[:, b, c, rows, cols]
                    out += [self.copy(j, len(ps) * NA + i * NY + k, sl, sl, at.at_b(k + 1)) for k in range(NY)]
                return out

            def x(self, j):
                out, ps = [], self.pieces(j)
                i = len(ps) * (NA + NY)
                for _, buf, rows, cols, shared in ps:
                    if not shared:
                        continue
                    for k in range(NA):
                        sl = buf.at[lax.rem(a + k + 1, A), :, c, rows, cols]
                        out.append(self.copy(j, i, sl, sl, other))
                        i += 1
                    for k in range(NY):
                        sl = buf.at[a, lax.rem(b + k + 1, B), c, rows, cols]
                        out.append(self.copy(j, i, sl, sl, other))
                        i += 1
                return out

            def c(self, j):
                ps = self.whole(j)
                i = self.send.shape[1] - len(ps)
                return [
                    self.copy(j, i + k, buf.at[:, :, c, rows, cols], buf.at[:, :, c, rows, cols], at.sibling())
                    for k, (buf, rows, cols) in enumerate(ps)
                ]

            def start_z(self, j):
                for r in self.z(j):
                    r.start()

            def start_y(self, j):
                for r in self.z(j):
                    r.wait_recv()
                for r in self.y(j):
                    r.start()

            def start_x(self, j):
                for r in self.y(j):
                    r.wait_recv()
                for r in self.x(j):
                    r.start()

            def start_c(self, j):
                for r in self.x(j):
                    r.wait_recv()
                for r in self.c(j):
                    r.start()

            def finish(self, j):
                for r in self.z(j) + self.y(j) + self.x(j):
                    r.wait_send()
                for r in self.c(j):
                    r.wait()

        all_r1 = pl.ds(0, r1)
        mine = wq.at[a, b, c]

        def q_pieces(i):
            lo, size = block(i) * CQ, CQ
            if share:
                size = CQ // 2
                lo = lo + x * size
            return [(mine, wq, all_r1, span(lo, size, size), share)]

        def q_whole(i):
            return [(wq, all_r1, span(block(i) * CQ, CQ, CQ))]

        def f_pieces(j):
            first = (wfc1_ref, f1_ref, all_r1, span(j * CF, CF, CF), False)
            if not share:
                return [first, (wfc2_ref, f2_ref, span(j * RF, RF, RF), pl.ds(0, D), False)]
            h, w = RF // 2, D // 2
            return [
                first,
                (wfc2_ref, f2_ref, span(j * RF, h, h), span(x * w, w, w), True),
                (wfc2_ref, f2_ref, span(j * RF + h, h, h), pl.ds(0, D), False),
            ]

        def f_whole(j):
            return [(f1_ref, all_r1, span(j * CF, CF, CF)), (f2_ref, span(j * RF, RF, RF), pl.ds(0, D))]

        tq, tf = Ticks(q_pieces, q_whole, qsend, qrecv), Ticks(f_pieces, f_whole, fsend, frecv)

        owns[0].wait()
        owns[1].wait()
        for i in range(AHEAD):
            tq.start_z(i)
        lf_ref[me] = l_ref[me]
        bout[me] = bias_ref[...]
        bvec[...] = jnp.zeros_like(bvec)

        def norm(i, _):
            rows = pl.ds(pl.multiple_of(i * RB, RB), RB)
            normed[rows, :] = normalize(tok_ref[rows, :].astype(f32))[0]
            return 0

        for r in m_lift:
            r.wait_recv()
        part[...] = nn(lf_ref[...].reshape(n, rows_a).astype(bf16), wa_ref[...]).reshape(n, 1, E)
        acc[0] = part[me]
        for r in m_part:
            r.start()
        for i in range(AHEAD, AHEAD + 2):
            tq.start_z(i)
        tq.start_y(0)
        lax.fori_loop(0, T // RB, norm, 0)
        tq.start_y(1)
        tq.start_x(0)
        for r in m_bias:
            r.wait_recv()
        for i in range(5):
            for p in range(n):
                lo = bases[i] + p * widths[i] // 128 * 128
                value = bout[p, :, offs[i] : offs[i] + blocks[i]]
                if widths[i] % 128 == 0:
                    bvec[:, lo : lo + blocks[i]] = value
                else:
                    bvec[:, lo : lo + blocks[i]] += value
        for r in m_part:
            r.wait_recv()
        mod[...] = jnp.sum(acc[...], axis=0) + bvec[:, bases[4] :]
        shift1, scale1, gate1, shift2, scale2, gate2 = [mod[:, i * D : (i + 1) * D] for i in range(6)]
        vec_ref[...] = jnp.zeros_like(vec_ref)
        for i, v in enumerate((shift2, scale2, gate2, gate1, bvec[:, bases[3] : bases[3] + D], scale1)):
            vec_ref[i : i + 1, :] = v
        bfc1_ref[...] = bvec[:, bases[2] : bases[2] + FF]

        def modulate(i, _):
            rows = pl.ds(pl.multiple_of(i * RB, RB), RB)
            h_ref[rows, :] = (normed[rows, :] * (1.0 + scale1) + shift1).astype(bf16)
            return 0

        lax.fori_loop(0, T // RB, modulate, 0)

        def kv_copy(m, k):
            return remote(
                qkv_ref.at[:, span(D + m * CQ, CQ, CQ)],
                kvr_ref.at[k - 1, :, span(m * CQ, CQ, CQ)],
                ksend.at[m, k - 1],
                krecv.at[m, k - 1],
                {"seq": lax.rem(x + k, s)},
            )

        def project(m):
            tq.finish(m)

            @pl.when(m < 6)
            def _():
                lo = block(m) * CQ
                cols = span(lo, CQ, CQ)
                from_v = (block(m) >= 4).astype(jnp.int32)
                bias = bvec[:, span(lo - from_v * D, CQ, CQ)]
                is_key = jnp.logical_and(block(m) >= 2, block(m) < 4)
                bias = jnp.where(is_key, jnp.zeros_like(bias), bias)
                out = nn(h_ref[...], wq[:, :, :, :, cols].reshape(D, CQ))
                qkv_ref[:, cols] = (out + bias).astype(bf16)

            @pl.when(m < 4)
            def _():
                for k in range(1, s):
                    kv_copy(m, k).start()

        def attend(pair):
            def cols(lo):
                return span(lo + pair * 128, 128, 128)

            q = qkv_ref[:, cols(0)] * bf16(HD**-0.5)
            ks = [qkv_ref[:, cols(D)]] + [kvr_ref[k, :, cols(0)] for k in range(s - 1)]
            vs = [qkv_ref[:, cols(2 * D)]] + [kvr_ref[k, :, cols(D)] for k in range(s - 1)]
            total = None
            for h in range(2):
                qh = pick(q, h)
                scores = [nt(k, qh) for k in ks]
                top = scores[0].max(axis=0, keepdims=True)
                for sc in scores[1:]:
                    top = jnp.maximum(top, sc.max(axis=0, keepdims=True))
                mass, out = None, None
                for sc, v in zip(scores, vs):
                    p = jnp.exp(sc - top)
                    got = p.sum(axis=0, keepdims=True)
                    mass = got if mass is None else mass + got
                    o = tn(pick(v, h), p.astype(bf16))
                    out = o if out is None else out + o
                out = out * (1.0 / mass)
                total = out if total is None else total + out
                lse_ref[pair, h : h + 1, :] = top + jnp.log(mass)
            attn_ref[:, cols(0)] = total.T.astype(bf16)

        def branch(i, _):
            cols = span(i * 256, 256, 256)
            weight = wq[:, :, :, :, span(3 * D + i * 256, 256, 256)].reshape(D, 256)
            got = nn(attn_ref[...], weight) + bvec[:, span(bases[1] + i * 256, 256, 256)]
            br_ref[:, cols] = got
            mid_ref[:, cols] = tok_ref[:, cols].astype(f32) + mod[:, span(2 * D + i * 256, 256, 256)] * got
            return 0

        out4 = pltpu.make_async_copy(wq, w4_ref, osem.at[0])

        def step(i, _):
            def when(lo, hi, f, shift):
                @pl.when(jnp.logical_and(i >= lo, i < hi))
                def _():
                    f(i - shift)

            when(0, NT - AHEAD, lambda j: tq.start_z(j + AHEAD), 0)
            when(NT - AHEAD, 2 * NT - AHEAD, lambda j: tf.start_z(j), NT - AHEAD)
            when(2, NT, tq.start_y, 0)
            when(NT, 2 * NT, tf.start_y, NT)
            when(2, NT + 1, tq.start_x, 1)
            when(NT + 1, 2 * NT + 1, tf.start_x, NT + 1)
            when(2, NT + 2, tq.start_c, 2)
            when(NT + 2, 2 * NT + 2, tf.start_c, NT + 2)
            when(3, NT + 3, project, 3)
            when(NT + 3, 2 * NT + 3, tf.finish, NT + 3)

            @pl.when(i == NT + 3)
            def _():
                out4.start()

            @pl.when(i == ATTEND)
            def _():
                for m in range(4):
                    for k in range(1, s):
                        kv_copy(m, k).wait()

            per = pairs // 4

            @pl.when(jnp.logical_and(i >= ATTEND, i < ATTEND + 4))
            def _():
                def one(o, _):
                    attend((i - ATTEND) * per + o)
                    return 0

                lax.fori_loop(0, per, one, 0)

            @pl.when(i == ATTEND + 4)
            def _():
                lax.fori_loop(0, D // 256, branch, 0)

            return 0

        owns[2].wait()
        owns[3].wait()
        lax.fori_loop(2, 2 * NT + 3, step, 0)
        out4.wait()
        for r in m_lift + m_bias + m_part:
            r.wait_send()

    vm, hbm = pl.BlockSpec(memory_space=pltpu.VMEM), pl.BlockSpec(memory_space=pl.ANY)
    sds, dma = jax.ShapeDtypeStruct, pltpu.SemaphoreType.DMA
    res = pl.pallas_call(
        kern,
        out_shape=[
            sds((T, 3 * D), bf16), sds((s - 1, T, 2 * D), bf16), sds((T, D), bf16), sds((T, D), bf16),
            sds((pairs, 2, T), f32), sds((T, D), f32), sds((T, D), f32), sds((8, D), f32), sds((1, FF), f32),
            sds((n, 1, rows_a), f32), sds((A, B, 2, r1, 4 * D), bf16), sds((A, B, 2, r1, FF), bf16),
            sds((A, B, 2, r2, D), bf16),
        ],
        in_specs=[vm] * 8,
        out_specs=[vm] * 10 + [hbm] * 3,
        scratch_shapes=[
            pltpu.VMEM((T, D), f32), pltpu.VMEM((A, B, 2, r1, 4 * D), bf16), pltpu.VMEM((n, 1, E), f32),
            pltpu.VMEM((n, 1, E), f32), pltpu.VMEM((n, 1, M), f32), pltpu.VMEM((1, n * sum(widths)), f32),
            pltpu.VMEM((1, E), f32), dma((3, n - 1)), dma((3, n - 1)), dma((NT, NQ)), dma((NT, NQ)),
            dma((NT, NF)), dma((NT, NF)), dma((4, s - 1)), dma((4, s - 1)), dma((4,)),
        ],
        compiler_params=pltpu.CompilerParams(
            collective_id=0, has_side_effects=True, vmem_limit_bytes=64 * 1024 * 1024 - 65536
        ),
        name="forward_attention",
    )(lifted, w_ada, packed, tokens, w_qkv, w_proj, w_fc1, w_fc2)
    qkv, kvr, hidden, attn, lse, branch, middle, vectors, b_fc1, lf, w4, f1, f2 = res
    return (
        qkv, kvr, hidden, attn, lse, branch, middle, vectors, b_fc1, lf,
        w4.reshape(D, 4 * D), f1.reshape(D, FF), f2.reshape(FF, D),
    )


def feed_forward(middle, branch, attn, g, vectors, b_fc1, w4, w1, w2, n):
    T, D = middle.shape
    FF = w1.shape[1]
    A, B = grid_of(n)
    J, r1, r2 = A * B, D // n, FF // n
    W = 2 * r2
    RB = min(T, 64)

    def kern(
        mid_ref, br_ref, attn_ref, g_ref, vec_ref, b1_ref, w4_ref, w1_ref, w2_ref,
        out_ref, dmid_ref, dattn_ref, sums_ref, bfc1_ref, gproj_ref, g1_ref, g2_ref,
        h2, h2t, dm, dh2, mlp, dbr, w1b, w2b, gb, cr, ys, yr, zs, zr, t1, c1, s1,
        pw, psem, wsem, osem, cs, crs, c1s, c1r, yss, yrs, zss, zrs,
    ):
        at = Place(n)
        greet(at.all())
        shift2, scale2, gate2, gate1, bias2 = [vec_ref[i : i + 1, :] for i in range(5)]

        def tile(t):
            k, m = t // B, lax.rem(t, B)
            return lax.rem(at.a + 1 + k, A) * B + lax.rem(at.b + 1 + m, B)

        def weights(t, slot):
            lo = pl.multiple_of(tile(t) * W, W)
            return (
                pltpu.make_async_copy(w1_ref.at[:, pl.ds(lo, W)], w1b.at[slot], wsem.at[0, slot]),
                pltpu.make_async_copy(w2_ref.at[pl.ds(lo, W), :], w2b.at[slot], wsem.at[1, slot]),
            )

        for w in weights(0, 0):
            w.start()
        proj_copy = pltpu.make_async_copy(w4_ref.at[:, pl.ds(3 * D, D)], pw, psem)
        proj_copy.start()

        def head(i, _):
            rows = pl.ds(pl.multiple_of(i * RB, RB), RB)
            normed, _r = normalize(mid_ref[rows, :])
            h2[rows, :] = (normed * (1.0 + scale2) + shift2).astype(bf16)
            dm[rows, :] = (g_ref[rows, :].astype(f32) * gate2).astype(bf16)
            return 0

        lax.fori_loop(0, T // RB, head, 0)
        for i in range(0, D, 256):
            h2t[i : i + 256, :] = h2[:, i : i + 256].T
        dh2[...] = jnp.zeros_like(dh2)
        mlp[...] = jnp.zeros_like(mlp)
        sums_ref[...] = jnp.zeros_like(sums_ref)

        def c2_copy(t):
            return remote(gb.at[t, 1 - at.c], cr.at[t], cs.at[t], crs.at[t], at.sibling())

        def c1_copy(t, slot):
            return remote(t1.at[slot, :, 1 - at.c], c1.at[t], c1s.at[t], c1r.at[t], at.sibling())

        def y_copy(k, m):
            return remote(ys.at[k, m], yr.at[k, m], yss.at[k, m], yrs.at[k, m], at.at_b(m + 1))

        def z_copy(k):
            return remote(zs.at[k], zr.at[k], zss.at[k], zrs.at[k], at.at_a(k + 1))

        def s1_copy(t, slot):
            lo = pl.multiple_of(tile(t) * W, W)
            return pltpu.make_async_copy(s1.at[slot], g1_ref.at[:, :, pl.ds(lo, W)], osem.at[slot])

        def chip_sum1(t, slot, first):
            c1_copy(t, slot).wait()

            @pl.when(jnp.logical_not(first))
            def _():
                s1_copy(t, slot).wait()

            def part(i, _):
                s1[slot, i] = add32(t1[slot, i, at.c], c1[t, i]).astype(bf16)
                return 0

            lax.fori_loop(0, J, part, 0)
            s1_copy(t, slot).start()

        R2 = min(r2, 64)

        def own_sum(t, k):
            c2_copy(t).wait()
            for m in range(B - 1):
                y_copy(k, m).wait()

        def send_y(k, m):
            t = k * B + m
            c2_copy(t).wait()

            def part(i, _):
                rows = pl.ds(pl.multiple_of(i * R2, R2), R2)
                ys[k, m, rows, :] = add32(gb[t, at.c, rows, :], cr[t, rows, :]).astype(bf16)
                return 0

            lax.fori_loop(0, r2 // R2, part, 0)
            y_copy(k, m).start()

        def send_z(k):
            t = k * B + B - 1
            own_sum(t, k)

            def part(i, _):
                rows = pl.ds(pl.multiple_of(i * R2, R2), R2)
                total = add32(gb[t, at.c, rows, :], cr[t, rows, :], *[yr[k, m, rows, :] for m in range(B - 1)])
                zs[k, rows, :] = total.astype(bf16)
                return 0

            lax.fori_loop(0, r2 // R2, part, 0)
            z_copy(k).start()

        def pair(k, _):
            for m in range(B):
                t = k * B + m
                slot = m % 2
                for w in weights(t, slot):
                    w.wait()

                @pl.when(t + 1 < J)
                def _():
                    for w in weights(t + 1, 1 - slot):
                        w.start()

                j = tile(t)
                act, slope = gelu_both(nn(h2[...], w1b[slot]) + b1_ref[j])
                act = act.astype(bf16)
                g2t = tn(act, dm[...]).astype(bf16)
                gb[t, 0] = g2t[:r2]
                gb[t, 1] = g2t[r2:]
                c2_copy(t).start()
                dpre = (nt(dm[...], w2b[slot]) * slope).astype(bf16)
                bfc1_ref[j] = jnp.sum(dpre.astype(f32), axis=0, keepdims=True)
                t1[slot] = nn(h2t[...], dpre).astype(bf16).reshape(J, 2, r1, W)
                c1_copy(t, slot).start()
                mlp[...] += nn(act, w2b[slot])
                dh2[...] += nt(dpre, w1b[slot])
                if m > 0:
                    chip_sum1(t - 1, 1 - slot, jnp.logical_and(k == 0, m < 3))
                    send_y(k, m - 1)
                else:

                    @pl.when(k > 0)
                    def _():
                        chip_sum1(t - 1, 1 - slot, k * B < 3)

                if m == B - 1:

                    @pl.when(k > 0)
                    def _():
                        send_z(k - 1)

            return 0

        lax.fori_loop(0, A, pair, 0)
        chip_sum1(J - 1, (B - 1) % 2, jnp.bool_(J < 3))

        def back(i, _):
            rows = pl.ds(pl.multiple_of(i * RB, RB), RB)
            mid = mid_ref[rows, :]
            gf = g_ref[rows, :].astype(f32)
            normed, rscale = normalize(mid)
            dh = dh2[rows, :]
            up = dh * (1.0 + scale2)
            dmid = gf + rscale * (
                up
                - jnp.mean(up, axis=-1, keepdims=True)
                - normed * jnp.mean(up * normed, axis=-1, keepdims=True)
            )
            dmid_ref[rows, :] = dmid
            db = (dmid * gate1).astype(bf16)
            dbr[rows, :] = db
            ml = mlp[rows, :] + bias2
            out_ref[rows, :] = (mid + gate2 * ml).astype(bf16)
            for row, v in enumerate((dh, dh * normed, gf * ml, dmid * br_ref[rows, :], dm[rows, :], db)):
                sums_ref[row : row + 1, :] += jnp.sum(v.astype(f32), axis=0, keepdims=True)
            return 0

        lax.fori_loop(0, T // RB, back, 0)
        proj_copy.wait()
        dattn_ref[...] = nt(dbr[...], pw[...]).astype(bf16)

        def proj(i, _):
            cols = pl.ds(pl.multiple_of(i * 256, 256), 256)
            gproj_ref[cols, :] = tn(attn_ref[:, cols], dbr[...]).astype(bf16)
            return 0

        lax.fori_loop(0, D // 256, proj, 0)

        last = J - 1
        own_sum(last, A - 1)
        for k in range(A - 1):
            z_copy(k).wait()

        def part(i, _):
            rows = pl.ds(pl.multiple_of(i * R2, R2), R2)
            total = add32(
                gb[last, at.c, rows, :],
                cr[last, rows, :],
                *[yr[A - 1, m, rows, :] for m in range(B - 1)],
                *[zr[k, rows, :] for k in range(A - 1)],
            )
            g2_ref[rows, :] = total.astype(bf16)
            return 0

        lax.fori_loop(0, r2 // R2, part, 0)
        s1_copy(J - 2, 0).wait()
        s1_copy(J - 1, 1).wait()

    vm, hbm = pl.BlockSpec(memory_space=pltpu.VMEM), pl.BlockSpec(memory_space=pl.ANY)
    sds = jax.ShapeDtypeStruct
    dma = pltpu.SemaphoreType.DMA
    return pl.pallas_call(
        kern,
        out_shape=[
            sds((T, D), bf16), sds((T, D), f32), sds((T, D), bf16), sds((8, D), f32), sds((J, 1, W), f32),
            sds((D, D), bf16), sds((J, r1, FF), bf16), sds((r2, D), bf16),
        ],
        in_specs=[vm] * 6 + [hbm] * 3,
        out_specs=[vm] * 6 + [hbm, vm],
        scratch_shapes=[
            pltpu.VMEM((T, D), bf16), pltpu.VMEM((D, T), bf16), pltpu.VMEM((T, D), bf16),
            pltpu.VMEM((T, D), f32), pltpu.VMEM((T, D), f32), pltpu.VMEM((T, D), bf16),
            pltpu.VMEM((2, D, W), bf16), pltpu.VMEM((2, W, D), bf16),
            pltpu.VMEM((J, 2, r2, D), bf16), pltpu.VMEM((J, r2, D), bf16),
            pltpu.VMEM((A, B - 1, r2, D), bf16), pltpu.VMEM((A, B - 1, r2, D), bf16),
            pltpu.VMEM((A - 1, r2, D), bf16), pltpu.VMEM((A - 1, r2, D), bf16),
            pltpu.VMEM((2, J, 2, r1, W), bf16), pltpu.VMEM((J, J, r1, W), bf16), pltpu.VMEM((2, J, r1, W), bf16),
            pltpu.VMEM((D, D), bf16), dma(()), dma((2, 2)), dma((2,)), dma((J,)), dma((J,)), dma((J,)), dma((J,)),
            dma((A, B - 1)), dma((A, B - 1)), dma((A - 1,)), dma((A - 1,)),
        ],
        compiler_params=pltpu.CompilerParams(
            collective_id=3, has_side_effects=True, vmem_limit_bytes=64 * 1024 * 1024 - 65536
        ),
        name="feed_forward",
    )(middle, branch, attn, g, vectors, b_fc1.reshape(J, 1, W), w4, w1, w2)


class RowSum:
    @staticmethod
    def scratch(U, r, W, A, B, cores):
        dma = pltpu.SemaphoreType.DMA
        shapes = [
            pltpu.VMEM((U, B - 1, A, r, W), bf16), pltpu.VMEM((U, A - 1, r, W), bf16),
            pltpu.VMEM((U, A - 1, r, W), bf16), pltpu.VMEM((U, r, W), bf16), pltpu.VMEM((U, r, W), bf16),
            dma((U, B - 1)), dma((U, B - 1)), dma((U, A - 1)), dma((U, A - 1)), dma((U,)), dma((U,)),
        ]
        if cores:
            shapes += [
                pltpu.VMEM((U, A * B, r, W), bf16), pltpu.VMEM((U, B - 1, A, r, W), bf16), dma((U,)), dma((U,)),
            ]
        return shapes

    def __init__(self, at, s, peer, refs, grad=None, half=None):
        self.at, self.s, self.peer = at, s, peer
        self.grad, self.half = grad, half
        self.yr, self.zs, self.zr, self.xs, self.xr = refs[:5]
        self.yss, self.yrs, self.zss, self.zrs, self.xss, self.xrs = refs[5:11]
        if grad is not None:
            self.cr, self.ys, self.css, self.crs = refs[11:]

    def c_copy(self, u):
        return remote(
            self.grad.at[u, :, 1 - self.at.c], self.cr.at[u], self.css.at[u], self.crs.at[u], self.at.sibling()
        )

    def y_source(self, u, m):
        return self.ys.at[u, m]

    def y_copy(self, u, m):
        src = self.y_source(u, m)
        return remote(src, self.yr.at[u, m], self.yss.at[u, m], self.yrs.at[u, m], self.at.at_b(m + 1))

    def z_copy(self, u, k):
        return remote(self.zs.at[u, k], self.zr.at[u, k], self.zss.at[u, k], self.zrs.at[u, k], self.at.at_a(k + 1))

    def x_copy(self, u):
        return remote(self.xs.at[u], self.xr.at[u], self.xss.at[u], self.xrs.at[u], self.peer)

    def chip(self, u, a, b):
        j = a * self.at.B + b
        return add32(self.grad[u, j, self.at.c], self.cr[u, j])

    def own(self, u, a):
        base = self.chip(u, a, self.at.b) if self.half is None else self.half(u, a)
        return add32(base, *[self.yr[u, m, a] for m in range(self.at.B - 1)])

    def send_y(self, u):
        self.c_copy(u).wait()
        for m in range(self.at.B - 1):
            b = lax.rem(self.at.b + m + 1, self.at.B)
            for a in range(self.at.A):
                self.ys[u, m, a] = self.chip(u, a, b).astype(bf16)
            self.y_copy(u, m).start()

    def send_z(self, u):
        for m in range(self.at.B - 1):
            self.y_copy(u, m).wait()
        for k in range(self.at.A - 1):
            self.zs[u, k] = self.own(u, lax.rem(self.at.a + k + 1, self.at.A)).astype(bf16)
            self.z_copy(u, k).start()

    def send_x(self, u):
        for k in range(self.at.A - 1):
            self.z_copy(u, k).wait()
        total = add32(self.own(u, self.at.a), *[self.zr[u, k] for k in range(self.at.A - 1)])
        if self.s != 2:
            return total
        self.xs[u] = total.astype(bf16)
        self.x_copy(u).start()
        return None

    def finish(self, u):
        self.x_copy(u).wait()
        return add32(self.xs[u], self.xr[u])


def attention_and_sums(
    qkv, kvr, d_attn, lse, hidden, tokens, vectors, d_middle, w_qkv, half_fc1, grad_proj, sum_fc2, sums, bias_fc1, lf, w_ada, n, s
):
    T, D = tokens.shape
    FF = half_fc1.shape[-1]
    A, B = grid_of(n)
    J, r1, r2 = A * B, D // n, FF // n
    GW = 256
    U = D // GW
    F = FF // U
    E = 6 * D
    RB = min(T, 64)
    rows_a = D // n
    m_bias = [2 * D // n, D // n, FF // n, D // n]
    starts = [0, 2 * D, 3 * D, 3 * D + FF]
    NBIAS = 4 * D + FF
    blocks = [max(v, 128) for v in m_bias]
    offs = [sum(blocks[:i]) for i in range(4)]
    M = sum(blocks)
    nq = len(RowSum.scratch(U, r1, 3 * GW, A, B, True))
    nf = len(RowSum.scratch(U, r1, F, A, B, False))

    def kern(*refs):
        it = iter(refs)

        def take(count):
            return [next(it) for _ in range(count)]

        qkv_ref, kvr_ref = take(2)
        e_ref, lse_ref, h_ref, tok_ref, sc_ref, dmid_ref, w_ref, f1_ref, gp_ref, f2_ref, sum_ref, bf_ref, lf_ref, wa_ref = take(14)
        gt_ref, oq_ref, op_ref, o1_ref, o2_ref, gw_ref, gb_ref, dl_ref, bo_ref = take(9)
        h1t, dqg, kvl, kvs, kvr, dg, gq, wq, f1o, x2 = take(10)
        dh1 = gt_ref
        wsem, fsem, kss, krs, x2s, x2r = take(6)
        scr_q, scr_p, scr_f = take(nq), take(nq), take(nf)
        dx, dm, lp, bsum, bx, bsx = take(6)
        asend, arecv, lsend, lrecv, bsend, brecv, xsend, xrecv = take(8)

        at = Place(n)
        me, x = at.me, lax.axis_index("seq")
        peers = fsdp_peers(n, me)

        def seq_dev(k):
            return {"seq": lax.rem(x + k, s)}

        greet([{"fsdp": p} for p in peers] + [seq_dev(k) for k in range(1, s)])
        other = seq_dev(1)
        sq = RowSum(at, s, other, scr_q, grad=gq)
        sp = RowSum(at, s, other, scr_p, grad=gp_ref)
        sf = RowSum(at, s, other, scr_f, half=lambda u, a: f1o[u, a])

        def f_source(u, m):
            b = lax.rem(at.b + m + 1, B)
            return f1_ref.at[:, b, :, pl.ds(pl.multiple_of(u * F, F), F)]

        sf.y_source = f_source
        own_f = [
            pltpu.make_async_copy(f1_ref.at[:, at.b, :, pl.ds(u * F, F)], f1o.at[u], fsem.at[u]) for u in range(U)
        ]
        sp.c_copy(0).start()
        for u in range(U):
            for m in range(B - 1):
                sf.y_copy(u, m).start()
        if s == 2:
            x2_copy = remote(f2_ref, x2, x2s, x2r, other)
            x2_copy.start()
        for o in own_f:
            o.start()

        def h_copy(i):
            k = i % 3
            return pltpu.make_async_copy(
                h_ref.at[:, pl.ds(i * GW, GW)], dg.at[:, pl.ds(k * GW, GW)], wsem.at[k]
            )

        for i in range(min(U, 3)):
            h_copy(i).start()
        for i in range(U):
            h_copy(i).wait()
            k = i % 3
            h1t[i * GW : (i + 1) * GW, :] = dg[:, k * GW : (k + 1) * GW].T
            if i + 3 < U:
                h_copy(i + 3).start()
        dh1[...] = jnp.zeros_like(dh1)
        for o in own_f:
            o.wait()

        def w_copy(u, i):
            lo = pl.multiple_of(i * D + u * GW, GW)
            return pltpu.make_async_copy(w_ref.at[:, pl.ds(lo, GW)], wq.at[i], wsem.at[i])

        def kv_copy(u, k):
            return remote(kvs.at[u, k - 1], kvr.at[u, k - 1], kss.at[u, k - 1], krs.at[u, k - 1], seq_dev(s - k))

        def attend(u):
            slot = lax.rem(u, 2)
            for o in range(2):
                pair = u * 2 + o
                cols, k_cols, v_cols = [pl.ds(pl.multiple_of(lo + pair * 128, 128), 128) for lo in (0, D, 2 * D)]
                here = slice(o * 128, o * 128 + 128)
                qv, e = qkv_ref[:, cols] * bf16(HD**-0.5), e_ref[:, cols]
                ks = [qkv_ref[:, k_cols]] + [kvr_ref[k, :, cols] for k in range(s - 1)]
                vs = [qkv_ref[:, v_cols]] + [kvr_ref[k, :, k_cols] for k in range(s - 1)]
                dqt, dks, dvs = None, [None] * s, [None] * s
                for h in range(2):
                    qh, eh = pick(qv, h), pick(e, h)
                    total = lse_ref[pair, h : h + 1, :]
                    probs, dprobs, cross = [], [], None
                    for j in range(s):
                        p = jnp.exp(nt(ks[j], qh) - total)
                        dp = nt(vs[j], eh)
                        part = (p * dp).sum(axis=0, keepdims=True)
                        cross = part if cross is None else cross + part
                        dv = nn(p.astype(bf16), eh)
                        dvs[j] = dv if dvs[j] is None else dvs[j] + dv
                        probs.append(p)
                        dprobs.append(dp)
                    for j in range(s):
                        ds = (probs[j] * (dprobs[j] - cross)).astype(bf16)
                        dk = nn(ds, qh)
                        dks[j] = dk if dks[j] is None else dks[j] + dk
                        t = tn(pick(ks[j], h), ds)
                        dqt = t if dqt is None else dqt + t
                dqg[slot, :, here] = (dqt * (HD**-0.5)).T.astype(bf16)
                kvl[slot, 0, :, here] = dks[0]
                kvl[slot, 1, :, here] = dvs[0]
                for j in range(1, s):
                    kvs[u, j - 1, 0, :, here] = dks[j].astype(bf16)
                    kvs[u, j - 1, 1, :, here] = dvs[j].astype(bf16)
            for k in range(1, s):
                kv_copy(u, k).start()

        def project(u):
            slot = lax.rem(u, 2)
            for k in range(1, s):
                kv_copy(u, k).wait()
            dg[:, :GW] = dqg[slot]
            for i in range(2):
                lo = (i + 1) * GW
                dg[:, lo : lo + GW] = add32(kvl[slot, i], *[kvr[u, k, i] for k in range(s - 1)]).astype(bf16)
            part = 256 // (2 * r1)
            for i in range(D // 256):
                g = nn(h1t[i * 256 : (i + 1) * 256, :], dg[...]).astype(bf16)
                gq[u, i * part : (i + 1) * part] = g.reshape(part, 2, r1, 3 * GW)
            sq.c_copy(u).start()
            here = pl.ds(pl.multiple_of(u * GW, GW), GW)
            bsum[:, here] = jnp.sum(dg[:, :GW].astype(f32), axis=0, keepdims=True)
            there = pl.ds(pl.multiple_of(D + u * GW, GW), GW)
            bsum[:, there] = jnp.sum(dg[:, 2 * GW :].astype(f32), axis=0, keepdims=True)
            for i in range(3):
                w_copy(u, i).wait()
            total = nt(dg[:, :GW], wq[0])
            for i in range(1, 3):
                total = total + nt(dg[:, i * GW : (i + 1) * GW], wq[i])
            dh1[...] += total

        def step(i, _):
            @pl.when(i < U)
            def _():
                attend(i)

            @pl.when(jnp.logical_and(i >= 1, i <= U))
            def _():
                project(i - 1)

            @pl.when(i < U)
            def _():
                for k in range(3):
                    w_copy(i, k).start()

            @pl.when(i == 0)
            def _():
                sp.send_y(0)

            @pl.when(i < U)
            def _():
                sf.send_z(i)

            @pl.when(i >= 2)
            def _():
                sq.send_y(i - 2)

            return 0

        lax.fori_loop(0, U + 2, step, 0)
        sp.send_z(0)
        for u in range(U - 2):
            sq.send_z(u)

        sums = [jnp.zeros((1, D), f32), jnp.zeros((1, D), f32)]
        scale1 = sc_ref[5:6, :]

        def back(i, carry):
            rows = pl.ds(pl.multiple_of(i * RB, RB), RB)
            normed, rscale = normalize(tok_ref[rows, :].astype(f32))
            dh = dh1[rows, :]
            up = dh * (1.0 + scale1)
            gt_ref[rows, :] = dmid_ref[rows, :] + rscale * (
                up
                - jnp.mean(up, axis=-1, keepdims=True)
                - normed * jnp.mean(up * normed, axis=-1, keepdims=True)
            )
            return (
                carry[0] + jnp.sum(dh, axis=0, keepdims=True),
                carry[1] + jnp.sum(dh * normed, axis=0, keepdims=True),
            )

        shift1_sum, scale1_sum = lax.fori_loop(0, T // RB, back, tuple(sums))
        parts = [shift1_sum, scale1_sum, sum_ref[3:4, :], sum_ref[0:1, :], sum_ref[1:2, :], sum_ref[2:3, :]]
        for i, v in enumerate(parts):
            dx[x, :, i * D : (i + 1) * D] = v
        mod_x = [remote(dx.at[x], dx.at[x], xsend.at[0, k - 1], xrecv.at[0, k - 1], seq_dev(k)) for k in range(1, s)]
        for c in mod_x:
            c.start()
        bsum[:, starts[1] : starts[1] + D] = sum_ref[5:6, :]
        bsum[:, starts[2] : starts[2] + FF] = bf_ref[...]
        bsum[:, starts[3] : starts[3] + D] = sum_ref[4:5, :]

        def block(p, i):
            lo = starts[i] + ((p * m_bias[i]) // blocks[i]) * blocks[i]
            return bsum.at[:, pl.ds(pl.multiple_of(lo, 128), blocks[i])]

        def bias_copy(k, p, i):
            dst = bx.at[me, :, pl.ds(offs[i], blocks[i])]
            return remote(block(p, i), dst, bsend.at[i, k], brecv.at[i, k], {"fsdp": p})

        bias_out = [bias_copy(k, p, i) for k, p in enumerate(peers) for i in range(4)]
        for c in bias_out:
            c.start()
        for i in range(4):
            lo = starts[i] + ((me * m_bias[i]) // blocks[i]) * blocks[i]
            bx[me, :, offs[i] : offs[i] + blocks[i]] = bsum[:, pl.ds(pl.multiple_of(lo, 128), blocks[i])]

        for u in range(U):
            if s == 2:
                sf.send_x(u)
            else:
                o1_ref[:, u * F : (u + 1) * F] = sf.send_x(u)
        sq.send_z(U - 2)
        for c in mod_x:
            c.wait()
        dm[me] = jnp.sum(dx[...], axis=0).astype(bf16).astype(f32)
        mod_all = [remote(dm.at[me], dm.at[me], asend.at[k], arecv.at[k], {"fsdp": p}) for k, p in enumerate(peers)]
        for c in mod_all:
            c.start()
        sq.send_z(U - 1)
        for c in bias_out:
            c.wait()
        bsx[x] = jnp.sum(bx[...], axis=0)
        bias_x = [remote(bsx.at[x], bsx.at[x], xsend.at[1, k - 1], xrecv.at[1, k - 1], seq_dev(k)) for k in range(1, s)]
        for c in bias_x:
            c.start()
        if s == 2:
            sp.send_x(0)
        else:
            op_ref[...] = sp.send_x(0)
        for c in mod_all:
            c.wait()
        dmod = dm[...].reshape(n, E).astype(bf16)
        lp[...] = nt(dmod, wa_ref[...]).reshape(n, 1, rows_a)
        dl_ref[me] = lp[me]
        lift = [remote(lp.at[p], dl_ref.at[me], lsend.at[k], lrecv.at[k], {"fsdp": p}) for k, p in enumerate(peers)]
        for c in lift:
            c.start()
        gw_ref[...] = tn(lf_ref[...].reshape(n, rows_a).astype(bf16), dmod)
        gb_ref[...] = jnp.sum(dm[...], axis=0)

        def put_q(u, value):
            for i in range(3):
                oq_ref[:, i * D + u * GW : i * D + (u + 1) * GW] = value[:, i * GW : (i + 1) * GW]

        for u in range(U):
            value = sq.send_x(u)
            if s != 2:
                put_q(u, value)
        if s == 2:
            x2_copy.wait()
            o2_ref[...] = add32(f2_ref[...], x2[...])
            for u in range(U):
                o1_ref[:, u * F : (u + 1) * F] = sf.finish(u)
            op_ref[...] = sp.finish(0)
            for u in range(U):
                put_q(u, sq.finish(u))
        else:
            o2_ref[...] = f2_ref[...].astype(f32)
        for c in bias_x:
            c.wait()
        bo_ref[...] = jnp.sum(bsx[...], axis=0)
        for c in lift:
            c.wait()

    vm, hbm = pl.BlockSpec(memory_space=pltpu.VMEM), pl.BlockSpec(memory_space=pl.ANY)
    sds, dma = jax.ShapeDtypeStruct, pltpu.SemaphoreType.DMA
    res = pl.pallas_call(
        kern,
        out_shape=[
            sds((T, D), f32), sds((r1, 3 * D), f32), sds((r1, D), f32), sds((r1, FF), f32), sds((r2, D), f32),
            sds((rows_a, E), f32), sds((1, E), f32), sds((n, 1, rows_a), f32), sds((1, M), f32),
        ],
        in_specs=[vm] * 4 + [hbm] + [vm] * 3 + [hbm, hbm] + [vm] * 6,
        out_specs=[vm] * 9,
        scratch_shapes=[
            pltpu.VMEM((D, T), bf16), pltpu.VMEM((2, T, GW), bf16),
            pltpu.VMEM((2, 2, T, GW), f32), pltpu.VMEM((U, s - 1, 2, T, GW), bf16),
            pltpu.VMEM((U, s - 1, 2, T, GW), bf16), pltpu.VMEM((T, 3 * GW), bf16),
            pltpu.VMEM((U, J, 2, r1, 3 * GW), bf16), pltpu.VMEM((3, D, GW), bf16),
            pltpu.VMEM((U, A, r1, F), bf16), pltpu.VMEM((r2, D), bf16),
            dma((3,)), dma((U,)), dma((U, s - 1)), dma((U, s - 1)), dma(()), dma(()),
        ]
        + RowSum.scratch(U, r1, 3 * GW, A, B, True)
        + RowSum.scratch(1, r1, D, A, B, True)
        + RowSum.scratch(U, r1, F, A, B, False)
        + [
            pltpu.VMEM((s, 1, E), f32), pltpu.VMEM((n, 1, E), f32), pltpu.VMEM((n, 1, rows_a), f32),
            pltpu.VMEM((1, NBIAS), f32), pltpu.VMEM((n, 1, M), f32), pltpu.VMEM((s, 1, M), f32),
            dma((n - 1,)), dma((n - 1,)), dma((n - 1,)), dma((n - 1,)),
            dma((4, n - 1)), dma((4, n - 1)), dma((2, s - 1)), dma((2, s - 1)),
        ],
        compiler_params=pltpu.CompilerParams(
            collective_id=4, has_side_effects=True, vmem_limit_bytes=64 * 1024 * 1024 - 65536
        ),
        name="attention_and_sums",
    )(
        qkv, kvr, d_attn, lse, hidden, tokens, vectors, d_middle, w_qkv, half_fc1.reshape(A, B, r1, FF),
        grad_proj.reshape(1, J, 2, r1, D), sum_fc2, sums, bias_fc1, lf, w_ada,
    )
    grad_tokens, t_qkv, t_proj, t_fc1, t_fc2, t_ada, ada_sums, d_lifted, bias = res
    if s != 2:
        t_qkv, t_proj, t_fc1, t_fc2 = lax.psum((t_qkv, t_proj, t_fc1, t_fc2), "seq")
    me = lax.axis_index("fsdp")
    biases = []
    for width, wide, off in zip(m_bias, blocks, offs):
        biases.append(lax.dynamic_slice_in_dim(bias[0, off : off + wide], (me * width) % wide, width))
    return grad_tokens, t_qkv, t_proj, t_fc1, t_fc2, t_ada, ada_sums, d_lifted, biases


def on_device(
    tokens,
    condition,
    w_ada,
    b_ada,
    w_qkv,
    b_qv,
    w_proj,
    b_proj,
    w_fc1,
    b_fc1,
    w_fc2,
    b_fc2,
    cotangent,
):
    n, s = lax.axis_size("fsdp"), lax.axis_size("seq")
    width = tokens.shape[-1]

    lifted, silu_back = jax.vjp(jax.nn.silu, condition.astype(f32))
    lifted_q = lifted.astype(bf16).astype(f32).reshape(n, 1, width // n)
    qkv, kvr, hidden_one, attn, lse, branch, middle, vectors, fc1_b, lf, w4, fc1_w, fc2_w = forward_attention(
        lifted_q, w_ada, [b_qv, b_proj, b_fc1, b_fc2, b_ada], tokens[0], w_qkv, w_proj, w_fc1, w_fc2, n, s
    )
    result, d_middle, d_attn, sums, bias_fc1, grad_proj, half_fc1, sum_fc2 = feed_forward(
        middle, branch, attn, cotangent[0], vectors, fc1_b, w4, fc1_w, fc2_w, n
    )
    grad_input, total_qkv, total_proj, total_fc1, total_fc2, total_ada, sums_ada, d_lifted, total_bias = (
        attention_and_sums(
            qkv, kvr, d_attn, lse, hidden_one, tokens[0], vectors, d_middle, w4, half_fc1,
            grad_proj, sum_fc2, sums, bias_fc1.reshape(1, -1), lf, w_ada, n, s,
        )
    )
    share = b_ada.shape[0]
    total_bada = lax.dynamic_slice_in_dim(sums_ada[0], lax.axis_index("fsdp") * share, share)
    grad_condition = silu_back(d_lifted.reshape(1, width))[0]
    total_bqv, total_bproj, total_bfc1, total_bfc2 = total_bias
    return (
        result[None],
        grad_input[None],
        grad_condition,
        total_ada,
        total_bada,
        total_qkv,
        total_bqv,
        total_proj,
        total_bproj,
        total_fc1,
        total_bfc1,
        total_fc2,
        total_bfc2,
    )


def solution(mesh):
    weights = (P("fsdp", None), P("fsdp")) * 5
    return jax.shard_map(
        on_device,
        mesh=mesh,
        in_specs=(P("fsdp", "seq", None), P("fsdp", None)) + weights + (P("fsdp", "seq", None),),
        out_specs=(P("fsdp", "seq", None), P("fsdp", "seq", None), P("fsdp", None)) + weights,
        check_vma=False,
    )
```

```python
from functools import partial

import jax
import jax.numpy as jnp
from jax import lax
from jax.experimental import pallas as pl
from jax.experimental.pallas import tpu as pltpu
from jax.sharding import PartitionSpec as P

HD = 64
norm_eps = 1e-06
f32 = jnp.float32
bf16 = jnp.bfloat16
MESH = pl.DeviceIdType.MESH


def grid_of(n):
    b = 2 if n == 16 else 4
    return n // (2 * b), b


def nt(a, b):
    return lax.dot_general(a, b, (((1,), (1,)), ((), ())), preferred_element_type=f32)


def nn(a, b):
    return lax.dot_general(a, b, (((1,), (0,)), ((), ())), preferred_element_type=f32)


def tn(a, b):
    return lax.dot_general(a, b, (((0,), (0,)), ((), ())), preferred_element_type=f32)


def fsdp_peers(n, me):
    return [lax.rem(me + k, n) for k in range(1, n)]


def head_mask(ref_shape, h):
    low = lax.broadcasted_iota(jnp.int32, ref_shape, 1) < HD
    return low if h == 0 else ~low


def pick(values, h):
    return jnp.where(head_mask(values.shape, h), values, jnp.zeros_like(values))


def remote(src, dst, send, recv, device):
    return pltpu.make_async_remote_copy(
        src_ref=src, dst_ref=dst, send_sem=send, recv_sem=recv, device_id=device, device_id_type=MESH
    )


def greet(devices):
    bar = pltpu.get_barrier_semaphore()
    for d in devices:
        pl.semaphore_signal(bar, inc=1, device_id=d, device_id_type=MESH)
    pl.semaphore_wait(bar, len(devices))


class Place:
    def __init__(self, n):
        self.A, self.B = grid_of(n)
        me = lax.axis_index("fsdp")
        self.me = me
        self.a, self.b, self.c = me // (2 * self.B), lax.rem(me // 2, self.B), lax.rem(me, 2)

    def dev(self, a, b, c):
        return {"fsdp": (a * self.B + b) * 2 + c}

    def at_a(self, k):
        return self.dev(lax.rem(self.a + k, self.A), self.b, self.c)

    def at_b(self, k):
        return self.dev(self.a, lax.rem(self.b + k, self.B), self.c)

    def sibling(self):
        return self.dev(self.a, self.b, 1 - self.c)

    def all(self):
        return [self.at_a(k) for k in range(1, self.A)] + [self.at_b(k) for k in range(1, self.B)] + [self.sibling()]


def add32(*values):
    total = values[0].astype(f32)
    for v in values[1:]:
        total = total + v.astype(f32)
    return total


def gelu_both(x):
    k = 0.7978845608028654
    sq = x * x
    th = jnp.tanh(k * (x + 0.044715 * (sq * x)))
    half = 0.5 * (1.0 + th)
    slope = half + (0.5 * k) * x * (1.0 - th * th) * (1.0 + (3 * 0.044715) * sq)
    return x * half, slope


def normalize(v):
    center = v - jnp.mean(v, axis=-1, keepdims=True)
    rscale = lax.rsqrt(jnp.mean(center * center, axis=-1, keepdims=True) + norm_eps)
    return center * rscale, rscale


def bias_block(width, n):
    return max(-(-((p * width) % 128 + width) // 128) * 128 for p in range(n))


def placed_bias(bias, n):
    width, wide = bias.shape[0], bias_block(bias.shape[0], n)
    bias = bias.astype(f32)[None]
    if wide == width:
        return bias
    at = (lax.axis_index("fsdp") * width) % 128
    return lax.dynamic_update_slice(jnp.zeros((1, wide), f32), bias, (0, at))


def forward_attention(lifted, w_ada, biases, tokens, w_qkv, w_proj, w_fc1, w_fc2, n, s):
    T, D = tokens.shape
    E = w_ada.shape[1]
    FF = w_fc1.shape[1]
    A, B = grid_of(n)
    rows_a = w_ada.shape[0]
    r1, r2 = w_qkv.shape[0], w_fc2.shape[0]
    widths = [v.shape[0] for v in biases]
    blocks = [bias_block(w, n) for w in widths]
    offs = [sum(blocks[:i]) for i in range(5)]
    bases = [n * sum(widths[:i]) for i in range(5)]
    packed = jnp.concatenate([placed_bias(v, n) for v in biases], axis=1)
    M = packed.shape[1]
    share = s == 2
    NT, NL = 8, 16
    CQ, CF, RF = 4 * D // NT, FF // NL, r2 // NL
    RB = min(T, 64)
    AHEAD, MODULATE, LAG, ATTEND = 2, 4, 6, NT + 7
    NA, NY = A - 1, B - 1
    NQ = NA + NY + 1
    NF = 3 * (NA + NY) + 2
    pairs = D // 128

    def kern(
        l_ref, wa_ref, bias_ref, tok_ref, wqkv_ref, wproj_ref, wfc1_ref, wfc2_ref,
        qkv_ref, kvr_ref, h_ref, attn_ref, lse_ref, br_ref, mid_ref, vec_ref, bfc1_ref, lf_ref, w4_ref, f1_ref, f2_ref,
        normed, wq, part, acc, bout, bvec, mod, msend, mrecv, qsend, qrecv, fsend, frecv, ksend, krecv, osem,
    ):
        at = Place(n)
        a, b, c, me, x = at.a, at.b, at.c, at.me, lax.axis_index("seq")
        peers = fsdp_peers(n, me)
        other = {"seq": lax.rem(x + 1, s)}
        greet([{"fsdp": p} for p in peers] + [{"seq": lax.rem(x + k, s)} for k in range(1, s)])

        def small(i, src, dst):
            return [
                remote(src(p), dst(k), msend.at[i, k], mrecv.at[i, k], {"fsdp": p}) for k, p in enumerate(peers)
            ]

        m_lift = small(0, lambda p: l_ref.at[p], lambda k: lf_ref.at[me])
        m_bias = small(1, lambda p: bias_ref, lambda k: bout.at[me])
        m_part = small(2, lambda p: part.at[p], lambda k: acc.at[k + 1])
        for r in m_lift + m_bias:
            r.start()
        owns = [
            pltpu.make_async_copy(wqkv_ref, wq.at[a, b, c, :, pl.ds(0, 3 * D)], osem.at[0]),
            pltpu.make_async_copy(wproj_ref, wq.at[a, b, c, :, pl.ds(3 * D, D)], osem.at[1]),
            pltpu.make_async_copy(wfc1_ref, f1_ref.at[a, b, c], osem.at[2]),
            pltpu.make_async_copy(wfc2_ref, f2_ref.at[a, b, c], osem.at[3]),
        ]
        for o in owns:
            o.start()

        def block(i):
            return jnp.where(i < 6, lax.rem(i + 2, 6), i)

        def span(lo, size, step):
            return pl.ds(pl.multiple_of(lo, step), size)

        class Ticks:
            def __init__(self, pieces, whole, send, recv):
                self.pieces, self.whole, self.send, self.recv = pieces, whole, send, recv

            def copy(self, j, i, src, dst, device):
                return remote(src, dst, self.send.at[j, i], self.recv.at[j, i], device)

            def z(self, j):
                return [
                    self.copy(j, i * NA + k, src.at[rows, cols], buf.at[a, b, c, rows, cols], at.at_a(k + 1))
                    for i, (src, buf, rows, cols, _) in enumerate(self.pieces(j))
                    for k in range(NA)
                ]

            def y(self, j):
                out, ps = [], self.pieces(j)
                for i, (_, buf, rows, cols, _) in enumerate(ps):
                    sl = buf.at[:, b, c, rows, cols]
                    out += [self.copy(j, len(ps) * NA + i * NY + k, sl, sl, at.at_b(k + 1)) for k in range(NY)]
                return out

            def x(self, j):
                out, ps = [], self.pieces(j)
                i = len(ps) * (NA + NY)
                for _, buf, rows, cols, shared in ps:
                    if not shared:
                        continue
                    for k in range(NA):
                        sl = buf.at[lax.rem(a + k + 1, A), :, c, rows, cols]
                        out.append(self.copy(j, i, sl, sl, other))
                        i += 1
                    for k in range(NY):
                        sl = buf.at[a, lax.rem(b + k + 1, B), c, rows, cols]
                        out.append(self.copy(j, i, sl, sl, other))
                        i += 1
                return out

            def c(self, j):
                ps = self.whole(j)
                i = self.send.shape[1] - len(ps)
                return [
                    self.copy(j, i + k, buf.at[:, :, c, rows, cols], buf.at[:, :, c, rows, cols], at.sibling())
                    for k, (buf, rows, cols) in enumerate(ps)
                ]

            def start_z(self, j):
                for r in self.z(j):
                    r.start()

            def start_y(self, j):
                for r in self.z(j):
                    r.wait_recv()
                for r in self.y(j):
                    r.start()

            def start_x(self, j):
                for r in self.y(j):
                    r.wait_recv()
                for r in self.x(j):
                    r.start()

            def start_c(self, j):
                for r in self.x(j):
                    r.wait_recv()
                for r in self.c(j):
                    r.start()

            def relay(self, j):
                self.start_x(j)
                self.start_c(j)

            def finish(self, j):
                for r in self.z(j) + self.y(j) + self.x(j):
                    r.wait_send()
                for r in self.c(j):
                    r.wait()

        all_r1 = pl.ds(0, r1)
        mine = wq.at[a, b, c]

        def q_pieces(i):
            return [(mine, wq, all_r1, span(block(i) * CQ, CQ, CQ), False)]

        def q_whole(i):
            return [(wq, all_r1, span(block(i) * CQ, CQ, CQ))]

        def f_pieces(j):
            w = D // 2 if share else D
            part = span(x * w, w, w) if share else pl.ds(0, D)
            return [
                (wfc1_ref, f1_ref, all_r1, span(j * CF, CF, CF), False),
                (wfc2_ref, f2_ref, span(j * RF, RF, RF), part, share),
            ]

        def f_whole(j):
            return [(f1_ref, all_r1, span(j * CF, CF, CF)), (f2_ref, span(j * RF, RF, RF), pl.ds(0, D))]

        tq, tf = Ticks(q_pieces, q_whole, qsend, qrecv), Ticks(f_pieces, f_whole, fsend, frecv)

        owns[0].wait()
        owns[1].wait()
        for i in range(AHEAD):
            tq.start_z(i)
        lf_ref[me] = l_ref[me]
        bout[me] = bias_ref[...]
        bvec[...] = jnp.zeros_like(bvec)

        def norm(i, _):
            rows = pl.ds(pl.multiple_of(i * RB, RB), RB)
            normed[rows, :] = normalize(tok_ref[rows, :].astype(f32))[0]
            return 0

        for r in m_lift:
            r.wait_recv()
        part[...] = nn(lf_ref[...].reshape(n, rows_a).astype(bf16), wa_ref[...]).reshape(n, 1, E)
        acc[0] = part[me]
        for r in m_part:
            r.start()

        def modulation():
            for r in m_bias + m_part:
                r.wait_recv()
            for i in range(5):
                for p in range(n):
                    lo = bases[i] + p * widths[i] // 128 * 128
                    value = bout[p, :, offs[i] : offs[i] + blocks[i]]
                    if widths[i] % 128 == 0:
                        bvec[:, lo : lo + blocks[i]] = value
                    else:
                        bvec[:, lo : lo + blocks[i]] += value
            mod[...] = jnp.sum(acc[...], axis=0) + bvec[:, bases[4] :]
            shift1, scale1, gate1, shift2, scale2, gate2 = [mod[:, i * D : (i + 1) * D] for i in range(6)]
            vec_ref[...] = jnp.zeros_like(vec_ref)
            for i, v in enumerate((shift2, scale2, gate2, gate1, bvec[:, bases[3] : bases[3] + D], scale1)):
                vec_ref[i : i + 1, :] = v
            bfc1_ref[...] = bvec[:, bases[2] : bases[2] + FF]

            def modulate(i, _):
                rows = pl.ds(pl.multiple_of(i * RB, RB), RB)
                h_ref[rows, :] = (normed[rows, :] * (1.0 + scale1) + shift1).astype(bf16)
                return 0

            lax.fori_loop(0, T // RB, modulate, 0)


        def kv_copy(m, k):
            return remote(
                qkv_ref.at[:, span(D + m * CQ, CQ, CQ)],
                kvr_ref.at[k - 1, :, span(m * CQ, CQ, CQ)],
                ksend.at[m, k - 1],
                krecv.at[m, k - 1],
                {"seq": lax.rem(x + k, s)},
            )

        def project(m):
            tq.finish(m)

            @pl.when(m < 6)
            def _():
                lo = block(m) * CQ
                cols = span(lo, CQ, CQ)
                from_v = (block(m) >= 4).astype(jnp.int32)
                bias = bvec[:, span(lo - from_v * D, CQ, CQ)]
                is_key = jnp.logical_and(block(m) >= 2, block(m) < 4)
                bias = jnp.where(is_key, jnp.zeros_like(bias), bias)
                out = nn(h_ref[...], wq[:, :, :, :, cols].reshape(D, CQ))
                qkv_ref[:, cols] = (out + bias).astype(bf16)

            @pl.when(m < 4)
            def _():
                for k in range(1, s):
                    kv_copy(m, k).start()

        def attend(pair):
            def cols(lo):
                return span(lo + pair * 128, 128, 128)

            q = qkv_ref[:, cols(0)] * bf16(HD**-0.5)
            ks = [qkv_ref[:, cols(D)]] + [kvr_ref[k, :, cols(0)] for k in range(s - 1)]
            vs = [qkv_ref[:, cols(2 * D)]] + [kvr_ref[k, :, cols(D)] for k in range(s - 1)]
            total = None
            for h in range(2):
                qh = pick(q, h)
                scores = [nt(k, qh) for k in ks]
                top = scores[0].max(axis=0, keepdims=True)
                for sc in scores[1:]:
                    top = jnp.maximum(top, sc.max(axis=0, keepdims=True))
                mass, out = None, None
                for sc, v in zip(scores, vs):
                    p = jnp.exp(sc - top)
                    got = p.sum(axis=0, keepdims=True)
                    mass = got if mass is None else mass + got
                    o = tn(pick(v, h), p.astype(bf16))
                    out = o if out is None else out + o
                out = out * (1.0 / mass)
                total = out if total is None else total + out
                lse_ref[pair, h : h + 1, :] = top + jnp.log(mass)
            attn_ref[:, cols(0)] = total.T.astype(bf16)

        def branch(i, _):
            cols = span(i * 256, 256, 256)
            weight = wq[:, :, :, :, span(3 * D + i * 256, 256, 256)].reshape(D, 256)
            got = nn(attn_ref[...], weight) + bvec[:, span(bases[1] + i * 256, 256, 256)]
            br_ref[:, cols] = got
            mid_ref[:, cols] = tok_ref[:, cols].astype(f32) + mod[:, span(2 * D + i * 256, 256, 256)] * got
            return 0

        out4 = pltpu.make_async_copy(wq, w4_ref, osem.at[0])

        def step(i, _):
            def when(lo, hi, f, shift):
                @pl.when(jnp.logical_and(i >= lo, i < hi))
                def _():
                    f(i - shift)

            when(0, NT - AHEAD, lambda j: tq.start_z(j + AHEAD), 0)
            when(NT - AHEAD, NT + NL - AHEAD, tf.start_z, NT - AHEAD)
            when(0, NT, tq.start_y, 0)
            when(NT, NT + NL, tf.start_y, NT)
            when(1, NT + 1, tq.relay, 1)
            when(NT + 1, NT + NL + 1, tf.start_x, NT + 1)
            when(NT + LAG, NT + NL + LAG, tf.start_c, NT + LAG)
            when(NT + LAG + 1, NT + NL + LAG + 1, tf.finish, NT + LAG + 1)

            @pl.when(i == 0)
            def _():
                lax.fori_loop(0, T // RB, norm, 0)

            pl.when(i == MODULATE)(modulation)
            when(MODULATE, MODULATE + NT, project, MODULATE)

            @pl.when(i == MODULATE + NT)
            def _():
                out4.start()

            @pl.when(i == ATTEND)
            def _():
                for m in range(4):
                    for k in range(1, s):
                        kv_copy(m, k).wait()

            when(ATTEND, ATTEND + pairs, attend, ATTEND)

            @pl.when(i == ATTEND + pairs)
            def _():
                lax.fori_loop(0, D // 256, branch, 0)

            return 0

        owns[2].wait()
        owns[3].wait()
        lax.fori_loop(0, NT + NL + LAG + 1, step, 0)
        out4.wait()
        for r in m_lift + m_bias + m_part:
            r.wait_send()

    vm, hbm = pl.BlockSpec(memory_space=pltpu.VMEM), pl.BlockSpec(memory_space=pl.ANY)
    sds, dma = jax.ShapeDtypeStruct, pltpu.SemaphoreType.DMA
    res = pl.pallas_call(
        kern,
        out_shape=[
            sds((T, 3 * D), bf16), sds((s - 1, T, 2 * D), bf16), sds((T, D), bf16), sds((T, D), bf16),
            sds((pairs, 2, T), f32), sds((T, D), f32), sds((T, D), f32), sds((8, D), f32), sds((1, FF), f32),
            sds((n, 1, rows_a), f32), sds((A, B, 2, r1, 4 * D), bf16), sds((A, B, 2, r1, FF), bf16),
            sds((A, B, 2, r2, D), bf16),
        ],
        in_specs=[vm] * 8,
        out_specs=[vm] * 10 + [hbm] * 3,
        scratch_shapes=[
            pltpu.VMEM((T, D), f32), pltpu.VMEM((A, B, 2, r1, 4 * D), bf16), pltpu.VMEM((n, 1, E), f32),
            pltpu.VMEM((n, 1, E), f32), pltpu.VMEM((n, 1, M), f32), pltpu.VMEM((1, n * sum(widths)), f32),
            pltpu.VMEM((1, E), f32), dma((3, n - 1)), dma((3, n - 1)), dma((NT, NQ)), dma((NT, NQ)),
            dma((NL, NF)), dma((NL, NF)), dma((4, s - 1)), dma((4, s - 1)), dma((4,)),
        ],
        compiler_params=pltpu.CompilerParams(
            collective_id=0, has_side_effects=True, vmem_limit_bytes=64 * 1024 * 1024 - 65536
        ),
        name="forward_attention",
    )(lifted, w_ada, packed, tokens, w_qkv, w_proj, w_fc1, w_fc2)
    qkv, kvr, hidden, attn, lse, branch, middle, vectors, b_fc1, lf, w4, f1, f2 = res
    return (
        qkv, kvr, hidden, attn, lse, branch, middle, vectors, b_fc1, lf,
        w4.reshape(D, 4 * D), f1.reshape(D, FF), f2.reshape(FF, D),
    )


def feed_forward(middle, branch, attn, g, vectors, b_fc1, w4, w1, w2, n):
    T, D = middle.shape
    FF = w1.shape[1]
    A, B = grid_of(n)
    J, r1, r2 = A * B, D // n, FF // n
    W = 2 * r2
    RB = min(T, 64)

    def kern(
        mid_ref, br_ref, attn_ref, g_ref, vec_ref, b1_ref, w4_ref, w1_ref, w2_ref,
        out_ref, dmid_ref, dattn_ref, sums_ref, bfc1_ref, gproj_ref, g1_ref, g2_ref,
        h2, h2t, dm, dh2, mlp, dbr, w1b, w2b, gb, cr, ys, yr, zs, zr, t1, c1, s1,
        pw, psem, wsem, osem, cs, crs, c1s, c1r, yss, yrs, zss, zrs,
    ):
        at = Place(n)
        greet(at.all())
        shift2, scale2, gate2, gate1, bias2 = [vec_ref[i : i + 1, :] for i in range(5)]

        def tile(t):
            k, m = t // B, lax.rem(t, B)
            return lax.rem(at.a + 1 + k, A) * B + lax.rem(at.b + 1 + m, B)

        def weights(t, slot):
            lo = pl.multiple_of(tile(t) * W, W)
            return (
                pltpu.make_async_copy(w1_ref.at[:, pl.ds(lo, W)], w1b.at[slot], wsem.at[0, slot]),
                pltpu.make_async_copy(w2_ref.at[pl.ds(lo, W), :], w2b.at[slot], wsem.at[1, slot]),
            )

        for w in weights(0, 0):
            w.start()
        proj_copy = pltpu.make_async_copy(w4_ref.at[:, pl.ds(3 * D, D)], pw, psem)
        proj_copy.start()

        def head(i, _):
            rows = pl.ds(pl.multiple_of(i * RB, RB), RB)
            normed, _r = normalize(mid_ref[rows, :])
            h2[rows, :] = (normed * (1.0 + scale2) + shift2).astype(bf16)
            dm[rows, :] = (g_ref[rows, :].astype(f32) * gate2).astype(bf16)
            return 0

        lax.fori_loop(0, T // RB, head, 0)
        for i in range(0, D, 256):
            h2t[i : i + 256, :] = h2[:, i : i + 256].T
        dh2[...] = jnp.zeros_like(dh2)
        mlp[...] = jnp.zeros_like(mlp)
        sums_ref[...] = jnp.zeros_like(sums_ref)

        def c2_copy(t):
            return remote(gb.at[t, 1 - at.c], cr.at[t], cs.at[t], crs.at[t], at.sibling())

        def c1_copy(t, slot):
            return remote(t1.at[slot, :, 1 - at.c], c1.at[t], c1s.at[t], c1r.at[t], at.sibling())

        def y_copy(k, m):
            return remote(ys.at[k, m], yr.at[k, m], yss.at[k, m], yrs.at[k, m], at.at_b(m + 1))

        def z_copy(k):
            return remote(zs.at[k], zr.at[k], zss.at[k], zrs.at[k], at.at_a(k + 1))

        def s1_copy(t, slot):
            lo = pl.multiple_of(tile(t) * W, W)
            return pltpu.make_async_copy(s1.at[slot], g1_ref.at[:, :, pl.ds(lo, W)], osem.at[slot])

        def chip_sum1(t, slot, first):
            c1_copy(t, slot).wait()

            @pl.when(jnp.logical_not(first))
            def _():
                s1_copy(t, slot).wait()

            def part(i, _):
                s1[slot, i] = add32(t1[slot, i, at.c], c1[t, i]).astype(bf16)
                return 0

            lax.fori_loop(0, J, part, 0)
            s1_copy(t, slot).start()

        R2 = min(r2, 64)

        def own_sum(t, k):
            c2_copy(t).wait()
            for m in range(B - 1):
                y_copy(k, m).wait()

        def send_y(k, m):
            t = k * B + m
            c2_copy(t).wait()

            def part(i, _):
                rows = pl.ds(pl.multiple_of(i * R2, R2), R2)
                ys[k, m, rows, :] = add32(gb[t, at.c, rows, :], cr[t, rows, :]).astype(bf16)
                return 0

            lax.fori_loop(0, r2 // R2, part, 0)
            y_copy(k, m).start()

        def send_z(k):
            t = k * B + B - 1
            own_sum(t, k)

            def part(i, _):
                rows = pl.ds(pl.multiple_of(i * R2, R2), R2)
                total = add32(gb[t, at.c, rows, :], cr[t, rows, :], *[yr[k, m, rows, :] for m in range(B - 1)])
                zs[k, rows, :] = total.astype(bf16)
                return 0

            lax.fori_loop(0, r2 // R2, part, 0)
            z_copy(k).start()

        def pair(k, _):
            for m in range(B):
                t = k * B + m
                slot = m % 2
                for w in weights(t, slot):
                    w.wait()

                @pl.when(t + 1 < J)
                def _():
                    for w in weights(t + 1, 1 - slot):
                        w.start()

                j = tile(t)
                act, slope = gelu_both(nn(h2[...], w1b[slot]) + b1_ref[j])
                act = act.astype(bf16)
                g2t = tn(act, dm[...]).astype(bf16)
                gb[t, 0] = g2t[:r2]
                gb[t, 1] = g2t[r2:]
                c2_copy(t).start()
                dpre = (nt(dm[...], w2b[slot]) * slope).astype(bf16)
                bfc1_ref[j] = jnp.sum(dpre.astype(f32), axis=0, keepdims=True)
                t1[slot] = nn(h2t[...], dpre).astype(bf16).reshape(J, 2, r1, W)
                c1_copy(t, slot).start()
                mlp[...] += nn(act, w2b[slot])
                dh2[...] += nt(dpre, w1b[slot])
                if m > 0:
                    chip_sum1(t - 1, 1 - slot, jnp.logical_and(k == 0, m < 3))
                    send_y(k, m - 1)
                else:

                    @pl.when(k > 0)
                    def _():
                        chip_sum1(t - 1, 1 - slot, k * B < 3)

                if m == B - 1:

                    @pl.when(k > 0)
                    def _():
                        send_z(k - 1)

            return 0

        lax.fori_loop(0, A, pair, 0)
        chip_sum1(J - 1, (B - 1) % 2, jnp.bool_(J < 3))

        def back(i, _):
            rows = pl.ds(pl.multiple_of(i * RB, RB), RB)
            mid = mid_ref[rows, :]
            gf = g_ref[rows, :].astype(f32)
            normed, rscale = normalize(mid)
            dh = dh2[rows, :]
            up = dh * (1.0 + scale2)
            dmid = gf + rscale * (
                up
                - jnp.mean(up, axis=-1, keepdims=True)
                - normed * jnp.mean(up * normed, axis=-1, keepdims=True)
            )
            dmid_ref[rows, :] = dmid
            db = (dmid * gate1).astype(bf16)
            dbr[rows, :] = db
            ml = mlp[rows, :] + bias2
            out_ref[rows, :] = (mid + gate2 * ml).astype(bf16)
            for row, v in enumerate((dh, dh * normed, gf * ml, dmid * br_ref[rows, :], dm[rows, :], db)):
                sums_ref[row : row + 1, :] += jnp.sum(v.astype(f32), axis=0, keepdims=True)
            return 0

        lax.fori_loop(0, T // RB, back, 0)
        proj_copy.wait()
        dattn_ref[...] = nt(dbr[...], pw[...]).astype(bf16)

        def proj(i, _):
            cols = pl.ds(pl.multiple_of(i * 256, 256), 256)
            gproj_ref[cols, :] = tn(attn_ref[:, cols], dbr[...]).astype(bf16)
            return 0

        lax.fori_loop(0, D // 256, proj, 0)

        last = J - 1
        own_sum(last, A - 1)
        for k in range(A - 1):
            z_copy(k).wait()

        def part(i, _):
            rows = pl.ds(pl.multiple_of(i * R2, R2), R2)
            total = add32(
                gb[last, at.c, rows, :],
                cr[last, rows, :],
                *[yr[A - 1, m, rows, :] for m in range(B - 1)],
                *[zr[k, rows, :] for k in range(A - 1)],
            )
            g2_ref[rows, :] = total.astype(bf16)
            return 0

        lax.fori_loop(0, r2 // R2, part, 0)
        s1_copy(J - 2, 0).wait()
        s1_copy(J - 1, 1).wait()

    vm, hbm = pl.BlockSpec(memory_space=pltpu.VMEM), pl.BlockSpec(memory_space=pl.ANY)
    sds = jax.ShapeDtypeStruct
    dma = pltpu.SemaphoreType.DMA
    return pl.pallas_call(
        kern,
        out_shape=[
            sds((T, D), bf16), sds((T, D), f32), sds((T, D), bf16), sds((8, D), f32), sds((J, 1, W), f32),
            sds((D, D), bf16), sds((J, r1, FF), bf16), sds((r2, D), bf16),
        ],
        in_specs=[vm] * 6 + [hbm] * 3,
        out_specs=[vm] * 6 + [hbm, vm],
        scratch_shapes=[
            pltpu.VMEM((T, D), bf16), pltpu.VMEM((D, T), bf16), pltpu.VMEM((T, D), bf16),
            pltpu.VMEM((T, D), f32), pltpu.VMEM((T, D), f32), pltpu.VMEM((T, D), bf16),
            pltpu.VMEM((2, D, W), bf16), pltpu.VMEM((2, W, D), bf16),
            pltpu.VMEM((J, 2, r2, D), bf16), pltpu.VMEM((J, r2, D), bf16),
            pltpu.VMEM((A, B - 1, r2, D), bf16), pltpu.VMEM((A, B - 1, r2, D), bf16),
            pltpu.VMEM((A - 1, r2, D), bf16), pltpu.VMEM((A - 1, r2, D), bf16),
            pltpu.VMEM((2, J, 2, r1, W), bf16), pltpu.VMEM((J, J, r1, W), bf16), pltpu.VMEM((2, J, r1, W), bf16),
            pltpu.VMEM((D, D), bf16), dma(()), dma((2, 2)), dma((2,)), dma((J,)), dma((J,)), dma((J,)), dma((J,)),
            dma((A, B - 1)), dma((A, B - 1)), dma((A - 1,)), dma((A - 1,)),
        ],
        compiler_params=pltpu.CompilerParams(
            collective_id=3, has_side_effects=True, vmem_limit_bytes=64 * 1024 * 1024 - 65536
        ),
        name="feed_forward",
    )(middle, branch, attn, g, vectors, b_fc1.reshape(J, 1, W), w4, w1, w2)


class RowSum:
    @staticmethod
    def scratch(U, r, W, A, B, cores):
        dma = pltpu.SemaphoreType.DMA
        shapes = [
            pltpu.VMEM((U, B - 1, A, r, W), bf16), pltpu.VMEM((U, A - 1, r, W), bf16),
            pltpu.VMEM((U, A - 1, r, W), bf16), pltpu.VMEM((U, r, W), bf16), pltpu.VMEM((U, r, W), bf16),
            dma((U, B - 1)), dma((U, B - 1)), dma((U, A - 1)), dma((U, A - 1)), dma((U,)), dma((U,)),
        ]
        if cores:
            shapes += [
                pltpu.VMEM((U, A * B, r, W), bf16), pltpu.VMEM((U, B - 1, A, r, W), bf16), dma((U,)), dma((U,)),
            ]
        return shapes

    def __init__(self, at, s, peer, refs, grad=None, half=None):
        self.at, self.s, self.peer = at, s, peer
        self.grad, self.half = grad, half
        self.yr, self.zs, self.zr, self.xs, self.xr = refs[:5]
        self.yss, self.yrs, self.zss, self.zrs, self.xss, self.xrs = refs[5:11]
        if grad is not None:
            self.cr, self.ys, self.css, self.crs = refs[11:]

    def c_copy(self, u):
        return remote(
            self.grad.at[u, :, 1 - self.at.c], self.cr.at[u], self.css.at[u], self.crs.at[u], self.at.sibling()
        )

    def y_source(self, u, m):
        return self.ys.at[u, m]

    def y_copy(self, u, m):
        src = self.y_source(u, m)
        return remote(src, self.yr.at[u, m], self.yss.at[u, m], self.yrs.at[u, m], self.at.at_b(m + 1))

    def z_copy(self, u, k):
        return remote(self.zs.at[u, k], self.zr.at[u, k], self.zss.at[u, k], self.zrs.at[u, k], self.at.at_a(k + 1))

    def x_copy(self, u):
        return remote(self.xs.at[u], self.xr.at[u], self.xss.at[u], self.xrs.at[u], self.peer)

    def chip(self, u, a, b):
        j = a * self.at.B + b
        return add32(self.grad[u, j, self.at.c], self.cr[u, j])

    def own(self, u, a):
        base = self.chip(u, a, self.at.b) if self.half is None else self.half(u, a)
        return add32(base, *[self.yr[u, m, a] for m in range(self.at.B - 1)])

    def send_y(self, u):
        self.c_copy(u).wait()
        for m in range(self.at.B - 1):
            b = lax.rem(self.at.b + m + 1, self.at.B)
            for a in range(self.at.A):
                self.ys[u, m, a] = self.chip(u, a, b).astype(bf16)
            self.y_copy(u, m).start()

    def send_z(self, u):
        for m in range(self.at.B - 1):
            self.y_copy(u, m).wait()
        for k in range(self.at.A - 1):
            self.zs[u, k] = self.own(u, lax.rem(self.at.a + k + 1, self.at.A)).astype(bf16)
            self.z_copy(u, k).start()

    def send_x(self, u):
        for k in range(self.at.A - 1):
            self.z_copy(u, k).wait()
        total = add32(self.own(u, self.at.a), *[self.zr[u, k] for k in range(self.at.A - 1)])
        if self.s != 2:
            return total
        self.xs[u] = total.astype(bf16)
        self.x_copy(u).start()
        return None

    def finish(self, u):
        self.x_copy(u).wait()
        return add32(self.xs[u], self.xr[u])


def attention_and_sums(
    qkv, kvr, d_attn, lse, hidden, tokens, vectors, d_middle, w_qkv, half_fc1, grad_proj, sum_fc2, sums, bias_fc1, lf, w_ada, n, s
):
    T, D = tokens.shape
    FF = half_fc1.shape[-1]
    A, B = grid_of(n)
    J, r1, r2 = A * B, D // n, FF // n
    GW = 256
    U = D // GW
    F = FF // U
    E = 6 * D
    RB = min(T, 64)
    rows_a = D // n
    m_bias = [2 * D // n, D // n, FF // n, D // n]
    starts = [0, 2 * D, 3 * D, 3 * D + FF]
    NBIAS = 4 * D + FF
    blocks = [max(v, 128) for v in m_bias]
    offs = [sum(blocks[:i]) for i in range(4)]
    M = sum(blocks)
    nq = len(RowSum.scratch(U, r1, 3 * GW, A, B, True))
    nf = len(RowSum.scratch(U, r1, F, A, B, False))

    def kern(*refs):
        it = iter(refs)

        def take(count):
            return [next(it) for _ in range(count)]

        qkv_ref, kvr_ref = take(2)
        e_ref, lse_ref, h_ref, tok_ref, sc_ref, dmid_ref, w_ref, f1_ref, gp_ref, f2_ref, sum_ref, bf_ref, lf_ref, wa_ref = take(14)
        gt_ref, oq_ref, op_ref, o1_ref, o2_ref, gw_ref, gb_ref, dl_ref, bo_ref = take(9)
        h1t, dqg, kvl, kvs, kvr, dg, gq, wq, f1o, x2 = take(10)
        dh1 = gt_ref
        wsem, fsem, kss, krs, x2s, x2r = take(6)
        scr_q, scr_p, scr_f = take(nq), take(nq), take(nf)
        dx, dm, lp, bsum, bx, bsx = take(6)
        asend, arecv, lsend, lrecv, bsend, brecv, xsend, xrecv = take(8)

        at = Place(n)
        me, x = at.me, lax.axis_index("seq")
        peers = fsdp_peers(n, me)

        def seq_dev(k):
            return {"seq": lax.rem(x + k, s)}

        greet([{"fsdp": p} for p in peers] + [seq_dev(k) for k in range(1, s)])
        other = seq_dev(1)
        sq = RowSum(at, s, other, scr_q, grad=gq)
        sp = RowSum(at, s, other, scr_p, grad=gp_ref)
        sf = RowSum(at, s, other, scr_f, half=lambda u, a: f1o[u, a])

        def f_source(u, m):
            b = lax.rem(at.b + m + 1, B)
            return f1_ref.at[:, b, :, pl.ds(pl.multiple_of(u * F, F), F)]

        sf.y_source = f_source
        own_f = [
            pltpu.make_async_copy(f1_ref.at[:, at.b, :, pl.ds(u * F, F)], f1o.at[u], fsem.at[u]) for u in range(U)
        ]
        sp.c_copy(0).start()
        for u in range(U):
            for m in range(B - 1):
                sf.y_copy(u, m).start()
        if s == 2:
            x2_copy = remote(f2_ref, x2, x2s, x2r, other)
            x2_copy.start()
        for o in own_f:
            o.start()

        def h_copy(i):
            k = i % 3
            return pltpu.make_async_copy(
                h_ref.at[:, pl.ds(i * GW, GW)], dg.at[:, pl.ds(k * GW, GW)], wsem.at[k]
            )

        for i in range(min(U, 3)):
            h_copy(i).start()
        for i in range(U):
            h_copy(i).wait()
            k = i % 3
            h1t[i * GW : (i + 1) * GW, :] = dg[:, k * GW : (k + 1) * GW].T
            if i + 3 < U:
                h_copy(i + 3).start()
        dh1[...] = jnp.zeros_like(dh1)
        for o in own_f:
            o.wait()

        def w_copy(u, i):
            lo = pl.multiple_of(i * D + u * GW, GW)
            return pltpu.make_async_copy(w_ref.at[:, pl.ds(lo, GW)], wq.at[i], wsem.at[i])

        def kv_copy(u, k):
            return remote(kvs.at[u, k - 1], kvr.at[u, k - 1], kss.at[u, k - 1], krs.at[u, k - 1], seq_dev(s - k))

        def attend(u):
            slot = lax.rem(u, 2)
            for o in range(2):
                pair = u * 2 + o
                cols, k_cols, v_cols = [pl.ds(pl.multiple_of(lo + pair * 128, 128), 128) for lo in (0, D, 2 * D)]
                here = slice(o * 128, o * 128 + 128)
                qv, e = qkv_ref[:, cols] * bf16(HD**-0.5), e_ref[:, cols]
                ks = [qkv_ref[:, k_cols]] + [kvr_ref[k, :, cols] for k in range(s - 1)]
                vs = [qkv_ref[:, v_cols]] + [kvr_ref[k, :, k_cols] for k in range(s - 1)]
                dqt, dks, dvs = None, [None] * s, [None] * s
                for h in range(2):
                    qh, eh = pick(qv, h), pick(e, h)
                    total = lse_ref[pair, h : h + 1, :]
                    probs, dprobs, cross = [], [], None
                    for j in range(s):
                        p = jnp.exp(nt(ks[j], qh) - total)
                        dp = nt(vs[j], eh)
                        part = (p * dp).sum(axis=0, keepdims=True)
                        cross = part if cross is None else cross + part
                        dv = nn(p.astype(bf16), eh)
                        dvs[j] = dv if dvs[j] is None else dvs[j] + dv
                        probs.append(p)
                        dprobs.append(dp)
                    for j in range(s):
                        ds = (probs[j] * (dprobs[j] - cross)).astype(bf16)
                        dk = nn(ds, qh)
                        dks[j] = dk if dks[j] is None else dks[j] + dk
                        t = tn(pick(ks[j], h), ds)
                        dqt = t if dqt is None else dqt + t
                dqg[slot, :, here] = (dqt * (HD**-0.5)).T.astype(bf16)
                kvl[slot, 0, :, here] = dks[0]
                kvl[slot, 1, :, here] = dvs[0]
                for j in range(1, s):
                    kvs[u, j - 1, 0, :, here] = dks[j].astype(bf16)
                    kvs[u, j - 1, 1, :, here] = dvs[j].astype(bf16)
            for k in range(1, s):
                kv_copy(u, k).start()

        def project(u):
            slot = lax.rem(u, 2)
            for k in range(1, s):
                kv_copy(u, k).wait()
            dg[:, :GW] = dqg[slot]
            for i in range(2):
                lo = (i + 1) * GW
                dg[:, lo : lo + GW] = add32(kvl[slot, i], *[kvr[u, k, i] for k in range(s - 1)]).astype(bf16)
            part = 256 // (2 * r1)
            for i in range(D // 256):
                g = nn(h1t[i * 256 : (i + 1) * 256, :], dg[...]).astype(bf16)
                gq[u, i * part : (i + 1) * part] = g.reshape(part, 2, r1, 3 * GW)
            sq.c_copy(u).start()
            here = pl.ds(pl.multiple_of(u * GW, GW), GW)
            bsum[:, here] = jnp.sum(dg[:, :GW].astype(f32), axis=0, keepdims=True)
            there = pl.ds(pl.multiple_of(D + u * GW, GW), GW)
            bsum[:, there] = jnp.sum(dg[:, 2 * GW :].astype(f32), axis=0, keepdims=True)
            for i in range(3):
                w_copy(u, i).wait()
            total = nt(dg[:, :GW], wq[0])
            for i in range(1, 3):
                total = total + nt(dg[:, i * GW : (i + 1) * GW], wq[i])
            dh1[...] += total

        def step(i, _):
            @pl.when(i < U)
            def _():
                attend(i)

            @pl.when(jnp.logical_and(i >= 1, i <= U))
            def _():
                project(i - 1)

            @pl.when(i < U)
            def _():
                for k in range(3):
                    w_copy(i, k).start()

            @pl.when(i == 0)
            def _():
                sp.send_y(0)

            @pl.when(i < U)
            def _():
                sf.send_z(i)

            @pl.when(i >= 2)
            def _():
                sq.send_y(i - 2)

            return 0

        lax.fori_loop(0, U + 2, step, 0)
        sp.send_z(0)
        for u in range(U - 2):
            sq.send_z(u)

        sums = [jnp.zeros((1, D), f32), jnp.zeros((1, D), f32)]
        scale1 = sc_ref[5:6, :]

        def back(i, carry):
            rows = pl.ds(pl.multiple_of(i * RB, RB), RB)
            normed, rscale = normalize(tok_ref[rows, :].astype(f32))
            dh = dh1[rows, :]
            up = dh * (1.0 + scale1)
            gt_ref[rows, :] = dmid_ref[rows, :] + rscale * (
                up
                - jnp.mean(up, axis=-1, keepdims=True)
                - normed * jnp.mean(up * normed, axis=-1, keepdims=True)
            )
            return (
                carry[0] + jnp.sum(dh, axis=0, keepdims=True),
                carry[1] + jnp.sum(dh * normed, axis=0, keepdims=True),
            )

        shift1_sum, scale1_sum = lax.fori_loop(0, T // RB, back, tuple(sums))
        parts = [shift1_sum, scale1_sum, sum_ref[3:4, :], sum_ref[0:1, :], sum_ref[1:2, :], sum_ref[2:3, :]]
        for i, v in enumerate(parts):
            dx[x, :, i * D : (i + 1) * D] = v
        mod_x = [remote(dx.at[x], dx.at[x], xsend.at[0, k - 1], xrecv.at[0, k - 1], seq_dev(k)) for k in range(1, s)]
        for c in mod_x:
            c.start()
        bsum[:, starts[1] : starts[1] + D] = sum_ref[5:6, :]
        bsum[:, starts[2] : starts[2] + FF] = bf_ref[...]
        bsum[:, starts[3] : starts[3] + D] = sum_ref[4:5, :]

        def block(p, i):
            lo = starts[i] + ((p * m_bias[i]) // blocks[i]) * blocks[i]
            return bsum.at[:, pl.ds(pl.multiple_of(lo, 128), blocks[i])]

        def bias_copy(k, p, i):
            dst = bx.at[me, :, pl.ds(offs[i], blocks[i])]
            return remote(block(p, i), dst, bsend.at[i, k], brecv.at[i, k], {"fsdp": p})

        bias_out = [bias_copy(k, p, i) for k, p in enumerate(peers) for i in range(4)]
        for c in bias_out:
            c.start()
        for i in range(4):
            lo = starts[i] + ((me * m_bias[i]) // blocks[i]) * blocks[i]
            bx[me, :, offs[i] : offs[i] + blocks[i]] = bsum[:, pl.ds(pl.multiple_of(lo, 128), blocks[i])]

        for u in range(U):
            if s == 2:
                sf.send_x(u)
            else:
                o1_ref[:, u * F : (u + 1) * F] = sf.send_x(u)
        sq.send_z(U - 2)
        for c in mod_x:
            c.wait()
        dm[me] = jnp.sum(dx[...], axis=0).astype(bf16).astype(f32)
        mod_all = [remote(dm.at[me], dm.at[me], asend.at[k], arecv.at[k], {"fsdp": p}) for k, p in enumerate(peers)]
        for c in mod_all:
            c.start()
        sq.send_z(U - 1)
        for c in bias_out:
            c.wait()
        bsx[x] = jnp.sum(bx[...], axis=0)
        bias_x = [remote(bsx.at[x], bsx.at[x], xsend.at[1, k - 1], xrecv.at[1, k - 1], seq_dev(k)) for k in range(1, s)]
        for c in bias_x:
            c.start()
        if s == 2:
            sp.send_x(0)
        else:
            op_ref[...] = sp.send_x(0)
        for c in mod_all:
            c.wait()
        dmod = dm[...].reshape(n, E).astype(bf16)
        lp[...] = nt(dmod, wa_ref[...]).reshape(n, 1, rows_a)
        dl_ref[me] = lp[me]
        lift = [remote(lp.at[p], dl_ref.at[me], lsend.at[k], lrecv.at[k], {"fsdp": p}) for k, p in enumerate(peers)]
        for c in lift:
            c.start()
        gw_ref[...] = tn(lf_ref[...].reshape(n, rows_a).astype(bf16), dmod)
        gb_ref[...] = jnp.sum(dm[...], axis=0)

        def put_q(u, value):
            for i in range(3):
                oq_ref[:, i * D + u * GW : i * D + (u + 1) * GW] = value[:, i * GW : (i + 1) * GW]

        for u in range(U):
            value = sq.send_x(u)
            if s != 2:
                put_q(u, value)
        if s == 2:
            x2_copy.wait()
            o2_ref[...] = add32(f2_ref[...], x2[...])
            for u in range(U):
                o1_ref[:, u * F : (u + 1) * F] = sf.finish(u)
            op_ref[...] = sp.finish(0)
            for u in range(U):
                put_q(u, sq.finish(u))
        else:
            o2_ref[...] = f2_ref[...].astype(f32)
        for c in bias_x:
            c.wait()
        bo_ref[...] = jnp.sum(bsx[...], axis=0)
        for c in lift:
            c.wait()

    vm, hbm = pl.BlockSpec(memory_space=pltpu.VMEM), pl.BlockSpec(memory_space=pl.ANY)
    sds, dma = jax.ShapeDtypeStruct, pltpu.SemaphoreType.DMA
    res = pl.pallas_call(
        kern,
        out_shape=[
            sds((T, D), f32), sds((r1, 3 * D), f32), sds((r1, D), f32), sds((r1, FF), f32), sds((r2, D), f32),
            sds((rows_a, E), f32), sds((1, E), f32), sds((n, 1, rows_a), f32), sds((1, M), f32),
        ],
        in_specs=[vm] * 4 + [hbm] + [vm] * 3 + [hbm, hbm] + [vm] * 6,
        out_specs=[vm] * 9,
        scratch_shapes=[
            pltpu.VMEM((D, T), bf16), pltpu.VMEM((2, T, GW), bf16),
            pltpu.VMEM((2, 2, T, GW), f32), pltpu.VMEM((U, s - 1, 2, T, GW), bf16),
            pltpu.VMEM((U, s - 1, 2, T, GW), bf16), pltpu.VMEM((T, 3 * GW), bf16),
            pltpu.VMEM((U, J, 2, r1, 3 * GW), bf16), pltpu.VMEM((3, D, GW), bf16),
            pltpu.VMEM((U, A, r1, F), bf16), pltpu.VMEM((r2, D), bf16),
            dma((3,)), dma((U,)), dma((U, s - 1)), dma((U, s - 1)), dma(()), dma(()),
        ]
        + RowSum.scratch(U, r1, 3 * GW, A, B, True)
        + RowSum.scratch(1, r1, D, A, B, True)
        + RowSum.scratch(U, r1, F, A, B, False)
        + [
            pltpu.VMEM((s, 1, E), f32), pltpu.VMEM((n, 1, E), f32), pltpu.VMEM((n, 1, rows_a), f32),
            pltpu.VMEM((1, NBIAS), f32), pltpu.VMEM((n, 1, M), f32), pltpu.VMEM((s, 1, M), f32),
            dma((n - 1,)), dma((n - 1,)), dma((n - 1,)), dma((n - 1,)),
            dma((4, n - 1)), dma((4, n - 1)), dma((2, s - 1)), dma((2, s - 1)),
        ],
        compiler_params=pltpu.CompilerParams(
            collective_id=4, has_side_effects=True, vmem_limit_bytes=64 * 1024 * 1024 - 65536
        ),
        name="attention_and_sums",
    )(
        qkv, kvr, d_attn, lse, hidden, tokens, vectors, d_middle, w_qkv, half_fc1.reshape(A, B, r1, FF),
        grad_proj.reshape(1, J, 2, r1, D), sum_fc2, sums, bias_fc1, lf, w_ada,
    )
    grad_tokens, t_qkv, t_proj, t_fc1, t_fc2, t_ada, ada_sums, d_lifted, bias = res
    if s != 2:
        t_qkv, t_proj, t_fc1, t_fc2 = lax.psum((t_qkv, t_proj, t_fc1, t_fc2), "seq")
    me = lax.axis_index("fsdp")
    biases = []
    for width, wide, off in zip(m_bias, blocks, offs):
        biases.append(lax.dynamic_slice_in_dim(bias[0, off : off + wide], (me * width) % wide, width))
    return grad_tokens, t_qkv, t_proj, t_fc1, t_fc2, t_ada, ada_sums, d_lifted, biases


def on_device(
    tokens,
    condition,
    w_ada,
    b_ada,
    w_qkv,
    b_qv,
    w_proj,
    b_proj,
    w_fc1,
    b_fc1,
    w_fc2,
    b_fc2,
    cotangent,
):
    n, s = lax.axis_size("fsdp"), lax.axis_size("seq")
    width = tokens.shape[-1]

    lifted, silu_back = jax.vjp(jax.nn.silu, condition.astype(f32))
    lifted_q = lifted.astype(bf16).astype(f32).reshape(n, 1, width // n)
    qkv, kvr, hidden_one, attn, lse, branch, middle, vectors, fc1_b, lf, w4, fc1_w, fc2_w = forward_attention(
        lifted_q, w_ada, [b_qv, b_proj, b_fc1, b_fc2, b_ada], tokens[0], w_qkv, w_proj, w_fc1, w_fc2, n, s
    )
    result, d_middle, d_attn, sums, bias_fc1, grad_proj, half_fc1, sum_fc2 = feed_forward(
        middle, branch, attn, cotangent[0], vectors, fc1_b, w4, fc1_w, fc2_w, n
    )
    grad_input, total_qkv, total_proj, total_fc1, total_fc2, total_ada, sums_ada, d_lifted, total_bias = (
        attention_and_sums(
            qkv, kvr, d_attn, lse, hidden_one, tokens[0], vectors, d_middle, w4, half_fc1,
            grad_proj, sum_fc2, sums, bias_fc1.reshape(1, -1), lf, w_ada, n, s,
        )
    )
    share = b_ada.shape[0]
    total_bada = lax.dynamic_slice_in_dim(sums_ada[0], lax.axis_index("fsdp") * share, share)
    grad_condition = silu_back(d_lifted.reshape(1, width))[0]
    total_bqv, total_bproj, total_bfc1, total_bfc2 = total_bias
    return (
        result[None],
        grad_input[None],
        grad_condition,
        total_ada,
        total_bada,
        total_qkv,
        total_bqv,
        total_proj,
        total_bproj,
        total_fc1,
        total_bfc1,
        total_fc2,
        total_bfc2,
    )


def solution(mesh):
    weights = (P("fsdp", None), P("fsdp")) * 5
    return jax.shard_map(
        on_device,
        mesh=mesh,
        in_specs=(P("fsdp", "seq", None), P("fsdp", None)) + weights + (P("fsdp", "seq", None),),
        out_specs=(P("fsdp", "seq", None), P("fsdp", "seq", None), P("fsdp", None)) + weights,
        check_vma=False,
    )
```

```python
from functools import partial

import jax
import jax.numpy as jnp
from jax import lax
from jax.experimental import pallas as pl
from jax.experimental.pallas import tpu as pltpu
from jax.sharding import PartitionSpec as P

HD = 64
norm_eps = 1e-06
f32 = jnp.float32
bf16 = jnp.bfloat16
MESH = pl.DeviceIdType.MESH


def grid_of(n):
    b = 2 if n == 16 else 4
    return n // (2 * b), b


def nt(a, b):
    return lax.dot_general(a, b, (((1,), (1,)), ((), ())), preferred_element_type=f32)


def nn(a, b):
    return lax.dot_general(a, b, (((1,), (0,)), ((), ())), preferred_element_type=f32)


def tn(a, b):
    return lax.dot_general(a, b, (((0,), (0,)), ((), ())), preferred_element_type=f32)


def fsdp_peers(n, me):
    return [lax.rem(me + k, n) for k in range(1, n)]


def head_mask(ref_shape, h):
    low = lax.broadcasted_iota(jnp.int32, ref_shape, 1) < HD
    return low if h == 0 else ~low


def pick(values, h):
    return jnp.where(head_mask(values.shape, h), values, jnp.zeros_like(values))


def remote(src, dst, send, recv, device):
    return pltpu.make_async_remote_copy(
        src_ref=src, dst_ref=dst, send_sem=send, recv_sem=recv, device_id=device, device_id_type=MESH
    )


def greet(devices):
    bar = pltpu.get_barrier_semaphore()
    for d in devices:
        pl.semaphore_signal(bar, inc=1, device_id=d, device_id_type=MESH)
    pl.semaphore_wait(bar, len(devices))


class Place:
    def __init__(self, n):
        self.A, self.B = grid_of(n)
        me = lax.axis_index("fsdp")
        self.me = me
        self.a, self.b, self.c = me // (2 * self.B), lax.rem(me // 2, self.B), lax.rem(me, 2)

    def dev(self, a, b, c):
        return {"fsdp": (a * self.B + b) * 2 + c}

    def at_a(self, k):
        return self.dev(lax.rem(self.a + k, self.A), self.b, self.c)

    def at_b(self, k):
        return self.dev(self.a, lax.rem(self.b + k, self.B), self.c)

    def sibling(self):
        return self.dev(self.a, self.b, 1 - self.c)

    def all(self):
        return [self.at_a(k) for k in range(1, self.A)] + [self.at_b(k) for k in range(1, self.B)] + [self.sibling()]


def add32(*values):
    total = values[0].astype(f32)
    for v in values[1:]:
        total = total + v.astype(f32)
    return total


def gelu_both(x):
    k = 0.7978845608028654
    sq = x * x
    th = jnp.tanh(k * (x + 0.044715 * (sq * x)))
    half = 0.5 * (1.0 + th)
    slope = half + (0.5 * k) * x * (1.0 - th * th) * (1.0 + (3 * 0.044715) * sq)
    return x * half, slope


def normalize(v):
    center = v - jnp.mean(v, axis=-1, keepdims=True)
    rscale = lax.rsqrt(jnp.mean(center * center, axis=-1, keepdims=True) + norm_eps)
    return center * rscale, rscale


def bias_block(width, n):
    return max(-(-((p * width) % 128 + width) // 128) * 128 for p in range(n))


def placed_bias(bias, n):
    width, wide = bias.shape[0], bias_block(bias.shape[0], n)
    bias = bias.astype(f32)[None]
    if wide == width:
        return bias
    at = (lax.axis_index("fsdp") * width) % 128
    return lax.dynamic_update_slice(jnp.zeros((1, wide), f32), bias, (0, at))


def forward_attention(lifted, w_ada, biases, tokens, w_qkv, w_proj, w_fc1, w_fc2, n, s):
    T, D = tokens.shape
    E = w_ada.shape[1]
    FF = w_fc1.shape[1]
    A, B = grid_of(n)
    rows_a = w_ada.shape[0]
    r1, r2 = w_qkv.shape[0], w_fc2.shape[0]
    widths = [v.shape[0] for v in biases]
    blocks = [bias_block(w, n) for w in widths]
    offs = [sum(blocks[:i]) for i in range(5)]
    bases = [n * sum(widths[:i]) for i in range(5)]
    packed = jnp.concatenate([placed_bias(v, n) for v in biases], axis=1)
    M = packed.shape[1]
    share = s == 2
    NT, NL = 8, 16
    CQ, CF, RF = 4 * D // NT, FF // NL, r2 // NL
    RB = min(T, 64)
    AHEAD, MODULATE, LAG, ATTEND = 2, 4, 6, NT + 7
    NA, NY = A - 1, B - 1
    NQ = NA + NY + 1
    NF = 3 * (NA + NY) + 2
    pairs = D // 128

    def kern(
        l_ref, wa_ref, bias_ref, tok_ref, wqkv_ref, wproj_ref, wfc1_ref, wfc2_ref,
        qkv_ref, kvr_ref, h_ref, attn_ref, lse_ref, br_ref, mid_ref, vec_ref, bfc1_ref, lf_ref, w4_ref, f1_ref, f2_ref,
        normed, wq, part, acc, bout, bvec, mod, msend, mrecv, qsend, qrecv, fsend, frecv, ksend, krecv, osem,
    ):
        at = Place(n)
        a, b, c, me, x = at.a, at.b, at.c, at.me, lax.axis_index("seq")
        peers = fsdp_peers(n, me)
        other = {"seq": lax.rem(x + 1, s)}
        greet([{"fsdp": p} for p in peers] + [{"seq": lax.rem(x + k, s)} for k in range(1, s)])

        def small(i, src, dst):
            return [
                remote(src(p), dst(k), msend.at[i, k], mrecv.at[i, k], {"fsdp": p}) for k, p in enumerate(peers)
            ]

        m_lift = small(0, lambda p: l_ref.at[p], lambda k: lf_ref.at[me])
        m_bias = small(1, lambda p: bias_ref, lambda k: bout.at[me])
        m_part = small(2, lambda p: part.at[p], lambda k: acc.at[k + 1])
        for r in m_lift + m_bias:
            r.start()
        owns = [
            pltpu.make_async_copy(wqkv_ref, wq.at[a, b, c, :, pl.ds(0, 3 * D)], osem.at[0]),
            pltpu.make_async_copy(wproj_ref, wq.at[a, b, c, :, pl.ds(3 * D, D)], osem.at[1]),
            pltpu.make_async_copy(wfc1_ref, f1_ref.at[a, b, c], osem.at[2]),
            pltpu.make_async_copy(wfc2_ref, f2_ref.at[a, b, c], osem.at[3]),
        ]
        for o in owns:
            o.start()

        def block(i):
            return jnp.where(i < 6, lax.rem(i + 2, 6), i)

        def span(lo, size, step):
            return pl.ds(pl.multiple_of(lo, step), size)

        class Ticks:
            def __init__(self, pieces, whole, send, recv):
                self.pieces, self.whole, self.send, self.recv = pieces, whole, send, recv

            def copy(self, j, i, src, dst, device):
                return remote(src, dst, self.send.at[j, i], self.recv.at[j, i], device)

            def z(self, j):
                return [
                    self.copy(j, i * NA + k, src.at[rows, cols], buf.at[a, b, c, rows, cols], at.at_a(k + 1))
                    for i, (src, buf, rows, cols, _) in enumerate(self.pieces(j))
                    for k in range(NA)
                ]

            def y(self, j):
                out, ps = [], self.pieces(j)
                for i, (_, buf, rows, cols, _) in enumerate(ps):
                    sl = buf.at[:, b, c, rows, cols]
                    out += [self.copy(j, len(ps) * NA + i * NY + k, sl, sl, at.at_b(k + 1)) for k in range(NY)]
                return out

            def x(self, j):
                out, ps = [], self.pieces(j)
                i = len(ps) * (NA + NY)
                for _, buf, rows, cols, shared in ps:
                    if not shared:
                        continue
                    for k in range(NA):
                        sl = buf.at[lax.rem(a + k + 1, A), :, c, rows, cols]
                        out.append(self.copy(j, i, sl, sl, other))
                        i += 1
                    for k in range(NY):
                        sl = buf.at[a, lax.rem(b + k + 1, B), c, rows, cols]
                        out.append(self.copy(j, i, sl, sl, other))
                        i += 1
                return out

            def c(self, j):
                ps = self.whole(j)
                i = self.send.shape[1] - len(ps)
                return [
                    self.copy(j, i + k, buf.at[:, :, c, rows, cols], buf.at[:, :, c, rows, cols], at.sibling())
                    for k, (buf, rows, cols) in enumerate(ps)
                ]

            def start_z(self, j):
                for r in self.z(j):
                    r.start()

            def start_y(self, j):
                for r in self.z(j):
                    r.wait_recv()
                for r in self.y(j):
                    r.start()

            def start_x(self, j):
                for r in self.y(j):
                    r.wait_recv()
                for r in self.x(j):
                    r.start()

            def start_c(self, j):
                for r in self.x(j):
                    r.wait_recv()
                for r in self.c(j):
                    r.start()

            def relay(self, j):
                self.start_x(j)
                self.start_c(j)

            def finish(self, j):
                for r in self.z(j) + self.y(j) + self.x(j):
                    r.wait_send()
                for r in self.c(j):
                    r.wait()

        all_r1 = pl.ds(0, r1)
        mine = wq.at[a, b, c]

        def q_pieces(i):
            return [(mine, wq, all_r1, span(block(i) * CQ, CQ, CQ), False)]

        def q_whole(i):
            return [(wq, all_r1, span(block(i) * CQ, CQ, CQ))]

        def f_pieces(j):
            w = D // 2 if share else D
            part = span(x * w, w, w) if share else pl.ds(0, D)
            return [
                (wfc1_ref, f1_ref, all_r1, span(j * CF, CF, CF), False),
                (wfc2_ref, f2_ref, span(j * RF, RF, RF), part, share),
            ]

        def f_whole(j):
            return [(f1_ref, all_r1, span(j * CF, CF, CF)), (f2_ref, span(j * RF, RF, RF), pl.ds(0, D))]

        tq, tf = Ticks(q_pieces, q_whole, qsend, qrecv), Ticks(f_pieces, f_whole, fsend, frecv)

        owns[0].wait()
        owns[1].wait()
        for i in range(AHEAD):
            tq.start_z(i)
        lf_ref[me] = l_ref[me]
        bout[me] = bias_ref[...]
        bvec[...] = jnp.zeros_like(bvec)

        def norm(i, _):
            rows = pl.ds(pl.multiple_of(i * RB, RB), RB)
            normed[rows, :] = normalize(tok_ref[rows, :].astype(f32))[0]
            return 0

        for r in m_lift:
            r.wait_recv()
        part[...] = nn(lf_ref[...].reshape(n, rows_a).astype(bf16), wa_ref[...]).reshape(n, 1, E)
        acc[0] = part[me]
        for r in m_part:
            r.start()

        def modulation():
            for r in m_bias + m_part:
                r.wait_recv()
            for i in range(5):
                for p in range(n):
                    lo = bases[i] + p * widths[i] // 128 * 128
                    value = bout[p, :, offs[i] : offs[i] + blocks[i]]
                    if widths[i] % 128 == 0:
                        bvec[:, lo : lo + blocks[i]] = value
                    else:
                        bvec[:, lo : lo + blocks[i]] += value
            mod[...] = jnp.sum(acc[...], axis=0) + bvec[:, bases[4] :]
            shift1, scale1, gate1, shift2, scale2, gate2 = [mod[:, i * D : (i + 1) * D] for i in range(6)]
            vec_ref[...] = jnp.zeros_like(vec_ref)
            for i, v in enumerate((shift2, scale2, gate2, gate1, bvec[:, bases[3] : bases[3] + D], scale1)):
                vec_ref[i : i + 1, :] = v
            bfc1_ref[...] = bvec[:, bases[2] : bases[2] + FF]

            def modulate(i, _):
                rows = pl.ds(pl.multiple_of(i * RB, RB), RB)
                h_ref[rows, :] = (normed[rows, :] * (1.0 + scale1) + shift1).astype(bf16)
                return 0

            lax.fori_loop(0, T // RB, modulate, 0)


        def kv_copy(m, k):
            return remote(
                qkv_ref.at[:, span(D + m * CQ, CQ, CQ)],
                kvr_ref.at[k - 1, :, span(m * CQ, CQ, CQ)],
                ksend.at[m, k - 1],
                krecv.at[m, k - 1],
                {"seq": lax.rem(x + k, s)},
            )

        def project(m):
            tq.finish(m)

            @pl.when(m < 6)
            def _():
                lo = block(m) * CQ
                cols = span(lo, CQ, CQ)
                from_v = (block(m) >= 4).astype(jnp.int32)
                bias = bvec[:, span(lo - from_v * D, CQ, CQ)]
                is_key = jnp.logical_and(block(m) >= 2, block(m) < 4)
                bias = jnp.where(is_key, jnp.zeros_like(bias), bias)
                out = nn(h_ref[...], wq[:, :, :, :, cols].reshape(D, CQ))
                qkv_ref[:, cols] = (out + bias).astype(bf16)

            @pl.when(m < 4)
            def _():
                for k in range(1, s):
                    kv_copy(m, k).start()

        def attend(pair):
            def cols(lo):
                return span(lo + pair * 128, 128, 128)

            q = qkv_ref[:, cols(0)] * bf16(HD**-0.5)
            ks = [qkv_ref[:, cols(D)]] + [kvr_ref[k, :, cols(0)] for k in range(s - 1)]
            vs = [qkv_ref[:, cols(2 * D)]] + [kvr_ref[k, :, cols(D)] for k in range(s - 1)]
            total = None
            for h in range(2):
                qh = pick(q, h)
                scores = [nt(k, qh) for k in ks]
                top = scores[0].max(axis=0, keepdims=True)
                for sc in scores[1:]:
                    top = jnp.maximum(top, sc.max(axis=0, keepdims=True))
                mass, out = None, None
                for sc, v in zip(scores, vs):
                    p = jnp.exp(sc - top)
                    got = p.sum(axis=0, keepdims=True)
                    mass = got if mass is None else mass + got
                    o = tn(pick(v, h), p.astype(bf16))
                    out = o if out is None else out + o
                out = out * (1.0 / mass)
                total = out if total is None else total + out
                lse_ref[pair, h : h + 1, :] = top + jnp.log(mass)
            attn_ref[:, cols(0)] = total.T.astype(bf16)

        def branch(i, _):
            cols = span(i * 256, 256, 256)
            weight = wq[:, :, :, :, span(3 * D + i * 256, 256, 256)].reshape(D, 256)
            got = nn(attn_ref[...], weight) + bvec[:, span(bases[1] + i * 256, 256, 256)]
            br_ref[:, cols] = got
            mid_ref[:, cols] = tok_ref[:, cols].astype(f32) + mod[:, span(2 * D + i * 256, 256, 256)] * got
            return 0

        out4 = pltpu.make_async_copy(wq, w4_ref, osem.at[0])

        def step(i, _):
            def when(lo, hi, f, shift):
                @pl.when(jnp.logical_and(i >= lo, i < hi))
                def _():
                    f(i - shift)

            when(0, NT - AHEAD, lambda j: tq.start_z(j + AHEAD), 0)
            when(NT - AHEAD, NT + NL - AHEAD, tf.start_z, NT - AHEAD)
            when(0, NT, tq.start_y, 0)
            when(NT, NT + NL, tf.start_y, NT)
            when(1, NT + 1, tq.relay, 1)
            when(NT + 1, NT + NL + 1, tf.start_x, NT + 1)
            when(NT + LAG, NT + NL + LAG, tf.start_c, NT + LAG)
            when(NT + LAG + 1, NT + NL + LAG + 1, tf.finish, NT + LAG + 1)

            @pl.when(i == 0)
            def _():
                lax.fori_loop(0, T // RB, norm, 0)

            pl.when(i == MODULATE)(modulation)
            when(MODULATE, MODULATE + NT, project, MODULATE)

            @pl.when(i == MODULATE + NT)
            def _():
                out4.start()

            @pl.when(i == ATTEND)
            def _():
                for m in range(4):
                    for k in range(1, s):
                        kv_copy(m, k).wait()

            when(ATTEND, ATTEND + pairs, attend, ATTEND)

            @pl.when(i == ATTEND + pairs)
            def _():
                lax.fori_loop(0, D // 256, branch, 0)

            return 0

        owns[2].wait()
        owns[3].wait()
        lax.fori_loop(0, NT + NL + LAG + 1, step, 0)
        out4.wait()
        for r in m_lift + m_bias + m_part:
            r.wait_send()

    vm, hbm = pl.BlockSpec(memory_space=pltpu.VMEM), pl.BlockSpec(memory_space=pl.ANY)
    sds, dma = jax.ShapeDtypeStruct, pltpu.SemaphoreType.DMA
    res = pl.pallas_call(
        kern,
        out_shape=[
            sds((T, 3 * D), bf16), sds((s - 1, T, 2 * D), bf16), sds((T, D), bf16), sds((T, D), bf16),
            sds((pairs, 2, T), f32), sds((T, D), f32), sds((T, D), f32), sds((8, D), f32), sds((1, FF), f32),
            sds((n, 1, rows_a), f32), sds((A, B, 2, r1, 4 * D), bf16), sds((A, B, 2, r1, FF), bf16),
            sds((A, B, 2, r2, D), bf16),
        ],
        in_specs=[vm] * 8,
        out_specs=[vm] * 10 + [hbm] * 3,
        scratch_shapes=[
            pltpu.VMEM((T, D), f32), pltpu.VMEM((A, B, 2, r1, 4 * D), bf16), pltpu.VMEM((n, 1, E), f32),
            pltpu.VMEM((n, 1, E), f32), pltpu.VMEM((n, 1, M), f32), pltpu.VMEM((1, n * sum(widths)), f32),
            pltpu.VMEM((1, E), f32), dma((3, n - 1)), dma((3, n - 1)), dma((NT, NQ)), dma((NT, NQ)),
            dma((NL, NF)), dma((NL, NF)), dma((4, s - 1)), dma((4, s - 1)), dma((4,)),
        ],
        compiler_params=pltpu.CompilerParams(
            collective_id=0, has_side_effects=True, vmem_limit_bytes=64 * 1024 * 1024 - 65536
        ),
        name="forward_attention",
    )(lifted, w_ada, packed, tokens, w_qkv, w_proj, w_fc1, w_fc2)
    qkv, kvr, hidden, attn, lse, branch, middle, vectors, b_fc1, lf, w4, f1, f2 = res
    return (
        qkv, kvr, hidden, attn, lse, branch, middle, vectors, b_fc1, lf,
        w4.reshape(D, 4 * D), f1.reshape(D, FF), f2.reshape(FF, D),
    )


def feed_forward(middle, branch, attn, g, vectors, b_fc1, w4, w1, w2, n, s):
    T, D = middle.shape
    FF = w1.shape[1]
    A, B = grid_of(n)
    J, r1, r2 = A * B, D // n, FF // n
    W = 2 * r2
    RB = min(T, 64)
    H = W // 2 if s == 2 else W

    def kern(
        mid_ref, br_ref, attn_ref, g_ref, vec_ref, b1_ref, w4_ref, w1_ref, w2_ref,
        out_ref, dmid_ref, dattn_ref, sums_ref, bfc1_ref, gproj_ref, g1_ref, g2_ref,
        h2, h2t, dm, dh2, mlp, dbr, w1b, w2b, gb, cr, ys, yr, zs, zr, t1, c1, s1, x1, o1, x1s, x1r,
        pw, psem, wsem, osem, cs, crs, c1s, c1r, yss, yrs, zss, zrs,
    ):
        at = Place(n)
        x = lax.axis_index("seq")
        other = {"seq": lax.rem(x + 1, s)}
        greet(at.all() + ([other] if s == 2 else []))
        shift2, scale2, gate2, gate1, bias2 = [vec_ref[i : i + 1, :] for i in range(5)]

        def tile(t):
            k, m = t // B, lax.rem(t, B)
            return lax.rem(at.a + 1 + k, A) * B + lax.rem(at.b + 1 + m, B)

        def weights(t, slot):
            lo = pl.multiple_of(tile(t) * W, W)
            return (
                pltpu.make_async_copy(w1_ref.at[:, pl.ds(lo, W)], w1b.at[slot], wsem.at[0, slot]),
                pltpu.make_async_copy(w2_ref.at[pl.ds(lo, W), :], w2b.at[slot], wsem.at[1, slot]),
            )

        for w in weights(0, 0):
            w.start()
        proj_copy = pltpu.make_async_copy(w4_ref.at[:, pl.ds(3 * D, D)], pw, psem)
        proj_copy.start()

        def head(i, _):
            rows = pl.ds(pl.multiple_of(i * RB, RB), RB)
            normed, _r = normalize(mid_ref[rows, :])
            h2[rows, :] = (normed * (1.0 + scale2) + shift2).astype(bf16)
            dm[rows, :] = (g_ref[rows, :].astype(f32) * gate2).astype(bf16)
            return 0

        lax.fori_loop(0, T // RB, head, 0)
        for i in range(0, D, 256):
            h2t[i : i + 256, :] = h2[:, i : i + 256].T
        dh2[...] = jnp.zeros_like(dh2)
        mlp[...] = jnp.zeros_like(mlp)
        sums_ref[...] = jnp.zeros_like(sums_ref)

        def c2_copy(t):
            return remote(gb.at[t, 1 - at.c], cr.at[t], cs.at[t], crs.at[t], at.sibling())

        def c1_copy(t, slot):
            return remote(t1.at[slot, :, 1 - at.c], c1.at[t], c1s.at[t], c1r.at[t], at.sibling())

        def y_copy(k, m):
            return remote(ys.at[k, m], yr.at[k, m], yss.at[k, m], yrs.at[k, m], at.at_b(m + 1))

        def z_copy(k):
            return remote(zs.at[k], zr.at[k], zss.at[k], zrs.at[k], at.at_a(k + 1))

        def out1_copy(t, slot):
            lo = pl.multiple_of(tile(t) * H, H)
            src = o1 if s == 2 else s1
            return pltpu.make_async_copy(src.at[slot], g1_ref.at[:, :, pl.ds(lo, H)], osem.at[slot])

        def half(k):
            return pl.ds(pl.multiple_of(k * H, H), H)

        def x1_copy(t, slot):
            return remote(s1.at[slot, :, :, half(1 - x)], x1.at[t], x1s.at[t], x1r.at[t], other)

        def when_not(first, f):
            if not isinstance(first, bool):
                pl.when(jnp.logical_not(first))(f)
            elif not first:
                f()

        def chip_sum1(t, slot, first):
            c1_copy(t, slot).wait()
            if s != 2:
                when_not(first, lambda: out1_copy(t, slot).wait())

            def part(i, _):
                s1[slot, i] = add32(t1[slot, i, at.c], c1[t, i]).astype(bf16)
                return 0

            lax.fori_loop(0, J, part, 0)
            if s == 2:
                x1_copy(t, slot).start()
            else:
                out1_copy(t, slot).start()

        def seq_sum1(t, slot, first):
            if s != 2:
                return
            x1_copy(t, slot).wait()
            when_not(first, lambda: out1_copy(t, slot).wait())

            def part(i, _):
                o1[slot, i] = add32(s1[slot, i, :, half(x)], x1[t, i]).astype(bf16)
                return 0

            lax.fori_loop(0, J, part, 0)
            out1_copy(t, slot).start()

        R2 = min(r2, 64)

        def own_sum(t, k):
            c2_copy(t).wait()
            for m in range(B - 1):
                y_copy(k, m).wait()

        def send_y(k, m):
            t = k * B + m
            c2_copy(t).wait()

            def part(i, _):
                rows = pl.ds(pl.multiple_of(i * R2, R2), R2)
                ys[k, m, rows, :] = add32(gb[t, at.c, rows, :], cr[t, rows, :]).astype(bf16)
                return 0

            lax.fori_loop(0, r2 // R2, part, 0)
            y_copy(k, m).start()

        def send_z(k):
            t = k * B + B - 1
            own_sum(t, k)

            def part(i, _):
                rows = pl.ds(pl.multiple_of(i * R2, R2), R2)
                total = add32(gb[t, at.c, rows, :], cr[t, rows, :], *[yr[k, m, rows, :] for m in range(B - 1)])
                zs[k, rows, :] = total.astype(bf16)
                return 0

            lax.fori_loop(0, r2 // R2, part, 0)
            z_copy(k).start()

        def pair(k, _):
            for m in range(B):
                t = k * B + m
                slot = m % 2
                for w in weights(t, slot):
                    w.wait()

                @pl.when(t + 1 < J)
                def _():
                    for w in weights(t + 1, 1 - slot):
                        w.start()

                j = tile(t)
                act, slope = gelu_both(nn(h2[...], w1b[slot]) + b1_ref[j])
                act = act.astype(bf16)
                g2t = tn(act, dm[...]).astype(bf16)
                gb[t, 0] = g2t[:r2]
                gb[t, 1] = g2t[r2:]
                c2_copy(t).start()
                dpre = (nt(dm[...], w2b[slot]) * slope).astype(bf16)
                bfc1_ref[j] = jnp.sum(dpre.astype(f32), axis=0, keepdims=True)
                t1[slot] = nn(h2t[...], dpre).astype(bf16).reshape(J, 2, r1, W)
                c1_copy(t, slot).start()
                mlp[...] += nn(act, w2b[slot])
                dh2[...] += nt(dpre, w1b[slot])
                if m > 0:
                    chip_sum1(t - 1, 1 - slot, jnp.logical_and(k == 0, m < 3))
                    if m > 1:
                        seq_sum1(t - 2, slot, jnp.logical_and(k == 0, m < 4))
                    else:

                        @pl.when(k > 0)
                        def _():
                            seq_sum1(t - 2, slot, k * B < 3)

                    send_y(k, m - 1)
                else:

                    @pl.when(k > 0)
                    def _():
                        chip_sum1(t - 1, 1 - slot, k * B < 3)
                        seq_sum1(t - 2, slot, k * B < 4)

                if m == B - 1:

                    @pl.when(k > 0)
                    def _():
                        send_z(k - 1)

            return 0

        lax.fori_loop(0, A, pair, 0)
        chip_sum1(J - 1, 1, J < 3)
        seq_sum1(J - 2, 0, J < 4)

        def back(i, _):
            rows = pl.ds(pl.multiple_of(i * RB, RB), RB)
            mid = mid_ref[rows, :]
            gf = g_ref[rows, :].astype(f32)
            normed, rscale = normalize(mid)
            dh = dh2[rows, :]
            up = dh * (1.0 + scale2)
            dmid = gf + rscale * (
                up
                - jnp.mean(up, axis=-1, keepdims=True)
                - normed * jnp.mean(up * normed, axis=-1, keepdims=True)
            )
            dmid_ref[rows, :] = dmid
            db = (dmid * gate1).astype(bf16)
            dbr[rows, :] = db
            ml = mlp[rows, :] + bias2
            out_ref[rows, :] = (mid + gate2 * ml).astype(bf16)
            for row, v in enumerate((dh, dh * normed, gf * ml, dmid * br_ref[rows, :], dm[rows, :], db)):
                sums_ref[row : row + 1, :] += jnp.sum(v.astype(f32), axis=0, keepdims=True)
            return 0

        lax.fori_loop(0, T // RB, back, 0)
        proj_copy.wait()
        dattn_ref[...] = nt(dbr[...], pw[...]).astype(bf16)

        def proj(i, _):
            cols = pl.ds(pl.multiple_of(i * 256, 256), 256)
            gproj_ref[cols, :] = tn(attn_ref[:, cols], dbr[...]).astype(bf16)
            return 0

        lax.fori_loop(0, D // 256, proj, 0)

        seq_sum1(J - 1, 1, J < 3)
        last = J - 1
        own_sum(last, A - 1)
        for k in range(A - 1):
            z_copy(k).wait()

        def part(i, _):
            rows = pl.ds(pl.multiple_of(i * R2, R2), R2)
            total = add32(
                gb[last, at.c, rows, :],
                cr[last, rows, :],
                *[yr[A - 1, m, rows, :] for m in range(B - 1)],
                *[zr[k, rows, :] for k in range(A - 1)],
            )
            g2_ref[rows, :] = total.astype(bf16)
            return 0

        lax.fori_loop(0, r2 // R2, part, 0)
        out1_copy(J - 2, 0).wait()
        out1_copy(J - 1, 1).wait()

    vm, hbm = pl.BlockSpec(memory_space=pltpu.VMEM), pl.BlockSpec(memory_space=pl.ANY)
    sds = jax.ShapeDtypeStruct
    dma = pltpu.SemaphoreType.DMA
    return pl.pallas_call(
        kern,
        out_shape=[
            sds((T, D), bf16), sds((T, D), f32), sds((T, D), bf16), sds((8, D), f32), sds((J, 1, W), f32),
            sds((D, D), bf16), sds((J, r1, J * H), bf16), sds((r2, D), bf16),
        ],
        in_specs=[vm] * 6 + [hbm] * 3,
        out_specs=[vm] * 6 + [hbm, vm],
        scratch_shapes=[
            pltpu.VMEM((T, D), bf16), pltpu.VMEM((D, T), bf16), pltpu.VMEM((T, D), bf16),
            pltpu.VMEM((T, D), f32), pltpu.VMEM((T, D), f32), pltpu.VMEM((T, D), bf16),
            pltpu.VMEM((2, D, W), bf16), pltpu.VMEM((2, W, D), bf16),
            pltpu.VMEM((J, 2, r2, D), bf16), pltpu.VMEM((J, r2, D), bf16),
            pltpu.VMEM((A, B - 1, r2, D), bf16), pltpu.VMEM((A, B - 1, r2, D), bf16),
            pltpu.VMEM((A - 1, r2, D), bf16), pltpu.VMEM((A - 1, r2, D), bf16),
            pltpu.VMEM((2, J, 2, r1, W), bf16), pltpu.VMEM((J, J, r1, W), bf16), pltpu.VMEM((2, J, r1, W), bf16),
            pltpu.VMEM((J, J, r1, H) if s == 2 else (8, 128), bf16), pltpu.VMEM((2, J, r1, H), bf16), dma((J,)), dma((J,)),
            pltpu.VMEM((D, D), bf16), dma(()), dma((2, 2)), dma((2,)), dma((J,)), dma((J,)), dma((J,)), dma((J,)),
            dma((A, B - 1)), dma((A, B - 1)), dma((A - 1,)), dma((A - 1,)),
        ],
        compiler_params=pltpu.CompilerParams(
            collective_id=3, has_side_effects=True, vmem_limit_bytes=64 * 1024 * 1024 - 65536
        ),
        name="feed_forward",
    )(middle, branch, attn, g, vectors, b_fc1.reshape(J, 1, W), w4, w1, w2)


class RowSum:
    @staticmethod
    def scratch(U, r, W, A, B, cores):
        dma = pltpu.SemaphoreType.DMA
        shapes = [
            pltpu.VMEM((U, B - 1, A, r, W), bf16), pltpu.VMEM((U, A - 1, r, W), bf16),
            pltpu.VMEM((U, A - 1, r, W), bf16), pltpu.VMEM((U, r, W), bf16), pltpu.VMEM((U, r, W), bf16),
            dma((U, B - 1)), dma((U, B - 1)), dma((U, A - 1)), dma((U, A - 1)), dma((U,)), dma((U,)),
        ]
        if cores:
            shapes += [
                pltpu.VMEM((U, A * B, r, W), bf16), pltpu.VMEM((U, B - 1, A, r, W), bf16), dma((U,)), dma((U,)),
            ]
        return shapes

    def __init__(self, at, s, peer, refs, grad=None, half=None):
        self.at, self.s, self.peer = at, s, peer
        self.grad, self.half = grad, half
        self.yr, self.zs, self.zr, self.xs, self.xr = refs[:5]
        self.yss, self.yrs, self.zss, self.zrs, self.xss, self.xrs = refs[5:11]
        if grad is not None:
            self.cr, self.ys, self.css, self.crs = refs[11:]

    def c_copy(self, u):
        return remote(
            self.grad.at[u, :, 1 - self.at.c], self.cr.at[u], self.css.at[u], self.crs.at[u], self.at.sibling()
        )

    def y_source(self, u, m):
        return self.ys.at[u, m]

    def y_copy(self, u, m):
        src = self.y_source(u, m)
        return remote(src, self.yr.at[u, m], self.yss.at[u, m], self.yrs.at[u, m], self.at.at_b(m + 1))

    def z_copy(self, u, k):
        return remote(self.zs.at[u, k], self.zr.at[u, k], self.zss.at[u, k], self.zrs.at[u, k], self.at.at_a(k + 1))

    def x_copy(self, u):
        return remote(self.xs.at[u], self.xr.at[u], self.xss.at[u], self.xrs.at[u], self.peer)

    def chip(self, u, a, b):
        j = a * self.at.B + b
        return add32(self.grad[u, j, self.at.c], self.cr[u, j])

    def own(self, u, a):
        base = self.chip(u, a, self.at.b) if self.half is None else self.half(u, a)
        return add32(base, *[self.yr[u, m, a] for m in range(self.at.B - 1)])

    def send_y(self, u):
        self.c_copy(u).wait()
        for m in range(self.at.B - 1):
            b = lax.rem(self.at.b + m + 1, self.at.B)
            for a in range(self.at.A):
                self.ys[u, m, a] = self.chip(u, a, b).astype(bf16)
            self.y_copy(u, m).start()

    def send_z(self, u):
        for m in range(self.at.B - 1):
            self.y_copy(u, m).wait()
        for k in range(self.at.A - 1):
            self.zs[u, k] = self.own(u, lax.rem(self.at.a + k + 1, self.at.A)).astype(bf16)
            self.z_copy(u, k).start()

    def send_x(self, u):
        for k in range(self.at.A - 1):
            self.z_copy(u, k).wait()
        total = add32(self.own(u, self.at.a), *[self.zr[u, k] for k in range(self.at.A - 1)])
        if self.s != 2:
            return total
        self.xs[u] = total.astype(bf16)
        self.x_copy(u).start()
        return None

    def finish(self, u):
        self.x_copy(u).wait()
        return add32(self.xs[u], self.xr[u])


def attention_and_sums(
    qkv, kvr, d_attn, lse, hidden, tokens, vectors, d_middle, w_qkv, half_fc1, grad_proj, sum_fc2, sums, bias_fc1, lf, w_ada, n, s
):
    T, D = tokens.shape
    FH = half_fc1.shape[-1]
    FF = 2 * FH if s == 2 else FH
    A, B = grid_of(n)
    J, r1, r2 = A * B, D // n, FF // n
    GW, LAGZ = 256, 3
    U = D // GW
    F = FH // U
    E = 6 * D
    RB = min(T, 64)
    rows_a = D // n
    m_bias = [2 * D // n, D // n, FF // n, D // n]
    starts = [0, 2 * D, 3 * D, 3 * D + FF]
    NBIAS = 4 * D + FF
    blocks = [max(v, 128) for v in m_bias]
    offs = [sum(blocks[:i]) for i in range(4)]
    M = sum(blocks)
    nq = len(RowSum.scratch(U, r1, 3 * GW, A, B, True))
    nf = len(RowSum.scratch(U, r1, F, A, B, False))

    def kern(*refs):
        it = iter(refs)

        def take(count):
            return [next(it) for _ in range(count)]

        qkv_ref, kvr_ref = take(2)
        e_ref, lse_ref, h_ref, tok_ref, sc_ref, dmid_ref, w_ref, f1_ref, gp_ref, f2_ref, sum_ref, bf_ref, lf_ref, wa_ref = take(14)
        gt_ref, oq_ref, op_ref, o1_ref, o2_ref, gw_ref, gb_ref, dl_ref, bo_ref = take(9)
        h1t, dqg, kvl, kvs, kvr, dg, gq, wq, f1o, x2 = take(10)
        dh1 = gt_ref
        wsem, fsem, kss, krs, x2s, x2r = take(6)
        scr_q, scr_p, scr_f = take(nq), take(nq), take(nf)
        dx, dm, lp, bsum, bx, bsx = take(6)
        asend, arecv, lsend, lrecv, bsend, brecv, xsend, xrecv = take(8)

        at = Place(n)
        me, x = at.me, lax.axis_index("seq")
        peers = fsdp_peers(n, me)

        def seq_dev(k):
            return {"seq": lax.rem(x + k, s)}

        greet([{"fsdp": p} for p in peers] + [seq_dev(k) for k in range(1, s)])
        other = seq_dev(1)
        sq = RowSum(at, s, other, scr_q, grad=gq)
        sp = RowSum(at, s, other, scr_p, grad=gp_ref)
        sf = RowSum(at, s, other, scr_f, half=lambda u, a: f1o[u, a])

        def f_source(u, m):
            b = lax.rem(at.b + m + 1, B)
            return f1_ref.at[:, b, :, pl.ds(pl.multiple_of(u * F, F), F)]

        sf.y_source = f_source
        own_f = [
            pltpu.make_async_copy(f1_ref.at[:, at.b, :, pl.ds(u * F, F)], f1o.at[u], fsem.at[u]) for u in range(U)
        ]
        spans = [pl.ds(2 * D, 4 * D), pl.ds(0, 2 * D)]

        def mod_x(i):
            sl = dx.at[x, :, spans[i]]
            return [remote(sl, sl, xsend.at[i, k - 1], xrecv.at[i, k - 1], seq_dev(k)) for k in range(1, s)]

        def mod_all(i):
            dm[me, :, spans[i]] = jnp.sum(dx[:, :, spans[i]], axis=0).astype(bf16).astype(f32)
            sl = dm.at[me, :, spans[i]]
            out = [remote(sl, sl, asend.at[i, k], arecv.at[i, k], {"fsdp": p}) for k, p in enumerate(peers)]
            for c in out:
                c.start()
            return out

        def bias_span(p, i):
            lo = starts[i] + ((p * m_bias[i]) // blocks[i]) * blocks[i]
            return pl.ds(pl.multiple_of(lo, 128), blocks[i])

        def bias_out(lo, hi):
            out = []
            for i in range(lo, hi):
                at_i = pl.ds(offs[i], blocks[i])
                bx[me, :, at_i] = bsum[:, bias_span(me, i)]
                for k, p in enumerate(peers):
                    dst = bx.at[me, :, at_i]
                    out.append(remote(bsum.at[:, bias_span(p, i)], dst, bsend.at[i, k], brecv.at[i, k], {"fsdp": p}))
            for c in out:
                c.start()
            return out

        for i, row in enumerate((3, 0, 1, 2)):
            dx[x, :, (i + 2) * D : (i + 3) * D] = sum_ref[row : row + 1, :]
        early_x = mod_x(0)
        for c in early_x:
            c.start()
        bsum[:, starts[1] : starts[1] + D] = sum_ref[5:6, :]
        bsum[:, starts[2] : starts[2] + FF] = bf_ref[...]
        bsum[:, starts[3] : starts[3] + D] = sum_ref[4:5, :]
        sp.c_copy(0).start()
        for u in range(U):
            for m in range(B - 1):
                sf.y_copy(u, m).start()
        early_bias = bias_out(1, 4)
        if s == 2:
            x2_copy = remote(f2_ref, x2, x2s, x2r, other)
            x2_copy.start()
        for o in own_f:
            o.start()

        def h_copy(i):
            k = i % 3
            return pltpu.make_async_copy(
                h_ref.at[:, pl.ds(i * GW, GW)], dg.at[:, pl.ds(k * GW, GW)], wsem.at[k]
            )

        for i in range(min(U, 3)):
            h_copy(i).start()
        for i in range(U):
            h_copy(i).wait()
            k = i % 3
            h1t[i * GW : (i + 1) * GW, :] = dg[:, k * GW : (k + 1) * GW].T
            if i + 3 < U:
                h_copy(i + 3).start()
        dh1[...] = jnp.zeros_like(dh1)
        for o in own_f:
            o.wait()
        for c in early_x:
            c.wait()
        early_all = mod_all(0)

        def w_copy(u, i):
            lo = pl.multiple_of(i * D + u * GW, GW)
            return pltpu.make_async_copy(w_ref.at[:, pl.ds(lo, GW)], wq.at[:, pl.ds(i * GW, GW)], wsem.at[i])

        def kv_copy(u, k):
            return remote(kvs.at[u, k - 1], kvr.at[u, k - 1], kss.at[u, k - 1], krs.at[u, k - 1], seq_dev(s - k))

        def attend(u):
            slot = lax.rem(u, 2)
            for o in range(GW // 128):
                pair = u * (GW // 128) + o
                cols, k_cols, v_cols = [pl.ds(pl.multiple_of(lo + pair * 128, 128), 128) for lo in (0, D, 2 * D)]
                here = slice(o * 128, o * 128 + 128)
                qv, e = qkv_ref[:, cols] * bf16(HD**-0.5), e_ref[:, cols]
                ks = [qkv_ref[:, k_cols]] + [kvr_ref[k, :, cols] for k in range(s - 1)]
                vs = [qkv_ref[:, v_cols]] + [kvr_ref[k, :, k_cols] for k in range(s - 1)]
                dqt, dks, dvs = None, [None] * s, [None] * s
                for h in range(2):
                    qh, eh = pick(qv, h), pick(e, h)
                    total = lse_ref[pair, h : h + 1, :]
                    probs, dprobs, cross = [], [], None
                    for j in range(s):
                        p = jnp.exp(nt(ks[j], qh) - total)
                        dp = nt(vs[j], eh)
                        part = (p * dp).sum(axis=0, keepdims=True)
                        cross = part if cross is None else cross + part
                        dv = nn(p.astype(bf16), eh)
                        dvs[j] = dv if dvs[j] is None else dvs[j] + dv
                        probs.append(p)
                        dprobs.append(dp)
                    for j in range(s):
                        ds = (probs[j] * (dprobs[j] - cross)).astype(bf16)
                        dk = nn(ds, qh)
                        dks[j] = dk if dks[j] is None else dks[j] + dk
                        t = tn(pick(ks[j], h), ds)
                        dqt = t if dqt is None else dqt + t
                dqg[slot, :, here] = (dqt * (HD**-0.5)).T.astype(bf16)
                kvl[slot, 0, :, here] = dks[0]
                kvl[slot, 1, :, here] = dvs[0]
                for j in range(1, s):
                    kvs[u, j - 1, 0, :, here] = dks[j].astype(bf16)
                    kvs[u, j - 1, 1, :, here] = dvs[j].astype(bf16)
            for k in range(1, s):
                kv_copy(u, k).start()

        def project(u):
            slot = lax.rem(u, 2)
            for k in range(1, s):
                kv_copy(u, k).wait()
            dg[:, :GW] = dqg[slot]
            for i in range(2):
                lo = (i + 1) * GW
                dg[:, lo : lo + GW] = add32(kvl[slot, i], *[kvr[u, k, i] for k in range(s - 1)]).astype(bf16)
            part = 256 // (2 * r1)
            for i in range(D // 256):
                g = nn(h1t[i * 256 : (i + 1) * 256, :], dg[...]).astype(bf16)
                gq[u, i * part : (i + 1) * part] = g.reshape(part, 2, r1, 3 * GW)
            sq.c_copy(u).start()
            here = pl.ds(pl.multiple_of(u * GW, GW), GW)
            bsum[:, here] = jnp.sum(dg[:, :GW].astype(f32), axis=0, keepdims=True)
            there = pl.ds(pl.multiple_of(D + u * GW, GW), GW)
            bsum[:, there] = jnp.sum(dg[:, 2 * GW :].astype(f32), axis=0, keepdims=True)
            for i in range(3):
                w_copy(u, i).wait()
            dh1[...] += nt(dg[...], wq[...])

        def step(i, _):
            @pl.when(i < U)
            def _():
                attend(i)

            @pl.when(jnp.logical_and(i >= 1, i <= U))
            def _():
                project(i - 1)

            @pl.when(i < U)
            def _():
                for k in range(3):
                    w_copy(i, k).start()

            @pl.when(i == 0)
            def _():
                sp.send_y(0)

            @pl.when(i < U)
            def _():
                sf.send_z(i)

            @pl.when(i >= 2)
            def _():
                sq.send_y(i - 2)

            @pl.when(i == LAGZ - 1)
            def _():
                sp.send_z(0)

            @pl.when(i >= LAGZ)
            def _():
                sq.send_z(i - LAGZ)

            return 0

        lax.fori_loop(0, U + 2, step, 0)

        sums = [jnp.zeros((1, D), f32), jnp.zeros((1, D), f32)]
        scale1 = sc_ref[5:6, :]

        def back(i, carry):
            rows = pl.ds(pl.multiple_of(i * RB, RB), RB)
            normed, rscale = normalize(tok_ref[rows, :].astype(f32))
            dh = dh1[rows, :]
            up = dh * (1.0 + scale1)
            gt_ref[rows, :] = dmid_ref[rows, :] + rscale * (
                up
                - jnp.mean(up, axis=-1, keepdims=True)
                - normed * jnp.mean(up * normed, axis=-1, keepdims=True)
            )
            return (
                carry[0] + jnp.sum(dh, axis=0, keepdims=True),
                carry[1] + jnp.sum(dh * normed, axis=0, keepdims=True),
            )

        shift1_sum, scale1_sum = lax.fori_loop(0, T // RB, back, tuple(sums))
        dx[x, :, :D] = shift1_sum
        dx[x, :, D : 2 * D] = scale1_sum
        late_x = mod_x(1)
        for c in late_x:
            c.start()
        late_bias = bias_out(0, 1)
        for c in late_x:
            c.wait()
        late_all = mod_all(1)

        for u in range(U + 2 - LAGZ, U):
            sq.send_z(u)
        for u in range(U):
            if s == 2:
                sf.send_x(u)
            else:
                o1_ref[:, u * F : (u + 1) * F] = sf.send_x(u)
        for c in early_bias + late_bias:
            c.wait()
        bsx[x] = jnp.sum(bx[...], axis=0)
        bias_x = [remote(bsx.at[x], bsx.at[x], xsend.at[2, k - 1], xrecv.at[2, k - 1], seq_dev(k)) for k in range(1, s)]
        for c in bias_x:
            c.start()
        if s == 2:
            sp.send_x(0)
        else:
            op_ref[...] = sp.send_x(0)
        for c in early_all + late_all:
            c.wait()
        dmod = dm[...].reshape(n, E).astype(bf16)
        lp[...] = nt(dmod, wa_ref[...]).reshape(n, 1, rows_a)
        dl_ref[me] = lp[me]
        lift = [remote(lp.at[p], dl_ref.at[me], lsend.at[k], lrecv.at[k], {"fsdp": p}) for k, p in enumerate(peers)]
        for c in lift:
            c.start()
        gw_ref[...] = tn(lf_ref[...].reshape(n, rows_a).astype(bf16), dmod)
        gb_ref[...] = jnp.sum(dm[...], axis=0)

        def put_q(u, value):
            for i in range(3):
                oq_ref[:, i * D + u * GW : i * D + (u + 1) * GW] = value[:, i * GW : (i + 1) * GW]

        for u in range(U):
            value = sq.send_x(u)
            if s != 2:
                put_q(u, value)
        if s == 2:
            x2_copy.wait()
            o2_ref[...] = add32(f2_ref[...], x2[...])
            for u in range(U):
                sf.x_copy(u).wait()
                for q in range(F // r2):
                    lo = 2 * (u * F + q * r2)
                    for k, got in ((x, sf.xs), (1 - x, sf.xr)):
                        cols = pl.ds(pl.multiple_of(lo + k * r2, 128), r2)
                        o1_ref[:, cols] = got[u, :, q * r2 : (q + 1) * r2].astype(f32)
            op_ref[...] = sp.finish(0)
            for u in range(U):
                put_q(u, sq.finish(u))
        else:
            o2_ref[...] = f2_ref[...].astype(f32)
        for c in bias_x:
            c.wait()
        bo_ref[...] = jnp.sum(bsx[...], axis=0)
        for c in lift:
            c.wait()

    vm, hbm = pl.BlockSpec(memory_space=pltpu.VMEM), pl.BlockSpec(memory_space=pl.ANY)
    sds, dma = jax.ShapeDtypeStruct, pltpu.SemaphoreType.DMA
    res = pl.pallas_call(
        kern,
        out_shape=[
            sds((T, D), f32), sds((r1, 3 * D), f32), sds((r1, D), f32), sds((r1, FF), f32), sds((r2, D), f32),
            sds((rows_a, E), f32), sds((1, E), f32), sds((n, 1, rows_a), f32), sds((1, M), f32),
        ],
        in_specs=[vm] * 4 + [hbm] + [vm] * 3 + [hbm, hbm] + [vm] * 6,
        out_specs=[vm] * 9,
        scratch_shapes=[
            pltpu.VMEM((D, T), bf16), pltpu.VMEM((2, T, GW), bf16),
            pltpu.VMEM((2, 2, T, GW), f32), pltpu.VMEM((U, s - 1, 2, T, GW), bf16),
            pltpu.VMEM((U, s - 1, 2, T, GW), bf16), pltpu.VMEM((T, 3 * GW), bf16),
            pltpu.VMEM((U, J, 2, r1, 3 * GW), bf16), pltpu.VMEM((D, 3 * GW), bf16),
            pltpu.VMEM((U, A, r1, F), bf16), pltpu.VMEM((r2, D), bf16),
            dma((3,)), dma((U,)), dma((U, s - 1)), dma((U, s - 1)), dma(()), dma(()),
        ]
        + RowSum.scratch(U, r1, 3 * GW, A, B, True)
        + RowSum.scratch(1, r1, D, A, B, True)
        + RowSum.scratch(U, r1, F, A, B, False)
        + [
            pltpu.VMEM((s, 1, E), f32), pltpu.VMEM((n, 1, E), f32), pltpu.VMEM((n, 1, rows_a), f32),
            pltpu.VMEM((1, NBIAS), f32), pltpu.VMEM((n, 1, M), f32), pltpu.VMEM((s, 1, M), f32),
            dma((2, n - 1)), dma((2, n - 1)), dma((n - 1,)), dma((n - 1,)),
            dma((4, n - 1)), dma((4, n - 1)), dma((3, s - 1)), dma((3, s - 1)),
        ],
        compiler_params=pltpu.CompilerParams(
            collective_id=4, has_side_effects=True, vmem_limit_bytes=64 * 1024 * 1024 - 65536
        ),
        name="attention_and_sums",
    )(
        qkv, kvr, d_attn, lse, hidden, tokens, vectors, d_middle, w_qkv, half_fc1.reshape(A, B, r1, FH),
        grad_proj.reshape(1, J, 2, r1, D), sum_fc2, sums, bias_fc1, lf, w_ada,
    )
    grad_tokens, t_qkv, t_proj, t_fc1, t_fc2, t_ada, ada_sums, d_lifted, bias = res
    if s != 2:
        t_qkv, t_proj, t_fc1, t_fc2 = lax.psum((t_qkv, t_proj, t_fc1, t_fc2), "seq")
    me = lax.axis_index("fsdp")
    biases = []
    for width, wide, off in zip(m_bias, blocks, offs):
        biases.append(lax.dynamic_slice_in_dim(bias[0, off : off + wide], (me * width) % wide, width))
    return grad_tokens, t_qkv, t_proj, t_fc1, t_fc2, t_ada, ada_sums, d_lifted, biases


def on_device(
    tokens,
    condition,
    w_ada,
    b_ada,
    w_qkv,
    b_qv,
    w_proj,
    b_proj,
    w_fc1,
    b_fc1,
    w_fc2,
    b_fc2,
    cotangent,
):
    n, s = lax.axis_size("fsdp"), lax.axis_size("seq")
    width = tokens.shape[-1]

    lifted, silu_back = jax.vjp(jax.nn.silu, condition.astype(f32))
    lifted_q = lifted.astype(bf16).astype(f32).reshape(n, 1, width // n)
    qkv, kvr, hidden_one, attn, lse, branch, middle, vectors, fc1_b, lf, w4, fc1_w, fc2_w = forward_attention(
        lifted_q, w_ada, [b_qv, b_proj, b_fc1, b_fc2, b_ada], tokens[0], w_qkv, w_proj, w_fc1, w_fc2, n, s
    )
    result, d_middle, d_attn, sums, bias_fc1, grad_proj, half_fc1, sum_fc2 = feed_forward(
        middle, branch, attn, cotangent[0], vectors, fc1_b, w4, fc1_w, fc2_w, n, s
    )
    grad_input, total_qkv, total_proj, total_fc1, total_fc2, total_ada, sums_ada, d_lifted, total_bias = (
        attention_and_sums(
            qkv, kvr, d_attn, lse, hidden_one, tokens[0], vectors, d_middle, w4, half_fc1,
            grad_proj, sum_fc2, sums, bias_fc1.reshape(1, -1), lf, w_ada, n, s,
        )
    )
    share = b_ada.shape[0]
    total_bada = lax.dynamic_slice_in_dim(sums_ada[0], lax.axis_index("fsdp") * share, share)
    grad_condition = silu_back(d_lifted.reshape(1, width))[0]
    total_bqv, total_bproj, total_bfc1, total_bfc2 = total_bias
    return (
        result[None],
        grad_input[None],
        grad_condition,
        total_ada,
        total_bada,
        total_qkv,
        total_bqv,
        total_proj,
        total_bproj,
        total_fc1,
        total_bfc1,
        total_fc2,
        total_bfc2,
    )


def solution(mesh):
    weights = (P("fsdp", None), P("fsdp")) * 5
    return jax.shard_map(
        on_device,
        mesh=mesh,
        in_specs=(P("fsdp", "seq", None), P("fsdp", None)) + weights + (P("fsdp", "seq", None),),
        out_specs=(P("fsdp", "seq", None), P("fsdp", "seq", None), P("fsdp", None)) + weights,
        check_vma=False,
    )
```

```python
from functools import partial

import jax
import jax.numpy as jnp
from jax import lax
from jax.experimental import pallas as pl
from jax.experimental.pallas import tpu as pltpu
from jax.sharding import PartitionSpec as P

HD = 64
norm_eps = 1e-06
f32 = jnp.float32
bf16 = jnp.bfloat16
MESH = pl.DeviceIdType.MESH


def grid_of(n):
    b = 2 if n == 16 else 4
    return n // (2 * b), b


def nt(a, b):
    return lax.dot_general(a, b, (((1,), (1,)), ((), ())), preferred_element_type=f32)


def nn(a, b):
    return lax.dot_general(a, b, (((1,), (0,)), ((), ())), preferred_element_type=f32)


def tn(a, b):
    return lax.dot_general(a, b, (((0,), (0,)), ((), ())), preferred_element_type=f32)


def fsdp_peers(n, me):
    return [lax.rem(me + k, n) for k in range(1, n)]


def head_mask(ref_shape, h):
    low = lax.broadcasted_iota(jnp.int32, ref_shape, 1) < HD
    return low if h == 0 else ~low


def pick(values, h):
    return jnp.where(head_mask(values.shape, h), values, jnp.zeros_like(values))


def remote(src, dst, send, recv, device):
    return pltpu.make_async_remote_copy(
        src_ref=src, dst_ref=dst, send_sem=send, recv_sem=recv, device_id=device, device_id_type=MESH
    )


def greet(devices):
    bar = pltpu.get_barrier_semaphore()
    for d in devices:
        pl.semaphore_signal(bar, inc=1, device_id=d, device_id_type=MESH)
    pl.semaphore_wait(bar, len(devices))


class Place:
    def __init__(self, n):
        self.A, self.B = grid_of(n)
        me = lax.axis_index("fsdp")
        self.me = me
        self.a, self.b, self.c = me // (2 * self.B), lax.rem(me // 2, self.B), lax.rem(me, 2)

    def dev(self, a, b, c):
        return {"fsdp": (a * self.B + b) * 2 + c}

    def at_a(self, k):
        return self.dev(lax.rem(self.a + k, self.A), self.b, self.c)

    def at_b(self, k):
        return self.dev(self.a, lax.rem(self.b + k, self.B), self.c)

    def sibling(self):
        return self.dev(self.a, self.b, 1 - self.c)

    def all(self):
        return [self.at_a(k) for k in range(1, self.A)] + [self.at_b(k) for k in range(1, self.B)] + [self.sibling()]


def add32(*values):
    total = values[0].astype(f32)
    for v in values[1:]:
        total = total + v.astype(f32)
    return total


def gelu_both(x):
    k = 0.7978845608028654
    sq = x * x
    th = jnp.tanh(k * (x + 0.044715 * (sq * x)))
    half = 0.5 * (1.0 + th)
    slope = half + (0.5 * k) * x * (1.0 - th * th) * (1.0 + (3 * 0.044715) * sq)
    return x * half, slope


def normalize(v):
    center = v - jnp.mean(v, axis=-1, keepdims=True)
    rscale = lax.rsqrt(jnp.mean(center * center, axis=-1, keepdims=True) + norm_eps)
    return center * rscale, rscale


def bias_block(width, n):
    return max(-(-((p * width) % 128 + width) // 128) * 128 for p in range(n))


def placed_bias(bias, n):
    width, wide = bias.shape[0], bias_block(bias.shape[0], n)
    bias = bias.astype(f32)[None]
    if wide == width:
        return bias
    at = (lax.axis_index("fsdp") * width) % 128
    if wide == 128:
        mine = lax.broadcasted_iota(jnp.int32, (1, wide), 1) // width == at // width
        return jnp.where(mine, jnp.concatenate([bias] * (wide // width), axis=1), 0.0)
    return lax.dynamic_update_slice(jnp.zeros((1, wide), f32), bias, (0, at))


def forward_attention(lifted, w_ada, biases, tokens, w_qkv, w_proj, w_fc1, w_fc2, n, s):
    T, D = tokens.shape
    E = w_ada.shape[1]
    FF = w_fc1.shape[1]
    A, B = grid_of(n)
    rows_a = w_ada.shape[0]
    r1, r2 = w_qkv.shape[0], w_fc2.shape[0]
    widths = [v.shape[0] for v in biases]
    blocks = [bias_block(w, n) for w in widths]
    offs = [sum(blocks[:i]) for i in range(5)]
    bases = [n * sum(widths[:i]) for i in range(5)]
    packed = jnp.concatenate([placed_bias(v, n) for v in biases], axis=1)
    M = packed.shape[1]
    share = s == 2
    NT, NL = 8, 16
    CQ, CF, RF = 4 * D // NT, FF // NL, r2 // NL
    RB = min(T, 64)
    AHEAD, MODULATE, LAG, ATTEND = 2, 4, 6, NT + 7
    NA, NY = A - 1, B - 1
    NQ = NA + NY + 1
    NF = 3 * (NA + NY) + 2
    pairs = D // 128

    def kern(
        l_ref, wa_ref, bias_ref, tok_ref, wqkv_ref, wproj_ref, wfc1_ref, wfc2_ref,
        qkv_ref, kvr_ref, h_ref, attn_ref, lse_ref, br_ref, mid_ref, vec_ref, bfc1_ref, lf_ref, w4_ref, f1_ref, f2_ref,
        normed, wq, part, acc, bout, bvec, mod, msend, mrecv, qsend, qrecv, fsend, frecv, ksend, krecv, osem,
    ):
        at = Place(n)
        a, b, c, me, x = at.a, at.b, at.c, at.me, lax.axis_index("seq")
        peers = fsdp_peers(n, me)
        other = {"seq": lax.rem(x + 1, s)}
        greet([{"fsdp": p} for p in peers] + [{"seq": lax.rem(x + k, s)} for k in range(1, s)])

        def small(i, src, dst):
            return [
                remote(src(p), dst(k), msend.at[i, k], mrecv.at[i, k], {"fsdp": p}) for k, p in enumerate(peers)
            ]

        m_lift = small(0, lambda p: l_ref.at[p], lambda k: lf_ref.at[me])
        m_bias = small(1, lambda p: bias_ref, lambda k: bout.at[me])
        m_part = small(2, lambda p: part.at[p], lambda k: acc.at[k + 1])
        for r in m_lift + m_bias:
            r.start()
        owns = [
            pltpu.make_async_copy(wqkv_ref, wq.at[a, b, c, :, pl.ds(0, 3 * D)], osem.at[0]),
            pltpu.make_async_copy(wproj_ref, wq.at[a, b, c, :, pl.ds(3 * D, D)], osem.at[1]),
            pltpu.make_async_copy(wfc1_ref, f1_ref.at[a, b, c], osem.at[2]),
            pltpu.make_async_copy(wfc2_ref, f2_ref.at[a, b, c], osem.at[3]),
        ]
        for o in owns:
            o.start()

        def block(i):
            return jnp.where(i < 6, lax.rem(i + 2, 6), i)

        def span(lo, size, step):
            return pl.ds(pl.multiple_of(lo, step), size)

        class Ticks:
            def __init__(self, pieces, whole, send, recv):
                self.pieces, self.whole, self.send, self.recv = pieces, whole, send, recv

            def copy(self, j, i, src, dst, device):
                return remote(src, dst, self.send.at[j, i], self.recv.at[j, i], device)

            def z(self, j):
                return [
                    self.copy(j, i * NA + k, src.at[rows, cols], buf.at[a, b, c, rows, cols], at.at_a(k + 1))
                    for i, (src, buf, rows, cols, _) in enumerate(self.pieces(j))
                    for k in range(NA)
                ]

            def y(self, j):
                out, ps = [], self.pieces(j)
                for i, (_, buf, rows, cols, _) in enumerate(ps):
                    sl = buf.at[:, b, c, rows, cols]
                    out += [self.copy(j, len(ps) * NA + i * NY + k, sl, sl, at.at_b(k + 1)) for k in range(NY)]
                return out

            def x(self, j):
                out, ps = [], self.pieces(j)
                i = len(ps) * (NA + NY)
                for _, buf, rows, cols, shared in ps:
                    if not shared:
                        continue
                    for k in range(NA):
                        sl = buf.at[lax.rem(a + k + 1, A), :, c, rows, cols]
                        out.append(self.copy(j, i, sl, sl, other))
                        i += 1
                    for k in range(NY):
                        sl = buf.at[a, lax.rem(b + k + 1, B), c, rows, cols]
                        out.append(self.copy(j, i, sl, sl, other))
                        i += 1
                return out

            def c(self, j):
                ps = self.whole(j)
                i = self.send.shape[1] - len(ps)
                return [
                    self.copy(j, i + k, buf.at[:, :, c, rows, cols], buf.at[:, :, c, rows, cols], at.sibling())
                    for k, (buf, rows, cols) in enumerate(ps)
                ]

            def start_z(self, j):
                for r in self.z(j):
                    r.start()

            def start_y(self, j):
                for r in self.z(j):
                    r.wait_recv()
                for r in self.y(j):
                    r.start()

            def start_x(self, j):
                for r in self.y(j):
                    r.wait_recv()
                for r in self.x(j):
                    r.start()

            def start_c(self, j):
                for r in self.x(j):
                    r.wait_recv()
                for r in self.c(j):
                    r.start()

            def relay(self, j):
                self.start_x(j)
                self.start_c(j)

            def finish(self, j):
                for r in self.z(j) + self.y(j) + self.x(j):
                    r.wait_send()
                for r in self.c(j):
                    r.wait()

        all_r1 = pl.ds(0, r1)
        mine = wq.at[a, b, c]

        def q_pieces(i):
            return [(mine, wq, all_r1, span(block(i) * CQ, CQ, CQ), False)]

        def q_whole(i):
            return [(wq, all_r1, span(block(i) * CQ, CQ, CQ))]

        def f_pieces(j):
            w = D // 2 if share else D
            part = span(x * w, w, w) if share else pl.ds(0, D)
            return [
                (wfc1_ref, f1_ref, all_r1, span(j * CF, CF, CF), False),
                (wfc2_ref, f2_ref, span(j * RF, RF, RF), part, share),
            ]

        def f_whole(j):
            return [(f1_ref, all_r1, span(j * CF, CF, CF)), (f2_ref, span(j * RF, RF, RF), pl.ds(0, D))]

        tq, tf = Ticks(q_pieces, q_whole, qsend, qrecv), Ticks(f_pieces, f_whole, fsend, frecv)

        owns[0].wait()
        owns[1].wait()
        for i in range(AHEAD):
            tq.start_z(i)
        lf_ref[me] = l_ref[me]
        bout[me] = bias_ref[...]
        bvec[...] = jnp.zeros_like(bvec)

        def norm(i, _):
            rows = pl.ds(pl.multiple_of(i * RB, RB), RB)
            normed[rows, :] = normalize(tok_ref[rows, :].astype(f32))[0]
            return 0

        for r in m_lift:
            r.wait_recv()
        part[...] = nn(lf_ref[...].reshape(n, rows_a).astype(bf16), wa_ref[...]).reshape(n, 1, E)
        acc[0] = part[me]
        for r in m_part:
            r.start()

        def modulation():
            for r in m_bias + m_part:
                r.wait_recv()
            for i in range(5):
                for p in range(n):
                    lo = bases[i] + p * widths[i] // 128 * 128
                    value = bout[p, :, offs[i] : offs[i] + blocks[i]]
                    if widths[i] % 128 == 0:
                        bvec[:, lo : lo + blocks[i]] = value
                    else:
                        bvec[:, lo : lo + blocks[i]] += value
            mod[...] = jnp.sum(acc[...], axis=0) + bvec[:, bases[4] :]
            shift1, scale1, gate1, shift2, scale2, gate2 = [mod[:, i * D : (i + 1) * D] for i in range(6)]
            vec_ref[...] = jnp.zeros_like(vec_ref)
            for i, v in enumerate((shift2, scale2, gate2, gate1, bvec[:, bases[3] : bases[3] + D], scale1)):
                vec_ref[i : i + 1, :] = v
            bfc1_ref[...] = bvec[:, bases[2] : bases[2] + FF]

            def modulate(i, _):
                rows = pl.ds(pl.multiple_of(i * RB, RB), RB)
                h_ref[rows, :] = (normed[rows, :] * (1.0 + scale1) + shift1).astype(bf16)
                return 0

            lax.fori_loop(0, T // RB, modulate, 0)


        def kv_copy(m, k):
            return remote(
                qkv_ref.at[:, span(D + m * CQ, CQ, CQ)],
                kvr_ref.at[k - 1, :, span(m * CQ, CQ, CQ)],
                ksend.at[m, k - 1],
                krecv.at[m, k - 1],
                {"seq": lax.rem(x + k, s)},
            )

        def project(m):
            tq.finish(m)

            @pl.when(m < 6)
            def _():
                lo = block(m) * CQ
                cols = span(lo, CQ, CQ)
                from_v = (block(m) >= 4).astype(jnp.int32)
                bias = bvec[:, span(lo - from_v * D, CQ, CQ)]
                is_key = jnp.logical_and(block(m) >= 2, block(m) < 4)
                bias = jnp.where(is_key, jnp.zeros_like(bias), bias)
                out = nn(h_ref[...], wq[:, :, :, :, cols].reshape(D, CQ))
                qkv_ref[:, cols] = (out + bias).astype(bf16)

            @pl.when(m < 4)
            def _():
                for k in range(1, s):
                    kv_copy(m, k).start()

        def attend(pair):
            def cols(lo):
                return span(lo + pair * 128, 128, 128)

            q = qkv_ref[:, cols(0)] * bf16(HD**-0.5)
            ks = [qkv_ref[:, cols(D)]] + [kvr_ref[k, :, cols(0)] for k in range(s - 1)]
            vs = [qkv_ref[:, cols(2 * D)]] + [kvr_ref[k, :, cols(D)] for k in range(s - 1)]
            total = None
            for h in range(2):
                qh = pick(q, h)
                scores = [nt(k, qh) for k in ks]
                top = scores[0].max(axis=0, keepdims=True)
                for sc in scores[1:]:
                    top = jnp.maximum(top, sc.max(axis=0, keepdims=True))
                mass, out = None, None
                for sc, v in zip(scores, vs):
                    p = jnp.exp(sc - top)
                    got = p.sum(axis=0, keepdims=True)
                    mass = got if mass is None else mass + got
                    o = tn(pick(v, h), p.astype(bf16))
                    out = o if out is None else out + o
                out = out * (1.0 / mass)
                total = out if total is None else total + out
                lse_ref[pair, h : h + 1, :] = top + jnp.log(mass)
            attn_ref[:, cols(0)] = total.T.astype(bf16)

        def branch(i, _):
            cols = span(i * 256, 256, 256)
            weight = wq[:, :, :, :, span(3 * D + i * 256, 256, 256)].reshape(D, 256)
            got = nn(attn_ref[...], weight) + bvec[:, span(bases[1] + i * 256, 256, 256)]
            br_ref[:, cols] = got
            mid_ref[:, cols] = tok_ref[:, cols].astype(f32) + mod[:, span(2 * D + i * 256, 256, 256)] * got
            return 0

        out4 = pltpu.make_async_copy(wq, w4_ref, osem.at[0])

        def step(i, _):
            def when(lo, hi, f, shift):
                @pl.when(jnp.logical_and(i >= lo, i < hi))
                def _():
                    f(i - shift)

            when(0, NT - AHEAD, lambda j: tq.start_z(j + AHEAD), 0)
            when(NT - AHEAD, NT + NL - AHEAD, tf.start_z, NT - AHEAD)
            when(0, NT, tq.start_y, 0)
            when(NT, NT + NL, tf.start_y, NT)
            when(1, NT + 1, tq.relay, 1)
            when(NT + 1, NT + NL + 1, tf.start_x, NT + 1)
            when(NT + LAG, NT + NL + LAG, tf.start_c, NT + LAG)
            when(NT + LAG + 1, NT + NL + LAG + 1, tf.finish, NT + LAG + 1)

            @pl.when(i == 0)
            def _():
                lax.fori_loop(0, T // RB, norm, 0)

            pl.when(i == MODULATE)(modulation)
            when(MODULATE, MODULATE + NT, project, MODULATE)

            @pl.when(i == MODULATE + NT)
            def _():
                out4.start()

            @pl.when(i == ATTEND)
            def _():
                for m in range(4):
                    for k in range(1, s):
                        kv_copy(m, k).wait()

            when(ATTEND, ATTEND + pairs, attend, ATTEND)

            @pl.when(i == ATTEND + pairs)
            def _():
                lax.fori_loop(0, D // 256, branch, 0)

            return 0

        owns[2].wait()
        owns[3].wait()
        lax.fori_loop(0, NT + NL + LAG + 1, step, 0)
        out4.wait()
        for r in m_lift + m_bias + m_part:
            r.wait_send()

    vm, hbm = pl.BlockSpec(memory_space=pltpu.VMEM), pl.BlockSpec(memory_space=pl.ANY)
    sds, dma = jax.ShapeDtypeStruct, pltpu.SemaphoreType.DMA
    res = pl.pallas_call(
        kern,
        out_shape=[
            sds((T, 3 * D), bf16), sds((s - 1, T, 2 * D), bf16), sds((T, D), bf16), sds((T, D), bf16),
            sds((pairs, 2, T), f32), sds((T, D), f32), sds((T, D), f32), sds((8, D), f32), sds((1, FF), f32),
            sds((n, 1, rows_a), f32), sds((A, B, 2, r1, 4 * D), bf16), sds((A, B, 2, r1, FF), bf16),
            sds((A, B, 2, r2, D), bf16),
        ],
        in_specs=[vm] * 8,
        out_specs=[vm] * 10 + [hbm] * 3,
        scratch_shapes=[
            pltpu.VMEM((T, D), f32), pltpu.VMEM((A, B, 2, r1, 4 * D), bf16), pltpu.VMEM((n, 1, E), f32),
            pltpu.VMEM((n, 1, E), f32), pltpu.VMEM((n, 1, M), f32), pltpu.VMEM((1, n * sum(widths)), f32),
            pltpu.VMEM((1, E), f32), dma((3, n - 1)), dma((3, n - 1)), dma((NT, NQ)), dma((NT, NQ)),
            dma((NL, NF)), dma((NL, NF)), dma((4, s - 1)), dma((4, s - 1)), dma((4,)),
        ],
        compiler_params=pltpu.CompilerParams(
            collective_id=0, has_side_effects=True, vmem_limit_bytes=64 * 1024 * 1024 - 65536
        ),
        name="forward_attention",
    )(lifted, w_ada, packed, tokens, w_qkv, w_proj, w_fc1, w_fc2)
    qkv, kvr, hidden, attn, lse, branch, middle, vectors, b_fc1, lf, w4, f1, f2 = res
    return (
        qkv, kvr, hidden, attn, lse, branch, middle, vectors, b_fc1, lf,
        w4.reshape(D, 4 * D), f1.reshape(D, FF), f2.reshape(FF, D),
    )


def feed_forward(middle, branch, attn, g, vectors, b_fc1, w4, w1, w2, n, s):
    T, D = middle.shape
    FF = w1.shape[1]
    A, B = grid_of(n)
    J, r1, r2 = A * B, D // n, FF // n
    W = 2 * r2
    RB = min(T, 64)
    H = W // 2 if s == 2 else W

    def kern(
        mid_ref, br_ref, attn_ref, g_ref, vec_ref, b1_ref, w4_ref, w1_ref, w2_ref,
        out_ref, dmid_ref, dattn_ref, sums_ref, bfc1_ref, gproj_ref, g1_ref, g2_ref,
        h2, h2t, dm, dh2, mlp, dbr, w1b, w2b, gb, cr, ys, yr, zs, zr, t1, c1, s1, keep, x1, o1, x1s, x1r,
        pw, psem, wsem, osem, cs, crs, c1s, c1r, yss, yrs, zss, zrs,
    ):
        at = Place(n)
        x = lax.axis_index("seq")
        other = {"seq": lax.rem(x + 1, s)}
        greet(at.all() + ([other] if s == 2 else []))
        shift2, scale2, gate2, gate1, bias2 = [vec_ref[i : i + 1, :] for i in range(5)]

        def tile(t):
            k, m = t // B, lax.rem(t, B)
            return lax.rem(at.a + 1 + k, A) * B + lax.rem(at.b + 1 + m, B)

        def weights(t, slot):
            lo = pl.multiple_of(tile(t) * W, W)
            return (
                pltpu.make_async_copy(w1_ref.at[:, pl.ds(lo, W)], w1b.at[slot], wsem.at[0, slot]),
                pltpu.make_async_copy(w2_ref.at[pl.ds(lo, W), :], w2b.at[slot], wsem.at[1, slot]),
            )

        for w in weights(0, 0):
            w.start()
        proj_copy = pltpu.make_async_copy(w4_ref.at[:, pl.ds(3 * D, D)], pw, psem)
        proj_copy.start()

        def head(i, _):
            rows = pl.ds(pl.multiple_of(i * RB, RB), RB)
            normed, _r = normalize(mid_ref[rows, :])
            h2[rows, :] = (normed * (1.0 + scale2) + shift2).astype(bf16)
            dm[rows, :] = (g_ref[rows, :].astype(f32) * gate2).astype(bf16)
            return 0

        lax.fori_loop(0, T // RB, head, 0)
        for i in range(0, D, 256):
            h2t[i : i + 256, :] = h2[:, i : i + 256].T
        dh2[...] = jnp.zeros_like(dh2)
        mlp[...] = jnp.zeros_like(mlp)
        sums_ref[...] = jnp.zeros_like(sums_ref)

        def c2_copy(t):
            return remote(gb.at[t, 1 - at.c], cr.at[t], cs.at[t], crs.at[t], at.sibling())

        def c1_copy(t, slot):
            return remote(t1.at[slot, :, 1 - at.c], c1.at[t], c1s.at[t], c1r.at[t], at.sibling())

        def y_copy(k, m):
            return remote(ys.at[k, m], yr.at[k, m], yss.at[k, m], yrs.at[k, m], at.at_b(m + 1))

        def z_copy(k):
            return remote(zs.at[k], zr.at[k], zss.at[k], zrs.at[k], at.at_a(k + 1))

        def out1_copy(t, slot):
            lo = pl.multiple_of(tile(t) * H, H)
            src = o1 if s == 2 else s1
            return pltpu.make_async_copy(src.at[slot], g1_ref.at[:, :, pl.ds(lo, H)], osem.at[slot])

        def half(k):
            return pl.ds(pl.multiple_of(k * H, H), H)

        def x1_copy(t, slot):
            return remote(s1.at[slot], x1.at[t], x1s.at[t], x1r.at[t], other)

        def when_not(first, f):
            if not isinstance(first, bool):
                pl.when(jnp.logical_not(first))(f)
            elif not first:
                f()

        def chip_sum1(t, slot, first):
            c1_copy(t, slot).wait()
            if s != 2:
                when_not(first, lambda: out1_copy(t, slot).wait())

            def part(i, _):
                if s == 2:
                    keep[slot, i] = add32(t1[slot, i, at.c, :, half(x)], c1[t, i, :, half(x)])
                    send = half(1 - x)
                    s1[slot, i] = add32(t1[slot, i, at.c, :, send], c1[t, i, :, send]).astype(bf16)
                else:
                    s1[slot, i] = add32(t1[slot, i, at.c], c1[t, i]).astype(bf16)
                return 0

            lax.fori_loop(0, J, part, 0)
            if s == 2:
                x1_copy(t, slot).start()
            else:
                out1_copy(t, slot).start()

        def seq_sum1(t, slot, first):
            if s != 2:
                return
            x1_copy(t, slot).wait()
            when_not(first, lambda: out1_copy(t, slot).wait())

            def part(i, _):
                o1[slot, i] = add32(keep[slot, i], x1[t, i]).astype(bf16)
                return 0

            lax.fori_loop(0, J, part, 0)
            out1_copy(t, slot).start()

        R2 = min(r2, 64)

        def own_sum(t, k):
            c2_copy(t).wait()
            for m in range(B - 1):
                y_copy(k, m).wait()

        def send_y(k, m):
            t = k * B + m
            c2_copy(t).wait()

            def part(i, _):
                rows = pl.ds(pl.multiple_of(i * R2, R2), R2)
                ys[k, m, rows, :] = add32(gb[t, at.c, rows, :], cr[t, rows, :]).astype(bf16)
                return 0

            lax.fori_loop(0, r2 // R2, part, 0)
            y_copy(k, m).start()

        def send_z(k):
            t = k * B + B - 1
            own_sum(t, k)

            def part(i, _):
                rows = pl.ds(pl.multiple_of(i * R2, R2), R2)
                total = add32(gb[t, at.c, rows, :], cr[t, rows, :], *[yr[k, m, rows, :] for m in range(B - 1)])
                zs[k, rows, :] = total.astype(bf16)
                return 0

            lax.fori_loop(0, r2 // R2, part, 0)
            z_copy(k).start()

        def pair(k, _):
            for m in range(B):
                t = k * B + m
                slot = m % 2
                for w in weights(t, slot):
                    w.wait()

                @pl.when(t + 1 < J)
                def _():
                    for w in weights(t + 1, 1 - slot):
                        w.start()

                j = tile(t)
                act, slope = gelu_both(nn(h2[...], w1b[slot]) + b1_ref[j])
                act = act.astype(bf16)
                g2t = tn(act, dm[...]).astype(bf16)
                gb[t, 0] = g2t[:r2]
                gb[t, 1] = g2t[r2:]
                c2_copy(t).start()
                dpre = (nt(dm[...], w2b[slot]) * slope).astype(bf16)
                bfc1_ref[j] = jnp.sum(dpre.astype(f32), axis=0, keepdims=True)
                t1[slot] = nn(h2t[...], dpre).astype(bf16).reshape(J, 2, r1, W)
                c1_copy(t, slot).start()
                mlp[...] += nn(act, w2b[slot])
                dh2[...] += nt(dpre, w1b[slot])
                if m > 0:
                    chip_sum1(t - 1, 1 - slot, jnp.logical_and(k == 0, m < 3))
                    if m > 1:
                        seq_sum1(t - 2, slot, jnp.logical_and(k == 0, m < 4))
                    else:

                        @pl.when(k > 0)
                        def _():
                            seq_sum1(t - 2, slot, k * B < 3)

                    send_y(k, m - 1)
                else:

                    @pl.when(k > 0)
                    def _():
                        chip_sum1(t - 1, 1 - slot, k * B < 3)
                        seq_sum1(t - 2, slot, k * B < 4)

                if m == B - 1:

                    @pl.when(k > 0)
                    def _():
                        send_z(k - 1)

            return 0

        lax.fori_loop(0, A, pair, 0)
        chip_sum1(J - 1, 1, J < 3)
        seq_sum1(J - 2, 0, J < 4)

        def back(i, _):
            rows = pl.ds(pl.multiple_of(i * RB, RB), RB)
            mid = mid_ref[rows, :]
            gf = g_ref[rows, :].astype(f32)
            normed, rscale = normalize(mid)
            dh = dh2[rows, :]
            up = dh * (1.0 + scale2)
            dmid = gf + rscale * (
                up
                - jnp.mean(up, axis=-1, keepdims=True)
                - normed * jnp.mean(up * normed, axis=-1, keepdims=True)
            )
            dmid_ref[rows, :] = dmid
            db = (dmid * gate1).astype(bf16)
            dbr[rows, :] = db
            ml = mlp[rows, :] + bias2
            out_ref[rows, :] = (mid + gate2 * ml).astype(bf16)
            for row, v in enumerate((dh, dh * normed, gf * ml, dmid * br_ref[rows, :], dm[rows, :], db)):
                sums_ref[row : row + 1, :] += jnp.sum(v.astype(f32), axis=0, keepdims=True)
            return 0

        lax.fori_loop(0, T // RB, back, 0)
        proj_copy.wait()
        dattn_ref[...] = nt(dbr[...], pw[...]).astype(bf16)

        def proj(i, _):
            cols = pl.ds(pl.multiple_of(i * 256, 256), 256)
            gproj_ref[cols, :] = tn(attn_ref[:, cols], dbr[...]).astype(bf16)
            return 0

        lax.fori_loop(0, D // 256, proj, 0)

        seq_sum1(J - 1, 1, J < 3)
        last = J - 1
        own_sum(last, A - 1)
        for k in range(A - 1):
            z_copy(k).wait()

        def part(i, _):
            rows = pl.ds(pl.multiple_of(i * R2, R2), R2)
            total = add32(
                gb[last, at.c, rows, :],
                cr[last, rows, :],
                *[yr[A - 1, m, rows, :] for m in range(B - 1)],
                *[zr[k, rows, :] for k in range(A - 1)],
            )
            g2_ref[rows, :] = total.astype(bf16)
            return 0

        lax.fori_loop(0, r2 // R2, part, 0)
        out1_copy(J - 2, 0).wait()
        out1_copy(J - 1, 1).wait()

    vm, hbm = pl.BlockSpec(memory_space=pltpu.VMEM), pl.BlockSpec(memory_space=pl.ANY)
    sds = jax.ShapeDtypeStruct
    dma = pltpu.SemaphoreType.DMA
    return pl.pallas_call(
        kern,
        out_shape=[
            sds((T, D), bf16), sds((T, D), f32), sds((T, D), bf16), sds((8, D), f32), sds((J, 1, W), f32),
            sds((D, D), bf16), sds((J, r1, J * H), bf16), sds((r2, D), bf16),
        ],
        in_specs=[vm] * 6 + [hbm] * 3,
        out_specs=[vm] * 6 + [hbm, vm],
        scratch_shapes=[
            pltpu.VMEM((T, D), bf16), pltpu.VMEM((D, T), bf16), pltpu.VMEM((T, D), bf16),
            pltpu.VMEM((T, D), f32), pltpu.VMEM((T, D), f32), pltpu.VMEM((T, D), bf16),
            pltpu.VMEM((2, D, W), bf16), pltpu.VMEM((2, W, D), bf16),
            pltpu.VMEM((J, 2, r2, D), bf16), pltpu.VMEM((J, r2, D), bf16),
            pltpu.VMEM((A, B - 1, r2, D), bf16), pltpu.VMEM((A, B - 1, r2, D), bf16),
            pltpu.VMEM((A - 1, r2, D), bf16), pltpu.VMEM((A - 1, r2, D), bf16),
            pltpu.VMEM((2, J, 2, r1, W), bf16), pltpu.VMEM((J, J, r1, W), bf16), pltpu.VMEM((2, J, r1, H), bf16),
            pltpu.VMEM((2, J, r1, H) if s == 2 else (8, 128), f32),
            pltpu.VMEM((J, J, r1, H) if s == 2 else (8, 128), bf16), pltpu.VMEM((2, J, r1, H), bf16), dma((J,)), dma((J,)),
            pltpu.VMEM((D, D), bf16), dma(()), dma((2, 2)), dma((2,)), dma((J,)), dma((J,)), dma((J,)), dma((J,)),
            dma((A, B - 1)), dma((A, B - 1)), dma((A - 1,)), dma((A - 1,)),
        ],
        compiler_params=pltpu.CompilerParams(
            collective_id=3, has_side_effects=True, vmem_limit_bytes=64 * 1024 * 1024 - 65536
        ),
        name="feed_forward",
    )(middle, branch, attn, g, vectors, b_fc1.reshape(J, 1, W), w4, w1, w2)


class RowSum:
    @staticmethod
    def scratch(U, r, W, A, B, cores, last=bf16):
        dma = pltpu.SemaphoreType.DMA
        shapes = [
            pltpu.VMEM((U, B - 1, A, r, W), bf16), pltpu.VMEM((U, A - 1, r, W), bf16),
            pltpu.VMEM((U, A - 1, r, W), bf16), pltpu.VMEM((U, r, W), last), pltpu.VMEM((U, r, W), last),
            dma((U, B - 1)), dma((U, B - 1)), dma((U, A - 1)), dma((U, A - 1)), dma((U,)), dma((U,)),
        ]
        if cores:
            shapes += [
                pltpu.VMEM((U, A * B, r, W), bf16), pltpu.VMEM((U, B - 1, A, r, W), bf16), dma((U,)), dma((U,)),
            ]
        return shapes

    def __init__(self, at, s, peer, refs, grad=None, half=None):
        self.at, self.s, self.peer = at, s, peer
        self.grad, self.half = grad, half
        self.yr, self.zs, self.zr, self.xs, self.xr = refs[:5]
        self.yss, self.yrs, self.zss, self.zrs, self.xss, self.xrs = refs[5:11]
        if grad is not None:
            self.cr, self.ys, self.css, self.crs = refs[11:]

    def c_copy(self, u):
        return remote(
            self.grad.at[u, :, 1 - self.at.c], self.cr.at[u], self.css.at[u], self.crs.at[u], self.at.sibling()
        )

    def y_source(self, u, m):
        return self.ys.at[u, m]

    def y_copy(self, u, m):
        src = self.y_source(u, m)
        return remote(src, self.yr.at[u, m], self.yss.at[u, m], self.yrs.at[u, m], self.at.at_b(m + 1))

    def z_copy(self, u, k):
        return remote(self.zs.at[u, k], self.zr.at[u, k], self.zss.at[u, k], self.zrs.at[u, k], self.at.at_a(k + 1))

    def x_copy(self, u):
        return remote(self.xs.at[u], self.xr.at[u], self.xss.at[u], self.xrs.at[u], self.peer)

    def chip(self, u, a, b):
        j = a * self.at.B + b
        return add32(self.grad[u, j, self.at.c], self.cr[u, j])

    def own(self, u, a):
        base = self.chip(u, a, self.at.b) if self.half is None else self.half(u, a)
        return add32(base, *[self.yr[u, m, a] for m in range(self.at.B - 1)])

    def send_y(self, u):
        self.c_copy(u).wait()
        for m in range(self.at.B - 1):
            b = lax.rem(self.at.b + m + 1, self.at.B)
            for a in range(self.at.A):
                self.ys[u, m, a] = self.chip(u, a, b).astype(bf16)
            self.y_copy(u, m).start()

    def send_z(self, u):
        for m in range(self.at.B - 1):
            self.y_copy(u, m).wait()
        for k in range(self.at.A - 1):
            self.zs[u, k] = self.own(u, lax.rem(self.at.a + k + 1, self.at.A)).astype(bf16)
            self.z_copy(u, k).start()

    def send_x(self, u):
        for k in range(self.at.A - 1):
            self.z_copy(u, k).wait()
        total = add32(self.own(u, self.at.a), *[self.zr[u, k] for k in range(self.at.A - 1)])
        if self.s != 2:
            return total
        self.xs[u] = total.astype(self.xs.dtype)
        self.x_copy(u).start()
        return None

    def finish(self, u):
        self.x_copy(u).wait()
        return add32(self.xs[u], self.xr[u])


def attention_and_sums(
    qkv, kvr, d_attn, lse, hidden, tokens, vectors, d_middle, w_qkv, half_fc1, grad_proj, sum_fc2, sums, bias_fc1, lf, w_ada, n, s
):
    T, D = tokens.shape
    FH = half_fc1.shape[-1]
    FF = 2 * FH if s == 2 else FH
    A, B = grid_of(n)
    J, r1, r2 = A * B, D // n, FF // n
    GW, LAGZ = 256, 3
    U = D // GW
    F = FH // U
    E = 6 * D
    RB = min(T, 64)
    rows_a = D // n
    m_bias = [2 * D // n, D // n, FF // n, D // n]
    starts = [0, 2 * D, 3 * D, 3 * D + FF]
    NBIAS = 4 * D + FF
    blocks = [max(v, 128) for v in m_bias]
    offs = [sum(blocks[:i]) for i in range(4)]
    M = sum(blocks)
    nq = len(RowSum.scratch(U, r1, 3 * GW, A, B, True))
    nf = len(RowSum.scratch(U, r1, F, A, B, False))

    def kern(*refs):
        it = iter(refs)

        def take(count):
            return [next(it) for _ in range(count)]

        qkv_ref, kvr_ref = take(2)
        e_ref, lse_ref, h_ref, tok_ref, sc_ref, dmid_ref, w_ref, f1_ref, gp_ref, f2_ref, sum_ref, bf_ref, lf_ref, wa_ref = take(14)
        gt_ref, oq_ref, op_ref, o1_ref, o2_ref, gw_ref, gb_ref, dl_ref, bo_ref = take(9)
        h1t, dqg, kvl, kvs, kvr, dg, gq, wq, f1o, x2 = take(10)
        dh1 = gt_ref
        wsem, fsem, kss, krs, x2s, x2r = take(6)
        scr_q, scr_p, scr_f = take(nq), take(nq), take(nf)
        dx, dm, lp, bsum, bx, bsx = take(6)
        asend, arecv, lsend, lrecv, bsend, brecv, xsend, xrecv = take(8)

        at = Place(n)
        me, x = at.me, lax.axis_index("seq")
        peers = fsdp_peers(n, me)

        def seq_dev(k):
            return {"seq": lax.rem(x + k, s)}

        greet([{"fsdp": p} for p in peers] + [seq_dev(k) for k in range(1, s)])
        other = seq_dev(1)
        sq = RowSum(at, s, other, scr_q, grad=gq)
        sp = RowSum(at, s, other, scr_p, grad=gp_ref)
        sf = RowSum(at, s, other, scr_f, half=lambda u, a: f1o[u, a])

        def f_source(u, m):
            b = lax.rem(at.b + m + 1, B)
            return f1_ref.at[:, b, :, pl.ds(pl.multiple_of(u * F, F), F)]

        sf.y_source = f_source
        own_f = [
            pltpu.make_async_copy(f1_ref.at[:, at.b, :, pl.ds(u * F, F)], f1o.at[u], fsem.at[u]) for u in range(U)
        ]
        spans = [pl.ds(2 * D, 4 * D), pl.ds(0, 2 * D)]

        def mod_x(i):
            sl = dx.at[x, :, spans[i]]
            return [remote(sl, sl, xsend.at[i, k - 1], xrecv.at[i, k - 1], seq_dev(k)) for k in range(1, s)]

        def mod_all(i):
            dm[me, :, spans[i]] = jnp.sum(dx[:, :, spans[i]], axis=0).astype(bf16).astype(f32)
            sl = dm.at[me, :, spans[i]]
            out = [remote(sl, sl, asend.at[i, k], arecv.at[i, k], {"fsdp": p}) for k, p in enumerate(peers)]
            for c in out:
                c.start()
            return out

        def bias_span(p, i):
            lo = starts[i] + ((p * m_bias[i]) // blocks[i]) * blocks[i]
            return pl.ds(pl.multiple_of(lo, 128), blocks[i])

        def bias_out(lo, hi):
            out = []
            for i in range(lo, hi):
                at_i = pl.ds(offs[i], blocks[i])
                bx[me, :, at_i] = bsum[:, bias_span(me, i)]
                for k, p in enumerate(peers):
                    dst = bx.at[me, :, at_i]
                    out.append(remote(bsum.at[:, bias_span(p, i)], dst, bsend.at[i, k], brecv.at[i, k], {"fsdp": p}))
            for c in out:
                c.start()
            return out

        for i, row in enumerate((3, 0, 1, 2)):
            dx[x, :, (i + 2) * D : (i + 3) * D] = sum_ref[row : row + 1, :]
        early_x = mod_x(0)
        for c in early_x:
            c.start()
        bsum[:, starts[1] : starts[1] + D] = sum_ref[5:6, :]
        bsum[:, starts[2] : starts[2] + FF] = bf_ref[...]
        bsum[:, starts[3] : starts[3] + D] = sum_ref[4:5, :]
        sp.c_copy(0).start()
        for u in range(U):
            for m in range(B - 1):
                sf.y_copy(u, m).start()
        early_bias = bias_out(1, 4)
        if s == 2:
            x2_copy = remote(f2_ref, x2, x2s, x2r, other)
            x2_copy.start()
        for o in own_f:
            o.start()

        def h_copy(i):
            k = i % 3
            return pltpu.make_async_copy(
                h_ref.at[:, pl.ds(i * GW, GW)], dg.at[:, pl.ds(k * GW, GW)], wsem.at[k]
            )

        for i in range(min(U, 3)):
            h_copy(i).start()
        for i in range(U):
            h_copy(i).wait()
            k = i % 3
            h1t[i * GW : (i + 1) * GW, :] = dg[:, k * GW : (k + 1) * GW].T
            if i + 3 < U:
                h_copy(i + 3).start()
        dh1[...] = jnp.zeros_like(dh1)
        for o in own_f:
            o.wait()
        for c in early_x:
            c.wait()
        early_all = mod_all(0)

        def w_copy(u, i):
            lo = pl.multiple_of(i * D + u * GW, GW)
            return pltpu.make_async_copy(w_ref.at[:, pl.ds(lo, GW)], wq.at[:, pl.ds(i * GW, GW)], wsem.at[i])

        def kv_copy(u, k):
            return remote(kvs.at[u, k - 1], kvr.at[u, k - 1], kss.at[u, k - 1], krs.at[u, k - 1], seq_dev(s - k))

        def attend(u):
            slot = lax.rem(u, 2)
            for o in range(GW // 128):
                pair = u * (GW // 128) + o
                cols, k_cols, v_cols = [pl.ds(pl.multiple_of(lo + pair * 128, 128), 128) for lo in (0, D, 2 * D)]
                here = slice(o * 128, o * 128 + 128)
                qv, e = qkv_ref[:, cols] * bf16(HD**-0.5), e_ref[:, cols]
                ks = [qkv_ref[:, k_cols]] + [kvr_ref[k, :, cols] for k in range(s - 1)]
                vs = [qkv_ref[:, v_cols]] + [kvr_ref[k, :, k_cols] for k in range(s - 1)]
                dqt, dks, dvs = None, [None] * s, [None] * s
                for h in range(2):
                    qh, eh = pick(qv, h), pick(e, h)
                    total = lse_ref[pair, h : h + 1, :]
                    probs, dprobs, cross = [], [], None
                    for j in range(s):
                        p = jnp.exp(nt(ks[j], qh) - total)
                        dp = nt(vs[j], eh)
                        part = (p * dp).sum(axis=0, keepdims=True)
                        cross = part if cross is None else cross + part
                        dv = nn(p.astype(bf16), eh)
                        dvs[j] = dv if dvs[j] is None else dvs[j] + dv
                        probs.append(p)
                        dprobs.append(dp)
                    for j in range(s):
                        ds = (probs[j] * (dprobs[j] - cross)).astype(bf16)
                        dk = nn(ds, qh)
                        dks[j] = dk if dks[j] is None else dks[j] + dk
                        t = tn(pick(ks[j], h), ds)
                        dqt = t if dqt is None else dqt + t
                dqg[slot, :, here] = (dqt * (HD**-0.5)).T.astype(bf16)
                kvl[slot, 0, :, here] = dks[0]
                kvl[slot, 1, :, here] = dvs[0]
                for j in range(1, s):
                    kvs[u, j - 1, 0, :, here] = dks[j].astype(bf16)
                    kvs[u, j - 1, 1, :, here] = dvs[j].astype(bf16)
            for k in range(1, s):
                kv_copy(u, k).start()

        def project(u):
            slot = lax.rem(u, 2)
            for k in range(1, s):
                kv_copy(u, k).wait()
            dg[:, :GW] = dqg[slot]
            for i in range(2):
                lo = (i + 1) * GW
                dg[:, lo : lo + GW] = add32(kvl[slot, i], *[kvr[u, k, i] for k in range(s - 1)]).astype(bf16)
            part = 256 // (2 * r1)
            for i in range(D // 256):
                g = nn(h1t[i * 256 : (i + 1) * 256, :], dg[...]).astype(bf16)
                gq[u, i * part : (i + 1) * part] = g.reshape(part, 2, r1, 3 * GW)
            sq.c_copy(u).start()
            here = pl.ds(pl.multiple_of(u * GW, GW), GW)
            bsum[:, here] = jnp.sum(dg[:, :GW].astype(f32), axis=0, keepdims=True)
            there = pl.ds(pl.multiple_of(D + u * GW, GW), GW)
            bsum[:, there] = jnp.sum(dg[:, 2 * GW :].astype(f32), axis=0, keepdims=True)
            for i in range(3):
                w_copy(u, i).wait()
            dh1[...] += nt(dg[...], wq[...])

        def step(i, _):
            @pl.when(i < U)
            def _():
                attend(i)

            @pl.when(jnp.logical_and(i >= 1, i <= U))
            def _():
                project(i - 1)

            @pl.when(i < U)
            def _():
                for k in range(3):
                    w_copy(i, k).start()

            @pl.when(i == 0)
            def _():
                sp.send_y(0)

            @pl.when(i < U)
            def _():
                sf.send_z(i)

            @pl.when(i >= 2)
            def _():
                sq.send_y(i - 2)

            @pl.when(i == LAGZ - 1)
            def _():
                sp.send_z(0)

            @pl.when(i >= LAGZ)
            def _():
                sq.send_z(i - LAGZ)

            return 0

        lax.fori_loop(0, U + 2, step, 0)

        sums = [jnp.zeros((1, D), f32), jnp.zeros((1, D), f32)]
        scale1 = sc_ref[5:6, :]

        def back(i, carry):
            rows = pl.ds(pl.multiple_of(i * RB, RB), RB)
            normed, rscale = normalize(tok_ref[rows, :].astype(f32))
            dh = dh1[rows, :]
            up = dh * (1.0 + scale1)
            gt_ref[rows, :] = dmid_ref[rows, :] + rscale * (
                up
                - jnp.mean(up, axis=-1, keepdims=True)
                - normed * jnp.mean(up * normed, axis=-1, keepdims=True)
            )
            return (
                carry[0] + jnp.sum(dh, axis=0, keepdims=True),
                carry[1] + jnp.sum(dh * normed, axis=0, keepdims=True),
            )

        shift1_sum, scale1_sum = lax.fori_loop(0, T // RB, back, tuple(sums))
        dx[x, :, :D] = shift1_sum
        dx[x, :, D : 2 * D] = scale1_sum
        late_x = mod_x(1)
        for c in late_x:
            c.start()
        late_bias = bias_out(0, 1)
        for c in late_x:
            c.wait()
        late_all = mod_all(1)

        for u in range(U + 2 - LAGZ, U):
            sq.send_z(u)
        for u in range(U):
            if s == 2:
                sf.send_x(u)
            else:
                o1_ref[:, u * F : (u + 1) * F] = sf.send_x(u)
        for c in early_bias + late_bias:
            c.wait()
        bsx[x] = jnp.sum(bx[...], axis=0)
        bias_x = [remote(bsx.at[x], bsx.at[x], xsend.at[2, k - 1], xrecv.at[2, k - 1], seq_dev(k)) for k in range(1, s)]
        for c in bias_x:
            c.start()
        if s == 2:
            sp.send_x(0)
        else:
            op_ref[...] = sp.send_x(0)
        for c in early_all + late_all:
            c.wait()
        dmod = dm[...].reshape(n, E).astype(bf16)
        lp[...] = nt(dmod, wa_ref[...]).reshape(n, 1, rows_a)
        dl_ref[me] = lp[me]
        lift = [remote(lp.at[p], dl_ref.at[me], lsend.at[k], lrecv.at[k], {"fsdp": p}) for k, p in enumerate(peers)]
        for c in lift:
            c.start()
        gw_ref[...] = tn(lf_ref[...].reshape(n, rows_a).astype(bf16), dmod)
        gb_ref[...] = jnp.sum(dm[...], axis=0)

        def put_q(u, value):
            for i in range(3):
                oq_ref[:, i * D + u * GW : i * D + (u + 1) * GW] = value[:, i * GW : (i + 1) * GW]

        for u in range(U):
            value = sq.send_x(u)
            if s != 2:
                put_q(u, value)
        if s == 2:
            x2_copy.wait()
            o2_ref[...] = add32(f2_ref[...], x2[...])
            for u in range(U):
                sf.x_copy(u).wait()
                for q in range(F // r2):
                    lo = 2 * (u * F + q * r2)
                    for k, got in ((x, sf.xs), (1 - x, sf.xr)):
                        cols = pl.ds(pl.multiple_of(lo + k * r2, 128), r2)
                        o1_ref[:, cols] = got[u, :, q * r2 : (q + 1) * r2]
            op_ref[...] = sp.finish(0)
            for u in range(U):
                put_q(u, sq.finish(u))
        else:
            o2_ref[...] = f2_ref[...].astype(f32)
        for c in bias_x:
            c.wait()
        bo_ref[...] = jnp.sum(bsx[...], axis=0)
        for c in lift:
            c.wait()

    vm, hbm = pl.BlockSpec(memory_space=pltpu.VMEM), pl.BlockSpec(memory_space=pl.ANY)
    sds, dma = jax.ShapeDtypeStruct, pltpu.SemaphoreType.DMA
    res = pl.pallas_call(
        kern,
        out_shape=[
            sds((T, D), f32), sds((r1, 3 * D), f32), sds((r1, D), f32), sds((r1, FF), f32), sds((r2, D), f32),
            sds((rows_a, E), f32), sds((1, E), f32), sds((n, 1, rows_a), f32), sds((1, M), f32),
        ],
        in_specs=[vm] * 4 + [hbm] + [vm] * 3 + [hbm, hbm] + [vm] * 6,
        out_specs=[vm] * 9,
        scratch_shapes=[
            pltpu.VMEM((D, T), bf16), pltpu.VMEM((2, T, GW), bf16),
            pltpu.VMEM((2, 2, T, GW), f32), pltpu.VMEM((U, s - 1, 2, T, GW), bf16),
            pltpu.VMEM((U, s - 1, 2, T, GW), bf16), pltpu.VMEM((T, 3 * GW), bf16),
            pltpu.VMEM((U, J, 2, r1, 3 * GW), bf16), pltpu.VMEM((D, 3 * GW), bf16),
            pltpu.VMEM((U, A, r1, F), bf16), pltpu.VMEM((r2, D), bf16),
            dma((3,)), dma((U,)), dma((U, s - 1)), dma((U, s - 1)), dma(()), dma(()),
        ]
        + RowSum.scratch(U, r1, 3 * GW, A, B, True)
        + RowSum.scratch(1, r1, D, A, B, True)
        + RowSum.scratch(U, r1, F, A, B, False, f32)
        + [
            pltpu.VMEM((s, 1, E), f32), pltpu.VMEM((n, 1, E), f32), pltpu.VMEM((n, 1, rows_a), f32),
            pltpu.VMEM((1, NBIAS), f32), pltpu.VMEM((n, 1, M), f32), pltpu.VMEM((s, 1, M), f32),
            dma((2, n - 1)), dma((2, n - 1)), dma((n - 1,)), dma((n - 1,)),
            dma((4, n - 1)), dma((4, n - 1)), dma((3, s - 1)), dma((3, s - 1)),
        ],
        compiler_params=pltpu.CompilerParams(
            collective_id=4, has_side_effects=True, vmem_limit_bytes=64 * 1024 * 1024 - 65536
        ),
        name="attention_and_sums",
    )(
        qkv, kvr, d_attn, lse, hidden, tokens, vectors, d_middle, w_qkv, half_fc1.reshape(A, B, r1, FH),
        grad_proj.reshape(1, J, 2, r1, D), sum_fc2, sums, bias_fc1, lf, w_ada,
    )
    grad_tokens, t_qkv, t_proj, t_fc1, t_fc2, t_ada, ada_sums, d_lifted, bias = res
    if s != 2:
        t_qkv, t_proj, t_fc1, t_fc2 = lax.psum((t_qkv, t_proj, t_fc1, t_fc2), "seq")
    me = lax.axis_index("fsdp")
    biases = []
    for width, wide, off in zip(m_bias, blocks, offs):
        biases.append(lax.dynamic_slice_in_dim(bias[0, off : off + wide], (me * width) % wide, width))
    return grad_tokens, t_qkv, t_proj, t_fc1, t_fc2, t_ada, ada_sums, d_lifted, biases


def on_device(
    tokens,
    condition,
    w_ada,
    b_ada,
    w_qkv,
    b_qv,
    w_proj,
    b_proj,
    w_fc1,
    b_fc1,
    w_fc2,
    b_fc2,
    cotangent,
):
    n, s = lax.axis_size("fsdp"), lax.axis_size("seq")
    width = tokens.shape[-1]

    lifted, silu_back = jax.vjp(jax.nn.silu, condition.astype(f32))
    lifted_q = lifted.astype(bf16).astype(f32).reshape(n, 1, width // n)
    qkv, kvr, hidden_one, attn, lse, branch, middle, vectors, fc1_b, lf, w4, fc1_w, fc2_w = forward_attention(
        lifted_q, w_ada, [b_qv, b_proj, b_fc1, b_fc2, b_ada], tokens[0], w_qkv, w_proj, w_fc1, w_fc2, n, s
    )
    result, d_middle, d_attn, sums, bias_fc1, grad_proj, half_fc1, sum_fc2 = feed_forward(
        middle, branch, attn, cotangent[0], vectors, fc1_b, w4, fc1_w, fc2_w, n, s
    )
    grad_input, total_qkv, total_proj, total_fc1, total_fc2, total_ada, sums_ada, d_lifted, total_bias = (
        attention_and_sums(
            qkv, kvr, d_attn, lse, hidden_one, tokens[0], vectors, d_middle, w4, half_fc1,
            grad_proj, sum_fc2, sums, bias_fc1.reshape(1, -1), lf, w_ada, n, s,
        )
    )
    share = b_ada.shape[0]
    total_bada = lax.dynamic_slice_in_dim(sums_ada[0], lax.axis_index("fsdp") * share, share)
    grad_condition = silu_back(d_lifted.reshape(1, width))[0]
    total_bqv, total_bproj, total_bfc1, total_bfc2 = total_bias
    return (
        result[None],
        grad_input[None],
        grad_condition,
        total_ada,
        total_bada,
        total_qkv,
        total_bqv,
        total_proj,
        total_bproj,
        total_fc1,
        total_bfc1,
        total_fc2,
        total_bfc2,
    )


def solution(mesh):
    weights = (P("fsdp", None), P("fsdp")) * 5
    return jax.shard_map(
        on_device,
        mesh=mesh,
        in_specs=(P("fsdp", "seq", None), P("fsdp", None)) + weights + (P("fsdp", "seq", None),),
        out_specs=(P("fsdp", "seq", None), P("fsdp", "seq", None), P("fsdp", None)) + weights,
        check_vma=False,
    )
```

```python
from functools import partial

import jax
import jax.numpy as jnp
from jax import lax
from jax.experimental import pallas as pl
from jax.experimental.pallas import tpu as pltpu
from jax.sharding import PartitionSpec as P

HD = 64
norm_eps = 1e-06
f32 = jnp.float32
bf16 = jnp.bfloat16
MESH = pl.DeviceIdType.MESH


def grid_of(n):
    b = 2 if n == 16 else 4
    return n // (2 * b), b


def nt(a, b):
    return lax.dot_general(a, b, (((1,), (1,)), ((), ())), preferred_element_type=f32)


def nn(a, b):
    return lax.dot_general(a, b, (((1,), (0,)), ((), ())), preferred_element_type=f32)


def tn(a, b):
    return lax.dot_general(a, b, (((0,), (0,)), ((), ())), preferred_element_type=f32)


def fsdp_peers(n, me):
    return [lax.rem(me + k, n) for k in range(1, n)]


def head_mask(ref_shape, h):
    low = lax.broadcasted_iota(jnp.int32, ref_shape, 1) < HD
    return low if h == 0 else ~low


def pick(values, h):
    return jnp.where(head_mask(values.shape, h), values, jnp.zeros_like(values))


def remote(src, dst, send, recv, device):
    return pltpu.make_async_remote_copy(
        src_ref=src, dst_ref=dst, send_sem=send, recv_sem=recv, device_id=device, device_id_type=MESH
    )


def greet(devices):
    bar = pltpu.get_barrier_semaphore()
    for d in devices:
        pl.semaphore_signal(bar, inc=1, device_id=d, device_id_type=MESH)
    pl.semaphore_wait(bar, len(devices))


class Place:
    def __init__(self, n):
        self.A, self.B = grid_of(n)
        me = lax.axis_index("fsdp")
        self.me = me
        self.a, self.b, self.c = me // (2 * self.B), lax.rem(me // 2, self.B), lax.rem(me, 2)

    def dev(self, a, b, c):
        return {"fsdp": (a * self.B + b) * 2 + c}

    def at_a(self, k):
        return self.dev(lax.rem(self.a + k, self.A), self.b, self.c)

    def at_b(self, k):
        return self.dev(self.a, lax.rem(self.b + k, self.B), self.c)

    def sibling(self):
        return self.dev(self.a, self.b, 1 - self.c)

    def all(self):
        return [self.at_a(k) for k in range(1, self.A)] + [self.at_b(k) for k in range(1, self.B)] + [self.sibling()]


def add32(*values):
    total = values[0].astype(f32)
    for v in values[1:]:
        total = total + v.astype(f32)
    return total


def gelu_both(x):
    k = 0.7978845608028654
    sq = x * x
    th = jnp.tanh(k * (x + 0.044715 * (sq * x)))
    half = 0.5 * (1.0 + th)
    slope = half + (0.5 * k) * x * (1.0 - th * th) * (1.0 + (3 * 0.044715) * sq)
    return x * half, slope


def normalize(v):
    center = v - jnp.mean(v, axis=-1, keepdims=True)
    rscale = lax.rsqrt(jnp.mean(center * center, axis=-1, keepdims=True) + norm_eps)
    return center * rscale, rscale


def bias_block(width, n):
    return max(-(-((p * width) % 128 + width) // 128) * 128 for p in range(n))


def placed_bias(bias, n):
    width, wide = bias.shape[0], bias_block(bias.shape[0], n)
    bias = bias.astype(f32)[None]
    if wide == width:
        return bias
    at = (lax.axis_index("fsdp") * width) % 128
    if wide == 128:
        mine = lax.broadcasted_iota(jnp.int32, (1, wide), 1) // width == at // width
        return jnp.where(mine, jnp.concatenate([bias] * (wide // width), axis=1), 0.0)
    return lax.dynamic_update_slice(jnp.zeros((1, wide), f32), bias, (0, at))


def forward_attention(lifted, w_ada, biases, tokens, w_qkv, w_proj, w_fc1, w_fc2, n, s):
    T, D = tokens.shape
    E = w_ada.shape[1]
    FF = w_fc1.shape[1]
    A, B = grid_of(n)
    rows_a = w_ada.shape[0]
    r1, r2 = w_qkv.shape[0], w_fc2.shape[0]
    widths = [v.shape[0] for v in biases]
    blocks = [bias_block(w, n) for w in widths]
    offs = [sum(blocks[:i]) for i in range(5)]
    bases = [n * sum(widths[:i]) for i in range(5)]
    packed = jnp.concatenate([placed_bias(v, n) for v in biases], axis=1)
    M = packed.shape[1]
    share = s == 2
    NT, NL = 8, 16
    CQ, CF, RF = 4 * D // NT, FF // NL, r2 // NL
    RB = min(T, 64)
    AHEAD, MODULATE, LAG, ATTEND = 2, 4, 6, NT + 7
    NA, NY = A - 1, B - 1
    NQ = NA + NY + 1
    NF = 3 * (NA + NY) + 2
    pairs = D // 128

    def kern(
        l_ref, wa_ref, bias_ref, tok_ref, wqkv_ref, wproj_ref, wfc1_ref, wfc2_ref,
        qkv_ref, kvr_ref, h_ref, attn_ref, lse_ref, br_ref, mid_ref, vec_ref, bfc1_ref, lf_ref, w4_ref, f1_ref, f2_ref,
        normed, wq, part, acc, bout, bvec, mod, msend, mrecv, qsend, qrecv, fsend, frecv, ksend, krecv, osem,
    ):
        at = Place(n)
        a, b, c, me, x = at.a, at.b, at.c, at.me, lax.axis_index("seq")
        peers = fsdp_peers(n, me)
        other = {"seq": lax.rem(x + 1, s)}
        greet([{"fsdp": p} for p in peers] + [{"seq": lax.rem(x + k, s)} for k in range(1, s)])

        def small(i, src, dst):
            return [
                remote(src(p), dst(k), msend.at[i, k], mrecv.at[i, k], {"fsdp": p}) for k, p in enumerate(peers)
            ]

        m_lift = small(0, lambda p: l_ref.at[p], lambda k: lf_ref.at[me])
        m_bias = small(1, lambda p: bias_ref, lambda k: bout.at[me])
        m_part = small(2, lambda p: part.at[p], lambda k: acc.at[k + 1])
        for r in m_lift + m_bias:
            r.start()
        owns = [
            pltpu.make_async_copy(wqkv_ref, wq.at[a, b, c, :, pl.ds(0, 3 * D)], osem.at[0]),
            pltpu.make_async_copy(wproj_ref, wq.at[a, b, c, :, pl.ds(3 * D, D)], osem.at[1]),
            pltpu.make_async_copy(wfc1_ref, f1_ref.at[a, b, c], osem.at[2]),
            pltpu.make_async_copy(wfc2_ref, f2_ref.at[a, b, c], osem.at[3]),
        ]
        for o in owns:
            o.start()

        def block(i):
            return jnp.where(i < 6, lax.rem(i + 2, 6), i)

        def span(lo, size, step):
            return pl.ds(pl.multiple_of(lo, step), size)

        class Ticks:
            def __init__(self, pieces, whole, send, recv):
                self.pieces, self.whole, self.send, self.recv = pieces, whole, send, recv

            def copy(self, j, i, src, dst, device):
                return remote(src, dst, self.send.at[j, i], self.recv.at[j, i], device)

            def z(self, j):
                return [
                    self.copy(j, i * NA + k, src.at[rows, cols], buf.at[a, b, c, rows, cols], at.at_a(k + 1))
                    for i, (src, buf, rows, cols, _) in enumerate(self.pieces(j))
                    for k in range(NA)
                ]

            def y(self, j):
                out, ps = [], self.pieces(j)
                for i, (_, buf, rows, cols, _) in enumerate(ps):
                    sl = buf.at[:, b, c, rows, cols]
                    out += [self.copy(j, len(ps) * NA + i * NY + k, sl, sl, at.at_b(k + 1)) for k in range(NY)]
                return out

            def x(self, j):
                out, ps = [], self.pieces(j)
                i = len(ps) * (NA + NY)
                for _, buf, rows, cols, shared in ps:
                    if not shared:
                        continue
                    for k in range(NA):
                        sl = buf.at[lax.rem(a + k + 1, A), :, c, rows, cols]
                        out.append(self.copy(j, i, sl, sl, other))
                        i += 1
                    for k in range(NY):
                        sl = buf.at[a, lax.rem(b + k + 1, B), c, rows, cols]
                        out.append(self.copy(j, i, sl, sl, other))
                        i += 1
                return out

            def c(self, j):
                ps = self.whole(j)
                i = self.send.shape[1] - len(ps)
                return [
                    self.copy(j, i + k, buf.at[:, :, c, rows, cols], buf.at[:, :, c, rows, cols], at.sibling())
                    for k, (buf, rows, cols) in enumerate(ps)
                ]

            def start_z(self, j):
                for r in self.z(j):
                    r.start()

            def start_y(self, j):
                for r in self.z(j):
                    r.wait_recv()
                for r in self.y(j):
                    r.start()

            def start_x(self, j):
                for r in self.y(j):
                    r.wait_recv()
                for r in self.x(j):
                    r.start()

            def start_c(self, j):
                for r in self.x(j):
                    r.wait_recv()
                for r in self.c(j):
                    r.start()

            def relay(self, j):
                self.start_x(j)
                self.start_c(j)

            def finish(self, j):
                for r in self.z(j) + self.y(j) + self.x(j):
                    r.wait_send()
                for r in self.c(j):
                    r.wait()

        all_r1 = pl.ds(0, r1)
        mine = wq.at[a, b, c]

        def q_pieces(i):
            return [(mine, wq, all_r1, span(block(i) * CQ, CQ, CQ), False)]

        def q_whole(i):
            return [(wq, all_r1, span(block(i) * CQ, CQ, CQ))]

        def f_pieces(j):
            w = D // 2 if share else D
            part = span(x * w, w, w) if share else pl.ds(0, D)
            return [
                (wfc1_ref, f1_ref, all_r1, span(j * CF, CF, CF), False),
                (wfc2_ref, f2_ref, span(j * RF, RF, RF), part, share),
            ]

        def f_whole(j):
            return [(f1_ref, all_r1, span(j * CF, CF, CF)), (f2_ref, span(j * RF, RF, RF), pl.ds(0, D))]

        tq, tf = Ticks(q_pieces, q_whole, qsend, qrecv), Ticks(f_pieces, f_whole, fsend, frecv)

        owns[0].wait()
        owns[1].wait()
        for i in range(AHEAD):
            tq.start_z(i)
        lf_ref[me] = l_ref[me]
        bout[me] = bias_ref[...]
        bvec[...] = jnp.zeros_like(bvec)

        def norm(i, _):
            rows = pl.ds(pl.multiple_of(i * RB, RB), RB)
            normed[rows, :] = normalize(tok_ref[rows, :].astype(f32))[0]
            return 0

        for r in m_lift:
            r.wait_recv()
        part[...] = nn(lf_ref[...].reshape(n, rows_a).astype(bf16), wa_ref[...]).reshape(n, 1, E)
        acc[0] = part[me]
        for r in m_part:
            r.start()

        def modulation():
            for r in m_bias + m_part:
                r.wait_recv()
            for i in range(5):
                for p in range(n):
                    lo = bases[i] + p * widths[i] // 128 * 128
                    value = bout[p, :, offs[i] : offs[i] + blocks[i]]
                    if widths[i] % 128 == 0:
                        bvec[:, lo : lo + blocks[i]] = value
                    else:
                        bvec[:, lo : lo + blocks[i]] += value
            mod[...] = jnp.sum(acc[...], axis=0) + bvec[:, bases[4] :]
            shift1, scale1, gate1, shift2, scale2, gate2 = [mod[:, i * D : (i + 1) * D] for i in range(6)]
            vec_ref[...] = jnp.zeros_like(vec_ref)
            for i, v in enumerate((shift2, scale2, gate2, gate1, bvec[:, bases[3] : bases[3] + D], scale1)):
                vec_ref[i : i + 1, :] = v
            bfc1_ref[...] = bvec[:, bases[2] : bases[2] + FF]

            def modulate(i, _):
                rows = pl.ds(pl.multiple_of(i * RB, RB), RB)
                h_ref[rows, :] = (normed[rows, :] * (1.0 + scale1) + shift1).astype(bf16)
                return 0

            lax.fori_loop(0, T // RB, modulate, 0)


        def kv_copy(m, k):
            return remote(
                qkv_ref.at[:, span(D + m * CQ, CQ, CQ)],
                kvr_ref.at[k - 1, :, span(m * CQ, CQ, CQ)],
                ksend.at[m, k - 1],
                krecv.at[m, k - 1],
                {"seq": lax.rem(x + k, s)},
            )

        def project(m):
            tq.finish(m)

            @pl.when(m < 6)
            def _():
                lo = block(m) * CQ
                cols = span(lo, CQ, CQ)
                from_v = (block(m) >= 4).astype(jnp.int32)
                bias = bvec[:, span(lo - from_v * D, CQ, CQ)]
                is_key = jnp.logical_and(block(m) >= 2, block(m) < 4)
                bias = jnp.where(is_key, jnp.zeros_like(bias), bias)
                out = nn(h_ref[...], wq[:, :, :, :, cols].reshape(D, CQ))
                qkv_ref[:, cols] = (out + bias).astype(bf16)

            @pl.when(m < 4)
            def _():
                for k in range(1, s):
                    kv_copy(m, k).start()

        def attend(pair):
            def cols(lo):
                return span(lo + pair * 128, 128, 128)

            q = qkv_ref[:, cols(0)] * bf16(HD**-0.5)
            ks = [qkv_ref[:, cols(D)]] + [kvr_ref[k, :, cols(0)] for k in range(s - 1)]
            vs = [qkv_ref[:, cols(2 * D)]] + [kvr_ref[k, :, cols(D)] for k in range(s - 1)]
            total = None
            for h in range(2):
                qh = pick(q, h)
                scores = [nt(k, qh) for k in ks]
                top = scores[0].max(axis=0, keepdims=True)
                for sc in scores[1:]:
                    top = jnp.maximum(top, sc.max(axis=0, keepdims=True))
                mass, out = None, None
                for sc, v in zip(scores, vs):
                    p = jnp.exp(sc - top)
                    got = p.sum(axis=0, keepdims=True)
                    mass = got if mass is None else mass + got
                    o = tn(pick(v, h), p.astype(bf16))
                    out = o if out is None else out + o
                out = out * (1.0 / mass)
                total = out if total is None else total + out
                lse_ref[pair, h : h + 1, :] = top + jnp.log(mass)
            attn_ref[:, cols(0)] = total.T.astype(bf16)

        def branch(i, _):
            cols = span(i * 256, 256, 256)
            weight = wq[:, :, :, :, span(3 * D + i * 256, 256, 256)].reshape(D, 256)
            got = nn(attn_ref[...], weight) + bvec[:, span(bases[1] + i * 256, 256, 256)]
            br_ref[:, cols] = got
            mid_ref[:, cols] = tok_ref[:, cols].astype(f32) + mod[:, span(2 * D + i * 256, 256, 256)] * got
            return 0

        out4 = pltpu.make_async_copy(wq, w4_ref, osem.at[0])

        def step(i, _):
            def when(lo, hi, f, shift):
                @pl.when(jnp.logical_and(i >= lo, i < hi))
                def _():
                    f(i - shift)

            when(0, NT - AHEAD, lambda j: tq.start_z(j + AHEAD), 0)
            when(NT - AHEAD, NT + NL - AHEAD, tf.start_z, NT - AHEAD)
            when(0, NT, tq.start_y, 0)
            when(NT, NT + NL, tf.start_y, NT)
            when(1, NT + 1, tq.relay, 1)
            when(NT + 1, NT + NL + 1, tf.start_x, NT + 1)
            when(NT + LAG, NT + NL + LAG, tf.start_c, NT + LAG)
            when(NT + LAG + 1, NT + NL + LAG + 1, tf.finish, NT + LAG + 1)

            @pl.when(i == 0)
            def _():
                lax.fori_loop(0, T // RB, norm, 0)

            pl.when(i == MODULATE)(modulation)
            when(MODULATE, MODULATE + NT, project, MODULATE)

            @pl.when(i == MODULATE + NT)
            def _():
                out4.start()

            @pl.when(i == ATTEND)
            def _():
                for m in range(4):
                    for k in range(1, s):
                        kv_copy(m, k).wait()

            when(ATTEND, ATTEND + pairs, attend, ATTEND)

            @pl.when(i == ATTEND + pairs)
            def _():
                lax.fori_loop(0, D // 256, branch, 0)

            return 0

        owns[2].wait()
        owns[3].wait()
        lax.fori_loop(0, NT + NL + LAG + 1, step, 0)
        out4.wait()
        for r in m_lift + m_bias + m_part:
            r.wait_send()

    vm, hbm = pl.BlockSpec(memory_space=pltpu.VMEM), pl.BlockSpec(memory_space=pl.ANY)
    sds, dma = jax.ShapeDtypeStruct, pltpu.SemaphoreType.DMA
    res = pl.pallas_call(
        kern,
        out_shape=[
            sds((T, 3 * D), bf16), sds((s - 1, T, 2 * D), bf16), sds((T, D), bf16), sds((T, D), bf16),
            sds((pairs, 2, T), f32), sds((T, D), f32), sds((T, D), f32), sds((8, D), f32), sds((1, FF), f32),
            sds((n, 1, rows_a), f32), sds((A, B, 2, r1, 4 * D), bf16), sds((A, B, 2, r1, FF), bf16),
            sds((A, B, 2, r2, D), bf16),
        ],
        in_specs=[vm] * 8,
        out_specs=[vm] * 10 + [hbm] * 3,
        scratch_shapes=[
            pltpu.VMEM((T, D), f32), pltpu.VMEM((A, B, 2, r1, 4 * D), bf16), pltpu.VMEM((n, 1, E), f32),
            pltpu.VMEM((n, 1, E), f32), pltpu.VMEM((n, 1, M), f32), pltpu.VMEM((1, n * sum(widths)), f32),
            pltpu.VMEM((1, E), f32), dma((3, n - 1)), dma((3, n - 1)), dma((NT, NQ)), dma((NT, NQ)),
            dma((NL, NF)), dma((NL, NF)), dma((4, s - 1)), dma((4, s - 1)), dma((4,)),
        ],
        compiler_params=pltpu.CompilerParams(
            collective_id=0, has_side_effects=True, vmem_limit_bytes=64 * 1024 * 1024 - 65536
        ),
        name="forward_attention",
    )(lifted, w_ada, packed, tokens, w_qkv, w_proj, w_fc1, w_fc2)
    qkv, kvr, hidden, attn, lse, branch, middle, vectors, b_fc1, lf, w4, f1, f2 = res
    return (
        qkv, kvr, hidden, attn, lse, branch, middle, vectors, b_fc1, lf,
        w4.reshape(D, 4 * D), f1.reshape(D, FF), f2.reshape(FF, D),
    )


def feed_forward(middle, branch, attn, g, vectors, b_fc1, w4, w1, w2, n, s):
    T, D = middle.shape
    FF = w1.shape[1]
    A, B = grid_of(n)
    J, r1, r2 = A * B, D // n, FF // n
    W = 2 * r2
    RB = min(T, 64)
    H = W // 2 if s == 2 else W

    def kern(
        mid_ref, br_ref, attn_ref, g_ref, vec_ref, b1_ref, w4_ref, w1_ref, w2_ref,
        out_ref, dmid_ref, dattn_ref, sums_ref, bfc1_ref, gproj_ref, g1_ref, g2_ref,
        h2, h2t, dm, dh2, mlp, dbr, w1b, w2b, gb, cr, ys, yr, zs, zr, t1, c1, s1, keep, x1, o1, x1s, x1r,
        pw, psem, wsem, osem, cs, crs, c1s, c1r, yss, yrs, zss, zrs,
    ):
        at = Place(n)
        x = lax.axis_index("seq")
        other = {"seq": lax.rem(x + 1, s)}
        greet(at.all() + ([other] if s == 2 else []))
        shift2, scale2, gate2, gate1, bias2 = [vec_ref[i : i + 1, :] for i in range(5)]

        def tile(t):
            k, m = t // B, lax.rem(t, B)
            return lax.rem(at.a + 1 + k, A) * B + lax.rem(at.b + 1 + m, B)

        def weights(t, slot):
            lo = pl.multiple_of(tile(t) * W, W)
            return (
                pltpu.make_async_copy(w1_ref.at[:, pl.ds(lo, W)], w1b.at[slot], wsem.at[0, slot]),
                pltpu.make_async_copy(w2_ref.at[pl.ds(lo, W), :], w2b.at[slot], wsem.at[1, slot]),
            )

        for w in weights(0, 0):
            w.start()
        proj_copy = pltpu.make_async_copy(w4_ref.at[:, pl.ds(3 * D, D)], pw, psem)
        proj_copy.start()

        def head(i, _):
            rows = pl.ds(pl.multiple_of(i * RB, RB), RB)
            normed, _r = normalize(mid_ref[rows, :])
            h2[rows, :] = (normed * (1.0 + scale2) + shift2).astype(bf16)
            dm[rows, :] = (g_ref[rows, :].astype(f32) * gate2).astype(bf16)
            return 0

        lax.fori_loop(0, T // RB, head, 0)
        for i in range(0, D, 256):
            h2t[i : i + 256, :] = h2[:, i : i + 256].T
        dh2[...] = jnp.zeros_like(dh2)
        mlp[...] = jnp.zeros_like(mlp)
        sums_ref[...] = jnp.zeros_like(sums_ref)

        def c2_copy(t):
            return remote(gb.at[t, 1 - at.c], cr.at[t], cs.at[t], crs.at[t], at.sibling())

        def c1_copy(t, slot):
            return remote(t1.at[slot, :, 1 - at.c], c1.at[t], c1s.at[t], c1r.at[t], at.sibling())

        def y_copy(k, m):
            return remote(ys.at[k, m], yr.at[k, m], yss.at[k, m], yrs.at[k, m], at.at_b(m + 1))

        def z_copy(k):
            return remote(zs.at[k], zr.at[k], zss.at[k], zrs.at[k], at.at_a(k + 1))

        def out1_copy(t, slot):
            lo = pl.multiple_of(tile(t) * H, H)
            src = o1 if s == 2 else s1
            return pltpu.make_async_copy(src.at[slot], g1_ref.at[:, :, pl.ds(lo, H)], osem.at[slot])

        def half(k):
            return pl.ds(pl.multiple_of(k * H, H), H)

        def x1_copy(t, slot):
            return remote(s1.at[slot], x1.at[t], x1s.at[t], x1r.at[t], other)

        def when_not(first, f):
            if not isinstance(first, bool):
                pl.when(jnp.logical_not(first))(f)
            elif not first:
                f()

        def chip_sum1(t, slot, first):
            c1_copy(t, slot).wait()
            if s != 2:
                when_not(first, lambda: out1_copy(t, slot).wait())

            def part(i, _):
                if s == 2:
                    keep[slot, i] = add32(t1[slot, i, at.c, :, half(x)], c1[t, i, :, half(x)])
                    send = half(1 - x)
                    s1[slot, i] = add32(t1[slot, i, at.c, :, send], c1[t, i, :, send]).astype(bf16)
                else:
                    s1[slot, i] = add32(t1[slot, i, at.c], c1[t, i]).astype(bf16)
                return 0

            lax.fori_loop(0, J, part, 0)
            if s == 2:
                x1_copy(t, slot).start()
            else:
                out1_copy(t, slot).start()

        def seq_sum1(t, slot, first):
            if s != 2:
                return
            x1_copy(t, slot).wait()
            when_not(first, lambda: out1_copy(t, slot).wait())

            def part(i, _):
                o1[slot, i] = add32(keep[slot, i], x1[t, i]).astype(bf16)
                return 0

            lax.fori_loop(0, J, part, 0)
            out1_copy(t, slot).start()

        R2 = min(r2, 64)

        def own_sum(t, k):
            c2_copy(t).wait()
            for m in range(B - 1):
                y_copy(k, m).wait()

        def send_y(k, m):
            t = k * B + m
            c2_copy(t).wait()

            def part(i, _):
                rows = pl.ds(pl.multiple_of(i * R2, R2), R2)
                ys[k, m, rows, :] = add32(gb[t, at.c, rows, :], cr[t, rows, :]).astype(bf16)
                return 0

            lax.fori_loop(0, r2 // R2, part, 0)
            y_copy(k, m).start()

        def send_z(k):
            t = k * B + B - 1
            own_sum(t, k)

            def part(i, _):
                rows = pl.ds(pl.multiple_of(i * R2, R2), R2)
                total = add32(gb[t, at.c, rows, :], cr[t, rows, :], *[yr[k, m, rows, :] for m in range(B - 1)])
                zs[k, rows, :] = total.astype(bf16)
                return 0

            lax.fori_loop(0, r2 // R2, part, 0)
            z_copy(k).start()

        def pair(k, _):
            for m in range(B):
                t = k * B + m
                slot = m % 2
                for w in weights(t, slot):
                    w.wait()

                @pl.when(t + 1 < J)
                def _():
                    for w in weights(t + 1, 1 - slot):
                        w.start()

                j = tile(t)
                act, slope = gelu_both(nn(h2[...], w1b[slot]) + b1_ref[j])
                act = act.astype(bf16)
                g2t = tn(act, dm[...]).astype(bf16)
                gb[t, 0] = g2t[:r2]
                gb[t, 1] = g2t[r2:]
                c2_copy(t).start()
                dpre = (nt(dm[...], w2b[slot]) * slope).astype(bf16)
                bfc1_ref[j] = jnp.sum(dpre.astype(f32), axis=0, keepdims=True)
                t1[slot] = nn(h2t[...], dpre).astype(bf16).reshape(J, 2, r1, W)
                c1_copy(t, slot).start()
                mlp[...] += nn(act, w2b[slot])
                dh2[...] += nt(dpre, w1b[slot])
                if m > 0:
                    chip_sum1(t - 1, 1 - slot, jnp.logical_and(k == 0, m < 3))
                    if m > 1:
                        seq_sum1(t - 2, slot, jnp.logical_and(k == 0, m < 4))
                    else:

                        @pl.when(k > 0)
                        def _():
                            seq_sum1(t - 2, slot, k * B < 3)

                    send_y(k, m - 1)
                else:

                    @pl.when(k > 0)
                    def _():
                        chip_sum1(t - 1, 1 - slot, k * B < 3)
                        seq_sum1(t - 2, slot, k * B < 4)

                if m == B - 1:

                    @pl.when(k > 0)
                    def _():
                        send_z(k - 1)

            return 0

        lax.fori_loop(0, A, pair, 0)
        chip_sum1(J - 1, 1, J < 3)
        seq_sum1(J - 2, 0, J < 4)

        def back(i, _):
            rows = pl.ds(pl.multiple_of(i * RB, RB), RB)
            mid = mid_ref[rows, :]
            gf = g_ref[rows, :].astype(f32)
            normed, rscale = normalize(mid)
            dh = dh2[rows, :]
            up = dh * (1.0 + scale2)
            dmid = gf + rscale * (
                up
                - jnp.mean(up, axis=-1, keepdims=True)
                - normed * jnp.mean(up * normed, axis=-1, keepdims=True)
            )
            dmid_ref[rows, :] = dmid
            db = (dmid * gate1).astype(bf16)
            dbr[rows, :] = db
            ml = mlp[rows, :] + bias2
            out_ref[rows, :] = (mid + gate2 * ml).astype(bf16)
            for row, v in enumerate((dh, dh * normed, gf * ml, dmid * br_ref[rows, :], dm[rows, :], db)):
                sums_ref[row : row + 1, :] += jnp.sum(v.astype(f32), axis=0, keepdims=True)
            return 0

        lax.fori_loop(0, T // RB, back, 0)
        proj_copy.wait()
        dattn_ref[...] = nt(dbr[...], pw[...]).astype(bf16)

        def proj(i, _):
            cols = pl.ds(pl.multiple_of(i * 256, 256), 256)
            gproj_ref[cols, :] = tn(attn_ref[:, cols], dbr[...]).astype(bf16)
            return 0

        lax.fori_loop(0, D // 256, proj, 0)

        seq_sum1(J - 1, 1, J < 3)
        last = J - 1
        own_sum(last, A - 1)
        for k in range(A - 1):
            z_copy(k).wait()

        def part(i, _):
            rows = pl.ds(pl.multiple_of(i * R2, R2), R2)
            total = add32(
                gb[last, at.c, rows, :],
                cr[last, rows, :],
                *[yr[A - 1, m, rows, :] for m in range(B - 1)],
                *[zr[k, rows, :] for k in range(A - 1)],
            )
            g2_ref[rows, :] = total.astype(bf16)
            return 0

        lax.fori_loop(0, r2 // R2, part, 0)
        out1_copy(J - 2, 0).wait()
        out1_copy(J - 1, 1).wait()

    vm, hbm = pl.BlockSpec(memory_space=pltpu.VMEM), pl.BlockSpec(memory_space=pl.ANY)
    sds = jax.ShapeDtypeStruct
    dma = pltpu.SemaphoreType.DMA
    return pl.pallas_call(
        kern,
        out_shape=[
            sds((T, D), bf16), sds((T, D), f32), sds((T, D), bf16), sds((8, D), f32), sds((J, 1, W), f32),
            sds((D, D), bf16), sds((J, r1, J * H), bf16), sds((r2, D), bf16),
        ],
        in_specs=[vm] * 6 + [hbm] * 3,
        out_specs=[vm] * 6 + [hbm, vm],
        scratch_shapes=[
            pltpu.VMEM((T, D), bf16), pltpu.VMEM((D, T), bf16), pltpu.VMEM((T, D), bf16),
            pltpu.VMEM((T, D), f32), pltpu.VMEM((T, D), f32), pltpu.VMEM((T, D), bf16),
            pltpu.VMEM((2, D, W), bf16), pltpu.VMEM((2, W, D), bf16),
            pltpu.VMEM((J, 2, r2, D), bf16), pltpu.VMEM((J, r2, D), bf16),
            pltpu.VMEM((A, B - 1, r2, D), bf16), pltpu.VMEM((A, B - 1, r2, D), bf16),
            pltpu.VMEM((A - 1, r2, D), bf16), pltpu.VMEM((A - 1, r2, D), bf16),
            pltpu.VMEM((2, J, 2, r1, W), bf16), pltpu.VMEM((J, J, r1, W), bf16), pltpu.VMEM((2, J, r1, H), bf16),
            pltpu.VMEM((2, J, r1, H) if s == 2 else (8, 128), f32),
            pltpu.VMEM((J, J, r1, H) if s == 2 else (8, 128), bf16), pltpu.VMEM((2, J, r1, H), bf16), dma((J,)), dma((J,)),
            pltpu.VMEM((D, D), bf16), dma(()), dma((2, 2)), dma((2,)), dma((J,)), dma((J,)), dma((J,)), dma((J,)),
            dma((A, B - 1)), dma((A, B - 1)), dma((A - 1,)), dma((A - 1,)),
        ],
        compiler_params=pltpu.CompilerParams(
            collective_id=3, has_side_effects=True, vmem_limit_bytes=64 * 1024 * 1024 - 65536
        ),
        name="feed_forward",
    )(middle, branch, attn, g, vectors, b_fc1.reshape(J, 1, W), w4, w1, w2)


class RowSum:
    @staticmethod
    def scratch(U, r, W, A, B, cores, last=bf16):
        dma = pltpu.SemaphoreType.DMA
        shapes = [
            pltpu.VMEM((U, B - 1, A, r, W), bf16), pltpu.VMEM((U, A - 1, r, W), bf16),
            pltpu.VMEM((U, A - 1, r, W), bf16), pltpu.VMEM((U, r, W), last), pltpu.VMEM((U, r, W), last),
            dma((U, B - 1)), dma((U, B - 1)), dma((U, A - 1)), dma((U, A - 1)), dma((U,)), dma((U,)),
        ]
        if cores:
            shapes += [
                pltpu.VMEM((U, A * B, r, W), bf16), pltpu.VMEM((U, B - 1, A, r, W), bf16), dma((U,)), dma((U,)),
            ]
        return shapes

    def __init__(self, at, s, peer, refs, grad=None, half=None):
        self.at, self.s, self.peer = at, s, peer
        self.grad, self.half = grad, half
        self.yr, self.zs, self.zr, self.xs, self.xr = refs[:5]
        self.yss, self.yrs, self.zss, self.zrs, self.xss, self.xrs = refs[5:11]
        if grad is not None:
            self.cr, self.ys, self.css, self.crs = refs[11:]

    def c_copy(self, u):
        return remote(
            self.grad.at[u, :, 1 - self.at.c], self.cr.at[u], self.css.at[u], self.crs.at[u], self.at.sibling()
        )

    def y_source(self, u, m):
        return self.ys.at[u, m]

    def y_copy(self, u, m):
        src = self.y_source(u, m)
        return remote(src, self.yr.at[u, m], self.yss.at[u, m], self.yrs.at[u, m], self.at.at_b(m + 1))

    def z_copy(self, u, k):
        return remote(self.zs.at[u, k], self.zr.at[u, k], self.zss.at[u, k], self.zrs.at[u, k], self.at.at_a(k + 1))

    def x_copy(self, u):
        return remote(self.xs.at[u], self.xr.at[u], self.xss.at[u], self.xrs.at[u], self.peer)

    def chip(self, u, a, b):
        j = a * self.at.B + b
        return add32(self.grad[u, j, self.at.c], self.cr[u, j])

    def own(self, u, a):
        base = self.chip(u, a, self.at.b) if self.half is None else self.half(u, a)
        return add32(base, *[self.yr[u, m, a] for m in range(self.at.B - 1)])

    def send_y(self, u):
        self.c_copy(u).wait()
        for m in range(self.at.B - 1):
            b = lax.rem(self.at.b + m + 1, self.at.B)
            for a in range(self.at.A):
                self.ys[u, m, a] = self.chip(u, a, b).astype(bf16)
            self.y_copy(u, m).start()

    def send_z(self, u):
        for m in range(self.at.B - 1):
            self.y_copy(u, m).wait()
        for k in range(self.at.A - 1):
            self.zs[u, k] = self.own(u, lax.rem(self.at.a + k + 1, self.at.A)).astype(bf16)
            self.z_copy(u, k).start()

    def send_x(self, u):
        for k in range(self.at.A - 1):
            self.z_copy(u, k).wait()
        total = add32(self.own(u, self.at.a), *[self.zr[u, k] for k in range(self.at.A - 1)])
        if self.s != 2:
            return total
        self.xs[u] = total.astype(self.xs.dtype)
        self.x_copy(u).start()
        return None

    def finish(self, u):
        self.x_copy(u).wait()
        return add32(self.xs[u], self.xr[u])


def attention_and_sums(
    qkv, kvr, d_attn, lse, hidden, tokens, vectors, d_middle, w_qkv, half_fc1, grad_proj, sum_fc2, sums, bias_fc1, lf, w_ada, n, s
):
    T, D = tokens.shape
    FH = half_fc1.shape[-1]
    FF = 2 * FH if s == 2 else FH
    A, B = grid_of(n)
    J, r1, r2 = A * B, D // n, FF // n
    GW, LAGZ = 256, 3
    U = D // GW
    F = FH // U
    E = 6 * D
    RB = min(T, 64)
    rows_a = D // n
    m_bias = [2 * D // n, D // n, FF // n, D // n]
    starts = [0, 2 * D, 3 * D, 3 * D + FF]
    NBIAS = 4 * D + FF
    blocks = [max(v, 128) for v in m_bias]
    offs = [sum(blocks[:i]) for i in range(4)]
    M = sum(blocks)
    nq = len(RowSum.scratch(U, r1, 3 * GW, A, B, True))
    nf = len(RowSum.scratch(U, r1, F, A, B, False))

    def kern(*refs):
        it = iter(refs)

        def take(count):
            return [next(it) for _ in range(count)]

        qkv_ref, kvr_ref = take(2)
        e_ref, lse_ref, h_ref, tok_ref, sc_ref, dmid_ref, w_ref, f1_ref, gp_ref, f2_ref, sum_ref, bf_ref, lf_ref, wa_ref = take(14)
        gt_ref, oq_ref, op_ref, o1_ref, o2_ref, gw_ref, gb_ref, dl_ref, bo_ref = take(9)
        h1t, dqg, kvl, kvs, kvr, dg, gq, wq, f1o, x2 = take(10)
        dh1 = gt_ref
        wsem, fsem, kss, krs, x2s, x2r = take(6)
        scr_q, scr_p, scr_f = take(nq), take(nq), take(nf)
        dx, dm, lp, bsum, bx, bsx = take(6)
        asend, arecv, lsend, lrecv, bsend, brecv, xsend, xrecv = take(8)

        at = Place(n)
        me, x = at.me, lax.axis_index("seq")
        peers = fsdp_peers(n, me)

        def seq_dev(k):
            return {"seq": lax.rem(x + k, s)}

        greet([{"fsdp": p} for p in peers] + [seq_dev(k) for k in range(1, s)])
        other = seq_dev(1)
        sq = RowSum(at, s, other, scr_q, grad=gq)
        sp = RowSum(at, s, other, scr_p, grad=gp_ref)
        sf = RowSum(at, s, other, scr_f, half=lambda u, a: f1o[u, a])

        def f_source(u, m):
            b = lax.rem(at.b + m + 1, B)
            return f1_ref.at[:, b, :, pl.ds(pl.multiple_of(u * F, F), F)]

        sf.y_source = f_source
        own_f = [
            pltpu.make_async_copy(f1_ref.at[:, at.b, :, pl.ds(u * F, F)], f1o.at[u], fsem.at[u]) for u in range(U)
        ]
        spans = [pl.ds(2 * D, 4 * D), pl.ds(0, 2 * D)]

        def mod_x(i):
            sl = dx.at[x, :, spans[i]]
            return [remote(sl, sl, xsend.at[i, k - 1], xrecv.at[i, k - 1], seq_dev(k)) for k in range(1, s)]

        def mod_all(i):
            dm[me, :, spans[i]] = jnp.sum(dx[:, :, spans[i]], axis=0).astype(bf16).astype(f32)
            sl = dm.at[me, :, spans[i]]
            out = [remote(sl, sl, asend.at[i, k], arecv.at[i, k], {"fsdp": p}) for k, p in enumerate(peers)]
            for c in out:
                c.start()
            return out

        def bias_span(p, i):
            lo = starts[i] + ((p * m_bias[i]) // blocks[i]) * blocks[i]
            return pl.ds(pl.multiple_of(lo, 128), blocks[i])

        def bias_out(lo, hi):
            out = []
            for i in range(lo, hi):
                at_i = pl.ds(offs[i], blocks[i])
                bx[me, :, at_i] = bsum[:, bias_span(me, i)]
                for k, p in enumerate(peers):
                    dst = bx.at[me, :, at_i]
                    out.append(remote(bsum.at[:, bias_span(p, i)], dst, bsend.at[i, k], brecv.at[i, k], {"fsdp": p}))
            for c in out:
                c.start()
            return out

        for i, row in enumerate((3, 0, 1, 2)):
            dx[x, :, (i + 2) * D : (i + 3) * D] = sum_ref[row : row + 1, :]
        early_x = mod_x(0)
        for c in early_x:
            c.start()
        bsum[:, starts[1] : starts[1] + D] = sum_ref[5:6, :]
        bsum[:, starts[2] : starts[2] + FF] = bf_ref[...]
        bsum[:, starts[3] : starts[3] + D] = sum_ref[4:5, :]
        sp.c_copy(0).start()
        for u in range(U):
            for m in range(B - 1):
                sf.y_copy(u, m).start()
        early_bias = bias_out(1, 4)
        if s == 2:
            x2_copy = remote(f2_ref, x2, x2s, x2r, other)
            x2_copy.start()
        for o in own_f:
            o.start()

        def h_copy(i):
            k = i % 3
            return pltpu.make_async_copy(
                h_ref.at[:, pl.ds(i * GW, GW)], dg.at[:, pl.ds(k * GW, GW)], wsem.at[k]
            )

        for i in range(min(U, 3)):
            h_copy(i).start()
        for i in range(U):
            h_copy(i).wait()
            k = i % 3
            h1t[i * GW : (i + 1) * GW, :] = dg[:, k * GW : (k + 1) * GW].T
            if i + 3 < U:
                h_copy(i + 3).start()
        dh1[...] = jnp.zeros_like(dh1)
        for o in own_f:
            o.wait()
        for c in early_x:
            c.wait()
        early_all = mod_all(0)

        def w_copy(u, i):
            lo = pl.multiple_of(i * D + u * GW, GW)
            return pltpu.make_async_copy(w_ref.at[:, pl.ds(lo, GW)], wq.at[:, pl.ds(i * GW, GW)], wsem.at[i])

        def kv_copy(u, k):
            return remote(kvs.at[u, k - 1], kvr.at[u, k - 1], kss.at[u, k - 1], krs.at[u, k - 1], seq_dev(s - k))

        def attend(u):
            slot = lax.rem(u, 2)
            for o in range(GW // 128):
                pair = u * (GW // 128) + o
                cols, k_cols, v_cols = [pl.ds(pl.multiple_of(lo + pair * 128, 128), 128) for lo in (0, D, 2 * D)]
                here = slice(o * 128, o * 128 + 128)
                qv, e = qkv_ref[:, cols] * bf16(HD**-0.5), e_ref[:, cols]
                ks = [qkv_ref[:, k_cols]] + [kvr_ref[k, :, cols] for k in range(s - 1)]
                vs = [qkv_ref[:, v_cols]] + [kvr_ref[k, :, k_cols] for k in range(s - 1)]
                dqt, dks, dvs = None, [None] * s, [None] * s
                for h in range(2):
                    qh, eh = pick(qv, h), pick(e, h)
                    total = lse_ref[pair, h : h + 1, :]
                    probs, dprobs, cross = [], [], None
                    for j in range(s):
                        p = jnp.exp(nt(ks[j], qh) - total)
                        dp = nt(vs[j], eh)
                        part = (p * dp).sum(axis=0, keepdims=True)
                        cross = part if cross is None else cross + part
                        dv = nn(p.astype(bf16), eh)
                        dvs[j] = dv if dvs[j] is None else dvs[j] + dv
                        probs.append(p)
                        dprobs.append(dp)
                    for j in range(s):
                        ds = (probs[j] * (dprobs[j] - cross)).astype(bf16)
                        dk = nn(ds, qh)
                        dks[j] = dk if dks[j] is None else dks[j] + dk
                        t = tn(pick(ks[j], h), ds)
                        dqt = t if dqt is None else dqt + t
                dqg[slot, :, here] = (dqt * (HD**-0.5)).T.astype(bf16)
                kvl[slot, 0, :, here] = dks[0]
                kvl[slot, 1, :, here] = dvs[0]
                for j in range(1, s):
                    kvs[u, j - 1, 0, :, here] = dks[j].astype(bf16)
                    kvs[u, j - 1, 1, :, here] = dvs[j].astype(bf16)
            for k in range(1, s):
                kv_copy(u, k).start()

        def project(u):
            slot = lax.rem(u, 2)
            for k in range(1, s):
                kv_copy(u, k).wait()
            dg[:, :GW] = dqg[slot]
            for i in range(2):
                lo = (i + 1) * GW
                dg[:, lo : lo + GW] = add32(kvl[slot, i], *[kvr[u, k, i] for k in range(s - 1)]).astype(bf16)
            part = 256 // (2 * r1)
            for i in range(D // 256):
                g = nn(h1t[i * 256 : (i + 1) * 256, :], dg[...]).astype(bf16)
                gq[u, i * part : (i + 1) * part] = g.reshape(part, 2, r1, 3 * GW)
            sq.c_copy(u).start()
            here = pl.ds(pl.multiple_of(u * GW, GW), GW)
            bsum[:, here] = jnp.sum(dg[:, :GW].astype(f32), axis=0, keepdims=True)
            there = pl.ds(pl.multiple_of(D + u * GW, GW), GW)
            bsum[:, there] = jnp.sum(dg[:, 2 * GW :].astype(f32), axis=0, keepdims=True)
            for i in range(3):
                w_copy(u, i).wait()
            dh1[...] += nt(dg[...], wq[...])

        def step(i, _):
            @pl.when(i < U)
            def _():
                attend(i)

            @pl.when(jnp.logical_and(i >= 1, i <= U))
            def _():
                project(i - 1)

            @pl.when(i < U)
            def _():
                for k in range(3):
                    w_copy(i, k).start()

            @pl.when(i == 0)
            def _():
                sp.send_y(0)

            @pl.when(i < U)
            def _():
                sf.send_z(i)

            @pl.when(i >= 2)
            def _():
                sq.send_y(i - 2)

            @pl.when(i == LAGZ - 1)
            def _():
                sp.send_z(0)

            @pl.when(i >= LAGZ)
            def _():
                sq.send_z(i - LAGZ)

            return 0

        lax.fori_loop(0, U + 2, step, 0)

        sums = [jnp.zeros((1, D), f32), jnp.zeros((1, D), f32)]
        scale1 = sc_ref[5:6, :]

        def back(i, carry):
            rows = pl.ds(pl.multiple_of(i * RB, RB), RB)
            normed, rscale = normalize(tok_ref[rows, :].astype(f32))
            dh = dh1[rows, :]
            up = dh * (1.0 + scale1)
            gt_ref[rows, :] = dmid_ref[rows, :] + rscale * (
                up
                - jnp.mean(up, axis=-1, keepdims=True)
                - normed * jnp.mean(up * normed, axis=-1, keepdims=True)
            )
            return (
                carry[0] + jnp.sum(dh, axis=0, keepdims=True),
                carry[1] + jnp.sum(dh * normed, axis=0, keepdims=True),
            )

        shift1_sum, scale1_sum = lax.fori_loop(0, T // RB, back, tuple(sums))
        dx[x, :, :D] = shift1_sum
        dx[x, :, D : 2 * D] = scale1_sum
        late_x = mod_x(1)
        for c in late_x:
            c.start()
        late_bias = bias_out(0, 1)
        for c in late_x:
            c.wait()
        late_all = mod_all(1)

        for u in range(U):
            if s == 2:
                sf.send_x(u)
            else:
                o1_ref[:, u * F : (u + 1) * F] = sf.send_x(u)
        for u in range(U + 2 - LAGZ, U):
            sq.send_z(u)
        for c in early_bias + late_bias:
            c.wait()
        bsx[x] = jnp.sum(bx[...], axis=0)
        bias_x = [remote(bsx.at[x], bsx.at[x], xsend.at[2, k - 1], xrecv.at[2, k - 1], seq_dev(k)) for k in range(1, s)]
        for c in bias_x:
            c.start()
        if s == 2:
            sp.send_x(0)
        else:
            op_ref[...] = sp.send_x(0)
        for c in early_all + late_all:
            c.wait()
        dmod = dm[...].reshape(n, E).astype(bf16)
        lp[...] = nt(dmod, wa_ref[...]).reshape(n, 1, rows_a)
        dl_ref[me] = lp[me]
        lift = [remote(lp.at[p], dl_ref.at[me], lsend.at[k], lrecv.at[k], {"fsdp": p}) for k, p in enumerate(peers)]
        for c in lift:
            c.start()
        gw_ref[...] = tn(lf_ref[...].reshape(n, rows_a).astype(bf16), dmod)
        gb_ref[...] = jnp.sum(dm[...], axis=0)

        def put_q(u, value):
            for i in range(3):
                oq_ref[:, i * D + u * GW : i * D + (u + 1) * GW] = value[:, i * GW : (i + 1) * GW]

        for u in range(U):
            value = sq.send_x(u)
            if s != 2:
                put_q(u, value)
        if s == 2:
            x2_copy.wait()
            o2_ref[...] = add32(f2_ref[...], x2[...])
            for u in range(U):
                sf.x_copy(u).wait()
                for q in range(F // r2):
                    lo = 2 * (u * F + q * r2)
                    for k, got in ((x, sf.xs), (1 - x, sf.xr)):
                        cols = pl.ds(pl.multiple_of(lo + k * r2, 128), r2)
                        o1_ref[:, cols] = got[u, :, q * r2 : (q + 1) * r2]
            op_ref[...] = sp.finish(0)
            for u in range(U):
                put_q(u, sq.finish(u))
        else:
            o2_ref[...] = f2_ref[...].astype(f32)
        for c in bias_x:
            c.wait()
        bo_ref[...] = jnp.sum(bsx[...], axis=0)
        for c in lift:
            c.wait()

    vm, hbm = pl.BlockSpec(memory_space=pltpu.VMEM), pl.BlockSpec(memory_space=pl.ANY)
    sds, dma = jax.ShapeDtypeStruct, pltpu.SemaphoreType.DMA
    res = pl.pallas_call(
        kern,
        out_shape=[
            sds((T, D), f32), sds((r1, 3 * D), f32), sds((r1, D), f32), sds((r1, FF), f32), sds((r2, D), f32),
            sds((rows_a, E), f32), sds((1, E), f32), sds((n, 1, rows_a), f32), sds((1, M), f32),
        ],
        in_specs=[vm] * 4 + [hbm] + [vm] * 3 + [hbm, hbm] + [vm] * 6,
        out_specs=[vm] * 9,
        scratch_shapes=[
            pltpu.VMEM((D, T), bf16), pltpu.VMEM((2, T, GW), bf16),
            pltpu.VMEM((2, 2, T, GW), f32), pltpu.VMEM((U, s - 1, 2, T, GW), bf16),
            pltpu.VMEM((U, s - 1, 2, T, GW), bf16), pltpu.VMEM((T, 3 * GW), bf16),
            pltpu.VMEM((U, J, 2, r1, 3 * GW), bf16), pltpu.VMEM((D, 3 * GW), bf16),
            pltpu.VMEM((U, A, r1, F), bf16), pltpu.VMEM((r2, D), bf16),
            dma((3,)), dma((U,)), dma((U, s - 1)), dma((U, s - 1)), dma(()), dma(()),
        ]
        + RowSum.scratch(U, r1, 3 * GW, A, B, True)
        + RowSum.scratch(1, r1, D, A, B, True)
        + RowSum.scratch(U, r1, F, A, B, False, f32)
        + [
            pltpu.VMEM((s, 1, E), f32), pltpu.VMEM((n, 1, E), f32), pltpu.VMEM((n, 1, rows_a), f32),
            pltpu.VMEM((1, NBIAS), f32), pltpu.VMEM((n, 1, M), f32), pltpu.VMEM((s, 1, M), f32),
            dma((2, n - 1)), dma((2, n - 1)), dma((n - 1,)), dma((n - 1,)),
            dma((4, n - 1)), dma((4, n - 1)), dma((3, s - 1)), dma((3, s - 1)),
        ],
        compiler_params=pltpu.CompilerParams(
            collective_id=4, has_side_effects=True, vmem_limit_bytes=64 * 1024 * 1024 - 65536
        ),
        name="attention_and_sums",
    )(
        qkv, kvr, d_attn, lse, hidden, tokens, vectors, d_middle, w_qkv, half_fc1.reshape(A, B, r1, FH),
        grad_proj.reshape(1, J, 2, r1, D), sum_fc2, sums, bias_fc1, lf, w_ada,
    )
    grad_tokens, t_qkv, t_proj, t_fc1, t_fc2, t_ada, ada_sums, d_lifted, bias = res
    if s != 2:
        t_qkv, t_proj, t_fc1, t_fc2 = lax.psum((t_qkv, t_proj, t_fc1, t_fc2), "seq")
    me = lax.axis_index("fsdp")
    biases = []
    for width, wide, off in zip(m_bias, blocks, offs):
        biases.append(lax.dynamic_slice_in_dim(bias[0, off : off + wide], (me * width) % wide, width))
    return grad_tokens, t_qkv, t_proj, t_fc1, t_fc2, t_ada, ada_sums, d_lifted, biases


def on_device(
    tokens,
    condition,
    w_ada,
    b_ada,
    w_qkv,
    b_qv,
    w_proj,
    b_proj,
    w_fc1,
    b_fc1,
    w_fc2,
    b_fc2,
    cotangent,
):
    n, s = lax.axis_size("fsdp"), lax.axis_size("seq")
    width = tokens.shape[-1]

    lifted, silu_back = jax.vjp(jax.nn.silu, condition.astype(f32))
    lifted_q = lifted.astype(bf16).astype(f32).reshape(n, 1, width // n)
    qkv, kvr, hidden_one, attn, lse, branch, middle, vectors, fc1_b, lf, w4, fc1_w, fc2_w = forward_attention(
        lifted_q, w_ada, [b_qv, b_proj, b_fc1, b_fc2, b_ada], tokens[0], w_qkv, w_proj, w_fc1, w_fc2, n, s
    )
    result, d_middle, d_attn, sums, bias_fc1, grad_proj, half_fc1, sum_fc2 = feed_forward(
        middle, branch, attn, cotangent[0], vectors, fc1_b, w4, fc1_w, fc2_w, n, s
    )
    grad_input, total_qkv, total_proj, total_fc1, total_fc2, total_ada, sums_ada, d_lifted, total_bias = (
        attention_and_sums(
            qkv, kvr, d_attn, lse, hidden_one, tokens[0], vectors, d_middle, w4, half_fc1,
            grad_proj, sum_fc2, sums, bias_fc1.reshape(1, -1), lf, w_ada, n, s,
        )
    )
    share = b_ada.shape[0]
    total_bada = lax.dynamic_slice_in_dim(sums_ada[0], lax.axis_index("fsdp") * share, share)
    grad_condition = silu_back(d_lifted.reshape(1, width))[0]
    total_bqv, total_bproj, total_bfc1, total_bfc2 = total_bias
    return (
        result[None],
        grad_input[None],
        grad_condition,
        total_ada,
        total_bada,
        total_qkv,
        total_bqv,
        total_proj,
        total_bproj,
        total_fc1,
        total_bfc1,
        total_fc2,
        total_bfc2,
    )


def solution(mesh):
    weights = (P("fsdp", None), P("fsdp")) * 5
    return jax.shard_map(
        on_device,
        mesh=mesh,
        in_specs=(P("fsdp", "seq", None), P("fsdp", None)) + weights + (P("fsdp", "seq", None),),
        out_specs=(P("fsdp", "seq", None), P("fsdp", "seq", None), P("fsdp", None)) + weights,
        check_vma=False,
    )
```
